32 devices in a mesh: dp: 16 (over z, y, x), rep: 2 (over core).
Axes of the slice: x: 2, y: 2, z: 4, core: 2. Of those that a mesh axis runs over, the one named last changes fastest.
Arguments:
- long_clips: bfloat16 [2, 32, 1024, 768], P(None, ('dp', 'rep')), may hold values from -6 to 6
- short_clips: bfloat16 [2, 128, 64, 768], P(None, ('dp', 'rep')), may hold values from -6 to 6
- long_index: int32 [2, 32, 1024], P(None, ('dp', 'rep')), may hold values from 0 to 6271, as said below
- short_index: int32 [2, 128, 64], P(None, ('dp', 'rep')), may hold values from 0 to 6271, as said below
- long_length: int32 [2, 32], P(None, ('dp', 'rep')), may hold values from 128 to 1024, as said below
- short_length: int32 [2, 128], replicated, may hold values from 0 to 64, as said below
- destination: int32 [2, 128], replicated, may hold values from 0 to 15, as said below
- long_target: bfloat16 [2, 32, 1024, 1024], P(None, ('dp', 'rep')), may hold values from -6 to 6
- short_target: bfloat16 [2, 128, 64, 1024], P(None, ('dp', 'rep')), may hold values from -6 to 6
- position: bfloat16 [6272, 768], replicated, may hold values from -3 to 3
- mixer_gain: float32 [768], replicated, may hold values from 0.5 to 1.5
- mixer_shift: float32 [768], replicated, may hold values from -1 to 1
- heads_weight: bfloat16 [768, 2304], replicated, may hold values from -0.21875 to 0.21875
- query_bias: float32 [768], replicated, may hold values from -1 to 1
- value_bias: float32 [768], replicated, may hold values from -1 to 1
- out_weight: bfloat16 [768, 768], replicated, may hold values from -1.25 to 1.25
- out_bias: float32 [768], replicated, may hold values from -1 to 1
- dense_gain: float32 [768], replicated, may hold values from 0.5 to 1.5
- dense_shift: float32 [768], replicated, may hold values from -1 to 1
- up_weight: bfloat16 [768, 3072], replicated, may hold values from -0.21875 to 0.21875
- up_bias: float32 [3072], replicated, may hold values from -1 to 1
- down_weight: bfloat16 [3072, 768], replicated, may hold values from -0.109375 to 0.109375
- down_bias: float32 [768], replicated, may hold values from -1 to 1
- align_weight: bfloat16 [768, 1024], replicated, may hold values from -0.21875 to 0.21875
- align_bias: float32 [1024], replicated, may hold values from -1 to 1
Outputs:
- long_output: bfloat16 [2, 32, 1024, 768], P(None, ('dp', 'rep'))
- short_output: bfloat16 [2, 64, 64, 768], P(None, ('dp', 'rep'))
- long_grad: bfloat16 [2, 32, 1024, 768], P(None, ('dp', 'rep'))
- short_grad: bfloat16 [2, 128, 64, 768], P(None, ('dp', 'rep'))
- position_grad: float32 [6272, 768], P('dp')
- mixer_gain_grad: float32 [768], P('dp')
- mixer_shift_grad: float32 [768], P('dp')
- heads_weight_grad: float32 [768, 2304], P('dp')
- query_bias_grad: float32 [768], P('dp')
- value_bias_grad: float32 [768], P('dp')
- out_weight_grad: float32 [768, 768], P('dp')
- out_bias_grad: float32 [768], P('dp')
- dense_gain_grad: float32 [768], P('dp')
- dense_shift_grad: float32 [768], P('dp')
- up_weight_grad: float32 [768, 3072], P('dp')
- up_bias_grad: float32 [3072], P('dp')
- down_weight_grad: float32 [3072, 768], P('dp')
- down_bias_grad: float32 [768], P('dp')
- align_weight_grad: float32 [768, 1024], P('dp')
- align_bias_grad: float32 [1024], P('dp')
The draws below stay inside these ranges and needn't reach their ends.
Inputs may be any that keep to these rules, and one draw needn't show every extreme that they name: `long_length`: 1024 is reached in every draw. `short_length`: 0 marks an empty slot. Entry (s * 2 + r) * 4 + j of a micro-batch's row is home slot j of the device with dp index s and rep index r; a live clip there goes to balanced slot j mod 2 of the device with dp index destination and rep index r. No two live clips meet in one balanced slot, a device sends at most one live clip to any one dp index in a micro-batch, and in every micro-batch some device receives 2 live clips. `destination`: set for empty slots too. `long_index`: the entries of one clip's row are distinct. `short_index`: the entries of one clip's row are distinct.
All inputs are finite; a program needn't handle non-finite values.
Results may differ from the reference program's by a relative error of at most 0.0095.
Values may be sent and summed in bfloat16 or wider, within the bound.
A program may use at most 576 MiB of HBM per device.

```python
import jax
import jax.numpy as jnp
from jax import lax

D = 768
HEADS = 12
HEAD_DIM = 64
FF = 3072
TEACH = 1024
PATCHES = 6272
LONG_CAP = 1024
TILE = 64
SHORT_BAL = 2
MICRO = 2
SHORT_HOME = 4
GROUP = 16
COPIES = 2
CLIPS = 32


def draw_long_length(key, part):
    span = LONG_CAP - LONG_CAP // 8
    first = jax.random.randint(jax.random.fold_in(key, 1), (MICRO, CLIPS), 0, span + 1)
    second = jax.random.randint(jax.random.fold_in(key, 2), (MICRO, CLIPS), 0, span + 1)
    length = LONG_CAP // 8 + first * second // span
    return length.at[0, 0].set(LONG_CAP).astype(jnp.int32)


def plan_micro(key):
    ids = jnp.arange(GROUP)
    scores = jax.random.permutation(jax.random.fold_in(key, 1), GROUP)
    scores = jnp.where(ids == GROUP // 2, -2, jnp.where(ids == 1, -1, scores))
    chosen = jnp.argsort(scores, stable=True)[:SHORT_HOME]
    offsets = chosen[jax.random.permutation(jax.random.fold_in(key, 2), SHORT_HOME)]
    pick = jax.random.randint(jax.random.fold_in(key, 3), (GROUP, SHORT_BAL, COPIES), 0, 3)
    forced = 1 + jax.random.randint(jax.random.fold_in(key, 4), (GROUP, SHORT_BAL, COPIES), 0, 2)
    pick = jnp.where(ids[:, None, None] == 0, forced, pick)
    slots = jnp.arange(SHORT_HOME)
    target = (ids[:, None] + offsets[None, :]) % GROUP
    wanted = pick[target, (slots % SHORT_BAL)[None, :]]
    live = wanted == (1 + slots // SHORT_BAL)[None, :, None]
    sizes = jnp.minimum(TILE, jax.random.randint(jax.random.fold_in(key, 5), (GROUP, SHORT_HOME, COPIES), 1, TILE + TILE // 2 + 1))
    length = jnp.where(live, sizes, 0)
    spread = jnp.broadcast_to(target[:, :, None], live.shape)
    return (jnp.transpose(length, (0, 2, 1)).reshape(-1), jnp.transpose(spread, (0, 2, 1)).reshape(-1))


def plan_short(key):
    base = jax.random.fold_in(key, 97)

    def single(micro):
        return plan_micro(jax.random.fold_in(base, micro))
    return jax.vmap(single)(jnp.arange(MICRO))


def draw_short_length(key, part):
    return plan_short(key)[0].astype(jnp.int32)


def draw_destination(key, part):
    return plan_short(key)[1].astype(jnp.int32)


def draw_long_index(key, part):
    subkeys = jax.random.split(key, MICRO * CLIPS)

    def single(sub):
        return jax.random.permutation(sub, PATCHES)[:LONG_CAP]
    return jax.vmap(single)(subkeys).reshape(MICRO, CLIPS, LONG_CAP).astype(jnp.int32)


def draw_short_index(key, part):
    subkeys = jax.random.split(key, MICRO * CLIPS * SHORT_HOME)

    def single(sub):
        return jax.random.permutation(sub, PATCHES)[:TILE]
    return jax.vmap(single)(subkeys).reshape(MICRO, CLIPS * SHORT_HOME, TILE).astype(jnp.int32)


def level_of(stream_key, extent, pieces, least, top_value):
    factor_of, own = 1.0, jax.random.fold_in(stream_key, 6)
    for dim, blocks in pieces:
        steps = jnp.exp(jax.random.uniform(jax.random.fold_in(own, dim), (blocks,), jnp.float32, least / len(pieces), top_value / len(pieces)))
        factor_of = factor_of * jnp.repeat(steps, extent[dim] // blocks).reshape([-1 if axis == dim else 1 for axis in range(len(extent))])
    return factor_of


def centred(own_key, extent, scale, most, cuts=(), held_as=jnp.bfloat16):
    array = jax.random.normal(own_key, extent, jnp.float32) * scale
    if len(cuts) > 0:
        array = level_of(own_key, extent, cuts, -0.22, 0.18) * array
    return jnp.clip(array, min=-most, max=most).astype(held_as)


def setup_inputs(seed: int = 0) -> dict:
    seeds = jax.random.split(jax.random.key(seed), 26)
    return {
        "long_clips": centred(seeds[0], (MICRO, CLIPS, LONG_CAP, D), 1.0, 6.0, ((1, 32),)),
        "short_clips": centred(seeds[1], (MICRO, CLIPS * SHORT_HOME, TILE, D), 1.0, 6.0, ((1, 32),)),
        "long_index": draw_long_index(jax.random.fold_in(seeds[25], 71), 0),
        "short_index": draw_short_index(jax.random.fold_in(seeds[25], 71), 0),
        "long_length": draw_long_length(jax.random.fold_in(seeds[25], 71), 0),
        "short_length": draw_short_length(jax.random.fold_in(seeds[25], 71), 0),
        "destination": draw_destination(jax.random.fold_in(seeds[25], 71), 0),
        "long_target": centred(seeds[7], (MICRO, CLIPS, LONG_CAP, TEACH), 1.0, 6.0, ((1, 32),)),
        "short_target": centred(seeds[8], (MICRO, CLIPS * SHORT_HOME, TILE, TEACH), 1.0, 6.0, ((1, 32),)),
        "position": centred(seeds[9], (PATCHES, D), 0.5, 3.0),
        "mixer_gain": jnp.clip(1.0 + 0.1 * jax.random.normal(seeds[10], (D,), jnp.float32), 0.5, 1.5),
        "mixer_shift": centred(seeds[11], (D,), 0.2, 1.0, (), jnp.float32),
        "heads_weight": centred(seeds[12], (D, 3 * D), D ** -0.5, 0.21875),
        "query_bias": centred(seeds[13], (D,), 0.2, 1.0, (), jnp.float32),
        "value_bias": centred(seeds[14], (D,), 0.2, 1.0, (), jnp.float32),
        "out_weight": centred(seeds[15], (D, D), (D // 32) ** -0.5, 1.25),
        "out_bias": centred(seeds[16], (D,), 0.2, 1.0, (), jnp.float32),
        "dense_gain": jnp.clip(1.0 + 0.1 * jax.random.normal(seeds[17], (D,), jnp.float32), 0.5, 1.5),
        "dense_shift": centred(seeds[18], (D,), 0.2, 1.0, (), jnp.float32),
        "up_weight": centred(seeds[19], (D, FF), D ** -0.5, 0.21875),
        "up_bias": centred(seeds[20], (FF,), 0.2, 1.0, (), jnp.float32),
        "down_weight": centred(seeds[21], (FF, D), FF ** -0.5, 0.109375),
        "down_bias": centred(seeds[22], (D,), 0.2, 1.0, (), jnp.float32),
        "align_weight": centred(seeds[23], (D, TEACH), D ** -0.5, 0.21875),
        "align_bias": centred(seeds[24], (TEACH,), 0.2, 1.0, (), jnp.float32),
    }


@jax.custom_vjp
def low(v):
    return lax.optimization_barrier(v.astype(jnp.bfloat16)).astype(jnp.float32)

@jax.custom_vjp
def low_back(v):
    return v

def low_keep(v):
    return (low(v), None)

def low_pass(kept, grad):
    return (grad,)

def back_keep(v):
    return (v, None)

def back_low(kept, grad):
    return (low(grad),)
low.defvjp(low_keep, low_pass)
low_back.defvjp(back_keep, back_low)
EPS = 1e-06
MASKED = -1000000000.0

def layer_norm(values, gain, shift):
    mean = lax.optimization_barrier(jnp.mean(values, axis=-1, keepdims=True))
    centered = values - mean
    spread = lax.optimization_barrier(jnp.mean(centered * centered, axis=-1, keepdims=True))
    return centered * lax.rsqrt(spread + EPS) * gain + shift

def matmul(left, right):
    return jnp.dot(left, right, precision=lax.Precision.HIGHEST)

def clip_block(params, rows, index, target, length):
    position, mixer_gain, mixer_shift, heads_weight, query_bias, value_bias, out_weight, out_bias, dense_gain, dense_shift, up_weight, up_bias, down_weight, down_bias, align_weight, align_bias = params
    count = rows.shape[0]
    valid = jnp.arange(count) < length
    start = rows + position[index]
    normed = low(layer_norm(start, mixer_gain, mixer_shift))
    triple = matmul(normed, heads_weight) + jnp.concatenate([query_bias, jnp.zeros_like(query_bias), value_bias])
    triple = low_back(low(triple))
    query = triple[:, :D].reshape(count, HEADS, HEAD_DIM)
    keys = triple[:, D:2 * D].reshape(count, HEADS, HEAD_DIM)
    values = triple[:, 2 * D:].reshape(count, HEADS, HEAD_DIM)
    scores = jnp.einsum('qhe,khe->hqk', query, keys, precision=lax.Precision.HIGHEST) * HEAD_DIM ** (-0.5)
    scores = low_back(jnp.where(valid[None, None, :], scores, MASKED))
    probs = low(jax.nn.softmax(scores, axis=-1))
    attended = jnp.einsum('hqk,khe->qhe', probs, values, precision=lax.Precision.HIGHEST).reshape(count, D)
    attended = low_back(low(attended))
    middle = start + low_back(matmul(attended, out_weight) + out_bias)
    dense = low(layer_norm(middle, dense_gain, dense_shift))
    upper = low_back(matmul(dense, up_weight) + up_bias)
    hidden = low(jax.nn.gelu(upper, approximate=False))
    result = low_back(middle + low_back(matmul(hidden, down_weight) + down_bias))
    projected = low_back(matmul(low(result), align_weight) + align_bias)
    diff = projected - target
    loss = 0.5 * jnp.sum(jnp.where(valid[:, None], diff * diff, 0.0))
    return (loss, jnp.where(valid[:, None], result, 0.0))

def reference(long_clips, short_clips, long_index, short_index, long_length, short_length, destination, long_target, short_target, position, mixer_gain, mixer_shift, heads_weight, query_bias, value_bias, out_weight, out_bias, dense_gain, dense_shift, up_weight, up_bias, down_weight, down_bias, align_weight, align_bias):
    params = tuple((item.astype(jnp.float32) for item in (position, mixer_gain, mixer_shift, heads_weight, query_bias, value_bias, out_weight, out_bias, dense_gain, dense_shift, up_weight, up_bias, down_weight, down_bias, align_weight, align_bias)))
    long_rows = long_clips.astype(jnp.float32).reshape(MICRO * CLIPS, LONG_CAP, D)
    short_rows = short_clips.astype(jnp.float32).reshape(MICRO * CLIPS, SHORT_HOME, TILE, D)
    long_idx = long_index.reshape(MICRO * CLIPS, LONG_CAP)
    short_idx = short_index.reshape(MICRO * CLIPS, SHORT_HOME, TILE)
    long_teach = long_target.astype(jnp.float32).reshape(MICRO * CLIPS, LONG_CAP, TEACH)
    short_teach = short_target.astype(jnp.float32).reshape(MICRO * CLIPS, SHORT_HOME, TILE, TEACH)
    long_len = long_length.reshape(MICRO * CLIPS)
    short_len = short_length.reshape(MICRO * CLIPS, SHORT_HOME)

    def total(weights, long_in, short_in):

        def long_step(carry, item):
            rows, index, teach, length = item
            loss, out = jax.checkpoint(clip_block)(weights, rows, index, teach, length)
            return (carry + loss, out)

        def short_step(carry, item):
            rows, index, teach, length = item
            grouped = jax.vmap(clip_block, in_axes=(None, 0, 0, 0, 0))
            loss, out = jax.checkpoint(grouped)(weights, rows, index, teach, length)
            return (carry + jnp.sum(loss), out)
        long_loss, long_out = lax.scan(long_step, jnp.float32(0.0), (long_in, long_idx, long_teach, long_len))
        short_loss, short_out = lax.scan(short_step, jnp.float32(0.0), (short_in, short_idx, short_teach, short_len))
        return (long_loss + short_loss, (long_out, short_out))
    loss, pullback, outputs = jax.vjp(total, params, long_rows, short_rows, has_aux=True)
    param_grads, long_grad, short_grad = pullback(jnp.ones_like(loss))
    long_out, short_out = outputs
    short_out = short_out.reshape(MICRO, CLIPS * SHORT_HOME, TILE, D)
    slot = jnp.arange(CLIPS * SHORT_HOME)
    holder = slot // SHORT_HOME
    place = (destination * COPIES + (holder % COPIES)[None, :]) * SHORT_BAL + (slot % SHORT_HOME % SHORT_BAL)[None, :]
    micro_ids = jnp.broadcast_to(jnp.arange(MICRO)[:, None], place.shape)
    balanced = jnp.zeros((MICRO, CLIPS * SHORT_BAL, TILE, D), jnp.float32).at[micro_ids, place].add(short_out)
    return (long_out.reshape(MICRO, CLIPS, LONG_CAP, D).astype(jnp.bfloat16), balanced.astype(jnp.bfloat16), long_grad.reshape(MICRO, CLIPS, LONG_CAP, D).astype(jnp.bfloat16), short_grad.reshape(MICRO, CLIPS * SHORT_HOME, TILE, D).astype(jnp.bfloat16), param_grads[0], param_grads[1], param_grads[2], param_grads[3], param_grads[4], param_grads[5], param_grads[6], param_grads[7], param_grads[8], param_grads[9], param_grads[10], param_grads[11], param_grads[12], param_grads[13], param_grads[14], param_grads[15])
```

```python
from functools import partial

import jax
import jax.numpy as jnp
from jax import lax
from jax.sharding import PartitionSpec as P

HEADS = 12


EPS = 1e-06
MASKED = -1000000000.0
WEIGHT_NAMES = (
    "position",
    "mixer_gain",
    "mixer_shift",
    "heads_weight",
    "query_bias",
    "value_bias",
    "out_weight",
    "out_bias",
    "dense_gain",
    "dense_shift",
    "up_weight",
    "up_bias",
    "down_weight",
    "down_bias",
    "align_weight",
    "align_bias",
)


def layer_norm(values, gain, shift):
    mean = jnp.mean(values, axis=-1, keepdims=True)
    centered = values - mean
    spread = jnp.mean(centered * centered, axis=-1, keepdims=True)
    return centered * lax.rsqrt(spread + EPS) * gain + shift


def matmul(left, right):
    return jnp.dot(left, right, preferred_element_type=jnp.float32)


def outer_sum(left, right):
    return jnp.einsum("rd,rc->dc", left, right, preferred_element_type=jnp.float32)


def times_transpose(left, right):
    return jnp.einsum("rc,dc->rd", left, right, preferred_element_type=jnp.float32)


def allowed_mask(query_seg, key_seg, key_ok):
    return (query_seg[:, None] == key_seg[None, :]) & key_ok[None, :]


def attend_block(query, keys, values, allowed, scale):
    scores = jnp.einsum("qhe,khe->hqk", query, keys, preferred_element_type=jnp.float32) * scale
    scores = jnp.where(allowed[None], scores, MASKED)
    top = jnp.max(scores, axis=-1, keepdims=True)
    weights = jnp.exp(scores - top)
    total = jnp.sum(weights, axis=-1, keepdims=True)
    probs = (weights / total).astype(jnp.bfloat16)
    output = jnp.einsum("hqk,khe->qhe", probs, values, preferred_element_type=jnp.float32)
    return (output, (top + jnp.log(total))[..., 0])


def attend_back(query, keys, values, grad_out, logsum, allowed, scale):
    scores = jnp.einsum("qhe,khe->hqk", query, keys, preferred_element_type=jnp.float32) * scale
    scores = jnp.where(allowed[None], scores, MASKED)
    probs = jnp.exp(scores - logsum[..., None])
    grad_values = jnp.einsum(
        "hqk,qhe->khe", probs.astype(jnp.bfloat16), grad_out, preferred_element_type=jnp.float32
    )
    grad_probs = jnp.einsum("qhe,khe->hqk", grad_out, values, preferred_element_type=jnp.float32)
    inner = jnp.sum(probs * grad_probs, axis=-1, keepdims=True)
    grad_scores = (probs * (grad_probs - inner)).astype(jnp.bfloat16)
    grad_query = (
        jnp.einsum("hqk,khe->qhe", grad_scores, keys, preferred_element_type=jnp.float32) * scale
    )
    grad_keys = (
        jnp.einsum("hqk,qhe->khe", grad_scores, query, preferred_element_type=jnp.float32) * scale
    )
    return (grad_query, grad_keys, grad_values)


def attention_forward(query, keys, values, regions, scale):
    outputs = []
    sums = []
    for first, count, segment, key_ok, block in regions:
        keys_here = keys[first : first + count]
        values_here = values[first : first + count]
        for begin in range(0, count, block):
            allowed = allowed_mask(segment[begin : begin + block], segment, key_ok)
            output, logsum = attend_block(
                query[first + begin : first + begin + block], keys_here, values_here, allowed, scale
            )
            outputs.append(output)
            sums.append(logsum)
    return (jnp.concatenate(outputs, axis=0), sums)


def attention_backward(query, keys, values, grad_out, sums, regions, scale):
    query_parts = []
    key_parts = []
    value_parts = []
    block_number = 0
    for first, count, segment, key_ok, block in regions:
        keys_here = keys[first : first + count]
        values_here = values[first : first + count]
        key_total = jnp.zeros(keys_here.shape, jnp.float32)
        value_total = jnp.zeros(values_here.shape, jnp.float32)
        for begin in range(0, count, block):
            allowed = allowed_mask(segment[begin : begin + block], segment, key_ok)
            rows_from = first + begin
            grad_query, grad_keys, grad_values = attend_back(
                query[rows_from : rows_from + block],
                keys_here,
                values_here,
                grad_out[rows_from : rows_from + block],
                sums[block_number],
                allowed,
                scale,
            )
            block_number += 1
            query_parts.append(grad_query)
            key_total = key_total + grad_keys
            value_total = value_total + grad_values
        key_parts.append(key_total)
        value_parts.append(value_total)
    return (
        jnp.concatenate(query_parts, axis=0),
        jnp.concatenate(key_parts, axis=0),
        jnp.concatenate(value_parts, axis=0),
    )


def align_back(rows, teach, row_ok, weight, bias):
    projected = matmul(rows, weight) + bias
    grad_proj = jnp.where(row_ok[:, None], projected - teach.astype(jnp.float32), 0.0).astype(
        jnp.bfloat16
    )
    return (
        times_transpose(grad_proj, weight).astype(jnp.bfloat16),
        outer_sum(rows, grad_proj),
        jnp.sum(grad_proj.astype(jnp.float32), axis=0),
    )


def shards(
    long_clips,
    short_clips,
    long_index,
    short_index,
    long_length,
    short_length,
    destination,
    long_target,
    short_target,
    position,
    mixer_gain,
    mixer_shift,
    heads_weight,
    query_bias,
    value_bias,
    out_weight,
    out_bias,
    dense_gain,
    dense_shift,
    up_weight,
    up_bias,
    down_weight,
    down_bias,
    align_weight,
    align_bias,
):
    peers = lax.axis_size("dp")
    copies = lax.axis_size("rep")
    mine = lax.axis_index("dp")
    own_copy = lax.axis_index("rep")
    micros = long_clips.shape[0]
    long_rows = long_clips.shape[2]
    width = long_clips.shape[3]
    home_slots = short_clips.shape[1]
    tile = short_clips.shape[2]
    bal_slots = home_slots // 2
    short_rows = home_slots * tile
    head_dim = width // HEADS
    scale = head_dim ** (-0.5)
    long_block = min(512, long_rows)
    triple_bias = jnp.concatenate([query_bias, jnp.zeros_like(query_bias), value_bias])
    params = (
        position, mixer_gain, mixer_shift, heads_weight, query_bias, value_bias, out_weight, out_bias,
        dense_gain, dense_shift, up_weight, up_bias, down_weight, down_bias, align_weight, align_bias,
    )
    totals = {
        name: jnp.zeros(value.shape, jnp.float32) for name, value in zip(WEIGHT_NAMES, params)
    }
    slot_pick = jnp.arange(home_slots)[:, None] % bal_slots == jnp.arange(bal_slots)[None, :]
    long_seg = jnp.zeros((long_rows,), jnp.int32)
    short_seg = jnp.arange(short_rows) // tile
    long_outs = []
    short_homes = []
    long_grads = []
    short_grads = []
    send_maps = []
    recv_maps = []
    for micro in range(micros):
        group_dest = lax.dynamic_index_in_dim(
            destination[micro].reshape(peers, copies, home_slots), own_copy, 1, keepdims=False
        )
        group_len = lax.dynamic_index_in_dim(
            short_length[micro].reshape(peers, copies, home_slots), own_copy, 1, keepdims=False
        )
        own_dest = lax.dynamic_index_in_dim(group_dest, mine, 0, keepdims=False)
        own_len = lax.dynamic_index_in_dim(group_len, mine, 0, keepdims=False)
        send_maps.append((own_dest[None, :] == jnp.arange(peers)[:, None]) & (own_len[None, :] > 0))
        incoming = (group_dest == mine) & (group_len > 0)
        recv_maps.append(jnp.any(incoming[:, :, None] & slot_pick[None], axis=1))
        stacked = jnp.concatenate(
            [long_clips[micro, 0], short_clips[micro].reshape(short_rows, width)], axis=0
        )
        stacked_index = jnp.concatenate([long_index[micro, 0], short_index[micro].reshape(short_rows)])
        targets = jnp.concatenate(
            [long_target[micro, 0], short_target[micro].reshape(short_rows, -1)], axis=0
        )
        long_ok = jnp.arange(long_rows) < long_length[micro, 0]
        short_ok = (jnp.arange(tile)[None, :] < own_len[:, None]).reshape(short_rows)
        row_ok = jnp.concatenate([long_ok, short_ok])
        regions = (
            (0, long_rows, long_seg, long_ok, long_block),
            (long_rows, short_rows, short_seg, short_ok, short_rows),
        )
        total_rows = stacked.shape[0]
        start = stacked.astype(jnp.float32) + jnp.take(position, stacked_index, axis=0).astype(
            jnp.float32
        )
        mixed, mixer_back = jax.vjp(layer_norm, start, mixer_gain, mixer_shift)
        normed = mixed.astype(jnp.bfloat16)
        triple = (matmul(normed, heads_weight) + triple_bias).astype(jnp.bfloat16)
        query = triple[:, :width].reshape(total_rows, HEADS, head_dim)
        keys_all = triple[:, width : 2 * width].reshape(total_rows, HEADS, head_dim)
        values_all = triple[:, 2 * width :].reshape(total_rows, HEADS, head_dim)
        attended_full, sums = attention_forward(query, keys_all, values_all, regions, scale)
        attended = attended_full.reshape(total_rows, width).astype(jnp.bfloat16)
        middle = start + matmul(attended, out_weight) + out_bias
        dense_full, dense_back = jax.vjp(layer_norm, middle, dense_gain, dense_shift)
        dense = dense_full.astype(jnp.bfloat16)
        upper = matmul(dense, up_weight) + up_bias
        hidden_full, gelu_back = jax.vjp(partial(jax.nn.gelu, approximate=False), upper)
        hidden = hidden_full.astype(jnp.bfloat16)
        result = middle + matmul(hidden, down_weight) + down_bias
        shown = jnp.where(row_ok[:, None], result, 0.0).astype(jnp.bfloat16)
        long_outs.append(shown[:long_rows])
        short_homes.append(shown[long_rows:].reshape(home_slots, tile, width))
        grad_result, weight_term, bias_term = align_back(
            shown, targets, row_ok, align_weight, align_bias
        )
        totals["align_weight"] = totals["align_weight"] + weight_term
        totals["align_bias"] = totals["align_bias"] + bias_term
        totals["down_weight"] = totals["down_weight"] + outer_sum(hidden, grad_result)
        totals["down_bias"] = totals["down_bias"] + jnp.sum(grad_result.astype(jnp.float32), axis=0)
        grad_hidden = times_transpose(grad_result, down_weight)
        grad_upper = gelu_back(grad_hidden)[0].astype(jnp.bfloat16)
        totals["up_weight"] = totals["up_weight"] + outer_sum(dense, grad_upper)
        totals["up_bias"] = totals["up_bias"] + jnp.sum(grad_upper.astype(jnp.float32), axis=0)
        grad_dense = times_transpose(grad_upper, up_weight)
        grad_mid_norm, gain_term, shift_term = dense_back(grad_dense)
        totals["dense_gain"] = totals["dense_gain"] + gain_term
        totals["dense_shift"] = totals["dense_shift"] + shift_term
        grad_middle = grad_result.astype(jnp.float32) + grad_mid_norm
        grad_branch = grad_middle.astype(jnp.bfloat16)
        totals["out_weight"] = totals["out_weight"] + outer_sum(attended, grad_branch)
        totals["out_bias"] = totals["out_bias"] + jnp.sum(grad_branch.astype(jnp.float32), axis=0)
        grad_attended = (
            times_transpose(grad_branch, out_weight)
            .astype(jnp.bfloat16)
            .reshape(total_rows, HEADS, head_dim)
        )
        grad_query, grad_keys, grad_values = attention_backward(
            query, keys_all, values_all, grad_attended, sums, regions, scale
        )
        grad_triple = jnp.concatenate(
            [
                grad_query.reshape(total_rows, width),
                grad_keys.reshape(total_rows, width),
                grad_values.reshape(total_rows, width),
            ],
            axis=1,
        ).astype(jnp.bfloat16)
        totals["heads_weight"] = totals["heads_weight"] + outer_sum(normed, grad_triple)
        triple_sums = jnp.sum(grad_triple.astype(jnp.float32), axis=0)
        totals["query_bias"] = totals["query_bias"] + triple_sums[:width]
        totals["value_bias"] = totals["value_bias"] + triple_sums[2 * width :]
        grad_normed = times_transpose(grad_triple, heads_weight)
        grad_start_norm, gain_term, shift_term = mixer_back(grad_normed)
        totals["mixer_gain"] = totals["mixer_gain"] + gain_term
        totals["mixer_shift"] = totals["mixer_shift"] + shift_term
        grad_start = grad_middle + grad_start_norm
        totals["position"] = totals["position"].at[stacked_index].add(grad_start)
        grad_low = grad_start.astype(jnp.bfloat16)
        long_grads.append(grad_low[:long_rows])
        short_grads.append(grad_low[long_rows:].reshape(home_slots, tile, width))
    send = jnp.stack(
        [
            jnp.einsum("pj,jtd->ptd", m.astype(jnp.bfloat16), h)
            for m, h in zip(send_maps, short_homes)
        ],
        axis=1,
    )
    got = lax.all_to_all(send, "dp", split_axis=0, concat_axis=0, tiled=True)
    short_outs = [
        jnp.einsum("pb,ptd->btd", recv_maps[m].astype(jnp.bfloat16), got[:, m]) for m in range(micros)
    ]
    return (
        jnp.stack(long_outs)[:, None],
        jnp.stack(short_outs),
        jnp.stack(long_grads)[:, None],
        jnp.stack(short_grads),
    ) + combine(totals, copies)


def combine(totals, copies):
    shared = []
    for name in WEIGHT_NAMES:
        total = totals[name]
        if total.ndim == 1:
            shared.append(lax.psum_scatter(lax.psum(total, "rep"), "dp", scatter_dimension=0, tiled=True))
            continue
        peers = lax.axis_size("dp")
        rows = total.shape[0] // peers
        wide = total.astype(jnp.bfloat16)
        padded = -(-rows // (8 * copies)) * 8 * copies
        if padded != rows:
            wide = wide.reshape(peers, rows, -1)
            wide = jnp.pad(wide, ((0, 0), (0, padded - rows), (0, 0)))
            wide = wide.reshape(peers * padded, -1)
        piece = lax.psum_scatter(wide, ("dp", "rep"), scatter_dimension=0, tiled=True)
        piece = lax.all_gather(piece, "rep", axis=0, tiled=True)[:rows]
        shared.append(piece.astype(jnp.float32))
    return tuple(shared)


def solution(mesh):
    placed = (
        P(None, ("dp", "rep"), None, None),
        P(None, ("dp", "rep"), None, None),
        P(None, ("dp", "rep"), None),
        P(None, ("dp", "rep"), None),
        P(None, ("dp", "rep")),
        P(),
        P(),
        P(None, ("dp", "rep"), None, None),
        P(None, ("dp", "rep"), None, None),
        P(),
        P(),
        P(),
        P(),
        P(),
        P(),
        P(),
        P(),
        P(),
        P(),
        P(),
        P(),
        P(),
        P(),
        P(),
        P(),
    )
    return jax.shard_map(
        shards,
        mesh=mesh,
        in_specs=placed,
        out_specs=(
            P(None, ("dp", "rep"), None, None),
            P(None, ("dp", "rep"), None, None),
            P(None, ("dp", "rep"), None, None),
            P(None, ("dp", "rep"), None, None),
            P("dp", None),
            P("dp"),
            P("dp"),
            P("dp", None),
            P("dp"),
            P("dp"),
            P("dp", None),
            P("dp"),
            P("dp"),
            P("dp"),
            P("dp", None),
            P("dp"),
            P("dp", None),
            P("dp"),
            P("dp", None),
            P("dp"),
        ),
        check_vma=False,
    )
```

```python
from functools import partial

import jax
import jax.numpy as jnp
from jax import lax
from jax.experimental import pallas as pl
from jax.experimental.pallas import tpu as pltpu
from jax.sharding import PartitionSpec as P

HEADS = 12
EPS = 1e-06
MASKED = -1000000000.0
WEIGHT_NAMES = (
    "position",
    "mixer_gain",
    "mixer_shift",
    "heads_weight",
    "query_bias",
    "value_bias",
    "out_weight",
    "out_bias",
    "dense_gain",
    "dense_shift",
    "up_weight",
    "up_bias",
    "down_weight",
    "down_bias",
    "align_weight",
    "align_bias",
)


BLOCK = 256
BF = jnp.bfloat16
F32 = jnp.float32
VMEM_LIMIT = 66_000_000


def dot(left, right, dims):
    return lax.dot_general(left, right, ((dims[:1], dims[1:]), ((), ())), preferred_element_type=F32)


def centre(values):
    mean = jnp.mean(values, axis=-1, keepdims=True)
    centered = values - mean
    spread = jnp.mean(centered * centered, axis=-1, keepdims=True)
    inverse = lax.rsqrt(spread + EPS)
    return centered * inverse, inverse


def centre_back(grad, unit, inverse):
    first = jnp.mean(grad, axis=-1, keepdims=True)
    second = jnp.mean(grad * unit, axis=-1, keepdims=True)
    return inverse * (grad - first - unit * second)


def valid_rows(tile_len, block, tile):
    row = lax.broadcasted_iota(jnp.int32, (BLOCK, 1), 0)
    parts = BLOCK // tile
    limit = tile_len[block * parts]
    for part in range(1, parts):
        limit = jnp.where(row >= part * tile, tile_len[block * parts + part], limit)
    return lax.rem(row, tile) < limit


def live_block(tile_len, block, tile):
    most = tile_len[block * (BLOCK // tile)]
    for part in range(1, BLOCK // tile):
        most = jnp.maximum(most, tile_len[block * (BLOCK // tile) + part])
    return most > 0


def project_kernel(
    tile, tile_len, held, source, index, *refs
):
    parts = BLOCK // tile
    pieces = refs[:parts]
    table_any, weight, bias, gain, shift, out, start_out, table, stage, rows, sem = refs[parts:]
    step = pl.program_id(0)
    width = weight.shape[0]
    chunk = stage.shape[1]
    chunks = table.shape[0] // chunk

    def fetch(number):
        return pltpu.make_async_copy(
            table_any.at[pl.ds(pl.multiple_of(number * chunk, 16), chunk), :],
            stage.at[lax.rem(number, 2)],
            sem.at[lax.rem(number, 2)],
        )

    @pl.when(step == 0)
    def _():
        fetch(0).start()

        def load(number, carry):
            @pl.when(number + 1 < chunks)
            def _():
                fetch(number + 1).start()

            fetch(number).wait()
            table[pl.ds(pl.multiple_of(number * chunk, 16), chunk), :] = stage[lax.rem(number, 2)].astype(F32)
            return carry

        lax.fori_loop(0, chunks, load, 0)

    @pl.when(live_block(tile_len, step, tile))
    def _():
        def gather(group, carry):
            base = pl.multiple_of(group * 8, 8)
            for row in range(8):
                place = index[step * BLOCK + base + row]
                rows[pl.ds(base + row, 1), :] = table[pl.ds(place, 1), :]
            return carry

        lax.fori_loop(0, BLOCK // 8, gather, 0)
        whole = jnp.concatenate([piece[...] for piece in pieces], axis=0).astype(F32)
        start = whole + rows[...]
        start_out[...] = start
        unit, _ = centre(start)
        normed = (unit * gain[...] + shift[...]).astype(BF)
        for part in range(3):
            cols = slice(part * width, (part + 1) * width)
            triple = (dot(normed, weight[:, cols], (1, 0)) + bias[:, cols]).astype(BF)
            if part == 0:
                triple = triple * BF(0.125)
            out[cols, :] = triple.T


def masked_tile(tile_scores, limit):
    key = lax.broadcasted_iota(jnp.int32, tile_scores.shape, 0)
    return jnp.where(key < limit, tile_scores, MASKED)


def block_mask(tile_len, first, tile):
    key = lax.broadcasted_iota(jnp.int32, (BLOCK, BLOCK), 0)
    asked = lax.broadcasted_iota(jnp.int32, (BLOCK, BLOCK), 1)
    limit = tile_len[first]
    for part in range(1, BLOCK // tile):
        limit = jnp.where(key >= part * tile, tile_len[first + part], limit)
    return (key // tile == asked // tile) & (lax.rem(key, tile) < limit)


def attend_kernel(tile, long_rows, clips, tile_len, length, count, query, keys, values, out, logsum):
    head_dim = query.shape[0] // 2
    most = long_rows // BLOCK

    def one(column, first, size, fix):
        for head in range(2):
            lanes = slice(head * head_dim, (head + 1) * head_dim)
            asked = query[lanes, pl.ds(column, BLOCK)]
            scores = []
            for number in range(size):
                held = keys[lanes, pl.ds(first + number * BLOCK, BLOCK)]
                scores.append(dot(held, asked, (0, 0)))
            scores[-1] = fix(scores[-1])
            top = jnp.max(scores[0], axis=0, keepdims=True)
            for score in scores[1:]:
                top = jnp.maximum(top, jnp.max(score, axis=0, keepdims=True))
            weights = [jnp.exp(score - top) for score in scores]
            total = sum(jnp.sum(weight, axis=0, keepdims=True) for weight in weights)
            gathered = None
            for number, weight in enumerate(weights):
                held = values[lanes, pl.ds(first + number * BLOCK, BLOCK)]
                term = dot(held, weight.astype(BF), (1, 0))
                gathered = term if gathered is None else gathered + term
            out[lanes, pl.ds(column, BLOCK)] = (gathered / total).astype(BF)
            logsum[0, pl.ds(head, 1), pl.ds(column, BLOCK)] = top + jnp.log(total)

    def clip(number, carry):
        first = pl.multiple_of(number * long_rows, BLOCK)
        blocks = count[number]
        rest = length[number]
        for size in range(1, most + 1):
            @pl.when(blocks == size)
            def _():
                def ask(block, inner):
                    one(
                        pl.multiple_of(first + block * BLOCK, BLOCK),
                        first,
                        size,
                        lambda score: masked_tile(score, rest - (size - 1) * BLOCK),
                    )
                    return inner

                lax.fori_loop(0, size, ask, 0)
        return carry

    lax.fori_loop(0, clips, clip, 0)

    def short(number, carry):
        column = pl.multiple_of(clips * long_rows + number * BLOCK, BLOCK)
        allowed = block_mask(tile_len, (clips * long_rows + number * BLOCK) // tile, tile)
        one(column, column, 1, lambda score: jnp.where(allowed, score, MASKED))
        return carry

    lax.fori_loop(0, count[clips], short, 0)


def attend_back_kernel(
    tile, long_rows, clips, tile_len, length, count, query, keys, values, grad, logsum,
    query_out, key_out, value_out, key_sum, value_sum,
):
    head_dim = query.shape[0] // 2
    most = long_rows // BLOCK

    def one(column, first, size, fix):
        for head in range(2):
            lanes = slice(head * head_dim, (head + 1) * head_dim)
            asked = query[lanes, pl.ds(column, BLOCK)]
            pulled = grad[lanes, pl.ds(column, BLOCK)]
            base = logsum[0, pl.ds(head, 1), pl.ds(column, BLOCK)]
            probs = []
            terms = []
            inner = None
            for number in range(size):
                here = pl.ds(first + number * BLOCK, BLOCK)
                score = dot(keys[lanes, here], asked, (0, 0))
                if number == size - 1:
                    score = fix(score)
                prob = jnp.exp(score - base)
                back = dot(values[lanes, here], pulled, (0, 0))
                term = prob * back
                part = jnp.sum(term, axis=0, keepdims=True)
                inner = part if inner is None else inner + part
                probs.append(prob)
                terms.append(term)
            query_sum = None
            for number in range(size):
                here = pl.ds(first + number * BLOCK, BLOCK)
                there = slice(number * BLOCK, (number + 1) * BLOCK)
                moved = (terms[number] - probs[number] * inner).astype(BF)
                value_sum[lanes, there] += dot(pulled, probs[number].astype(BF), (1, 1))
                key_sum[lanes, there] += dot(asked, moved, (1, 1))
                term = dot(keys[lanes, here], moved, (1, 0))
                query_sum = term if query_sum is None else query_sum + term
            query_out[lanes, pl.ds(column, BLOCK)] = (query_sum * 0.125).astype(BF)

    def flush(first, size):
        key_out[:, pl.ds(first, size * BLOCK)] = key_sum[:, : size * BLOCK].astype(BF)
        value_out[:, pl.ds(first, size * BLOCK)] = value_sum[:, : size * BLOCK].astype(BF)

    def clear(size):
        key_sum[:, : size * BLOCK] = jnp.zeros((2 * head_dim, size * BLOCK), F32)
        value_sum[:, : size * BLOCK] = jnp.zeros((2 * head_dim, size * BLOCK), F32)

    def clip(number, carry):
        first = pl.multiple_of(number * long_rows, BLOCK)
        blocks = count[number]
        rest = length[number]
        for size in range(1, most + 1):
            @pl.when(blocks == size)
            def _():
                clear(size)

                def ask(block, inner):
                    one(
                        pl.multiple_of(first + block * BLOCK, BLOCK),
                        first,
                        size,
                        lambda score: masked_tile(score, rest - (size - 1) * BLOCK),
                    )
                    return inner

                lax.fori_loop(0, size, ask, 0)
                flush(first, size)
        return carry

    lax.fori_loop(0, clips, clip, 0)

    def short(number, carry):
        column = pl.multiple_of(clips * long_rows + number * BLOCK, BLOCK)
        allowed = block_mask(tile_len, (clips * long_rows + number * BLOCK) // tile, tile)
        clear(1)
        one(column, column, 1, lambda score: jnp.where(allowed, score, MASKED))
        flush(column, 1)
        return carry

    lax.fori_loop(0, count[clips], short, 0)


def gelu_both(upper):
    spread = 0.5 * (1.0 + lax.erf(upper * 0.7071067811865476))
    bell = jnp.exp(-0.5 * upper * upper) * 0.3989422804014327
    return upper * spread, spread + upper * bell


def write_out(pairs, stage, sem):
    waiting = [None, None]
    for number, (source, target) in enumerate(pairs):
        slot = number % 2
        if waiting[slot] is not None:
            waiting[slot].wait()
        value = source()
        view = stage.at[slot, :, : value.shape[1]]
        stage[slot, :, : value.shape[1]] = value.astype(BF)
        copy = pltpu.make_async_copy(view, target, sem.at[slot])
        copy.start()
        waiting[slot] = copy
    for copy in waiting:
        if copy is not None:
            copy.wait()


def middle_kernel(tile, long_blocks, tile_len, held, source, attended_t, start_in, *refs):
    parts = BLOCK // tile
    targets = refs[:parts]
    (
        out_w, out_b, gain, shift, up_w, up_b, down_w, down_b, align_w, align_b,
        long_out, short_out, pull_out, grad_out, vector_out,
        out_g, up_g, down_g, align_g,
        out_acc, up_acc, down_acc, align_acc, hidden, slope, stage, sem,
    ) = refs[parts:]
    step = pl.program_id(0)
    width = out_w.shape[0]
    wide = up_w.shape[1]
    teach = align_w.shape[1]
    pieces = wide // width
    live = live_block(tile_len, step, tile)

    @pl.when(step == 0)
    def _():
        for acc in (out_acc, up_acc, down_acc, align_acc):
            acc[...] = jnp.zeros_like(acc)
        vector_out[...] = jnp.zeros_like(vector_out)

    def put(value):
        @pl.when(step < long_blocks)
        def _():
            long_out[...] = value

        @pl.when(step >= long_blocks)
        def _():
            short_out[...] = value

    def add_vector(row, value):
        size = value.shape[1]
        vector_out[row : row + 1, :size] += value

    def over_rows(value):
        return jnp.sum(value, axis=0, keepdims=True)

    @pl.when(jnp.logical_not(live))
    def _():
        put(jnp.zeros((BLOCK, width), BF))

    @pl.when(live)
    def _():
        ok = valid_rows(tile_len, step, tile)
        across = attended_t[...]
        middle = start_in[...] + dot(across, out_w[...], (0, 0)) + out_b[...]
        unit, inverse = centre(middle)
        dense = (unit * gain[...] + shift[...]).astype(BF)
        result = middle + down_b[...]
        for piece in range(pieces):
            cols = slice(piece * width, (piece + 1) * width)
            upper = dot(dense, up_w[:, cols], (1, 0)) + up_b[:, cols]
            bent, tilt = gelu_both(upper)
            low = bent.astype(BF)
            hidden[:, cols] = low
            slope[:, cols] = tilt
            result = result + dot(low, down_w[cols, :], (1, 0))
        shown = jnp.where(ok, result, 0.0).astype(BF)
        put(shown)
        projected = dot(shown, align_w[...], (1, 0)) + align_b[...]
        target = jnp.concatenate([piece[...] for piece in targets], axis=0).astype(F32)
        miss = jnp.where(ok, projected - target, 0.0).astype(BF)
        add_vector(5, over_rows(miss.astype(F32)))
        align_acc[...] += dot(shown, miss, (0, 0))
        pulled = dot(miss, align_w[...], (1, 1)).astype(BF)
        pulled_wide = pulled.astype(F32)
        add_vector(4, over_rows(pulled_wide))
        grad_dense = None
        for piece in range(pieces):
            cols = slice(piece * width, (piece + 1) * width)
            grad_upper = dot(pulled, down_w[cols, :], (1, 1)) * slope[:, cols]
            low = grad_upper.astype(BF)
            vector_out[0:1, cols] += over_rows(low.astype(F32))
            down_acc[piece] += dot(hidden[:, cols], pulled, (0, 0))
            up_acc[piece] += dot(dense, low, (0, 0))
            term = dot(low, up_w[:, cols], (1, 1))
            grad_dense = term if grad_dense is None else grad_dense + term
        add_vector(2, over_rows(grad_dense * unit))
        add_vector(3, over_rows(grad_dense))
        grad_middle = pulled_wide + centre_back(grad_dense * gain[...], unit, inverse)
        grad_out[...] = grad_middle
        branch = grad_middle.astype(BF)
        add_vector(1, over_rows(branch.astype(F32)))
        out_acc[...] += dot(across, branch, (1, 0))
        pull_out[...] = dot(out_w[...], branch, (1, 1)).astype(BF)

    @pl.when(step == pl.num_programs(0) - 1)
    def _():
        pairs = [(lambda: out_acc[...], out_g)]
        for piece in range(pieces):
            cols = pl.ds(piece * width, width)
            pairs.append((lambda piece=piece: up_acc[piece], up_g.at[:, cols]))
            pairs.append((lambda piece=piece: down_acc[piece], down_g.at[cols, :]))
        for begin in range(0, teach, width):
            end = min(teach, begin + width)
            pairs.append(
                (lambda begin=begin, end=end: align_acc[:, begin:end], align_g.at[:, pl.ds(begin, end - begin)])
            )
        write_out(pairs, stage, sem)


def entry_kernel(tile, long_blocks, tile_len, held, index, *refs):
    (
        query_t, key_t, value_t, start_in, grad_in, weight, gain, shift,
        long_out, short_out, vector_out, weight_g, position_g,
        weight_acc, position_acc, moved, stage, sem,
    ) = refs
    step = pl.program_id(0)
    width = weight.shape[0]
    live = live_block(tile_len, step, tile)

    @pl.when(step == 0)
    def _():
        weight_acc[...] = jnp.zeros_like(weight_acc)
        vector_out[...] = jnp.zeros_like(vector_out)

        def clear(number, carry):
            position_acc[pl.ds(pl.multiple_of(number * 64, 64), 64), :] = jnp.zeros((64, width), F32)
            return carry

        lax.fori_loop(0, position_acc.shape[0] // 64, clear, 0)

    def put(value):
        @pl.when(step < long_blocks)
        def _():
            long_out[...] = value

        @pl.when(step >= long_blocks)
        def _():
            short_out[...] = value

    def over_rows(value):
        return jnp.sum(value, axis=0, keepdims=True)

    @pl.when(jnp.logical_not(live))
    def _():
        put(jnp.zeros((BLOCK, width), BF))

    @pl.when(live)
    def _():
        unit, inverse = centre(start_in[...])
        normed = (unit * gain[...] + shift[...]).astype(BF)
        grad_normed = None
        for part in range(3):
            cols = slice(part * width, (part + 1) * width)
            across = (query_t, key_t, value_t)[part][...]
            if part != 1:
                vector_out[part : part + 1, :] += over_rows(across.T.astype(F32))
            weight_acc[:, cols] += dot(normed, across, (0, 1))
            term = dot(across, weight[:, cols], (0, 1))
            grad_normed = term if grad_normed is None else grad_normed + term
        vector_out[1:2, :] += over_rows(grad_normed * unit)
        vector_out[3:4, :] += over_rows(grad_normed)
        grad_start = grad_in[...] + centre_back(grad_normed * gain[...], unit, inverse)
        put(grad_start.astype(BF))
        moved[...] = grad_start
        parts = BLOCK // tile

        def spread(number, carry):
            first = number * tile

            def some(group, inner):
                base = pl.multiple_of(first + group * 8, 8)
                for row in range(8):
                    place = index[step * BLOCK + base + row]
                    position_acc[pl.ds(place, 1), :] += moved[pl.ds(base + row, 1), :]
                return inner

            groups = (tile_len[step * parts + number] + 7) // 8
            lax.fori_loop(0, groups, some, 0)
            return carry

        lax.fori_loop(0, parts, spread, 0)

    @pl.when(step == pl.num_programs(0) - 1)
    def _():
        pairs = []
        for part in range(3):
            cols = slice(part * width, (part + 1) * width)
            pairs.append((lambda cols=cols: weight_acc[:, cols], weight_g.at[:, pl.ds(part * width, width)]))
        write_out(pairs, stage, sem)
        chunk = 448

        def copy(number):
            return pltpu.make_async_copy(
                stage.at[lax.rem(number, 2), pl.ds(0, chunk), :],
                position_g.at[pl.ds(pl.multiple_of(number * chunk, 16), chunk), :],
                sem.at[lax.rem(number, 2)],
            )

        def drain(number, carry):
            @pl.when(number >= 2)
            def _():
                copy(number - 2).wait()

            stage[lax.rem(number, 2), pl.ds(0, chunk), :] = position_acc[
                pl.ds(pl.multiple_of(number * chunk, 16), chunk), :
            ].astype(BF)
            copy(number).start()
            return carry

        chunks = position_acc.shape[0] // chunk
        lax.fori_loop(0, chunks, drain, 0)
        copy(chunks - 2).wait()
        copy(chunks - 1).wait()


def whole(shape):
    return pl.BlockSpec(shape, lambda *_: (0,) * len(shape), pipeline_mode=pl.Buffered(1))


def plan_rows(lengths, short_len, tile, long_rows):
    micros = lengths.shape[0]
    per = long_rows // tile
    starts = jnp.arange(per) * tile
    long_tiles = jnp.clip(lengths[:, None] - starts[None, :], 0, tile).reshape(-1)
    slots = short_len.shape[0]
    live = short_len > 0
    before = jnp.arange(slots)[None, :] < jnp.arange(slots)[:, None]
    rank_live = jnp.sum(jnp.where(before & live[None, :], 1, 0), axis=1)
    rank_dead = jnp.sum(jnp.where(before & ~live[None, :], 1, 0), axis=1)
    total = jnp.sum(live.astype(jnp.int32))
    rank = jnp.where(live, rank_live, total + rank_dead)
    chosen = rank[None, :] == jnp.arange(slots)[:, None]
    order = jnp.sum(jnp.where(chosen, jnp.arange(slots)[None, :], 0), axis=1)
    packed_len = jnp.sum(jnp.where(chosen, short_len[None, :], 0), axis=1)
    tile_len = jnp.concatenate([long_tiles, packed_len]).astype(jnp.int32)
    source = jnp.concatenate([jnp.arange(micros * per), micros * per + order]).astype(jnp.int32)
    parts = BLOCK // tile
    blocks = tile_len.shape[0] // parts
    active = jnp.max(tile_len.reshape(blocks, parts), axis=1) > 0
    ids = jnp.arange(blocks)
    held = jnp.max(jnp.where((ids[None, :] <= ids[:, None]) & active[None, :], ids[None, :], 0), axis=1)
    count = jnp.concatenate([-(-lengths // BLOCK), -(-total[None] // parts)]).astype(jnp.int32)
    return tile_len, source, held.astype(jnp.int32), count, chosen


def run_block(
    rows, index, targets, tile_len, source, held, count, lengths, tile, long_rows, micros, weights
):
    w = weights
    total, width = rows.shape
    wide = w["up_weight"].shape[1]
    teach = targets.shape[1]
    patches = w["position"].shape[0]
    blocks = total // BLOCK
    parts = BLOCK // tile
    long_blocks = micros * long_rows // BLOCK
    short_total = total - micros * long_rows
    pairs = HEADS // 2
    pair = width // pairs
    lane = lambda name: w[name].reshape(1, -1)
    params = lambda **more: pltpu.CompilerParams(vmem_limit_bytes=VMEM_LIMIT, **more)
    tiles = lambda last: [
        pl.BlockSpec((tile, last), lambda i, tl, hd, src, *_, part=part: (src[hd[i] * parts + part], 0))
        for part in range(parts)
    ]
    by_block = lambda last: pl.BlockSpec((BLOCK, last), lambda i, tl, hd, *_: (hd[i], 0))
    by_column = lambda first: pl.BlockSpec((first, BLOCK), lambda i, tl, hd, *_: (0, hd[i]))
    long_spec = pl.BlockSpec((BLOCK, width), lambda i, *_: (jnp.minimum(i, long_blocks - 1), 0))
    short_spec = pl.BlockSpec((BLOCK, width), lambda i, *_: (jnp.maximum(i - long_blocks, 0), 0))
    anywhere = pl.BlockSpec(memory_space=pl.ANY)
    bias = jnp.concatenate([w["query_bias"], jnp.zeros_like(w["query_bias"]), w["value_bias"]]).reshape(1, -1)

    triple_t, start = pl.pallas_call(
        partial(project_kernel, tile),
        grid_spec=pltpu.PrefetchScalarGridSpec(
            num_scalar_prefetch=4,
            grid=(blocks,),
            in_specs=tiles(width)
            + [anywhere, whole((width, 3 * width)), whole((1, 3 * width)), whole((1, width)), whole((1, width))],
            out_specs=[by_column(3 * width), by_block(width)],
            scratch_shapes=[
                pltpu.VMEM((patches, width), F32),
                pltpu.VMEM((2, 448, width), BF),
                pltpu.VMEM((BLOCK, width), F32),
                pltpu.SemaphoreType.DMA((2,)),
            ],
        ),
        out_shape=[
            jax.ShapeDtypeStruct((3 * width, total), BF),
            jax.ShapeDtypeStruct((total, width), F32),
        ],
        compiler_params=params(),
        name="project",
    )(
        tile_len, held, source, index, *([rows] * parts), w["position"], w["heads_weight"], bias,
        lane("mixer_gain"), lane("mixer_shift"),
    )

    def heads_spec(offset):
        return pl.BlockSpec((pair, total), lambda i, *_: (i + offset * pairs, 0))

    sums_spec = pl.BlockSpec((1, 2, total), lambda i, *_: (i, 0, 0))
    attended_t, sums = pl.pallas_call(
        partial(attend_kernel, tile, long_rows, micros),
        grid_spec=pltpu.PrefetchScalarGridSpec(
            num_scalar_prefetch=3,
            grid=(pairs,),
            in_specs=[heads_spec(0), heads_spec(1), heads_spec(2)],
            out_specs=[heads_spec(0), sums_spec],
        ),
        out_shape=[
            jax.ShapeDtypeStruct((width, total), BF),
            jax.ShapeDtypeStruct((pairs, 2, total), F32),
        ],
        compiler_params=params(),
        name="attend",
    )(tile_len, lengths, count, triple_t, triple_t, triple_t)

    middle_out = pl.pallas_call(
        partial(middle_kernel, tile, long_blocks),
        grid_spec=pltpu.PrefetchScalarGridSpec(
            num_scalar_prefetch=3,
            grid=(blocks,),
            in_specs=[by_column(width), by_block(width)]
            + tiles(teach)
            + [
                whole((width, width)), whole((1, width)), whole((1, width)), whole((1, width)),
                whole((width, wide)), whole((1, wide)), whole((wide, width)), whole((1, width)),
                whole((width, teach)), whole((1, teach)),
            ],
            out_specs=[
                long_spec, short_spec, by_column(width), by_block(width), whole((8, wide)),
                anywhere, anywhere, anywhere, anywhere,
            ],
            scratch_shapes=[
                pltpu.VMEM((width, width), F32),
                pltpu.VMEM((wide // width, width, width), F32),
                pltpu.VMEM((wide // width, width, width), F32),
                pltpu.VMEM((width, teach), F32),
                pltpu.VMEM((BLOCK, wide), BF),
                pltpu.VMEM((BLOCK, wide), F32),
                pltpu.VMEM((2, width, width), BF),
                pltpu.SemaphoreType.DMA((2,)),
            ],
        ),
        out_shape=[
            jax.ShapeDtypeStruct((micros * long_rows, width), BF),
            jax.ShapeDtypeStruct((short_total, width), BF),
            jax.ShapeDtypeStruct((width, total), BF),
            jax.ShapeDtypeStruct((total, width), F32),
            jax.ShapeDtypeStruct((8, wide), F32),
            jax.ShapeDtypeStruct((width, width), BF),
            jax.ShapeDtypeStruct((width, wide), BF),
            jax.ShapeDtypeStruct((wide, width), BF),
            jax.ShapeDtypeStruct((width, teach), BF),
        ],
        compiler_params=params(),
        name="middle",
    )(
        tile_len, held, source, attended_t, start, *([targets] * parts),
        w["out_weight"], lane("out_bias"), lane("dense_gain"), lane("dense_shift"),
        w["up_weight"], lane("up_bias"), w["down_weight"], lane("down_bias"),
        w["align_weight"], lane("align_bias"),
    )
    long_out, short_out, pulled_t, grad_middle, vector, out_g, up_g, down_g, align_g = middle_out

    grads = pl.pallas_call(
        partial(attend_back_kernel, tile, long_rows, micros),
        grid_spec=pltpu.PrefetchScalarGridSpec(
            num_scalar_prefetch=3,
            grid=(pairs,),
            in_specs=[heads_spec(0), heads_spec(1), heads_spec(2), heads_spec(0), sums_spec],
            out_specs=[heads_spec(0)] * 3,
            scratch_shapes=[pltpu.VMEM((pair, long_rows), F32)] * 2,
        ),
        out_shape=[jax.ShapeDtypeStruct((width, total), BF)] * 3,
        compiler_params=params(),
        name="attend_back",
    )(tile_len, lengths, count, triple_t, triple_t, triple_t, pulled_t, sums)

    long_grad, short_grad, entry_vector, heads_g, position_g = pl.pallas_call(
        partial(entry_kernel, tile, long_blocks),
        grid_spec=pltpu.PrefetchScalarGridSpec(
            num_scalar_prefetch=3,
            grid=(blocks,),
            in_specs=[by_column(width)] * 3
            + [by_block(width), by_block(width), whole((width, 3 * width)), whole((1, width)), whole((1, width))],
            out_specs=[long_spec, short_spec, whole((8, width)), anywhere, anywhere],
            scratch_shapes=[
                pltpu.VMEM((width, 3 * width), F32),
                pltpu.VMEM((patches, width), F32),
                pltpu.VMEM((BLOCK, width), F32),
                pltpu.VMEM((2, width, width), BF),
                pltpu.SemaphoreType.DMA((2,)),
            ],
        ),
        out_shape=[
            jax.ShapeDtypeStruct((micros * long_rows, width), BF),
            jax.ShapeDtypeStruct((short_total, width), BF),
            jax.ShapeDtypeStruct((8, width), F32),
            jax.ShapeDtypeStruct((width, 3 * width), BF),
            jax.ShapeDtypeStruct((patches, width), BF),
        ],
        compiler_params=params(),
        name="entry",
    )(
        tile_len, held, index, *grads, start, grad_middle, w["heads_weight"], lane("mixer_gain"), lane("mixer_shift"),
    )
    matrices = {
        "position": position_g, "heads_weight": heads_g, "out_weight": out_g, "up_weight": up_g,
        "down_weight": down_g, "align_weight": align_g,
    }
    vectors = {
        "up_bias": vector[0], "out_bias": vector[1, :width], "dense_gain": vector[2, :width],
        "dense_shift": vector[3, :width], "down_bias": vector[4, :width], "align_bias": vector[5, :teach],
        "query_bias": entry_vector[0], "mixer_gain": entry_vector[1], "value_bias": entry_vector[2],
        "mixer_shift": entry_vector[3],
    }
    return long_out, short_out, long_grad, short_grad, matrices, vectors


def shards(
    long_clips,
    short_clips,
    long_index,
    short_index,
    long_length,
    short_length,
    destination,
    long_target,
    short_target,
    position,
    mixer_gain,
    mixer_shift,
    heads_weight,
    query_bias,
    value_bias,
    out_weight,
    out_bias,
    dense_gain,
    dense_shift,
    up_weight,
    up_bias,
    down_weight,
    down_bias,
    align_weight,
    align_bias,
):
    peers = lax.axis_size("dp")
    copies = lax.axis_size("rep")
    mine = lax.axis_index("dp")
    own_copy = lax.axis_index("rep")
    micros, _, long_rows, width = long_clips.shape
    home_slots, tile = short_clips.shape[1:3]
    bal_slots = home_slots // 2
    slots = micros * home_slots
    weights = dict(
        zip(
            WEIGHT_NAMES,
            (
                position, mixer_gain, mixer_shift, heads_weight, query_bias, value_bias, out_weight, out_bias,
                dense_gain, dense_shift, up_weight, up_bias, down_weight, down_bias, align_weight, align_bias,
            ),
        )
    )
    group_dest = lax.dynamic_index_in_dim(
        destination.reshape(micros, peers, copies, home_slots), own_copy, 2, keepdims=False
    )
    group_len = lax.dynamic_index_in_dim(
        short_length.reshape(micros, peers, copies, home_slots), own_copy, 2, keepdims=False
    )
    own_dest = lax.dynamic_index_in_dim(group_dest, mine, 1, keepdims=False).reshape(slots)
    own_len = lax.dynamic_index_in_dim(group_len, mine, 1, keepdims=False).reshape(slots)
    lengths = long_length[:, 0]
    tile_len, source, held, count, chosen = plan_rows(lengths, own_len, tile, long_rows)
    packed_index = jnp.sum(
        jnp.where(chosen[:, :, None], short_index.reshape(1, slots, tile), 0), axis=1
    )
    index = jnp.concatenate([long_index.reshape(-1), packed_index.reshape(-1)])
    rows = jnp.concatenate([long_clips.reshape(-1, width), short_clips.reshape(-1, width)], axis=0)
    teach = long_target.shape[-1]
    targets = jnp.concatenate([long_target.reshape(-1, teach), short_target.reshape(-1, teach)], axis=0)
    long_out, short_out, long_grad, short_grad, matrices, vectors = run_block(
        rows, index, targets, tile_len, source, held, count, lengths, tile, long_rows, micros, weights
    )
    pick = chosen.astype(jnp.bfloat16)
    slot_micro = jnp.arange(slots) // home_slots
    wanted = (
        (own_dest[None, None, :] == jnp.arange(peers)[:, None, None])
        & (own_len[None, None, :] > 0)
        & (slot_micro[None, None, :] == jnp.arange(micros)[None, :, None])
    )
    send_map = jnp.einsum("pms,ks->pmk", wanted.astype(jnp.bfloat16), pick).reshape(peers * micros, slots)
    send = jnp.dot(send_map.astype(jnp.bfloat16), short_out.reshape(slots, tile * width))
    got = lax.all_to_all(
        send.reshape(peers, micros, tile, width), "dp", split_axis=0, concat_axis=0, tiled=True
    )
    slot_pick = jnp.arange(home_slots)[:, None] % bal_slots == jnp.arange(bal_slots)[None, :]
    incoming = (group_dest == mine) & (group_len > 0)
    recv_map = jnp.any(incoming[..., None] & slot_pick[None, None], axis=2)
    short_bal = jnp.einsum("mpb,pmtd->mbtd", recv_map.astype(jnp.bfloat16), got)
    short_home = jnp.dot(pick.T, short_grad.reshape(slots, tile * width))
    return (
        long_out.reshape(micros, 1, long_rows, width),
        short_bal,
        long_grad.reshape(micros, 1, long_rows, width),
        short_home.reshape(micros, home_slots, tile, width),
    ) + combine(matrices, vectors, copies)


def combine(matrices, vectors, copies):
    peers = lax.axis_size("dp")
    mine = lax.axis_index("dp")
    names = [name for name in WEIGHT_NAMES if name in vectors]
    flat = jnp.concatenate([vectors[name].reshape(peers, -1) for name in names], axis=1)
    flat = lax.psum(flat, ("dp", "rep"))
    flat = lax.dynamic_index_in_dim(flat, mine, 0, keepdims=False)
    shared = {}
    begin = 0
    for name in names:
        size = vectors[name].shape[0] // peers
        shared[name] = flat[begin : begin + size]
        begin += size
    for name, wide in matrices.items():
        rows = wide.shape[0] // peers
        padded = -(-rows // (8 * copies)) * 8 * copies
        if padded != rows:
            wide = wide.reshape(peers, rows, -1)
            wide = jnp.pad(wide, ((0, 0), (0, padded - rows), (0, 0)))
            wide = wide.reshape(peers * padded, -1)
        piece = lax.psum_scatter(wide, ("dp", "rep"), scatter_dimension=0, tiled=True)
        piece = lax.all_gather(piece, "rep", axis=0, tiled=True)[:rows]
        shared[name] = piece.astype(jnp.float32)
    return tuple(shared[name] for name in WEIGHT_NAMES)


def solution(mesh):
    placed = (
        P(None, ("dp", "rep"), None, None),
        P(None, ("dp", "rep"), None, None),
        P(None, ("dp", "rep"), None),
        P(None, ("dp", "rep"), None),
        P(None, ("dp", "rep")),
        P(),
        P(),
        P(None, ("dp", "rep"), None, None),
        P(None, ("dp", "rep"), None, None),
        P(),
        P(),
        P(),
        P(),
        P(),
        P(),
        P(),
        P(),
        P(),
        P(),
        P(),
        P(),
        P(),
        P(),
        P(),
        P(),
    )
    return jax.shard_map(
        shards,
        mesh=mesh,
        in_specs=placed,
        out_specs=(
            P(None, ("dp", "rep"), None, None),
            P(None, ("dp", "rep"), None, None),
            P(None, ("dp", "rep"), None, None),
            P(None, ("dp", "rep"), None, None),
            P("dp", None),
            P("dp"),
            P("dp"),
            P("dp", None),
            P("dp"),
            P("dp"),
            P("dp", None),
            P("dp"),
            P("dp"),
            P("dp"),
            P("dp", None),
            P("dp"),
            P("dp", None),
            P("dp"),
            P("dp", None),
            P("dp"),
        ),
        check_vma=False,
    )
```

```python
from functools import partial

import jax
import jax.numpy as jnp
from jax import lax
from jax.experimental import pallas as pl
from jax.experimental.pallas import tpu as pltpu
from jax.sharding import PartitionSpec as P

HEADS = 12
EPS = 1e-06
MASKED = -1000000000.0
WEIGHT_NAMES = (
    "position",
    "mixer_gain",
    "mixer_shift",
    "heads_weight",
    "query_bias",
    "value_bias",
    "out_weight",
    "out_bias",
    "dense_gain",
    "dense_shift",
    "up_weight",
    "up_bias",
    "down_weight",
    "down_bias",
    "align_weight",
    "align_bias",
)


BLOCK = 256
BF = jnp.bfloat16
F32 = jnp.float32
VMEM_LIMIT = 66_000_000


def dot(left, right, dims):
    return lax.dot_general(left, right, ((dims[:1], dims[1:]), ((), ())), preferred_element_type=F32)


def centre(values):
    mean = jnp.mean(values, axis=-1, keepdims=True)
    centered = values - mean
    spread = jnp.mean(centered * centered, axis=-1, keepdims=True)
    inverse = lax.rsqrt(spread + EPS)
    return centered * inverse, inverse


def centre_back(grad, unit, inverse):
    first = jnp.mean(grad, axis=-1, keepdims=True)
    second = jnp.mean(grad * unit, axis=-1, keepdims=True)
    return inverse * (grad - first - unit * second)


def valid_rows(tile_len, block, tile):
    row = lax.broadcasted_iota(jnp.int32, (BLOCK, 1), 0)
    parts = BLOCK // tile
    limit = tile_len[block * parts]
    for part in range(1, parts):
        limit = jnp.where(row >= part * tile, tile_len[block * parts + part], limit)
    return lax.rem(row, tile) < limit


def live_block(tile_len, block, tile):
    most = tile_len[block * (BLOCK // tile)]
    for part in range(1, BLOCK // tile):
        most = jnp.maximum(most, tile_len[block * (BLOCK // tile) + part])
    return most > 0


def project_kernel(
    tile, tile_len, held, source, index, *refs
):
    parts = BLOCK // tile
    pieces = refs[:parts]
    table_any, weight, bias, gain, shift, out, start_out, table, stage, rows, sem = refs[parts:]
    step = pl.program_id(0)
    width = weight.shape[0]
    chunk = stage.shape[1]
    chunks = table.shape[0] // chunk

    def fetch(number):
        return pltpu.make_async_copy(
            table_any.at[pl.ds(pl.multiple_of(number * chunk, 16), chunk), :],
            stage.at[lax.rem(number, 2)],
            sem.at[lax.rem(number, 2)],
        )

    @pl.when(step == 0)
    def _():
        fetch(0).start()

        def load(number, carry):
            @pl.when(number + 1 < chunks)
            def _():
                fetch(number + 1).start()

            fetch(number).wait()
            table[pl.ds(pl.multiple_of(number * chunk, 16), chunk), :] = stage[lax.rem(number, 2)].astype(F32)
            return carry

        lax.fori_loop(0, chunks, load, 0)

    @pl.when(live_block(tile_len, step, tile))
    def _():
        def gather(group, carry):
            base = pl.multiple_of(group * 8, 8)
            for row in range(8):
                place = index[step * BLOCK + base + row]
                rows[pl.ds(base + row, 1), :] = table[pl.ds(place, 1), :]
            return carry

        lax.fori_loop(0, BLOCK // 8, gather, 0)
        whole = jnp.concatenate([piece[...] for piece in pieces], axis=0).astype(F32)
        start = whole + rows[...]
        start_out[...] = start
        unit, _ = centre(start)
        normed = (unit * gain[...] + shift[...]).astype(BF)
        for part in range(3):
            cols = slice(part * width, (part + 1) * width)
            triple = (dot(normed, weight[:, cols], (1, 0)) + bias[:, cols]).astype(BF)
            if part == 0:
                triple = triple * BF(0.125)
            out[cols, :] = triple.T


def masked_tile(tile_scores, limit):
    key = lax.broadcasted_iota(jnp.int32, tile_scores.shape, 0)
    return jnp.where(key < limit, tile_scores, MASKED)


def block_mask(tile_len, first, tile):
    key = lax.broadcasted_iota(jnp.int32, (BLOCK, BLOCK), 0)
    asked = lax.broadcasted_iota(jnp.int32, (BLOCK, BLOCK), 1)
    limit = tile_len[first]
    for part in range(1, BLOCK // tile):
        limit = jnp.where(key >= part * tile, tile_len[first + part], limit)
    return (key // tile == asked // tile) & (lax.rem(key, tile) < limit)


def attend_kernel(tile, long_rows, clips, tile_len, length, count, query, keys, values, out, logsum):
    head_dim = query.shape[0] // 2
    most = long_rows // BLOCK

    def one(column, first, size, fix):
        for head in range(2):
            lanes = slice(head * head_dim, (head + 1) * head_dim)
            asked = query[lanes, pl.ds(column, BLOCK)]
            scores = []
            for number in range(size):
                held = keys[lanes, pl.ds(first + number * BLOCK, BLOCK)]
                scores.append(dot(held, asked, (0, 0)))
            scores[-1] = fix(scores[-1])
            top = jnp.max(scores[0], axis=0, keepdims=True)
            for score in scores[1:]:
                top = jnp.maximum(top, jnp.max(score, axis=0, keepdims=True))
            weights = [jnp.exp(score - top) for score in scores]
            total = sum(jnp.sum(weight, axis=0, keepdims=True) for weight in weights)
            gathered = None
            for number, weight in enumerate(weights):
                held = values[lanes, pl.ds(first + number * BLOCK, BLOCK)]
                term = dot(held, weight.astype(BF), (1, 0))
                gathered = term if gathered is None else gathered + term
            out[lanes, pl.ds(column, BLOCK)] = (gathered / total).astype(BF)
            logsum[0, pl.ds(head, 1), pl.ds(column, BLOCK)] = top + jnp.log(total)

    def clip(number, carry):
        first = pl.multiple_of(number * long_rows, BLOCK)
        blocks = count[number]
        rest = length[number]
        for size in range(1, most + 1):
            @pl.when(blocks == size)
            def _():
                def ask(block, inner):
                    one(
                        pl.multiple_of(first + block * BLOCK, BLOCK),
                        first,
                        size,
                        lambda score: masked_tile(score, rest - (size - 1) * BLOCK),
                    )
                    return inner

                lax.fori_loop(0, size, ask, 0)
        return carry

    lax.fori_loop(0, clips, clip, 0)

    def short(number, carry):
        column = pl.multiple_of(clips * long_rows + number * BLOCK, BLOCK)
        allowed = block_mask(tile_len, (clips * long_rows + number * BLOCK) // tile, tile)
        one(column, column, 1, lambda score: jnp.where(allowed, score, MASKED))
        return carry

    lax.fori_loop(0, count[clips], short, 0)


def attend_back_kernel(
    tile, long_rows, clips, tile_len, length, count, query, keys, values, grad, logsum,
    query_out, key_out, value_out, key_sum, value_sum,
):
    head_dim = query.shape[0] // 2
    most = long_rows // BLOCK

    def one(column, first, size, fix):
        for head in range(2):
            lanes = slice(head * head_dim, (head + 1) * head_dim)
            asked = query[lanes, pl.ds(column, BLOCK)]
            pulled = grad[lanes, pl.ds(column, BLOCK)]
            base = logsum[0, pl.ds(head, 1), pl.ds(column, BLOCK)]
            probs = []
            terms = []
            inner = None
            for number in range(size):
                here = pl.ds(first + number * BLOCK, BLOCK)
                score = dot(keys[lanes, here], asked, (0, 0))
                if number == size - 1:
                    score = fix(score)
                prob = jnp.exp(score - base)
                back = dot(values[lanes, here], pulled, (0, 0))
                term = prob * back
                part = jnp.sum(term, axis=0, keepdims=True)
                inner = part if inner is None else inner + part
                probs.append(prob)
                terms.append(term)
            query_sum = None
            for number in range(size):
                here = pl.ds(first + number * BLOCK, BLOCK)
                there = slice(number * BLOCK, (number + 1) * BLOCK)
                moved = (terms[number] - probs[number] * inner).astype(BF)
                value_sum[lanes, there] += dot(pulled, probs[number].astype(BF), (1, 1))
                key_sum[lanes, there] += dot(asked, moved, (1, 1))
                term = dot(keys[lanes, here], moved, (1, 0))
                query_sum = term if query_sum is None else query_sum + term
            query_out[lanes, pl.ds(column, BLOCK)] = (query_sum * 0.125).astype(BF)

    def flush(first, size):
        key_out[:, pl.ds(first, size * BLOCK)] = key_sum[:, : size * BLOCK].astype(BF)
        value_out[:, pl.ds(first, size * BLOCK)] = value_sum[:, : size * BLOCK].astype(BF)

    def clear(size):
        key_sum[:, : size * BLOCK] = jnp.zeros((2 * head_dim, size * BLOCK), F32)
        value_sum[:, : size * BLOCK] = jnp.zeros((2 * head_dim, size * BLOCK), F32)

    def clip(number, carry):
        first = pl.multiple_of(number * long_rows, BLOCK)
        blocks = count[number]
        rest = length[number]
        for size in range(1, most + 1):
            @pl.when(blocks == size)
            def _():
                clear(size)

                def ask(block, inner):
                    one(
                        pl.multiple_of(first + block * BLOCK, BLOCK),
                        first,
                        size,
                        lambda score: masked_tile(score, rest - (size - 1) * BLOCK),
                    )
                    return inner

                lax.fori_loop(0, size, ask, 0)
                flush(first, size)
        return carry

    lax.fori_loop(0, clips, clip, 0)

    def short(number, carry):
        column = pl.multiple_of(clips * long_rows + number * BLOCK, BLOCK)
        allowed = block_mask(tile_len, (clips * long_rows + number * BLOCK) // tile, tile)
        clear(1)
        one(column, column, 1, lambda score: jnp.where(allowed, score, MASKED))
        flush(column, 1)
        return carry

    lax.fori_loop(0, count[clips], short, 0)


def gelu_both(upper):
    spread = 0.5 * (1.0 + lax.erf(upper * 0.7071067811865476))
    bell = jnp.exp(-0.5 * upper * upper) * 0.3989422804014327
    return upper * spread, spread + upper * bell


def write_out(entries, sem):
    waiting = [None, None]
    for number, (source, stage, target) in enumerate(entries):
        slot = number % 2
        if waiting[slot] is not None:
            waiting[slot].wait()
        value = source()
        view = stage.at[slot, :, : value.shape[1], : value.shape[2]]
        stage[slot, :, : value.shape[1], : value.shape[2]] = value.astype(BF)
        copy = pltpu.make_async_copy(view, target, sem.at[slot])
        copy.start()
        waiting[slot] = copy
    for copy in waiting:
        if copy is not None:
            copy.wait()


def middle_kernel(tile, long_blocks, tile_len, held, source, attended_t, start_in, *refs):
    parts = BLOCK // tile
    targets = refs[:parts]
    (
        out_w, out_b, gain, shift, up_w, up_b, down_w, down_b, align_w, align_b,
        long_out, short_out, pull_out, grad_out, vector_out, sums_out,
        out_acc, up_acc, down_acc, align_acc, hidden, slope, stage, stage_down, sem,
    ) = refs[parts:]
    step = pl.program_id(0)
    width = out_w.shape[0]
    wide = up_w.shape[1]
    teach = align_w.shape[1]
    pieces = wide // width
    live = live_block(tile_len, step, tile)

    @pl.when(step == 0)
    def _():
        for acc in (out_acc, up_acc, down_acc, align_acc):
            acc[...] = jnp.zeros_like(acc)
        vector_out[...] = jnp.zeros_like(vector_out)

    def put(value):
        @pl.when(step < long_blocks)
        def _():
            long_out[...] = value

        @pl.when(step >= long_blocks)
        def _():
            short_out[...] = value

    def add_vector(row, value):
        size = value.shape[1]
        vector_out[row : row + 1, :size] += value

    def over_rows(value):
        return jnp.sum(value, axis=0, keepdims=True)

    @pl.when(jnp.logical_not(live))
    def _():
        put(jnp.zeros((BLOCK, width), BF))

    @pl.when(live)
    def _():
        ok = valid_rows(tile_len, step, tile)
        across = attended_t[...]
        middle = start_in[...] + dot(across, out_w[...], (0, 0)) + out_b[...]
        unit, inverse = centre(middle)
        dense = (unit * gain[...] + shift[...]).astype(BF)
        result = middle + down_b[...]
        for piece in range(pieces):
            cols = slice(piece * width, (piece + 1) * width)
            upper = dot(dense, up_w[:, cols], (1, 0)) + up_b[:, cols]
            bent, tilt = gelu_both(upper)
            low = bent.astype(BF)
            hidden[:, cols] = low
            slope[:, cols] = tilt
            result = result + dot(low, down_w[cols, :], (1, 0))
        shown = jnp.where(ok, result, 0.0).astype(BF)
        put(shown)
        projected = dot(shown, align_w[...], (1, 0)) + align_b[...]
        target = jnp.concatenate([piece[...] for piece in targets], axis=0).astype(F32)
        miss = jnp.where(ok, projected - target, 0.0).astype(BF)
        add_vector(5, over_rows(miss.astype(F32)))
        align_acc[...] += dot(shown, miss, (0, 0))
        pulled = dot(miss, align_w[...], (1, 1)).astype(BF)
        pulled_wide = pulled.astype(F32)
        add_vector(4, over_rows(pulled_wide))
        grad_dense = None
        for piece in range(pieces):
            cols = slice(piece * width, (piece + 1) * width)
            grad_upper = dot(pulled, down_w[cols, :], (1, 1)) * slope[:, cols]
            low = grad_upper.astype(BF)
            vector_out[0:1, cols] += over_rows(low.astype(F32))
            down_acc[piece] += dot(hidden[:, cols], pulled, (0, 0))
            up_acc[piece] += dot(dense, low, (0, 0))
            term = dot(low, up_w[:, cols], (1, 1))
            grad_dense = term if grad_dense is None else grad_dense + term
        add_vector(2, over_rows(grad_dense * unit))
        add_vector(3, over_rows(grad_dense))
        grad_middle = pulled_wide + centre_back(grad_dense * gain[...], unit, inverse)
        grad_out[...] = grad_middle
        branch = grad_middle.astype(BF)
        add_vector(1, over_rows(branch.astype(F32)))
        out_acc[...] += dot(across, branch, (1, 0))
        pull_out[...] = dot(out_w[...], branch, (1, 1)).astype(BF)

    @pl.when(step == pl.num_programs(0) - 1)
    def _():
        groups, unit_rows = stage.shape[1:3]
        deep = pieces * unit_rows
        some, tall = stage_down.shape[1:3]

        def grouped(value):
            return value.reshape(groups, unit_rows, value.shape[-1])

        entries = []
        for piece in range(pieces):
            if groups >= pieces:
                target = sums_out.at[pl.ds(piece * some, some), pl.ds(0, tall), :]
            else:
                target = sums_out.at[:, pl.ds(piece * tall, tall), :]
            entries.append((lambda piece=piece: down_acc[piece].reshape(some, tall, width), stage_down, target))
        for piece in range(pieces):
            target = sums_out.at[:, pl.ds(deep + piece * unit_rows, unit_rows), :]
            entries.append((lambda piece=piece: grouped(up_acc[piece]), stage, target))
        begin = 2 * deep
        entries.append((lambda: grouped(out_acc[...]), stage, sums_out.at[:, pl.ds(begin, unit_rows), :]))
        begin += unit_rows
        entries.append(
            (lambda: grouped(align_acc[:, :width]), stage, sums_out.at[:, pl.ds(begin, unit_rows), :])
        )
        begin += unit_rows
        extra = teach - width
        third = unit_rows * extra // width
        for part in range(width // extra):
            entries.append(
                (
                    lambda part=part: grouped(align_acc[:, width:])[:, part * third : (part + 1) * third],
                    stage,
                    sums_out.at[:, pl.ds(begin, third), pl.ds(part * extra, extra)],
                )
            )
        write_out(entries, sem)


def entry_kernel(tile, long_blocks, tile_len, held, index, *refs):
    (
        query_t, key_t, value_t, start_in, grad_in, weight, gain, shift,
        long_out, short_out, vector_out, sums_out,
        weight_acc, position_acc, moved, stage, stage_rows, sem,
    ) = refs
    step = pl.program_id(0)
    width = weight.shape[0]
    live = live_block(tile_len, step, tile)

    @pl.when(step == 0)
    def _():
        weight_acc[...] = jnp.zeros_like(weight_acc)
        vector_out[...] = jnp.zeros_like(vector_out)

        def clear(number, carry):
            position_acc[pl.ds(pl.multiple_of(number * 64, 64), 64), :] = jnp.zeros((64, width), F32)
            return carry

        lax.fori_loop(0, position_acc.shape[0] // 64, clear, 0)
        left = position_acc.shape[0] % 64
        if left:
            position_acc[position_acc.shape[0] - left :, :] = jnp.zeros((left, width), F32)

    def put(value):
        @pl.when(step < long_blocks)
        def _():
            long_out[...] = value

        @pl.when(step >= long_blocks)
        def _():
            short_out[...] = value

    def over_rows(value):
        return jnp.sum(value, axis=0, keepdims=True)

    @pl.when(jnp.logical_not(live))
    def _():
        put(jnp.zeros((BLOCK, width), BF))

    @pl.when(live)
    def _():
        unit, inverse = centre(start_in[...])
        normed = (unit * gain[...] + shift[...]).astype(BF)
        grad_normed = None
        for part in range(3):
            cols = slice(part * width, (part + 1) * width)
            across = (query_t, key_t, value_t)[part][...]
            if part != 1:
                vector_out[part : part + 1, :] += over_rows(across.T.astype(F32))
            weight_acc[:, cols] += dot(normed, across, (0, 1))
            term = dot(across, weight[:, cols], (0, 1))
            grad_normed = term if grad_normed is None else grad_normed + term
        vector_out[1:2, :] += over_rows(grad_normed * unit)
        vector_out[3:4, :] += over_rows(grad_normed)
        grad_start = grad_in[...] + centre_back(grad_normed * gain[...], unit, inverse)
        put(grad_start.astype(BF))
        moved[...] = grad_start
        parts = BLOCK // tile

        def spread(number, carry):
            first = number * tile

            def some(group, inner):
                base = pl.multiple_of(first + group * 8, 8)
                for row in range(8):
                    place = index[step * BLOCK + base + row]
                    position_acc[pl.ds(place, 1), :] += moved[pl.ds(base + row, 1), :]
                return inner

            groups = (tile_len[step * parts + number] + 7) // 8
            lax.fori_loop(0, groups, some, 0)
            return carry

        lax.fori_loop(0, parts, spread, 0)

    @pl.when(step == pl.num_programs(0) - 1)
    def _():
        groups, unit_rows = stage.shape[1:3]
        chunk = stage_rows.shape[1]
        patches = position_acc.shape[0] - 8
        taken = patches // groups if groups > 1 else chunk
        begin = sums_out.shape[1] - 3 * unit_rows
        entries = []
        for part in range(3):
            cols = slice(part * width, (part + 1) * width)
            entries.append(
                (
                    lambda cols=cols: weight_acc[:, cols].reshape(groups, unit_rows, width),
                    stage,
                    sums_out.at[:, pl.ds(begin + part * unit_rows, unit_rows), :],
                )
            )
        write_out(entries, sem)

        def copy(number):
            if groups > 1:
                target = sums_out.at[number, pl.ds(0, chunk), :]
            else:
                target = sums_out.at[0, pl.ds(pl.multiple_of(number * chunk, 16), chunk), :]
            return pltpu.make_async_copy(stage_rows.at[lax.rem(number, 2)], target, sem.at[lax.rem(number, 2)])

        def drain(number, carry):
            @pl.when(number >= 2)
            def _():
                copy(number - 2).wait()

            stage_rows[lax.rem(number, 2)] = position_acc[
                pl.ds(pl.multiple_of(number * taken, 8), chunk), :
            ].astype(BF)
            copy(number).start()
            return carry

        chunks = patches // taken
        lax.fori_loop(0, chunks, drain, 0)
        copy(chunks - 2).wait()
        copy(chunks - 1).wait()


def whole(shape):
    return pl.BlockSpec(shape, lambda *_: (0,) * len(shape), pipeline_mode=pl.Buffered(1))


def plan_rows(lengths, short_len, tile, long_rows):
    micros = lengths.shape[0]
    per = long_rows // tile
    starts = jnp.arange(per) * tile
    long_tiles = jnp.clip(lengths[:, None] - starts[None, :], 0, tile).reshape(-1)
    slots = short_len.shape[0]
    live = short_len > 0
    before = jnp.arange(slots)[None, :] < jnp.arange(slots)[:, None]
    rank_live = jnp.sum(jnp.where(before & live[None, :], 1, 0), axis=1)
    rank_dead = jnp.sum(jnp.where(before & ~live[None, :], 1, 0), axis=1)
    total = jnp.sum(live.astype(jnp.int32))
    rank = jnp.where(live, rank_live, total + rank_dead)
    chosen = rank[None, :] == jnp.arange(slots)[:, None]
    order = jnp.sum(jnp.where(chosen, jnp.arange(slots)[None, :], 0), axis=1)
    packed_len = jnp.sum(jnp.where(chosen, short_len[None, :], 0), axis=1)
    tile_len = jnp.concatenate([long_tiles, packed_len]).astype(jnp.int32)
    source = jnp.concatenate([jnp.arange(micros * per), micros * per + order]).astype(jnp.int32)
    parts = BLOCK // tile
    blocks = tile_len.shape[0] // parts
    active = jnp.max(tile_len.reshape(blocks, parts), axis=1) > 0
    ids = jnp.arange(blocks)
    held = jnp.max(jnp.where((ids[None, :] <= ids[:, None]) & active[None, :], ids[None, :], 0), axis=1)
    count = jnp.concatenate([-(-lengths // BLOCK), -(-total[None] // parts)]).astype(jnp.int32)
    return tile_len, source, held.astype(jnp.int32), count, chosen


def run_block(
    rows, index, targets, tile_len, source, held, count, lengths, tile, long_rows, micros, weights, groups
):
    w = weights
    total, width = rows.shape
    wide = w["up_weight"].shape[1]
    teach = targets.shape[1]
    patches = w["position"].shape[0]
    blocks = total // BLOCK
    parts = BLOCK // tile
    long_blocks = micros * long_rows // BLOCK
    short_total = total - micros * long_rows
    pairs = HEADS // 2
    pair = width // pairs
    unit_rows = width // groups
    pieces = wide // width
    early_rows = (2 * pieces + 2) * unit_rows + unit_rows * (teach - width) // width
    early_rows = -(-early_rows // 512) * 512
    chunk = -(-(patches // groups) // 16) * 16 if groups > 1 else patches // 14
    late_rows = (chunk if groups > 1 else patches) + 3 * unit_rows
    lane = lambda name: w[name].reshape(1, -1)
    params = lambda **more: pltpu.CompilerParams(vmem_limit_bytes=VMEM_LIMIT, **more)
    tiles = lambda last: [
        pl.BlockSpec((tile, last), lambda i, tl, hd, src, *_, part=part: (src[hd[i] * parts + part], 0))
        for part in range(parts)
    ]
    by_block = lambda last: pl.BlockSpec((BLOCK, last), lambda i, tl, hd, *_: (hd[i], 0))
    by_column = lambda first: pl.BlockSpec((first, BLOCK), lambda i, tl, hd, *_: (0, hd[i]))
    long_spec = pl.BlockSpec((BLOCK, width), lambda i, *_: (jnp.minimum(i, long_blocks - 1), 0))
    short_spec = pl.BlockSpec((BLOCK, width), lambda i, *_: (jnp.maximum(i - long_blocks, 0), 0))
    anywhere = pl.BlockSpec(memory_space=pl.ANY)
    bias = jnp.concatenate([w["query_bias"], jnp.zeros_like(w["query_bias"]), w["value_bias"]]).reshape(1, -1)

    triple_t, start = pl.pallas_call(
        partial(project_kernel, tile),
        grid_spec=pltpu.PrefetchScalarGridSpec(
            num_scalar_prefetch=4,
            grid=(blocks,),
            in_specs=tiles(width)
            + [anywhere, whole((width, 3 * width)), whole((1, 3 * width)), whole((1, width)), whole((1, width))],
            out_specs=[by_column(3 * width), by_block(width)],
            scratch_shapes=[
                pltpu.VMEM((patches, width), F32),
                pltpu.VMEM((2, 448, width), BF),
                pltpu.VMEM((BLOCK, width), F32),
                pltpu.SemaphoreType.DMA((2,)),
            ],
        ),
        out_shape=[
            jax.ShapeDtypeStruct((3 * width, total), BF),
            jax.ShapeDtypeStruct((total, width), F32),
        ],
        compiler_params=params(),
        name="project",
    )(
        tile_len, held, source, index, *([rows] * parts), w["position"], w["heads_weight"], bias,
        lane("mixer_gain"), lane("mixer_shift"),
    )

    def heads_spec(offset):
        return pl.BlockSpec((pair, total), lambda i, *_: (i + offset * pairs, 0))

    sums_spec = pl.BlockSpec((1, 2, total), lambda i, *_: (i, 0, 0))
    attended_t, sums = pl.pallas_call(
        partial(attend_kernel, tile, long_rows, micros),
        grid_spec=pltpu.PrefetchScalarGridSpec(
            num_scalar_prefetch=3,
            grid=(pairs,),
            in_specs=[heads_spec(0), heads_spec(1), heads_spec(2)],
            out_specs=[heads_spec(0), sums_spec],
        ),
        out_shape=[
            jax.ShapeDtypeStruct((width, total), BF),
            jax.ShapeDtypeStruct((pairs, 2, total), F32),
        ],
        compiler_params=params(),
        name="attend",
    )(tile_len, lengths, count, triple_t, triple_t, triple_t)

    middle_out = pl.pallas_call(
        partial(middle_kernel, tile, long_blocks),
        grid_spec=pltpu.PrefetchScalarGridSpec(
            num_scalar_prefetch=3,
            grid=(blocks,),
            in_specs=[by_column(width), by_block(width)]
            + tiles(teach)
            + [
                whole((width, width)), whole((1, width)), whole((1, width)), whole((1, width)),
                whole((width, wide)), whole((1, wide)), whole((wide, width)), whole((1, width)),
                whole((width, teach)), whole((1, teach)),
            ],
            out_specs=[
                long_spec, short_spec, by_column(width), by_block(width), whole((8, wide)),
                anywhere,
            ],
            scratch_shapes=[
                pltpu.VMEM((width, width), F32),
                pltpu.VMEM((wide // width, width, width), F32),
                pltpu.VMEM((wide // width, width, width), F32),
                pltpu.VMEM((width, teach), F32),
                pltpu.VMEM((BLOCK, wide), BF),
                pltpu.VMEM((BLOCK, wide), F32),
                pltpu.VMEM((2, groups, unit_rows, width), BF),
                pltpu.VMEM((2, max(groups // pieces, 1), width // max(groups // pieces, 1), width), BF),
                pltpu.SemaphoreType.DMA((2,)),
            ],
        ),
        out_shape=[
            jax.ShapeDtypeStruct((micros * long_rows, width), BF),
            jax.ShapeDtypeStruct((short_total, width), BF),
            jax.ShapeDtypeStruct((width, total), BF),
            jax.ShapeDtypeStruct((total, width), F32),
            jax.ShapeDtypeStruct((8, wide), F32),
            jax.ShapeDtypeStruct((groups, early_rows, width), BF),
        ],
        compiler_params=params(),
        name="middle",
    )(
        tile_len, held, source, attended_t, start, *([targets] * parts),
        w["out_weight"], lane("out_bias"), lane("dense_gain"), lane("dense_shift"),
        w["up_weight"], lane("up_bias"), w["down_weight"], lane("down_bias"),
        w["align_weight"], lane("align_bias"),
    )
    long_out, short_out, pulled_t, grad_middle, vector, early = middle_out

    grads = pl.pallas_call(
        partial(attend_back_kernel, tile, long_rows, micros),
        grid_spec=pltpu.PrefetchScalarGridSpec(
            num_scalar_prefetch=3,
            grid=(pairs,),
            in_specs=[heads_spec(0), heads_spec(1), heads_spec(2), heads_spec(0), sums_spec],
            out_specs=[heads_spec(0)] * 3,
            scratch_shapes=[pltpu.VMEM((pair, long_rows), F32)] * 2,
        ),
        out_shape=[jax.ShapeDtypeStruct((width, total), BF)] * 3,
        compiler_params=params(),
        name="attend_back",
    )(tile_len, lengths, count, triple_t, triple_t, triple_t, pulled_t, sums)

    long_grad, short_grad, entry_vector, late = pl.pallas_call(
        partial(entry_kernel, tile, long_blocks),
        grid_spec=pltpu.PrefetchScalarGridSpec(
            num_scalar_prefetch=3,
            grid=(blocks,),
            in_specs=[by_column(width)] * 3
            + [by_block(width), by_block(width), whole((width, 3 * width)), whole((1, width)), whole((1, width))],
            out_specs=[long_spec, short_spec, whole((8, width)), anywhere],
            scratch_shapes=[
                pltpu.VMEM((width, 3 * width), F32),
                pltpu.VMEM((patches + 8, width), F32),
                pltpu.VMEM((BLOCK, width), F32),
                pltpu.VMEM((2, groups, unit_rows, width), BF),
                pltpu.VMEM((2, chunk, width), BF),
                pltpu.SemaphoreType.DMA((2,)),
            ],
        ),
        out_shape=[
            jax.ShapeDtypeStruct((micros * long_rows, width), BF),
            jax.ShapeDtypeStruct((short_total, width), BF),
            jax.ShapeDtypeStruct((8, width), F32),
            jax.ShapeDtypeStruct((groups, late_rows, width), BF),
        ],
        compiler_params=params(),
        name="entry",
    )(
        tile_len, held, index, *grads, start, grad_middle, w["heads_weight"], lane("mixer_gain"), lane("mixer_shift"),
    )
    return long_out, short_out, long_grad, short_grad, early, late, jnp.concatenate([vector, entry_vector], axis=1)


def bit_of(number, bit):
    return lax.rem(number // (1 << bit), 2)


def reduce_plan(peers, early_rows, late_rows):
    bits = peers.bit_length() - 1
    forward = list(range(bits))
    swapped = forward[1::-1] + forward[2:]
    last = forward[2:] + forward[:2]
    pieces = []
    for source, rows in ((0, early_rows), (1, late_rows)):
        unit = 16
        units = rows // 2 // unit
        first = (2 * units + 2) // 5
        share = (first, first, units - 2 * first)
        begin = 0
        for order, parts in zip((forward, swapped, last), share):
            pieces.append((source, begin, parts * unit, tuple(order)))
            begin += parts * unit
    return pieces


def reduce_kernel(
    peers, halves, pieces, early, late, vector, early_out, late_out, vector_out, *scratch
):
    bits = peers.bit_length() - 1
    amount = len(pieces)
    kept = scratch[:amount]
    mates = scratch[amount : 2 * amount]
    mine_in = scratch[2 * amount : 3 * amount]
    landed = [scratch[3 * amount + k * bits : 3 * amount + (k + 1) * bits] for k in range(amount)]
    (
        vector_land, mate_send, mate_recv, load_sem, hop_send, hop_recv, end_send, end_recv, end_load,
        vector_send, vector_recv,
    ) = scratch[3 * amount + amount * bits :]
    d = lax.axis_index("dp")
    r = lax.axis_index("rep")
    other = 1 - r
    mate = (d, other)
    partner = [(d + (1 - 2 * bit_of(d, bit)) * (1 << bit), r) for bit in range(bits)]
    sources = (early, late)
    outs = (early_out, late_out)
    barrier = pltpu.get_barrier_semaphore()
    for device in [mate] + partner:
        pl.semaphore_signal(barrier, inc=1, device_id=device, device_id_type=pl.DeviceIdType.MESH)
    pl.semaphore_wait(barrier, bits + 1)

    def remote(source, target, send, recv, device):
        copy = pltpu.make_async_remote_copy(
            src_ref=source, dst_ref=target, send_sem=send, recv_sem=recv,
            device_id=device, device_id_type=pl.DeviceIdType.MESH,
        )
        copy.start()
        return copy

    def rows_at(source, core, begin, rows):
        return pl.ds(pl.multiple_of(core * halves[source] + begin, 16), rows)

    vector_out[...] = vector[...]
    mate_copies = []
    loads = []
    for k, (source, begin, rows, order) in enumerate(pieces):
        mate_copies.append(
            remote(
                sources[source].at[:, rows_at(source, other, begin, rows), :], mates[k],
                mate_send.at[k], mate_recv.at[k], mate,
            )
        )
        load = pltpu.make_async_copy(
            sources[source].at[:, rows_at(source, r, begin, rows), :], mine_in[k], load_sem.at[k]
        )
        load.start()
        loads.append(load)

    hops = {}
    ends = []

    def base_at(order, stage):
        base = 0
        for place in range(stage):
            base = base + bit_of(d, order[place]) * (1 << (bits - 1 - place))
        return base

    def send(k, stage):
        source, begin, rows, order = pieces[k]
        if stage == bits:
            result = kept[k].at[base_at(order, bits)]
            where = rows_at(source, r, begin, rows)
            ends.append(remote(result, outs[source].at[where, :], end_send.at[k], end_recv.at[k], mate))
            own = pltpu.make_async_copy(result, outs[source].at[where, :], end_load.at[k])
            own.start()
            ends.append(own)
            return
        size = 1 << (bits - 1 - stage)
        first = base_at(order, stage) + (1 - bit_of(d, order[stage])) * size
        hops[k, stage] = remote(
            kept[k].at[pl.ds(first, size)], landed[k][stage], hop_send.at[k, stage], hop_recv.at[k, stage],
            partner[order[stage]],
        )

    def join(k):
        order = pieces[k][3]
        loads[k].wait()
        mate_copies[k].wait_recv()

        def add(chunk, carry):
            place = 0
            for step in range(bits):
                place = place + bit_of(chunk, order[step]) * (1 << (bits - 1 - step))
            kept[k][place] = mine_in[k][chunk] + mates[k][chunk]
            return carry

        lax.fori_loop(0, peers, add, 0)

    def gather(k, stage):
        order = pieces[k][3]
        hops[k, stage].wait_recv()
        base = base_at(order, stage + 1)

        def add(chunk, carry):
            kept[k][base + chunk] = kept[k][base + chunk] + landed[k][stage][chunk]
            return carry

        lax.fori_loop(0, 1 << (bits - 1 - stage), add, 0)

    half = amount // 2
    events = sorted(
        (stage + (1 if k >= half else 0), -stage, k) for k in range(amount) for stage in range(bits + 1)
    )
    vector_copies = []

    def vector_step(stage):
        if stage > 0:
            vector_copies[-1].wait()
            vector_out[...] = vector_out[...] + vector_land[stage - 1]
        if stage <= bits:
            device = mate if stage == 0 else partner[stage - 1]
            vector_copies.append(
                remote(vector_out, vector_land.at[stage], vector_send.at[stage], vector_recv.at[stage], device)
            )

    seen = -1
    for time, negative, k in events:
        if time != seen:
            if time <= bits + 1:
                vector_step(time)
            seen = time
        stage = -negative
        if stage == 0:
            join(k)
        else:
            gather(k, stage - 1)
        send(k, stage)
    for copy in mate_copies + list(hops.values()):
        copy.wait_send()
    for copy in ends:
        copy.wait()


def reduce_all(early, late, vector):
    peers, early_rows, width = early.shape
    late_rows = late.shape[1]
    bits = peers.bit_length() - 1
    pieces = reduce_plan(peers, early_rows, late_rows)
    amount = len(pieces)
    scratch = [pltpu.VMEM((peers, rows, width), BF) for _, _, rows, _ in pieces] * 3
    for _, _, rows, _ in pieces:
        for stage in range(bits):
            scratch.append(pltpu.VMEM((1 << (bits - 1 - stage), rows, width), BF))
    scratch.append(pltpu.VMEM((bits + 1,) + vector.shape, F32))
    one = pltpu.SemaphoreType.DMA((amount,))
    many = pltpu.SemaphoreType.DMA((amount, bits))
    few = pltpu.SemaphoreType.DMA((bits + 1,))
    scratch += [one, one, one, many, many, one, one, one, few, few]
    anywhere = pl.BlockSpec(memory_space=pl.ANY)
    near = pl.BlockSpec(memory_space=pltpu.VMEM)
    return pl.pallas_call(
        partial(reduce_kernel, peers, (early_rows // 2, late_rows // 2), pieces),
        in_specs=[anywhere, anywhere, near],
        out_specs=[anywhere, anywhere, near],
        out_shape=[
            jax.ShapeDtypeStruct((early_rows, width), BF),
            jax.ShapeDtypeStruct((late_rows, width), BF),
            jax.ShapeDtypeStruct(vector.shape, F32),
        ],
        scratch_shapes=scratch,
        compiler_params=pltpu.CompilerParams(
            vmem_limit_bytes=VMEM_LIMIT, collective_id=0, has_side_effects=True
        ),
        name="reduce",
    )(early, late, vector)


def unpack(early, late, unit_rows, kept, teach):
    width = early.shape[1]
    pieces = 4
    deep = pieces * unit_rows

    def beside(first, count):
        return jnp.concatenate(
            [early[first + k * unit_rows : first + (k + 1) * unit_rows] for k in range(count)], axis=1
        )

    extra = teach - width
    third = unit_rows * extra // width
    begin = 2 * deep + 2 * unit_rows
    tail = early[begin : begin + third]
    tail = jnp.concatenate([tail[:, k * extra : (k + 1) * extra] for k in range(width // extra)], axis=0)
    first = late.shape[0] - 3 * unit_rows
    return {
        "down_weight": early[:deep],
        "up_weight": beside(deep, pieces),
        "out_weight": early[2 * deep : 2 * deep + unit_rows],
        "align_weight": jnp.concatenate([early[2 * deep + unit_rows : begin], tail], axis=1),
        "position": late[:kept],
        "heads_weight": jnp.concatenate(
            [late[first + k * unit_rows : first + (k + 1) * unit_rows] for k in range(3)], axis=1
        ),
    }


def vector_list(vector, width, wide, teach):
    return {
        "up_bias": vector[0, :wide], "out_bias": vector[1, :width], "dense_gain": vector[2, :width],
        "dense_shift": vector[3, :width], "down_bias": vector[4, :width], "align_bias": vector[5, :teach],
        "query_bias": vector[0, wide:], "mixer_gain": vector[1, wide:], "value_bias": vector[2, wide:],
        "mixer_shift": vector[3, wide:],
    }


def shards(
    long_clips,
    short_clips,
    long_index,
    short_index,
    long_length,
    short_length,
    destination,
    long_target,
    short_target,
    position,
    mixer_gain,
    mixer_shift,
    heads_weight,
    query_bias,
    value_bias,
    out_weight,
    out_bias,
    dense_gain,
    dense_shift,
    up_weight,
    up_bias,
    down_weight,
    down_bias,
    align_weight,
    align_bias,
):
    peers = lax.axis_size("dp")
    copies = lax.axis_size("rep")
    mine = lax.axis_index("dp")
    own_copy = lax.axis_index("rep")
    micros, _, long_rows, width = long_clips.shape
    home_slots, tile = short_clips.shape[1:3]
    bal_slots = home_slots // 2
    slots = micros * home_slots
    weights = dict(
        zip(
            WEIGHT_NAMES,
            (
                position, mixer_gain, mixer_shift, heads_weight, query_bias, value_bias, out_weight, out_bias,
                dense_gain, dense_shift, up_weight, up_bias, down_weight, down_bias, align_weight, align_bias,
            ),
        )
    )
    group_dest = lax.dynamic_index_in_dim(
        destination.reshape(micros, peers, copies, home_slots), own_copy, 2, keepdims=False
    )
    group_len = lax.dynamic_index_in_dim(
        short_length.reshape(micros, peers, copies, home_slots), own_copy, 2, keepdims=False
    )
    own_dest = lax.dynamic_index_in_dim(group_dest, mine, 1, keepdims=False).reshape(slots)
    own_len = lax.dynamic_index_in_dim(group_len, mine, 1, keepdims=False).reshape(slots)
    lengths = long_length[:, 0]
    tile_len, source, held, count, chosen = plan_rows(lengths, own_len, tile, long_rows)
    packed_index = jnp.sum(
        jnp.where(chosen[:, :, None], short_index.reshape(1, slots, tile), 0), axis=1
    )
    index = jnp.concatenate([long_index.reshape(-1), packed_index.reshape(-1)])
    rows = jnp.concatenate([long_clips.reshape(-1, width), short_clips.reshape(-1, width)], axis=0)
    teach = long_target.shape[-1]
    targets = jnp.concatenate([long_target.reshape(-1, teach), short_target.reshape(-1, teach)], axis=0)
    groups = peers if copies == 2 and width % (16 * peers) == 0 else 1
    long_out, short_out, long_grad, short_grad, early, late, vector = run_block(
        rows, index, targets, tile_len, source, held, count, lengths, tile, long_rows, micros, weights, groups
    )
    pick = chosen.astype(jnp.bfloat16)
    slot_micro = jnp.arange(slots) // home_slots
    wanted = (
        (own_dest[None, None, :] == jnp.arange(peers)[:, None, None])
        & (own_len[None, None, :] > 0)
        & (slot_micro[None, None, :] == jnp.arange(micros)[None, :, None])
    )
    send_map = jnp.einsum("pms,ks->pmk", wanted.astype(jnp.bfloat16), pick).reshape(peers * micros, slots)
    send = jnp.dot(send_map.astype(jnp.bfloat16), short_out.reshape(slots, tile * width))
    got = lax.all_to_all(
        send.reshape(peers, micros, tile, width), "dp", split_axis=0, concat_axis=0, tiled=True
    )
    slot_pick = jnp.arange(home_slots)[:, None] % bal_slots == jnp.arange(bal_slots)[None, :]
    incoming = (group_dest == mine) & (group_len > 0)
    recv_map = jnp.any(incoming[..., None] & slot_pick[None, None], axis=2)
    short_bal = jnp.einsum("mpb,pmtd->mbtd", recv_map.astype(jnp.bfloat16), got)
    short_home = jnp.dot(pick.T, short_grad.reshape(slots, tile * width))
    return (
        long_out.reshape(micros, 1, long_rows, width),
        short_bal,
        long_grad.reshape(micros, 1, long_rows, width),
        short_home.reshape(micros, home_slots, tile, width),
    ) + combine(early, late, vector, copies, groups, position.shape[0], up_weight.shape[1], teach)


def combine(early, late, vector, copies, groups, patches, wide, teach):
    peers = lax.axis_size("dp")
    mine = lax.axis_index("dp")
    width = early.shape[2]
    if groups == peers:
        early, late, vector = reduce_all(early, late, vector)
        matrices = unpack(early, late, width // peers, patches // peers, teach)
    else:
        vector = lax.psum(vector, ("dp", "rep"))
        matrices = unpack(early[0], late[0], width, patches, teach)
    vectors = vector_list(vector, width, wide, teach)
    names = [name for name in WEIGHT_NAMES if name in vectors]
    flat = jnp.concatenate([vectors[name].reshape(peers, -1) for name in names], axis=1)
    flat = lax.dynamic_index_in_dim(flat, mine, 0, keepdims=False)
    shared = {}
    begin = 0
    for name in names:
        size = vectors[name].shape[0] // peers
        shared[name] = flat[begin : begin + size]
        begin += size
    for name, piece in matrices.items():
        if groups != peers:
            rows = piece.shape[0] // peers
            padded = -(-rows // (8 * copies)) * 8 * copies
            if padded != rows:
                piece = piece.reshape(peers, rows, -1)
                piece = jnp.pad(piece, ((0, 0), (0, padded - rows), (0, 0)))
                piece = piece.reshape(peers * padded, -1)
            piece = lax.psum_scatter(piece, ("dp", "rep"), scatter_dimension=0, tiled=True)
            piece = lax.all_gather(piece, "rep", axis=0, tiled=True)[:rows]
        shared[name] = piece.astype(jnp.float32)
    return tuple(shared[name] for name in WEIGHT_NAMES)


def solution(mesh):
    placed = (
        P(None, ("dp", "rep"), None, None),
        P(None, ("dp", "rep"), None, None),
        P(None, ("dp", "rep"), None),
        P(None, ("dp", "rep"), None),
        P(None, ("dp", "rep")),
        P(),
        P(),
        P(None, ("dp", "rep"), None, None),
        P(None, ("dp", "rep"), None, None),
        P(),
        P(),
        P(),
        P(),
        P(),
        P(),
        P(),
        P(),
        P(),
        P(),
        P(),
        P(),
        P(),
        P(),
        P(),
        P(),
    )
    return jax.shard_map(
        shards,
        mesh=mesh,
        in_specs=placed,
        out_specs=(
            P(None, ("dp", "rep"), None, None),
            P(None, ("dp", "rep"), None, None),
            P(None, ("dp", "rep"), None, None),
            P(None, ("dp", "rep"), None, None),
            P("dp", None),
            P("dp"),
            P("dp"),
            P("dp", None),
            P("dp"),
            P("dp"),
            P("dp", None),
            P("dp"),
            P("dp"),
            P("dp"),
            P("dp", None),
            P("dp"),
            P("dp", None),
            P("dp"),
            P("dp", None),
            P("dp"),
        ),
        check_vma=False,
    )
```

```python
from functools import partial

import jax
import jax.numpy as jnp
from jax import lax
from jax.experimental import pallas as pl
from jax.experimental.pallas import tpu as pltpu
from jax.sharding import PartitionSpec as P

HEADS = 12
EPS = 1e-06
MASKED = -1000000000.0
WEIGHT_NAMES = (
    "position",
    "mixer_gain",
    "mixer_shift",
    "heads_weight",
    "query_bias",
    "value_bias",
    "out_weight",
    "out_bias",
    "dense_gain",
    "dense_shift",
    "up_weight",
    "up_bias",
    "down_weight",
    "down_bias",
    "align_weight",
    "align_bias",
)


BLOCK = 256
BF = jnp.bfloat16
F32 = jnp.float32
VMEM_LIMIT = 66_000_000


def dot(left, right, dims):
    return lax.dot_general(left, right, ((dims[:1], dims[1:]), ((), ())), preferred_element_type=F32)


def centre(values):
    mean = jnp.mean(values, axis=-1, keepdims=True)
    centered = values - mean
    spread = jnp.mean(centered * centered, axis=-1, keepdims=True)
    inverse = lax.rsqrt(spread + EPS)
    return centered * inverse, inverse


def centre_back(grad, unit, inverse):
    first = jnp.mean(grad, axis=-1, keepdims=True)
    second = jnp.mean(grad * unit, axis=-1, keepdims=True)
    return inverse * (grad - first - unit * second)


def valid_rows(tile_len, block, tile):
    row = lax.broadcasted_iota(jnp.int32, (BLOCK, 1), 0)
    parts = BLOCK // tile
    limit = tile_len[block * parts]
    for part in range(1, parts):
        limit = jnp.where(row >= part * tile, tile_len[block * parts + part], limit)
    return lax.rem(row, tile) < limit


def plan_kernel(tile, long_rows, home, copies, lengths, short_len, tile_len, source, count):
    micros = lengths.shape[0]
    per = long_rows // tile
    step = 128 // tile
    base = (lax.axis_index("dp") * copies + lax.axis_index("rep")) * home

    def put(place, origin, size):
        source[place] = origin
        tile_len[place] = size

    place = jnp.int32(0)
    taken = []
    for micro in range(micros):
        length = lengths[micro, 0]
        some = lax.div(length + 127, 128) * step
        count[micro] = lax.div(length + BLOCK - 1, BLOCK)
        count[micros + 1 + micro] = place

        def add(number, carry, micro=micro, length=length, place=place):
            put(place + number, micro * per + number, jnp.clip(length - number * tile, 0, tile))
            return carry

        lax.fori_loop(0, some, add, 0)
        taken.append(some)
        place = place + some
    first = place
    slots = micros * home
    sizes = [short_len[slot // home, base + slot % home] for slot in range(slots)]
    for wanted in (True, False):
        for slot, size in enumerate(sizes):
            fits = (size > 0) if wanted else (size <= 0)

            @pl.when(fits)
            def _():
                put(place, micros * per + slot, size)

            place = place + jnp.where(fits, 1, 0)
        if wanted:
            parts = BLOCK // tile
            count[micros] = lax.div(place - first + parts - 1, parts)
            count[2 * micros + 1] = first
            count[2 * micros + 2] = lax.div(place + parts - 1, parts)
    for micro in range(micros):
        def fill(number, carry, micro=micro, place=place - taken[micro]):
            put(place + number, micro * per + number, 0)
            return carry

        lax.fori_loop(taken[micro], per, fill, 0)
        place = place + per - taken[micro]


def pieced(step, source, parts, near, far, border):
    chosen = [
        jnp.where(source[step * parts + part] < border, near[part][...], far[part][...]) for part in range(parts)
    ]
    return jnp.concatenate(chosen, axis=0).astype(F32)


def put_tiles(step, value, source, border, tile, stage, sem, near, far):
    parts = BLOCK // tile
    slot = lax.rem(step, 2)

    def settle(which):
        for part in range(parts):
            pltpu.make_async_copy(
                stage.at[which, pl.ds(part * tile, tile), :], near.at[pl.ds(0, tile), :], sem.at[which, part]
            ).wait()

    @pl.when(step >= 2)
    def _():
        settle(slot)

    stage[slot] = value
    for part in range(parts):
        origin = source[step * parts + part]
        view = stage.at[slot, pl.ds(part * tile, tile), :]

        @pl.when(origin < border)
        def _():
            where = pl.ds(pl.multiple_of(origin * tile, tile), tile)
            pltpu.make_async_copy(view, near.at[where, :], sem.at[slot, part]).start()

        @pl.when(origin >= border)
        def _():
            where = pl.ds(pl.multiple_of((origin - border) * tile, tile), tile)
            pltpu.make_async_copy(view, far.at[where, :], sem.at[slot, part]).start()

    @pl.when(step == pl.num_programs(0) - 1)
    def _():
        settle(1 - slot)
        settle(slot)


def project_kernel(tile, border, last, tile_len, source, count, index, *refs):
    parts = BLOCK // tile
    near = refs[:parts]
    far = refs[parts : 2 * parts]
    table_any, weight, vectors, out, start_out, table, stage, rows, sem = refs[2 * parts :]
    step = pl.program_id(0)
    width = weight.shape[0]
    chunk = stage.shape[1]
    chunks = table.shape[0] // chunk

    def fetch(number):
        return pltpu.make_async_copy(
            table_any.at[pl.ds(pl.multiple_of(number * chunk, 16), chunk), :],
            stage.at[lax.rem(number, 2)],
            sem.at[lax.rem(number, 2)],
        )

    @pl.when(step == 0)
    def _():
        fetch(0).start()
        rows[...] = jnp.zeros_like(rows)

        def load(number, carry):
            @pl.when(number + 1 < chunks)
            def _():
                fetch(number + 1).start()

            fetch(number).wait()
            table[pl.ds(pl.multiple_of(number * chunk, 16), chunk), :] = stage[lax.rem(number, 2)].astype(F32)
            return carry

        lax.fori_loop(0, chunks, load, 0)

    @pl.when(step == count[last])
    def _():
        out[...] = jnp.zeros_like(out)

    @pl.when(step < count[last])
    def _():
        def gather(part, carry):
            origin = source[step * parts + part] * tile
            first = part * tile

            def some(group, inner):
                base = pl.multiple_of(first + group * 8, 8)
                for row in range(8):
                    place = index[origin + group * 8 + row]
                    rows[pl.ds(base + row, 1), :] = table[pl.ds(place, 1), :]
                return inner

            lax.fori_loop(0, lax.div(tile_len[step * parts + part] + 7, 8), some, 0)
            return carry

        lax.fori_loop(0, parts, gather, 0)
        start = pieced(step, source, parts, near, far, border) + rows[...]
        start_out[...] = start
        unit, _ = centre(start)
        normed = (unit * vectors[0:1, :width] + vectors[1:2, :width]).astype(BF)
        for part in range(3):
            cols = slice(part * width, (part + 1) * width)
            triple = dot(normed, weight[:, cols], (1, 0))
            if part == 0:
                triple = (triple + vectors[2:3, :width]).astype(BF) * BF(0.125)
            elif part == 1:
                triple = triple.astype(BF)
            else:
                triple = (triple + vectors[3:4, :width]).astype(BF)
            out[cols, :] = triple.T


def masked_tile(tile_scores, limit):
    key = lax.broadcasted_iota(jnp.int32, tile_scores.shape, 0)
    return jnp.where(key < limit, tile_scores, MASKED)


def block_mask(tile_len, first, tile):
    key = lax.broadcasted_iota(jnp.int32, (BLOCK, BLOCK), 0)
    asked = lax.broadcasted_iota(jnp.int32, (BLOCK, BLOCK), 1)
    limit = tile_len[first]
    for part in range(1, BLOCK // tile):
        limit = jnp.where(key >= part * tile, tile_len[first + part], limit)
    return (key // tile == asked // tile) & (lax.rem(key, tile) < limit)


def attend_kernel(tile, long_rows, clips, tile_len, length, count, query, keys, values, out, logsum, even, odd):
    head_dim = query.shape[0] // 2
    most = long_rows // BLOCK
    boards = (even, odd)

    def score(head, column, first, size, fix):
        lanes = slice(head * head_dim, (head + 1) * head_dim)
        asked = query[lanes, pl.ds(column, BLOCK)]
        for number in range(size):
            part = dot(keys[lanes, pl.ds(first + number * BLOCK, BLOCK)], asked, (0, 0))
            if number == size - 1:
                part = fix(part)
            boards[head][number * BLOCK : (number + 1) * BLOCK, :] = part

    def finish(head, column, first, size):
        lanes = slice(head * head_dim, (head + 1) * head_dim)
        board = boards[head]
        top = jnp.max(board[: size * BLOCK, :], axis=0, keepdims=True)
        total = None
        gathered = None
        for number in range(size):
            weight = jnp.exp(board[number * BLOCK : (number + 1) * BLOCK, :] - top)
            part = jnp.sum(weight, axis=0, keepdims=True)
            held = values[lanes, pl.ds(first + number * BLOCK, BLOCK)]
            term = dot(held, weight.astype(BF), (1, 0))
            total = part if total is None else total + part
            gathered = term if gathered is None else gathered + term
        out[lanes, pl.ds(column, BLOCK)] = (gathered / total).astype(BF)
        logsum[0, pl.ds(head, 1), pl.ds(column, BLOCK)] = top + jnp.log(total)

    def rows(first, size, fix):
        def at(block):
            return pl.multiple_of(first + block * BLOCK, 128)

        score(0, at(0), first, size, fix)

        def ask(block, carry):
            score(1, at(block), first, size, fix)
            finish(0, at(block), first, size)
            score(0, at(jnp.minimum(block + 1, size - 1)), first, size, fix)
            finish(1, at(block), first, size)
            return carry

        lax.fori_loop(0, size, ask, 0)

    def clip(number, carry):
        first = pl.multiple_of(count[clips + 1 + number] * tile, 128)
        blocks = count[number]
        rest = length[number]
        for size in range(1, most + 1):
            @pl.when(blocks == size)
            def _():
                rows(first, size, lambda part: masked_tile(part, rest - (size - 1) * BLOCK))
        return carry

    out[...] = jnp.zeros_like(out)
    lax.fori_loop(0, clips, clip, 0)

    def short(number, carry):
        begin = count[2 * clips + 1] + number * (BLOCK // tile)
        column = pl.multiple_of(begin * tile, 128)
        allowed = block_mask(tile_len, begin, tile)
        rows(column, 1, lambda part: jnp.where(allowed, part, MASKED))
        return carry

    lax.fori_loop(0, count[clips], short, 0)


def attend_back_kernel(
    tile, long_rows, clips, tile_len, length, count, query, keys, values, grad, logsum,
    query_out, key_out, value_out, key_sum, value_sum, even, odd, even_back, odd_back,
):
    head_dim = query.shape[0] // 2
    most = long_rows // BLOCK
    boards = (even, odd)
    backs = (even_back, odd_back)

    def score(head, column, first, size, fix):
        lanes = slice(head * head_dim, (head + 1) * head_dim)
        asked = query[lanes, pl.ds(column, BLOCK)]
        pulled = grad[lanes, pl.ds(column, BLOCK)]
        for number in range(size):
            here = pl.ds(first + number * BLOCK, BLOCK)
            there = slice(number * BLOCK, (number + 1) * BLOCK)
            part = dot(keys[lanes, here], asked, (0, 0))
            if number == size - 1:
                part = fix(part)
            boards[head][there, :] = part
            backs[head][there, :] = dot(values[lanes, here], pulled, (0, 0))

    def finish(head, column, first, size, limit):
        lanes = slice(head * head_dim, (head + 1) * head_dim)
        asked = query[lanes, pl.ds(column, BLOCK)]
        pulled = grad[lanes, pl.ds(column, BLOCK)]
        own = lax.broadcasted_iota(jnp.int32, (1, BLOCK), 1) < limit
        base = jnp.where(own, logsum[0, pl.ds(head, 1), pl.ds(column, BLOCK)], -1e3 * MASKED)
        inner = None
        for number in range(size):
            there = slice(number * BLOCK, (number + 1) * BLOCK)
            prob = jnp.exp(boards[head][there, :] - base)
            boards[head][there, :] = prob
            part = jnp.sum(prob * backs[head][there, :], axis=0, keepdims=True)
            inner = part if inner is None else inner + part
            value_sum[lanes, there] += dot(pulled, prob.astype(BF), (1, 1))
        query_sum = None
        for number in range(size):
            here = pl.ds(first + number * BLOCK, BLOCK)
            there = slice(number * BLOCK, (number + 1) * BLOCK)
            moved = (boards[head][there, :] * (backs[head][there, :] - inner)).astype(BF)
            key_sum[lanes, there] += dot(asked, moved, (1, 1))
            term = dot(keys[lanes, here], moved, (1, 0))
            query_sum = term if query_sum is None else query_sum + term
        query_out[lanes, pl.ds(column, BLOCK)] = (query_sum * 0.125).astype(BF)

    def rows(first, size, fix, rest):
        def at(block):
            return pl.multiple_of(first + block * BLOCK, 128)

        key_sum[:, : size * BLOCK] = jnp.zeros((2 * head_dim, size * BLOCK), F32)
        value_sum[:, : size * BLOCK] = jnp.zeros((2 * head_dim, size * BLOCK), F32)
        score(0, at(0), first, size, fix)

        def ask(block, carry):
            limit = rest - block * BLOCK
            after = jnp.minimum(block + 1, size - 1)
            score(1, at(block), first, size, fix)
            finish(0, at(block), first, size, limit)
            score(0, at(after), first, size, fix)
            finish(1, at(block), first, size, limit)
            return carry

        lax.fori_loop(0, size, ask, 0)
        key_out[:, pl.ds(first, size * BLOCK)] = key_sum[:, : size * BLOCK].astype(BF)
        value_out[:, pl.ds(first, size * BLOCK)] = value_sum[:, : size * BLOCK].astype(BF)

    def clip(number, carry):
        first = pl.multiple_of(count[clips + 1 + number] * tile, 128)
        blocks = count[number]
        rest = length[number]
        for size in range(1, most + 1):
            @pl.when(blocks == size)
            def _():
                rows(first, size, lambda part: masked_tile(part, rest - (size - 1) * BLOCK), rest)
        return carry

    for empty in (query_out, key_out, value_out):
        empty[...] = jnp.zeros_like(empty)
    lax.fori_loop(0, clips, clip, 0)

    def short(number, carry):
        begin = count[2 * clips + 1] + number * (BLOCK // tile)
        column = pl.multiple_of(begin * tile, 128)
        allowed = block_mask(tile_len, begin, tile)
        rows(column, 1, lambda part: jnp.where(allowed, part, MASKED), BLOCK)
        return carry

    lax.fori_loop(0, count[clips], short, 0)


def gelu_both(upper):
    spread = 0.5 * (1.0 + lax.erf(upper * 0.7071067811865476))
    bell = jnp.exp(-0.5 * upper * upper) * 0.3989422804014327
    return upper * spread, spread + upper * bell


def write_out(entries, sem):
    waiting = [None, None]
    for number, (source, stage, target) in enumerate(entries):
        slot = number % 2
        if waiting[slot] is not None:
            waiting[slot].wait()
        value = source()
        view = stage.at[slot, :, : value.shape[1], : value.shape[2]]
        stage[slot, :, : value.shape[1], : value.shape[2]] = value.astype(BF)
        copy = pltpu.make_async_copy(view, target, sem.at[slot])
        copy.start()
        waiting[slot] = copy
    for copy in waiting:
        if copy is not None:
            copy.wait()


def middle_kernel(tile, border, last, tile_len, source, count, attended_t, start_in, *refs):
    parts = BLOCK // tile
    near = refs[:parts]
    far = refs[parts : 2 * parts]
    (
        out_w, up_w, down_w, align_w, vectors,
        long_out, short_out, pull_out, grad_out, vector_out, sums_out,
        out_acc, up_acc, down_acc, align_acc, hidden, slope, stage, stage_down, show, show_sem, sem,
    ) = refs[2 * parts :]
    step = pl.program_id(0)
    width = out_w.shape[0]
    wide = up_w.shape[1]
    teach = align_w.shape[1]
    pieces = wide // width
    live = step < count[last]

    @pl.when(step == 0)
    def _():
        for acc in (out_acc, up_acc, down_acc, align_acc):
            acc[...] = jnp.zeros_like(acc)
        vector_out[...] = jnp.zeros_like(vector_out)

    def put(value):
        put_tiles(step, value, source, border, tile, show, show_sem, long_out, short_out)

    def add_vector(row, value):
        size = value.shape[1]
        vector_out[row : row + 1, :size] += value

    def over_rows(value):
        return jnp.sum(value, axis=0, keepdims=True)

    @pl.when(step == count[last])
    def _():
        pull_out[...] = jnp.zeros_like(pull_out)

    @pl.when(jnp.logical_not(live))
    def _():
        put(jnp.zeros((BLOCK, width), BF))

    @pl.when(live)
    def _():
        ok = valid_rows(tile_len, step, tile)
        across = attended_t[...]
        middle = start_in[...] + dot(across, out_w[...], (0, 0)) + vectors[4:5, :width]
        unit, inverse = centre(middle)
        dense = (unit * vectors[5:6, :width] + vectors[6:7, :width]).astype(BF)
        result = middle + vectors[7:8, :width]
        for piece in range(pieces):
            cols = slice(piece * width, (piece + 1) * width)
            upper = dot(dense, up_w[:, cols], (1, 0)) + vectors[8:9, cols]
            bent, tilt = gelu_both(upper)
            low = bent.astype(BF)
            hidden[:, cols] = low
            slope[:, cols] = tilt
            result = result + dot(low, down_w[cols, :], (1, 0))
        shown = jnp.where(ok, result, 0.0).astype(BF)
        put(shown)
        projected = dot(shown, align_w[...], (1, 0)) + vectors[9:10, :teach]
        target = pieced(step, source, parts, near, far, border)
        miss = jnp.where(ok, projected - target, 0.0).astype(BF)
        add_vector(5, over_rows(miss.astype(F32)))
        align_acc[...] += dot(shown, miss, (0, 0))
        pulled = dot(miss, align_w[...], (1, 1)).astype(BF)
        pulled_wide = pulled.astype(F32)
        add_vector(4, over_rows(pulled_wide))
        grad_dense = None
        for piece in range(pieces):
            cols = slice(piece * width, (piece + 1) * width)
            grad_upper = dot(pulled, down_w[cols, :], (1, 1)) * slope[:, cols]
            low = grad_upper.astype(BF)
            vector_out[0:1, cols] += over_rows(low.astype(F32))
            down_acc[piece] += dot(hidden[:, cols], pulled, (0, 0))
            up_acc[piece] += dot(dense, low, (0, 0))
            term = dot(low, up_w[:, cols], (1, 1))
            grad_dense = term if grad_dense is None else grad_dense + term
        add_vector(2, over_rows(grad_dense * unit))
        add_vector(3, over_rows(grad_dense))
        grad_middle = pulled_wide + centre_back(grad_dense * vectors[5:6, :width], unit, inverse)
        grad_out[...] = grad_middle
        branch = grad_middle.astype(BF)
        add_vector(1, over_rows(branch.astype(F32)))
        out_acc[...] += dot(across, branch, (1, 0))
        pull_out[...] = dot(out_w[...], branch, (1, 1)).astype(BF)

    @pl.when(step == pl.num_programs(0) - 1)
    def _():
        groups, unit_rows = stage.shape[1:3]
        deep = pieces * unit_rows
        some, tall = stage_down.shape[1:3]

        def grouped(value):
            return value.reshape(groups, unit_rows, value.shape[-1])

        entries = []
        for piece in range(pieces):
            if groups >= pieces:
                target = sums_out.at[pl.ds(piece * some, some), pl.ds(0, tall), :]
            else:
                target = sums_out.at[:, pl.ds(piece * tall, tall), :]
            entries.append((lambda piece=piece: down_acc[piece].reshape(some, tall, width), stage_down, target))
        for piece in range(pieces):
            target = sums_out.at[:, pl.ds(deep + piece * unit_rows, unit_rows), :]
            entries.append((lambda piece=piece: grouped(up_acc[piece]), stage, target))
        begin = 2 * deep
        entries.append((lambda: grouped(out_acc[...]), stage, sums_out.at[:, pl.ds(begin, unit_rows), :]))
        begin += unit_rows
        entries.append(
            (lambda: grouped(align_acc[:, :width]), stage, sums_out.at[:, pl.ds(begin, unit_rows), :])
        )
        begin += unit_rows
        extra = teach - width
        third = unit_rows * extra // width
        for part in range(width // extra):
            entries.append(
                (
                    lambda part=part: grouped(align_acc[:, width:])[:, part * third : (part + 1) * third],
                    stage,
                    sums_out.at[:, pl.ds(begin, third), pl.ds(part * extra, extra)],
                )
            )
        write_out(entries, sem)


def entry_kernel(tile, border, last, tile_len, source, count, index, *refs):
    (
        query_t, key_t, value_t, start_in, grad_in, weight, vectors,
        long_out, short_out, vector_out, sums_out,
        weight_acc, position_acc, moved, stage, stage_rows, show, show_sem, sem,
    ) = refs
    step = pl.program_id(0)
    width = weight.shape[0]
    live = step < count[last]

    @pl.when(step == 0)
    def _():
        weight_acc[...] = jnp.zeros_like(weight_acc)
        vector_out[...] = jnp.zeros_like(vector_out)

        def clear(number, carry):
            position_acc[pl.ds(pl.multiple_of(number * 64, 64), 64), :] = jnp.zeros((64, width), F32)
            return carry

        lax.fori_loop(0, position_acc.shape[0] // 64, clear, 0)
        left = position_acc.shape[0] % 64
        if left:
            position_acc[position_acc.shape[0] - left :, :] = jnp.zeros((left, width), F32)

    def put(value):
        put_tiles(step, value, source, border, tile, show, show_sem, long_out, short_out)

    def over_rows(value):
        return jnp.sum(value, axis=0, keepdims=True)

    @pl.when(jnp.logical_not(live))
    def _():
        put(jnp.zeros((BLOCK, width), BF))

    @pl.when(live)
    def _():
        unit, inverse = centre(start_in[...])
        normed = (unit * vectors[0:1, :width] + vectors[1:2, :width]).astype(BF)
        grad_normed = None
        for part in range(3):
            cols = slice(part * width, (part + 1) * width)
            across = (query_t, key_t, value_t)[part][...]
            if part != 1:
                vector_out[part : part + 1, :] += over_rows(across.T.astype(F32))
            weight_acc[:, cols] += dot(normed, across, (0, 1))
            term = dot(across, weight[:, cols], (0, 1))
            grad_normed = term if grad_normed is None else grad_normed + term
        vector_out[1:2, :] += over_rows(grad_normed * unit)
        vector_out[3:4, :] += over_rows(grad_normed)
        grad_start = grad_in[...] + centre_back(grad_normed * vectors[0:1, :width], unit, inverse)
        put(grad_start.astype(BF))
        moved[...] = grad_start
        parts = BLOCK // tile

        def spread(number, carry):
            first = number * tile
            origin = source[step * parts + number] * tile

            def some(group, inner):
                base = pl.multiple_of(first + group * 8, 8)
                for row in range(8):
                    place = index[origin + group * 8 + row]
                    position_acc[pl.ds(place, 1), :] += moved[pl.ds(base + row, 1), :]
                return inner

            lax.fori_loop(0, lax.div(tile_len[step * parts + number] + 7, 8), some, 0)
            return carry

        lax.fori_loop(0, parts, spread, 0)

    @pl.when(step == pl.num_programs(0) - 1)
    def _():
        groups, unit_rows = stage.shape[1:3]
        chunk = stage_rows.shape[1]
        patches = position_acc.shape[0] - 8
        taken = patches // groups if groups > 1 else chunk
        begin = sums_out.shape[1] - 3 * unit_rows
        entries = []
        for part in range(3):
            cols = slice(part * width, (part + 1) * width)
            entries.append(
                (
                    lambda cols=cols: weight_acc[:, cols].reshape(groups, unit_rows, width),
                    stage,
                    sums_out.at[:, pl.ds(begin + part * unit_rows, unit_rows), :],
                )
            )
        write_out(entries, sem)

        def copy(number):
            if groups > 1:
                target = sums_out.at[number, pl.ds(0, chunk), :]
            else:
                target = sums_out.at[0, pl.ds(pl.multiple_of(number * chunk, 16), chunk), :]
            return pltpu.make_async_copy(stage_rows.at[lax.rem(number, 2)], target, sem.at[lax.rem(number, 2)])

        def drain(number, carry):
            @pl.when(number >= 2)
            def _():
                copy(number - 2).wait()

            stage_rows[lax.rem(number, 2)] = position_acc[
                pl.ds(pl.multiple_of(number * taken, 8), chunk), :
            ].astype(BF)
            copy(number).start()
            return carry

        chunks = patches // taken
        lax.fori_loop(0, chunks, drain, 0)
        copy(chunks - 2).wait()
        copy(chunks - 1).wait()


def send_kernel(home, copies, short_len, destination, shown, out):
    base = (lax.axis_index("dp") * copies + lax.axis_index("rep")) * home
    out[...] = jnp.zeros_like(out)
    for slot in range(shown.shape[0]):
        micro, place = slot // home, base + slot % home

        @pl.when(short_len[micro, place] > 0)
        def _():
            out[destination[micro, place], micro] = shown[slot]


def finish_kernel(
    home, copies, short_len, destination, got, early, late, vector,
    balanced, position_g, heads_g, out_g, up_g, down_g, align_g, thin, up_row, align_row, sem,
):
    peers = got.shape[0]
    micros, bal = balanced.shape[:2]
    width = position_g.shape[1]
    unit_rows = out_g.shape[0]
    pieces = up_g.shape[1] // width
    d = lax.axis_index("dp")
    r = lax.axis_index("rep")
    number = 0
    found_all = []
    for micro in range(micros):
        for slot in range(bal):
            def look(peer, found):
                base = (peer * copies + r) * home
                for place in range(slot, home, bal):
                    fits = (short_len[micro, base + place] > 0) & (destination[micro, base + place] == d)
                    found = jnp.where(fits, peer, found)
                return found

            found = lax.fori_loop(0, peers, look, jnp.int32(-1))
            found_all.append(found)

            @pl.when(found >= 0)
            def _():
                pltpu.make_async_copy(
                    got.at[jnp.maximum(found, 0), micro], balanced.at[micro, slot], sem.at[number]
                ).start()

            @pl.when(found < 0)
            def _():
                balanced[micro, slot] = jnp.zeros(balanced.shape[2:], BF)

            number += 1
    position_g[...] = late[: position_g.shape[0], :].astype(F32)
    first = late.shape[0] - 3 * unit_rows
    for part in range(3):
        heads_g[:, part * width : (part + 1) * width] = late[
            first + part * unit_rows : first + (part + 1) * unit_rows, :
        ].astype(F32)
    deep = pieces * unit_rows
    down_g[...] = early[:deep, :].astype(F32)
    for part in range(pieces):
        up_g[:, part * width : (part + 1) * width] = early[
            deep + part * unit_rows : deep + (part + 1) * unit_rows, :
        ].astype(F32)
    out_g[...] = early[2 * deep : 2 * deep + unit_rows, :].astype(F32)
    align_g[:, :width] = early[2 * deep + unit_rows : 2 * deep + 2 * unit_rows, :].astype(F32)
    extra = align_g.shape[1] - width
    third = unit_rows * extra // width
    begin = 2 * deep + 2 * unit_rows
    for part in range(width // extra):
        align_g[part * third : (part + 1) * third, width:] = early[
            begin : begin + third, part * extra : (part + 1) * extra
        ].astype(F32)

    def pick(value, size):
        row = lax.broadcasted_iota(jnp.int32, (value.shape[1], size), 0)
        col = lax.broadcasted_iota(jnp.int32, (value.shape[1], size), 1)
        chosen = jnp.where(row == d * size + col, 1.0, 0.0)
        return jnp.dot(value, chosen, preferred_element_type=F32, precision=lax.Precision.HIGHEST)

    thin[0] = pick(vector[:, :width], thin.shape[2])
    thin[1] = pick(vector[:, pieces * width :], thin.shape[2])
    up_row[...] = pick(vector[:, : pieces * width], up_row.shape[1])
    align_row[...] = pick(vector[:, : align_g.shape[1]], align_row.shape[1])
    for number, found in enumerate(found_all):
        @pl.when(found >= 0)
        def _():
            pltpu.make_async_copy(
                got.at[0, number // bal], balanced.at[number // bal, number % bal], sem.at[number]
            ).wait()


def whole(shape):
    return pl.BlockSpec(shape, lambda *_: (0,) * len(shape), pipeline_mode=pl.Buffered(1))


def params(**more):
    return pltpu.CompilerParams(vmem_limit_bytes=VMEM_LIMIT, **more)


def run_block(
    long_rows_in, short_rows_in, index, long_target, short_target, tile_len, source, count, lengths,
    tile, long_rows, micros, weights, groups,
):
    w = weights
    width = long_rows_in.shape[1]
    total = long_rows_in.shape[0] + short_rows_in.shape[0]
    wide = w["up_weight"].shape[1]
    teach = long_target.shape[1]
    patches = w["position"].shape[0]
    blocks = total // BLOCK
    parts = BLOCK // tile
    border = micros * long_rows // tile
    last = 2 * micros + 2
    pairs = HEADS // 2
    pair = width // pairs
    unit_rows = width // groups
    pieces = wide // width
    early_rows = (2 * pieces + 2) * unit_rows + unit_rows * (teach - width) // width
    early_rows = -(-early_rows // 512) * 512
    chunk = -(-(patches // groups) // 16) * 16 if groups > 1 else patches // 14
    late_rows = (chunk if groups > 1 else patches) + 3 * unit_rows
    names = (
        "mixer_gain", "mixer_shift", "query_bias", "value_bias", "out_bias", "dense_gain", "dense_shift",
        "down_bias", "up_bias", "align_bias",
    )
    rows = [jnp.pad(w[name], (0, wide - w[name].shape[0])) for name in names]
    vectors = jnp.stack(rows + [jnp.zeros((wide,), F32)] * (16 - len(rows)))

    def kept(i, count):
        return jnp.minimum(i, count[last] - 1)

    def tiles(width):
        near = [
            pl.BlockSpec(
                (tile, width),
                lambda i, tl, src, cnt, *_, part=part: (jnp.minimum(src[kept(i, cnt) * parts + part], border - 1), 0),
            )
            for part in range(parts)
        ]
        far = [
            pl.BlockSpec(
                (tile, width),
                lambda i, tl, src, cnt, *_, part=part: (jnp.maximum(src[kept(i, cnt) * parts + part] - border, 0), 0),
            )
            for part in range(parts)
        ]
        return near + far

    by_block = lambda last_dim: pl.BlockSpec((BLOCK, last_dim), lambda i, tl, src, cnt, *_: (kept(i, cnt), 0))
    by_column = lambda first: pl.BlockSpec((first, BLOCK), lambda i, tl, src, cnt, *_: (0, kept(i, cnt)))
    guarded = lambda first: pl.BlockSpec(
        (first, BLOCK), lambda i, tl, src, cnt, *_: (0, jnp.minimum(i, cnt[last]))
    )
    anywhere = pl.BlockSpec(memory_space=pl.ANY)
    show = [
        pltpu.VMEM((2, BLOCK, width), BF),
        pltpu.SemaphoreType.DMA((2, parts)),
        pltpu.SemaphoreType.DMA((2,)),
    ]
    shown_shapes = [
        jax.ShapeDtypeStruct(long_rows_in.shape, BF),
        jax.ShapeDtypeStruct(short_rows_in.shape, BF),
    ]

    triple_t, start = pl.pallas_call(
        partial(project_kernel, tile, border, last),
        grid_spec=pltpu.PrefetchScalarGridSpec(
            num_scalar_prefetch=4,
            grid=(blocks,),
            in_specs=tiles(width) + [anywhere, whole((width, 3 * width)), whole(vectors.shape)],
            out_specs=[guarded(3 * width), by_block(width)],
            scratch_shapes=[
                pltpu.VMEM((patches, width), F32),
                pltpu.VMEM((2, 448, width), BF),
                pltpu.VMEM((BLOCK, width), F32),
                pltpu.SemaphoreType.DMA((2,)),
            ],
        ),
        out_shape=[
            jax.ShapeDtypeStruct((3 * width, total), BF),
            jax.ShapeDtypeStruct((total, width), F32),
        ],
        compiler_params=params(),
        name="project",
    )(
        tile_len, source, count, index, *([long_rows_in] * parts), *([short_rows_in] * parts),
        w["position"], w["heads_weight"], vectors,
    )

    def heads_spec(offset):
        return pl.BlockSpec((pair, total), lambda i, *_: (i + offset * pairs, 0))

    board = pltpu.VMEM((long_rows, BLOCK), F32)
    sums_spec = pl.BlockSpec((1, 2, total), lambda i, *_: (i, 0, 0))
    attended_t, sums = pl.pallas_call(
        partial(attend_kernel, tile, long_rows, micros),
        grid_spec=pltpu.PrefetchScalarGridSpec(
            num_scalar_prefetch=3,
            grid=(pairs,),
            in_specs=[heads_spec(0), heads_spec(1), heads_spec(2)],
            out_specs=[heads_spec(0), sums_spec],
            scratch_shapes=[board] * 2,
        ),
        out_shape=[
            jax.ShapeDtypeStruct((width, total), BF),
            jax.ShapeDtypeStruct((pairs, 2, total), F32),
        ],
        compiler_params=params(),
        name="attend",
    )(tile_len, lengths, count, triple_t, triple_t, triple_t)

    some = max(groups // pieces, 1)
    long_out, short_out, pulled_t, grad_middle, vector, early = pl.pallas_call(
        partial(middle_kernel, tile, border, last),
        grid_spec=pltpu.PrefetchScalarGridSpec(
            num_scalar_prefetch=3,
            grid=(blocks,),
            in_specs=[by_column(width), by_block(width)]
            + tiles(teach)
            + [
                whole((width, width)), whole((width, wide)), whole((wide, width)), whole((width, teach)),
                whole(vectors.shape),
            ],
            out_specs=[
                anywhere, anywhere, guarded(width), by_block(width), whole((8, wide)), anywhere,
            ],
            scratch_shapes=[
                pltpu.VMEM((width, width), F32),
                pltpu.VMEM((pieces, width, width), F32),
                pltpu.VMEM((pieces, width, width), F32),
                pltpu.VMEM((width, teach), F32),
                pltpu.VMEM((BLOCK, wide), BF),
                pltpu.VMEM((BLOCK, wide), F32),
                pltpu.VMEM((2, groups, unit_rows, width), BF),
                pltpu.VMEM((2, some, width // some, width), BF),
            ]
            + show,
        ),
        out_shape=shown_shapes
        + [
            jax.ShapeDtypeStruct((width, total), BF),
            jax.ShapeDtypeStruct((total, width), F32),
            jax.ShapeDtypeStruct((8, wide), F32),
            jax.ShapeDtypeStruct((groups, early_rows, width), BF),
        ],
        compiler_params=params(),
        name="middle",
    )(
        tile_len, source, count, attended_t, start, *([long_target] * parts), *([short_target] * parts),
        w["out_weight"], w["up_weight"], w["down_weight"], w["align_weight"], vectors,
    )

    grads = pl.pallas_call(
        partial(attend_back_kernel, tile, long_rows, micros),
        grid_spec=pltpu.PrefetchScalarGridSpec(
            num_scalar_prefetch=3,
            grid=(pairs,),
            in_specs=[heads_spec(0), heads_spec(1), heads_spec(2), heads_spec(0), sums_spec],
            out_specs=[heads_spec(0)] * 3,
            scratch_shapes=[pltpu.VMEM((pair, long_rows), F32)] * 2 + [board] * 4,
        ),
        out_shape=[jax.ShapeDtypeStruct((width, total), BF)] * 3,
        compiler_params=params(),
        name="attend_back",
    )(tile_len, lengths, count, triple_t, triple_t, triple_t, pulled_t, sums)

    long_grad, short_grad, entry_vector, late = pl.pallas_call(
        partial(entry_kernel, tile, border, last),
        grid_spec=pltpu.PrefetchScalarGridSpec(
            num_scalar_prefetch=4,
            grid=(blocks,),
            in_specs=[by_column(width)] * 3
            + [by_block(width), by_block(width), whole((width, 3 * width)), whole(vectors.shape)],
            out_specs=[anywhere, anywhere, whole((8, width)), anywhere],
            scratch_shapes=[
                pltpu.VMEM((width, 3 * width), F32),
                pltpu.VMEM((patches + 8, width), F32),
                pltpu.VMEM((BLOCK, width), F32),
                pltpu.VMEM((2, groups, unit_rows, width), BF),
                pltpu.VMEM((2, chunk, width), BF),
            ]
            + show,
        ),
        out_shape=shown_shapes
        + [
            jax.ShapeDtypeStruct((8, width), F32),
            jax.ShapeDtypeStruct((groups, late_rows, width), BF),
        ],
        compiler_params=params(),
        name="entry",
    )(tile_len, source, count, index, *grads, start, grad_middle, w["heads_weight"], vectors)
    return long_out, short_out, long_grad, short_grad, early, late, jnp.concatenate([vector, entry_vector], axis=1)


def bit_of(number, bit):
    return lax.rem(number // (1 << bit), 2)


def reduce_plan(peers, early_rows, late_rows):
    bits = peers.bit_length() - 1
    forward = list(range(bits))
    swapped = forward[1::-1] + forward[2:]
    last = forward[2:] + forward[:2]
    pieces = []
    for source, rows in ((0, early_rows), (1, late_rows)):
        unit = 16
        units = rows // 2 // unit
        begin = 0
        for sub in range(2):
            here = units // 2 + (1 if sub < units % 2 else 0)
            first = int(here * 0.4 + 0.5)
            for order, parts in zip((forward, swapped, last), (first, first, here - 2 * first)):
                if parts > 0:
                    pieces.append((source * 2 + sub, source, begin, parts * unit, tuple(order)))
                    begin += parts * unit
    return pieces


def reduce_kernel(
    peers, halves, pieces, early, late, vector, early_out, late_out, vector_out, *scratch
):
    bits = peers.bit_length() - 1
    amount = len(pieces)
    kept = scratch[:amount]
    mates = scratch[amount : 2 * amount]
    mine_in = scratch[2 * amount : 3 * amount]
    landed = [scratch[3 * amount + k * bits : 3 * amount + (k + 1) * bits] for k in range(amount)]
    (
        vector_land, mate_send, mate_recv, load_sem, hop_send, hop_recv, end_send, end_recv, end_load,
        vector_send, vector_recv,
    ) = scratch[3 * amount + amount * bits :]
    d = lax.axis_index("dp")
    r = lax.axis_index("rep")
    other = 1 - r
    mate = (d, other)
    partner = [(d + (1 - 2 * bit_of(d, bit)) * (1 << bit), r) for bit in range(bits)]
    sources = (early, late)
    outs = (early_out, late_out)
    barrier = pltpu.get_barrier_semaphore()
    for device in [mate] + partner:
        pl.semaphore_signal(barrier, inc=1, device_id=device, device_id_type=pl.DeviceIdType.MESH)
    pl.semaphore_wait(barrier, bits + 1)

    def remote(source, target, send, recv, device):
        copy = pltpu.make_async_remote_copy(
            src_ref=source, dst_ref=target, send_sem=send, recv_sem=recv,
            device_id=device, device_id_type=pl.DeviceIdType.MESH,
        )
        copy.start()
        return copy

    def rows_at(source, core, begin, rows):
        return pl.ds(pl.multiple_of(core * halves[source] + begin, 16), rows)

    vector_out[...] = vector[...]
    mate_copies = []
    loads = []
    for k, (_, source, begin, rows, order) in enumerate(pieces):
        mate_copies.append(
            remote(
                sources[source].at[:, rows_at(source, other, begin, rows), :], mates[k],
                mate_send.at[k], mate_recv.at[k], mate,
            )
        )
        load = pltpu.make_async_copy(
            sources[source].at[:, rows_at(source, r, begin, rows), :], mine_in[k], load_sem.at[k]
        )
        load.start()
        loads.append(load)

    hops = {}
    ends = []

    def base_at(order, stage):
        base = 0
        for place in range(stage):
            base = base + bit_of(d, order[place]) * (1 << (bits - 1 - place))
        return base

    def send(k, stage):
        _, source, begin, rows, order = pieces[k]
        if stage == bits:
            result = kept[k].at[base_at(order, bits)]
            where = rows_at(source, r, begin, rows)
            ends.append(remote(result, outs[source].at[where, :], end_send.at[k], end_recv.at[k], mate))
            own = pltpu.make_async_copy(result, outs[source].at[where, :], end_load.at[k])
            own.start()
            ends.append(own)
            return
        size = 1 << (bits - 1 - stage)
        first = base_at(order, stage) + (1 - bit_of(d, order[stage])) * size
        hops[k, stage] = remote(
            kept[k].at[pl.ds(first, size)], landed[k][stage], hop_send.at[k, stage], hop_recv.at[k, stage],
            partner[order[stage]],
        )

    def join(k):
        order = pieces[k][4]
        loads[k].wait()
        mate_copies[k].wait_recv()

        def add(chunk, carry):
            place = 0
            for step in range(bits):
                place = place + bit_of(chunk, order[step]) * (1 << (bits - 1 - step))
            kept[k][place] = mine_in[k][chunk] + mates[k][chunk]
            return carry

        lax.fori_loop(0, peers, add, 0)

    def gather(k, stage):
        order = pieces[k][4]
        hops[k, stage].wait_recv()
        base = base_at(order, stage + 1)

        def add(chunk, carry):
            kept[k][base + chunk] = kept[k][base + chunk] + landed[k][stage][chunk]
            return carry

        lax.fori_loop(0, 1 << (bits - 1 - stage), add, 0)

    events = sorted(
        (stage + pieces[k][0], -stage, k) for k in range(amount) for stage in range(bits + 1)
    )
    vector_copies = []

    def vector_step(stage):
        if stage > 0:
            vector_copies[-1].wait()
            vector_out[...] = vector_out[...] + vector_land[stage - 1]
        if stage <= bits:
            device = mate if stage == 0 else partner[stage - 1]
            vector_copies.append(
                remote(vector_out, vector_land.at[stage], vector_send.at[stage], vector_recv.at[stage], device)
            )

    seen = -1
    for time, negative, k in events:
        if time != seen:
            if time <= bits + 1:
                vector_step(time)
            seen = time
        stage = -negative
        if stage == 0:
            join(k)
        else:
            gather(k, stage - 1)
        send(k, stage)
    for copy in mate_copies + list(hops.values()):
        copy.wait_send()
    for copy in ends:
        copy.wait()


def reduce_all(early, late, vector):
    peers, early_rows, width = early.shape
    late_rows = late.shape[1]
    bits = peers.bit_length() - 1
    pieces = reduce_plan(peers, early_rows, late_rows)
    amount = len(pieces)
    scratch = [pltpu.VMEM((peers, rows, width), BF) for _, _, _, rows, _ in pieces] * 3
    for _, _, _, rows, _ in pieces:
        for stage in range(bits):
            scratch.append(pltpu.VMEM((1 << (bits - 1 - stage), rows, width), BF))
    scratch.append(pltpu.VMEM((bits + 1,) + vector.shape, F32))
    one = pltpu.SemaphoreType.DMA((amount,))
    many = pltpu.SemaphoreType.DMA((amount, bits))
    few = pltpu.SemaphoreType.DMA((bits + 1,))
    scratch += [one, one, one, many, many, one, one, one, few, few]
    anywhere = pl.BlockSpec(memory_space=pl.ANY)
    near = pl.BlockSpec(memory_space=pltpu.VMEM)
    return pl.pallas_call(
        partial(reduce_kernel, peers, (early_rows // 2, late_rows // 2), pieces),
        in_specs=[anywhere, anywhere, near],
        out_specs=[anywhere, anywhere, near],
        out_shape=[
            jax.ShapeDtypeStruct((early_rows, width), BF),
            jax.ShapeDtypeStruct((late_rows, width), BF),
            jax.ShapeDtypeStruct(vector.shape, F32),
        ],
        scratch_shapes=scratch,
        compiler_params=pltpu.CompilerParams(
            vmem_limit_bytes=VMEM_LIMIT, collective_id=0, has_side_effects=True
        ),
        name="reduce",
    )(early, late, vector)


def unpack(early, late, unit_rows, kept, teach, pieces):
    width = early.shape[1]
    deep = pieces * unit_rows

    def beside(held, first, count):
        return jnp.concatenate(
            [held[first + k * unit_rows : first + (k + 1) * unit_rows] for k in range(count)], axis=1
        )

    extra = teach - width
    third = unit_rows * extra // width
    begin = 2 * deep + 2 * unit_rows
    tail = early[begin : begin + third]
    tail = jnp.concatenate([tail[:, k * extra : (k + 1) * extra] for k in range(width // extra)], axis=0)
    return {
        "down_weight": early[:deep],
        "up_weight": beside(early, deep, pieces),
        "out_weight": early[2 * deep : 2 * deep + unit_rows],
        "align_weight": jnp.concatenate([early[2 * deep + unit_rows : begin], tail], axis=1),
        "position": late[:kept],
        "heads_weight": beside(late, late.shape[0] - 3 * unit_rows, 3),
    }


def shards(
    long_clips,
    short_clips,
    long_index,
    short_index,
    long_length,
    short_length,
    destination,
    long_target,
    short_target,
    position,
    mixer_gain,
    mixer_shift,
    heads_weight,
    query_bias,
    value_bias,
    out_weight,
    out_bias,
    dense_gain,
    dense_shift,
    up_weight,
    up_bias,
    down_weight,
    down_bias,
    align_weight,
    align_bias,
):
    peers = lax.axis_size("dp")
    copies = lax.axis_size("rep")
    micros, _, long_rows, width = long_clips.shape
    home_slots, tile = short_clips.shape[1:3]
    bal_slots = home_slots // 2
    slots = micros * home_slots
    wide = up_weight.shape[1]
    teach = long_target.shape[-1]
    patches = position.shape[0]
    weights = dict(
        zip(
            WEIGHT_NAMES,
            (
                position, mixer_gain, mixer_shift, heads_weight, query_bias, value_bias, out_weight, out_bias,
                dense_gain, dense_shift, up_weight, up_bias, down_weight, down_bias, align_weight, align_bias,
            ),
        )
    )
    scalars = pl.BlockSpec(memory_space=pltpu.SMEM)
    anywhere = pl.BlockSpec(memory_space=pl.ANY)
    tile_total = micros * long_rows // tile + slots
    tile_len, source, count = pl.pallas_call(
        partial(plan_kernel, tile, long_rows, home_slots, copies),
        in_specs=[scalars, scalars],
        out_specs=[scalars] * 3,
        out_shape=[
            jax.ShapeDtypeStruct((tile_total,), jnp.int32),
            jax.ShapeDtypeStruct((tile_total,), jnp.int32),
            jax.ShapeDtypeStruct((2 * micros + 3,), jnp.int32),
        ],
        name="plan",
    )(long_length, short_length)
    index = jnp.concatenate([long_index.reshape(-1), short_index.reshape(-1)])
    groups = peers if copies == 2 and width % (16 * peers) == 0 else 1
    long_out, short_out, long_grad, short_grad, early, late, vector = run_block(
        long_clips.reshape(-1, width), short_clips.reshape(-1, width), index,
        long_target.reshape(-1, teach), short_target.reshape(-1, teach),
        tile_len, source, count, long_length.reshape(-1), tile, long_rows, micros, weights, groups,
    )
    send = pl.pallas_call(
        partial(send_kernel, home_slots, copies),
        in_specs=[scalars, scalars, whole((slots, tile, width))],
        out_specs=pl.BlockSpec(memory_space=pltpu.VMEM) if groups == peers else scalars,
        out_shape=jax.ShapeDtypeStruct((peers, micros, tile, width), BF),
        compiler_params=params(),
        name="send",
    )(short_length, destination, short_out.reshape(slots, tile, width)) if groups == peers else send_all(
        short_length, destination, short_out.reshape(slots, tile, width), peers, copies, home_slots
    )
    got = lax.all_to_all(send, "dp", split_axis=0, concat_axis=0, tiled=True)
    unit_rows = width // peers
    if groups == peers:
        early, late, vector = reduce_all(early, late, vector)
    else:
        matrices = unpack(early[0], late[0], width, patches, teach, wide // width)
        early, late = share_out(matrices, peers, copies, unit_rows, wide // width)
        vector = lax.psum(vector, ("dp", "rep"))
    near = pl.BlockSpec(memory_space=pltpu.VMEM)
    outs = pl.pallas_call(
        partial(finish_kernel, home_slots, copies),
        in_specs=[scalars, scalars, anywhere, near, near, near],
        out_specs=[near] * 10,
        out_shape=[
            jax.ShapeDtypeStruct((micros, bal_slots, tile, width), BF),
            jax.ShapeDtypeStruct((patches // peers, width), F32),
            jax.ShapeDtypeStruct((unit_rows, 3 * width), F32),
            jax.ShapeDtypeStruct((unit_rows, width), F32),
            jax.ShapeDtypeStruct((unit_rows, wide), F32),
            jax.ShapeDtypeStruct((wide // peers, width), F32),
            jax.ShapeDtypeStruct((unit_rows, teach), F32),
            jax.ShapeDtypeStruct((2, 8, unit_rows), F32),
            jax.ShapeDtypeStruct((8, wide // peers), F32),
            jax.ShapeDtypeStruct((8, teach // peers), F32),
        ],
        scratch_shapes=[pltpu.SemaphoreType.DMA((micros * bal_slots,))],
        compiler_params=params(),
        name="finish",
    )(short_length, destination, got, early, late, vector)
    short_bal, position_g, heads_g, out_g, up_g, down_g, align_g, thin, up_row, align_row = outs
    shared = {
        "position": position_g, "heads_weight": heads_g, "out_weight": out_g, "up_weight": up_g,
        "down_weight": down_g, "align_weight": align_g,
        "up_bias": up_row[0], "align_bias": align_row[5],
        "out_bias": thin[0, 1], "dense_gain": thin[0, 2], "dense_shift": thin[0, 3], "down_bias": thin[0, 4],
        "query_bias": thin[1, 0], "mixer_gain": thin[1, 1], "value_bias": thin[1, 2], "mixer_shift": thin[1, 3],
    }
    return (
        long_out.reshape(micros, 1, long_rows, width),
        short_bal,
        long_grad.reshape(micros, 1, long_rows, width),
        short_grad.reshape(micros, home_slots, tile, width),
    ) + tuple(shared[name] for name in WEIGHT_NAMES)


def send_all(short_length, destination, shown, peers, copies, home):
    micros = short_length.shape[0]
    mine = lax.axis_index("dp") * copies + lax.axis_index("rep")

    def own(table):
        table = table.reshape(micros, peers * copies, home)
        return lax.dynamic_index_in_dim(table, mine, 1, keepdims=False)

    wanted = (own(destination)[None] == jnp.arange(peers)[:, None, None]) & (own(short_length)[None] > 0)
    shown = shown.reshape((micros, home) + shown.shape[1:])
    return jnp.einsum("pmj,mjtd->pmtd", wanted.astype(BF), shown)


def share_out(matrices, peers, copies, unit_rows, pieces):
    shared = {}
    for name, piece in matrices.items():
        rows = piece.shape[0] // peers
        padded = -(-rows // (8 * copies)) * 8 * copies
        if padded != rows:
            piece = piece.reshape(peers, rows, -1)
            piece = jnp.pad(piece, ((0, 0), (0, padded - rows), (0, 0)))
            piece = piece.reshape(peers * padded, -1)
        piece = lax.psum_scatter(piece, ("dp", "rep"), scatter_dimension=0, tiled=True)
        shared[name] = lax.all_gather(piece, "rep", axis=0, tiled=True)[:rows]
    width = shared["out_weight"].shape[1]
    up = shared["up_weight"].reshape(unit_rows, pieces, width).transpose(1, 0, 2).reshape(-1, width)
    heads = shared["heads_weight"].reshape(unit_rows, 3, width).transpose(1, 0, 2).reshape(-1, width)
    align = shared["align_weight"]
    extra = align.shape[1] - width
    parts = width // extra
    tail = align[:, width:].reshape(parts, unit_rows // parts, extra).transpose(1, 0, 2).reshape(-1, width)
    early = jnp.concatenate([shared["down_weight"], up, shared["out_weight"], align[:, :width], tail], axis=0)
    return early, jnp.concatenate([shared["position"], heads], axis=0)


def solution(mesh):
    placed = (
        P(None, ("dp", "rep"), None, None),
        P(None, ("dp", "rep"), None, None),
        P(None, ("dp", "rep"), None),
        P(None, ("dp", "rep"), None),
        P(None, ("dp", "rep")),
        P(),
        P(),
        P(None, ("dp", "rep"), None, None),
        P(None, ("dp", "rep"), None, None),
        P(),
        P(),
        P(),
        P(),
        P(),
        P(),
        P(),
        P(),
        P(),
        P(),
        P(),
        P(),
        P(),
        P(),
        P(),
        P(),
    )
    return jax.shard_map(
        shards,
        mesh=mesh,
        in_specs=placed,
        out_specs=(
            P(None, ("dp", "rep"), None, None),
            P(None, ("dp", "rep"), None, None),
            P(None, ("dp", "rep"), None, None),
            P(None, ("dp", "rep"), None, None),
            P("dp", None),
            P("dp"),
            P("dp"),
            P("dp", None),
            P("dp"),
            P("dp"),
            P("dp", None),
            P("dp"),
            P("dp"),
            P("dp"),
            P("dp", None),
            P("dp"),
            P("dp", None),
            P("dp"),
            P("dp", None),
            P("dp"),
        ),
        check_vma=False,
    )
```

```python
from functools import partial

import jax
import jax.numpy as jnp
from jax import lax
from jax.experimental import pallas as pl
from jax.experimental.pallas import tpu as pltpu
from jax.sharding import PartitionSpec as P

HEADS = 12
EPS = 1e-06
MASKED = -1000000000.0
WEIGHT_NAMES = (
    "position",
    "mixer_gain",
    "mixer_shift",
    "heads_weight",
    "query_bias",
    "value_bias",
    "out_weight",
    "out_bias",
    "dense_gain",
    "dense_shift",
    "up_weight",
    "up_bias",
    "down_weight",
    "down_bias",
    "align_weight",
    "align_bias",
)


BLOCK = 256
BF = jnp.bfloat16
F32 = jnp.float32
VMEM_LIMIT = 66_000_000


def dot(left, right, dims):
    return lax.dot_general(left, right, ((dims[:1], dims[1:]), ((), ())), preferred_element_type=F32)


def centre(values):
    mean = jnp.mean(values, axis=-1, keepdims=True)
    centered = values - mean
    spread = jnp.mean(centered * centered, axis=-1, keepdims=True)
    inverse = lax.rsqrt(spread + EPS)
    return centered * inverse, inverse


def centre_back(grad, unit, inverse):
    first = jnp.mean(grad, axis=-1, keepdims=True)
    second = jnp.mean(grad * unit, axis=-1, keepdims=True)
    return inverse * (grad - first - unit * second)


def valid_rows(tile_len, block, tile):
    row = lax.broadcasted_iota(jnp.int32, (BLOCK, 1), 0)
    parts = BLOCK // tile
    limit = tile_len[block * parts]
    for part in range(1, parts):
        limit = jnp.where(row >= part * tile, tile_len[block * parts + part], limit)
    return lax.rem(row, tile) < limit


def plan_kernel(tile, long_rows, home, copies, lengths, short_len, *refs):
    amount = len(refs) - 6
    small, (tile_len, source, count, vectors, up_out, align_out) = refs[:amount], refs[amount:]
    for number, value in enumerate(small[:-2]):
        vectors[number : number + 1, :] = value[...].reshape(1, -1)
    up_out[...] = small[-2][...].reshape(1, -1)
    align_out[...] = small[-1][...].reshape(1, -1)
    micros = lengths.shape[0]
    per = long_rows // tile
    step = 128 // tile
    base = (lax.axis_index("dp") * copies + lax.axis_index("rep")) * home

    def put(place, origin, size):
        source[place] = origin
        tile_len[place] = size

    place = jnp.int32(0)
    taken = []
    for micro in range(micros):
        length = lengths[micro, 0]
        some = lax.div(length + 127, 128) * step
        count[micro] = lax.div(length + BLOCK - 1, BLOCK)
        count[micros + 1 + micro] = place

        def add(number, carry, micro=micro, length=length, place=place):
            put(place + number, micro * per + number, jnp.clip(length - number * tile, 0, tile))
            return carry

        lax.fori_loop(0, some, add, 0)
        taken.append(some)
        place = place + some
    first = place
    slots = micros * home
    sizes = [short_len[slot // home, base + slot % home] for slot in range(slots)]
    for wanted in (True, False):
        for slot, size in enumerate(sizes):
            fits = (size > 0) if wanted else (size <= 0)

            @pl.when(fits)
            def _():
                put(place, micros * per + slot, size)

            place = place + jnp.where(fits, 1, 0)
        if wanted:
            parts = BLOCK // tile
            count[micros] = lax.div(place - first + parts - 1, parts)
            count[2 * micros + 1] = first
            count[2 * micros + 2] = lax.div(place + parts - 1, parts)
    for micro in range(micros):
        def fill(number, carry, micro=micro, place=place - taken[micro]):
            put(place + number, micro * per + number, 0)
            return carry

        lax.fori_loop(taken[micro], per, fill, 0)
        place = place + per - taken[micro]


def pieced(step, source, parts, near, far, border):
    chosen = [
        jnp.where(source[step * parts + part] < border, near[part][...], far[part][...]) for part in range(parts)
    ]
    return jnp.concatenate(chosen, axis=0).astype(F32)


def put_tiles(step, value, source, border, tile, stage, sem, near, far):
    parts = BLOCK // tile
    slot = lax.rem(step, 2)

    def settle(which):
        for part in range(parts):
            pltpu.make_async_copy(
                stage.at[which, pl.ds(part * tile, tile), :], near.at[pl.ds(0, tile), :], sem.at[which, part]
            ).wait()

    @pl.when(step >= 2)
    def _():
        settle(slot)

    stage[slot] = value
    for part in range(parts):
        origin = source[step * parts + part]
        view = stage.at[slot, pl.ds(part * tile, tile), :]

        @pl.when(origin < border)
        def _():
            where = pl.ds(pl.multiple_of(origin * tile, tile), tile)
            pltpu.make_async_copy(view, near.at[where, :], sem.at[slot, part]).start()

        @pl.when(origin >= border)
        def _():
            where = pl.ds(pl.multiple_of((origin - border) * tile, tile), tile)
            pltpu.make_async_copy(view, far.at[where, :], sem.at[slot, part]).start()

    @pl.when(step == pl.num_programs(0) - 1)
    def _():
        settle(1 - slot)
        settle(slot)


def project_kernel(tile, border, last, tile_len, source, count, index, *refs):
    parts = BLOCK // tile
    near = refs[:parts]
    far = refs[parts : 2 * parts]
    table_any, weight_any, vectors, out, start_out, table, stage, rows, weight, weight_sem, sem = refs[2 * parts :]
    step = pl.program_id(0)
    width = weight.shape[0]
    depth, chunk = stage.shape[:2]
    chunks = table.shape[0] // chunk

    def fetch(number):
        return pltpu.make_async_copy(
            table_any.at[pl.ds(pl.multiple_of(number * chunk, 16), chunk), :],
            stage.at[lax.rem(number, depth)],
            sem.at[lax.rem(number, depth)],
        )

    @pl.when(step == 0)
    def _():
        for number in range(depth):
            fetch(number).start()
        weight_load = pltpu.make_async_copy(weight_any, weight, weight_sem.at[0])
        weight_load.start()
        rows[...] = jnp.zeros_like(rows)

        def load(number, carry):
            fetch(number).wait()
            table[pl.ds(pl.multiple_of(number * chunk, 16), chunk), :] = stage[lax.rem(number, depth)].astype(F32)

            @pl.when(number + depth < chunks)
            def _():
                fetch(number + depth).start()

            return carry

        lax.fori_loop(0, chunks, load, 0)
        weight_load.wait()

    @pl.when(step == count[last])
    def _():
        out[...] = jnp.zeros_like(out)

    @pl.when(step < count[last])
    def _():
        def gather(part, carry):
            origin = source[step * parts + part] * tile
            first = part * tile

            def some(group, inner):
                base = pl.multiple_of(first + group * 8, 8)
                for row in range(8):
                    place = index[origin + group * 8 + row]
                    rows[pl.ds(base + row, 1), :] = table[pl.ds(place, 1), :]
                return inner

            lax.fori_loop(0, lax.div(tile_len[step * parts + part] + 7, 8), some, 0)
            return carry

        lax.fori_loop(0, parts, gather, 0)
        start = pieced(step, source, parts, near, far, border) + rows[...]
        start_out[...] = start
        unit, _ = centre(start)
        normed = (unit * vectors[0:1, :width] + vectors[1:2, :width]).astype(BF)
        for part in range(3):
            cols = slice(part * width, (part + 1) * width)
            triple = dot(normed, weight[:, cols], (1, 0))
            if part == 0:
                triple = (triple + vectors[2:3, :width]).astype(BF) * BF(0.125)
            elif part == 1:
                triple = triple.astype(BF)
            else:
                triple = (triple + vectors[3:4, :width]).astype(BF)
            out[cols, :] = triple.T


def masked_tile(tile_scores, limit):
    key = lax.broadcasted_iota(jnp.int32, tile_scores.shape, 0)
    return jnp.where(key < limit, tile_scores, MASKED)


def block_mask(tile_len, first, tile):
    key = lax.broadcasted_iota(jnp.int32, (BLOCK, BLOCK), 0)
    asked = lax.broadcasted_iota(jnp.int32, (BLOCK, BLOCK), 1)
    limit = tile_len[first]
    for part in range(1, BLOCK // tile):
        limit = jnp.where(key >= part * tile, tile_len[first + part], limit)
    return (key // tile == asked // tile) & (lax.rem(key, tile) < limit)


def attend_kernel(tile, long_rows, clips, tile_len, length, count, query, keys, values, out, logsum, even, odd):
    head_dim = query.shape[0] // 2
    most = long_rows // BLOCK
    boards = (even, odd)

    def score(head, column, first, size, fix):
        lanes = slice(head * head_dim, (head + 1) * head_dim)
        asked = query[lanes, pl.ds(column, BLOCK)]
        for number in range(size):
            part = dot(keys[lanes, pl.ds(first + number * BLOCK, BLOCK)], asked, (0, 0))
            if number == size - 1:
                part = fix(part)
            boards[head][number * BLOCK : (number + 1) * BLOCK, :] = part

    def finish(head, column, first, size):
        lanes = slice(head * head_dim, (head + 1) * head_dim)
        board = boards[head]
        top = jnp.max(board[: size * BLOCK, :], axis=0, keepdims=True)
        total = None
        gathered = None
        for number in range(size):
            weight = jnp.exp(board[number * BLOCK : (number + 1) * BLOCK, :] - top)
            part = jnp.sum(weight, axis=0, keepdims=True)
            held = values[lanes, pl.ds(first + number * BLOCK, BLOCK)]
            term = dot(held, weight.astype(BF), (1, 0))
            total = part if total is None else total + part
            gathered = term if gathered is None else gathered + term
        out[lanes, pl.ds(column, BLOCK)] = (gathered / total).astype(BF)
        logsum[0, pl.ds(head, 1), pl.ds(column, BLOCK)] = top + jnp.log(total)

    def rows(first, size, fix):
        def at(block):
            return pl.multiple_of(first + block * BLOCK, 128)

        score(0, at(0), first, size, fix)

        def ask(block, carry):
            score(1, at(block), first, size, fix)
            finish(0, at(block), first, size)
            score(0, at(jnp.minimum(block + 1, size - 1)), first, size, fix)
            finish(1, at(block), first, size)
            return carry

        lax.fori_loop(0, size, ask, 0)

    def clip(number, carry):
        first = pl.multiple_of(count[clips + 1 + number] * tile, 128)
        blocks = count[number]
        rest = length[number]
        for size in range(1, most + 1):
            @pl.when(blocks == size)
            def _():
                rows(first, size, lambda part: masked_tile(part, rest - (size - 1) * BLOCK))
        return carry

    out[...] = jnp.zeros_like(out)
    lax.fori_loop(0, clips, clip, 0)

    def short(number, carry):
        begin = count[2 * clips + 1] + number * (BLOCK // tile)
        column = pl.multiple_of(begin * tile, 128)
        allowed = block_mask(tile_len, begin, tile)
        rows(column, 1, lambda part: jnp.where(allowed, part, MASKED))
        return carry

    lax.fori_loop(0, count[clips], short, 0)


def attend_back_kernel(
    tile, long_rows, clips, tile_len, length, count, query, keys, values, grad, logsum,
    query_out, key_out, value_out, key_sum, value_sum, even, odd, even_back, odd_back,
):
    head_dim = query.shape[0] // 2
    most = long_rows // BLOCK
    boards = (even, odd)
    backs = (even_back, odd_back)

    def score(head, column, first, size, fix):
        lanes = slice(head * head_dim, (head + 1) * head_dim)
        asked = query[lanes, pl.ds(column, BLOCK)]
        pulled = grad[lanes, pl.ds(column, BLOCK)]
        for number in range(size):
            here = pl.ds(first + number * BLOCK, BLOCK)
            there = slice(number * BLOCK, (number + 1) * BLOCK)
            part = dot(keys[lanes, here], asked, (0, 0))
            if number == size - 1:
                part = fix(part)
            boards[head][there, :] = part
            backs[head][there, :] = dot(values[lanes, here], pulled, (0, 0))

    def finish(head, column, first, size, limit):
        lanes = slice(head * head_dim, (head + 1) * head_dim)
        asked = query[lanes, pl.ds(column, BLOCK)]
        pulled = grad[lanes, pl.ds(column, BLOCK)]
        own = lax.broadcasted_iota(jnp.int32, (1, BLOCK), 1) < limit
        base = jnp.where(own, logsum[0, pl.ds(head, 1), pl.ds(column, BLOCK)], -1e3 * MASKED)
        inner = None
        for number in range(size):
            there = slice(number * BLOCK, (number + 1) * BLOCK)
            prob = jnp.exp(boards[head][there, :] - base)
            boards[head][there, :] = prob
            part = jnp.sum(prob * backs[head][there, :], axis=0, keepdims=True)
            inner = part if inner is None else inner + part
            value_sum[lanes, there] += dot(pulled, prob.astype(BF), (1, 1))
        query_sum = None
        for number in range(size):
            here = pl.ds(first + number * BLOCK, BLOCK)
            there = slice(number * BLOCK, (number + 1) * BLOCK)
            moved = (boards[head][there, :] * (backs[head][there, :] - inner)).astype(BF)
            key_sum[lanes, there] += dot(asked, moved, (1, 1))
            term = dot(keys[lanes, here], moved, (1, 0))
            query_sum = term if query_sum is None else query_sum + term
        query_out[lanes, pl.ds(column, BLOCK)] = (query_sum * 0.125).astype(BF)

    def rows(first, size, fix, rest):
        def at(block):
            return pl.multiple_of(first + block * BLOCK, 128)

        key_sum[:, : size * BLOCK] = jnp.zeros((2 * head_dim, size * BLOCK), F32)
        value_sum[:, : size * BLOCK] = jnp.zeros((2 * head_dim, size * BLOCK), F32)
        score(0, at(0), first, size, fix)

        def ask(block, carry):
            limit = rest - block * BLOCK
            after = jnp.minimum(block + 1, size - 1)
            score(1, at(block), first, size, fix)
            finish(0, at(block), first, size, limit)
            score(0, at(after), first, size, fix)
            finish(1, at(block), first, size, limit)
            return carry

        lax.fori_loop(0, size, ask, 0)
        key_out[:, pl.ds(first, size * BLOCK)] = key_sum[:, : size * BLOCK].astype(BF)
        value_out[:, pl.ds(first, size * BLOCK)] = value_sum[:, : size * BLOCK].astype(BF)

    def clip(number, carry):
        first = pl.multiple_of(count[clips + 1 + number] * tile, 128)
        blocks = count[number]
        rest = length[number]
        for size in range(1, most + 1):
            @pl.when(blocks == size)
            def _():
                rows(first, size, lambda part: masked_tile(part, rest - (size - 1) * BLOCK), rest)
        return carry

    for empty in (query_out, key_out, value_out):
        empty[...] = jnp.zeros_like(empty)
    lax.fori_loop(0, clips, clip, 0)

    def short(number, carry):
        begin = count[2 * clips + 1] + number * (BLOCK // tile)
        column = pl.multiple_of(begin * tile, 128)
        allowed = block_mask(tile_len, begin, tile)
        rows(column, 1, lambda part: jnp.where(allowed, part, MASKED), BLOCK)
        return carry

    lax.fori_loop(0, count[clips], short, 0)


def gelu_both(upper):
    spread = 0.5 * (1.0 + lax.erf(upper * 0.7071067811865476))
    bell = jnp.exp(-0.5 * upper * upper) * 0.3989422804014327
    return upper * spread, spread + upper * bell


def write_out(entries):
    waiting = {}
    counts = {}
    for source, stage, sem, target in entries:
        key = id(stage)
        slot = counts.get(key, 0) % stage.shape[0]
        counts[key] = counts.get(key, 0) + 1
        if (key, slot) in waiting:
            waiting[key, slot].wait()
        value = source()
        view = stage.at[slot, :, : value.shape[1], : value.shape[2]]
        stage[slot, :, : value.shape[1], : value.shape[2]] = value.astype(BF)
        copy = pltpu.make_async_copy(view, target, sem.at[slot])
        copy.start()
        waiting[key, slot] = copy
    for copy in waiting.values():
        copy.wait()


def middle_kernel(tile, border, last, tile_len, source, count, attended_t, start_in, *refs):
    parts = BLOCK // tile
    near = refs[:parts]
    far = refs[parts : 2 * parts]
    (
        out_any, up_any, down_any, align_any, vectors, up_b, align_b,
        long_out, short_out, pull_out, grad_out, vector_out, sums_out,
        out_acc, up_acc, down_acc, align_acc, hidden, slope, stage, stage_down,
        out_w, up_w, down_w, align_w, weight_sem, down_sem, show, show_sem, sem,
    ) = refs[2 * parts :]
    step = pl.program_id(0)
    width = out_w.shape[0]
    wide = up_w.shape[1]
    teach = align_w.shape[1]
    pieces = wide // width
    live = step < count[last]
    loads = [
        pltpu.make_async_copy(source_ref, target, weight_sem.at[number])
        for number, (source_ref, target) in enumerate(
            ((out_any, out_w), (up_any, up_w), (down_any, down_w), (align_any, align_w))
        )
    ]

    @pl.when(step == 0)
    def _():
        for load in loads:
            load.start()
        for acc in (out_acc, up_acc, down_acc, align_acc):
            acc[...] = jnp.zeros_like(acc)
        vector_out[...] = jnp.zeros_like(vector_out)
        loads[0].wait()

    def put(value):
        put_tiles(step, value, source, border, tile, show, show_sem, long_out, short_out)

    def add_vector(row, value):
        size = value.shape[1]
        vector_out[row : row + 1, :size] += value

    def over_rows(value):
        return jnp.sum(value, axis=0, keepdims=True)

    @pl.when(step == count[last])
    def _():
        pull_out[...] = jnp.zeros_like(pull_out)

    @pl.when(jnp.logical_not(live))
    def _():
        put(jnp.zeros((BLOCK, width), BF))

    @pl.when(live)
    def _():
        ok = valid_rows(tile_len, step, tile)
        across = attended_t[...]
        middle = start_in[...] + dot(across, out_w[...], (0, 0)) + vectors[4:5, :width]
        unit, inverse = centre(middle)
        dense = (unit * vectors[5:6, :width] + vectors[6:7, :width]).astype(BF)
        result = middle + vectors[7:8, :width]

        @pl.when(step == 0)
        def _():
            for load in loads[1:]:
                load.wait()

        for piece in range(pieces):
            cols = slice(piece * width, (piece + 1) * width)
            upper = dot(dense, up_w[:, cols], (1, 0)) + up_b[:, cols]
            bent, tilt = gelu_both(upper)
            low = bent.astype(BF)
            hidden[:, cols] = low
            slope[:, cols] = tilt
            result = result + dot(low, down_w[cols, :], (1, 0))
        shown = jnp.where(ok, result, 0.0).astype(BF)
        put(shown)
        projected = dot(shown, align_w[...], (1, 0)) + align_b[...]
        target = pieced(step, source, parts, near, far, border)
        miss = jnp.where(ok, projected - target, 0.0).astype(BF)
        add_vector(5, over_rows(miss.astype(F32)))
        align_acc[...] += dot(shown, miss, (0, 0))
        pulled = dot(miss, align_w[...], (1, 1)).astype(BF)
        pulled_wide = pulled.astype(F32)
        add_vector(4, over_rows(pulled_wide))
        grad_dense = None
        for piece in range(pieces):
            cols = slice(piece * width, (piece + 1) * width)
            grad_upper = dot(pulled, down_w[cols, :], (1, 1)) * slope[:, cols]
            low = grad_upper.astype(BF)
            vector_out[0:1, cols] += over_rows(low.astype(F32))
            down_acc[piece] += dot(hidden[:, cols], pulled, (0, 0))
            up_acc[piece] += dot(dense, low, (0, 0))
            term = dot(low, up_w[:, cols], (1, 1))
            grad_dense = term if grad_dense is None else grad_dense + term
        add_vector(2, over_rows(grad_dense * unit))
        add_vector(3, over_rows(grad_dense))
        grad_middle = pulled_wide + centre_back(grad_dense * vectors[5:6, :width], unit, inverse)
        grad_out[...] = grad_middle
        branch = grad_middle.astype(BF)
        add_vector(1, over_rows(branch.astype(F32)))
        out_acc[...] += dot(across, branch, (1, 0))
        pull_out[...] = dot(out_w[...], branch, (1, 1)).astype(BF)

    @pl.when(step == pl.num_programs(0) - 1)
    def _():
        groups, unit_rows = stage.shape[1:3]
        deep = pieces * unit_rows
        some, tall = stage_down.shape[1:3]

        def grouped(value):
            return value.reshape(groups, unit_rows, value.shape[-1])

        entries = []
        for piece in range(pieces):
            if groups >= pieces:
                target = sums_out.at[pl.ds(piece * some, some), pl.ds(0, tall), :]
            else:
                target = sums_out.at[:, pl.ds(piece * tall, tall), :]
            entries.append(
                (lambda piece=piece: down_acc[piece].reshape(some, tall, width), stage_down, down_sem, target)
            )
            target = sums_out.at[:, pl.ds(deep + piece * unit_rows, unit_rows), :]
            entries.append((lambda piece=piece: grouped(up_acc[piece]), stage, sem, target))
        begin = 2 * deep
        entries.append((lambda: grouped(out_acc[...]), stage, sem, sums_out.at[:, pl.ds(begin, unit_rows), :]))
        begin += unit_rows
        entries.append(
            (lambda: grouped(align_acc[:, :width]), stage, sem, sums_out.at[:, pl.ds(begin, unit_rows), :])
        )
        begin += unit_rows
        extra = teach - width
        third = unit_rows * extra // width
        for part in range(width // extra):
            entries.append(
                (
                    lambda part=part: grouped(align_acc[:, width:])[:, part * third : (part + 1) * third],
                    stage,
                    sem,
                    sums_out.at[:, pl.ds(begin, third), pl.ds(part * extra, extra)],
                )
            )
        write_out(entries)


def entry_kernel(tile, border, last, tile_len, source, count, index, *refs):
    (
        query_t, key_t, value_t, start_in, grad_in, weight_any, vectors,
        long_out, short_out, vector_out, sums_out,
        weight_acc, position_acc, moved, stage, stage_rows, weight, weight_sem, rows_sem, show, show_sem, sem,
    ) = refs
    step = pl.program_id(0)
    width = weight.shape[0]
    live = step < count[last]

    @pl.when(step == 0)
    def _():
        load = pltpu.make_async_copy(weight_any, weight, weight_sem.at[0])
        load.start()
        weight_acc[...] = jnp.zeros_like(weight_acc)
        vector_out[...] = jnp.zeros_like(vector_out)

        def clear(number, carry):
            position_acc[pl.ds(pl.multiple_of(number * 64, 64), 64), :] = jnp.zeros((64, width), F32)
            return carry

        lax.fori_loop(0, position_acc.shape[0] // 64, clear, 0)
        left = position_acc.shape[0] % 64
        if left:
            position_acc[position_acc.shape[0] - left :, :] = jnp.zeros((left, width), F32)
        load.wait()

    def put(value):
        put_tiles(step, value, source, border, tile, show, show_sem, long_out, short_out)

    def over_rows(value):
        return jnp.sum(value, axis=0, keepdims=True)

    @pl.when(jnp.logical_not(live))
    def _():
        put(jnp.zeros((BLOCK, width), BF))

    @pl.when(live)
    def _():
        unit, inverse = centre(start_in[...])
        normed = (unit * vectors[0:1, :width] + vectors[1:2, :width]).astype(BF)
        grad_normed = None
        for part in range(3):
            cols = slice(part * width, (part + 1) * width)
            across = (query_t, key_t, value_t)[part][...]
            if part != 1:
                vector_out[part : part + 1, :] += over_rows(across.T.astype(F32))
            weight_acc[:, cols] += dot(normed, across, (0, 1))
            term = dot(across, weight[:, cols], (0, 1))
            grad_normed = term if grad_normed is None else grad_normed + term
        vector_out[1:2, :] += over_rows(grad_normed * unit)
        vector_out[3:4, :] += over_rows(grad_normed)
        grad_start = grad_in[...] + centre_back(grad_normed * vectors[0:1, :width], unit, inverse)
        put(grad_start.astype(BF))
        moved[...] = grad_start
        parts = BLOCK // tile

        def spread(number, carry):
            first = number * tile
            origin = source[step * parts + number] * tile

            def some(group, inner):
                base = pl.multiple_of(first + group * 8, 8)
                for row in range(8):
                    place = index[origin + group * 8 + row]
                    position_acc[pl.ds(place, 1), :] += moved[pl.ds(base + row, 1), :]
                return inner

            lax.fori_loop(0, lax.div(tile_len[step * parts + number] + 7, 8), some, 0)
            return carry

        lax.fori_loop(0, parts, spread, 0)

    @pl.when(step == pl.num_programs(0) - 1)
    def _():
        groups, unit_rows = stage.shape[1:3]
        depth, chunk = stage_rows.shape[:2]
        patches = position_acc.shape[0] - 8
        taken = patches // groups if groups > 1 else chunk
        begin = sums_out.shape[1] - 3 * unit_rows
        entries = []
        for part in range(3):
            cols = slice(part * width, (part + 1) * width)
            entries.append(
                (
                    lambda cols=cols: weight_acc[:, cols].reshape(groups, unit_rows, width),
                    stage,
                    sem,
                    sums_out.at[:, pl.ds(begin + part * unit_rows, unit_rows), :],
                )
            )
        write_out(entries)

        def copy(number):
            if groups > 1:
                target = sums_out.at[number, pl.ds(0, chunk), :]
            else:
                target = sums_out.at[0, pl.ds(pl.multiple_of(number * chunk, 16), chunk), :]
            slot = lax.rem(number, depth)
            return pltpu.make_async_copy(stage_rows.at[slot], target, rows_sem.at[slot])

        def drain(number, carry):
            @pl.when(number >= depth)
            def _():
                copy(number - depth).wait()

            stage_rows[lax.rem(number, depth)] = position_acc[
                pl.ds(pl.multiple_of(number * taken, 8), chunk), :
            ].astype(BF)
            copy(number).start()
            return carry

        chunks = patches // taken
        lax.fori_loop(0, chunks, drain, 0)
        for late in range(depth):
            copy(chunks - depth + late).wait()


def send_kernel(home, copies, short_len, destination, shown, out):
    base = (lax.axis_index("dp") * copies + lax.axis_index("rep")) * home
    out[...] = jnp.zeros_like(out)
    for slot in range(shown.shape[0]):
        micro, place = slot // home, base + slot % home

        @pl.when(short_len[micro, place] > 0)
        def _():
            out[destination[micro, place], micro] = shown[slot]


def finish_kernel(
    home, copies, short_len, destination, got, early, late, vector,
    balanced, position_g, heads_g, out_g, up_g, down_g, align_g, *rest,
):
    vector_outs, sem = rest[:-1], rest[-1]
    peers = got.shape[0]
    micros, bal = balanced.shape[:2]
    width = position_g.shape[1]
    unit_rows = out_g.shape[0]
    pieces = up_g.shape[1] // width
    d = lax.axis_index("dp")
    r = lax.axis_index("rep")
    number = 0
    found_all = []
    for micro in range(micros):
        for slot in range(bal):
            def look(peer, found):
                base = (peer * copies + r) * home
                for place in range(slot, home, bal):
                    fits = (short_len[micro, base + place] > 0) & (destination[micro, base + place] == d)
                    found = jnp.where(fits, peer, found)
                return found

            found = lax.fori_loop(0, peers, look, jnp.int32(-1))
            found_all.append(found)

            @pl.when(found >= 0)
            def _():
                pltpu.make_async_copy(
                    got.at[jnp.maximum(found, 0), micro], balanced.at[micro, slot], sem.at[number]
                ).start()

            @pl.when(found < 0)
            def _():
                balanced[micro, slot] = jnp.zeros(balanced.shape[2:], BF)

            number += 1
    position_g[...] = late[: position_g.shape[0], :].astype(F32)
    first = late.shape[0] - 3 * unit_rows
    for part in range(3):
        heads_g[:, part * width : (part + 1) * width] = late[
            first + part * unit_rows : first + (part + 1) * unit_rows, :
        ].astype(F32)
    deep = pieces * unit_rows
    down_g[...] = early[:deep, :].astype(F32)
    for part in range(pieces):
        up_g[:, part * width : (part + 1) * width] = early[
            deep + part * unit_rows : deep + (part + 1) * unit_rows, :
        ].astype(F32)
    out_g[...] = early[2 * deep : 2 * deep + unit_rows, :].astype(F32)
    align_g[:, :width] = early[2 * deep + unit_rows : 2 * deep + 2 * unit_rows, :].astype(F32)
    extra = align_g.shape[1] - width
    third = unit_rows * extra // width
    begin = 2 * deep + 2 * unit_rows
    for part in range(width // extra):
        align_g[part * third : (part + 1) * third, width:] = early[
            begin : begin + third, part * extra : (part + 1) * extra
        ].astype(F32)

    places = [(1, 0), (2, 0), (3, 0), (4, 0), (0, 1), (1, 1), (2, 1), (3, 1), (0, 0), (5, 0)]
    for target, (row, late_part) in zip(vector_outs, places):
        size = target.shape[1]
        first = d * size
        window = size if size % 128 == 0 else -(-size // 128) * 128 + 128
        begin = late_part * pieces * width
        origin = jnp.minimum(lax.div(first, 128) * 128, vector.shape[1] - begin - window)
        value = vector[:, pl.ds(pl.multiple_of(begin + origin, 128), window)]
        at = lax.broadcasted_iota(jnp.int32, (window, size), 0)
        want = lax.broadcasted_iota(jnp.int32, (window, size), 1) + (first - origin)
        chosen = jnp.where(at == want, 1.0, 0.0)
        picked = jnp.dot(value, chosen, preferred_element_type=F32, precision=lax.Precision.HIGHEST)
        target[...] = picked[row : row + 1]
    for number, found in enumerate(found_all):
        @pl.when(found >= 0)
        def _():
            pltpu.make_async_copy(
                got.at[0, number // bal], balanced.at[number // bal, number % bal], sem.at[number]
            ).wait()


SMALL_NAMES = (
    "mixer_gain", "mixer_shift", "query_bias", "value_bias", "out_bias", "dense_gain", "dense_shift",
    "down_bias", "up_bias", "align_bias",
)


def whole(shape):
    return pl.BlockSpec(shape, lambda *_: (0,) * len(shape), pipeline_mode=pl.Buffered(1))


def params(**more):
    return pltpu.CompilerParams(vmem_limit_bytes=VMEM_LIMIT, **more)


def run_block(
    long_rows_in, short_rows_in, index, long_target, short_target, tile_len, source, count, lengths,
    tile, long_rows, micros, weights, groups, vectors, up_b, align_b,
):
    w = weights
    width = long_rows_in.shape[1]
    total = long_rows_in.shape[0] + short_rows_in.shape[0]
    wide = w["up_weight"].shape[1]
    teach = long_target.shape[1]
    patches = w["position"].shape[0]
    blocks = total // BLOCK
    parts = BLOCK // tile
    border = micros * long_rows // tile
    last = 2 * micros + 2
    pairs = HEADS // 2
    pair = width // pairs
    unit_rows = width // groups
    pieces = wide // width
    early_rows = (2 * pieces + 2) * unit_rows + unit_rows * (teach - width) // width
    early_rows = -(-early_rows // 512) * 512
    chunk = -(-(patches // groups) // 16) * 16 if groups > 1 else patches // 14
    late_rows = (chunk if groups > 1 else patches) + 3 * unit_rows
    def kept(i, count):
        return jnp.minimum(i, count[last] - 1)

    def tiles(width):
        near = [
            pl.BlockSpec(
                (tile, width),
                lambda i, tl, src, cnt, *_, part=part: (jnp.minimum(src[kept(i, cnt) * parts + part], border - 1), 0),
            )
            for part in range(parts)
        ]
        far = [
            pl.BlockSpec(
                (tile, width),
                lambda i, tl, src, cnt, *_, part=part: (jnp.maximum(src[kept(i, cnt) * parts + part] - border, 0), 0),
            )
            for part in range(parts)
        ]
        return near + far

    by_block = lambda last_dim: pl.BlockSpec((BLOCK, last_dim), lambda i, tl, src, cnt, *_: (kept(i, cnt), 0))
    by_column = lambda first: pl.BlockSpec((first, BLOCK), lambda i, tl, src, cnt, *_: (0, kept(i, cnt)))
    guarded = lambda first: pl.BlockSpec(
        (first, BLOCK), lambda i, tl, src, cnt, *_: (0, jnp.minimum(i, cnt[last]))
    )
    anywhere = pl.BlockSpec(memory_space=pl.ANY)
    show = [
        pltpu.VMEM((2, BLOCK, width), BF),
        pltpu.SemaphoreType.DMA((2, parts)),
        pltpu.SemaphoreType.DMA((2,)),
    ]
    shown_shapes = [
        jax.ShapeDtypeStruct(long_rows_in.shape, BF),
        jax.ShapeDtypeStruct(short_rows_in.shape, BF),
    ]

    triple_t, start = pl.pallas_call(
        partial(project_kernel, tile, border, last),
        grid_spec=pltpu.PrefetchScalarGridSpec(
            num_scalar_prefetch=4,
            grid=(blocks,),
            in_specs=tiles(width) + [anywhere, anywhere, whole(vectors.shape)],
            out_specs=[guarded(3 * width), by_block(width)],
            scratch_shapes=[
                pltpu.VMEM((patches, width), F32),
                pltpu.VMEM((4, patches // 14, width), BF),
                pltpu.VMEM((BLOCK, width), F32),
                pltpu.VMEM((width, 3 * width), BF),
                pltpu.SemaphoreType.DMA((1,)),
                pltpu.SemaphoreType.DMA((4,)),
            ],
        ),
        out_shape=[
            jax.ShapeDtypeStruct((3 * width, total), BF),
            jax.ShapeDtypeStruct((total, width), F32),
        ],
        compiler_params=params(),
        name="project",
    )(
        tile_len, source, count, index, *([long_rows_in] * parts), *([short_rows_in] * parts),
        w["position"], w["heads_weight"], vectors,
    )

    def heads_spec(offset):
        return pl.BlockSpec((pair, total), lambda i, *_: (i + offset * pairs, 0))

    board = pltpu.VMEM((long_rows, BLOCK), F32)
    sums_spec = pl.BlockSpec((1, 2, total), lambda i, *_: (i, 0, 0))
    attended_t, sums = pl.pallas_call(
        partial(attend_kernel, tile, long_rows, micros),
        grid_spec=pltpu.PrefetchScalarGridSpec(
            num_scalar_prefetch=3,
            grid=(pairs,),
            in_specs=[heads_spec(0), heads_spec(1), heads_spec(2)],
            out_specs=[heads_spec(0), sums_spec],
            scratch_shapes=[board] * 2,
        ),
        out_shape=[
            jax.ShapeDtypeStruct((width, total), BF),
            jax.ShapeDtypeStruct((pairs, 2, total), F32),
        ],
        compiler_params=params(),
        name="attend",
    )(tile_len, lengths, count, triple_t, triple_t, triple_t)

    some = max(groups // pieces, 1)
    long_out, short_out, pulled_t, grad_middle, vector, early = pl.pallas_call(
        partial(middle_kernel, tile, border, last),
        grid_spec=pltpu.PrefetchScalarGridSpec(
            num_scalar_prefetch=3,
            grid=(blocks,),
            in_specs=[by_column(width), by_block(width)]
            + tiles(teach)
            + [
                anywhere, anywhere, anywhere, anywhere,
                whole(vectors.shape), whole(up_b.shape), whole(align_b.shape),
            ],
            out_specs=[
                anywhere, anywhere, guarded(width), by_block(width), whole((8, wide)), anywhere,
            ],
            scratch_shapes=[
                pltpu.VMEM((width, width), F32),
                pltpu.VMEM((pieces, width, width), F32),
                pltpu.VMEM((pieces, width, width), F32),
                pltpu.VMEM((width, teach), F32),
                pltpu.VMEM((BLOCK, wide), BF),
                pltpu.VMEM((BLOCK, wide), F32),
                pltpu.VMEM((2, groups, unit_rows, width), BF),
                pltpu.VMEM((2, some, width // some, width), BF),
                pltpu.VMEM((width, width), BF),
                pltpu.VMEM((width, wide), BF),
                pltpu.VMEM((wide, width), BF),
                pltpu.VMEM((width, teach), BF),
                pltpu.SemaphoreType.DMA((4,)),
                pltpu.SemaphoreType.DMA((2,)),
            ]
            + show,
        ),
        out_shape=shown_shapes
        + [
            jax.ShapeDtypeStruct((width, total), BF),
            jax.ShapeDtypeStruct((total, width), F32),
            jax.ShapeDtypeStruct((8, wide), F32),
            jax.ShapeDtypeStruct((groups, early_rows, width), BF),
        ],
        compiler_params=params(),
        name="middle",
    )(
        tile_len, source, count, attended_t, start, *([long_target] * parts), *([short_target] * parts),
        w["out_weight"], w["up_weight"], w["down_weight"], w["align_weight"], vectors, up_b, align_b,
    )

    grads = pl.pallas_call(
        partial(attend_back_kernel, tile, long_rows, micros),
        grid_spec=pltpu.PrefetchScalarGridSpec(
            num_scalar_prefetch=3,
            grid=(pairs,),
            in_specs=[heads_spec(0), heads_spec(1), heads_spec(2), heads_spec(0), sums_spec],
            out_specs=[heads_spec(0)] * 3,
            scratch_shapes=[pltpu.VMEM((pair, long_rows), F32)] * 2 + [board] * 4,
        ),
        out_shape=[jax.ShapeDtypeStruct((width, total), BF)] * 3,
        compiler_params=params(),
        name="attend_back",
    )(tile_len, lengths, count, triple_t, triple_t, triple_t, pulled_t, sums)

    long_grad, short_grad, entry_vector, late = pl.pallas_call(
        partial(entry_kernel, tile, border, last),
        grid_spec=pltpu.PrefetchScalarGridSpec(
            num_scalar_prefetch=4,
            grid=(blocks,),
            in_specs=[by_column(width)] * 3
            + [by_block(width), by_block(width), anywhere, whole(vectors.shape)],
            out_specs=[anywhere, anywhere, whole((8, width)), anywhere],
            scratch_shapes=[
                pltpu.VMEM((width, 3 * width), F32),
                pltpu.VMEM((patches + 8, width), F32),
                pltpu.VMEM((BLOCK, width), F32),
                pltpu.VMEM((2, groups, unit_rows, width), BF),
                pltpu.VMEM((4, chunk, width), BF),
                pltpu.VMEM((width, 3 * width), BF),
                pltpu.SemaphoreType.DMA((1,)),
                pltpu.SemaphoreType.DMA((4,)),
            ]
            + show,
        ),
        out_shape=shown_shapes
        + [
            jax.ShapeDtypeStruct((8, width), F32),
            jax.ShapeDtypeStruct((groups, late_rows, width), BF),
        ],
        compiler_params=params(),
        name="entry",
    )(tile_len, source, count, index, *grads, start, grad_middle, w["heads_weight"], vectors)
    return long_out, short_out, long_grad, short_grad, early, late, vector, entry_vector


def bit_of(number, bit):
    return lax.rem(number // (1 << bit), 2)


def reduce_plan(peers, early_rows, late_rows):
    bits = peers.bit_length() - 1
    forward = list(range(bits))
    swapped = forward[1::-1] + forward[2:]
    last = forward[2:] + forward[:2]
    pieces = []
    for source, rows in ((0, early_rows), (1, late_rows)):
        unit = 16
        units = rows // 2 // unit
        begin = 0
        for sub in range(2):
            here = units // 2 + (1 if sub < units % 2 else 0)
            first = int(here * 0.4 + 0.5)
            for order, parts in zip((forward, swapped, last), (first, first, here - 2 * first)):
                if parts > 0:
                    pieces.append((source * 2 + sub, source, begin, parts * unit, tuple(order)))
                    begin += parts * unit
    return pieces


def reduce_kernel(
    peers, halves, pieces, early, late, vector, entry_vector, early_out, late_out, vector_out, *scratch
):
    bits = peers.bit_length() - 1
    amount = len(pieces)
    kept = scratch[:amount]
    mates = scratch[amount : 2 * amount]
    mine_in = scratch[2 * amount : 3 * amount]
    landed = [scratch[3 * amount + k * bits : 3 * amount + (k + 1) * bits] for k in range(amount)]
    (
        vector_land, mate_send, mate_recv, load_sem, hop_send, hop_recv, end_send, end_recv, end_load,
        vector_send, vector_recv,
    ) = scratch[3 * amount + amount * bits :]
    d = lax.axis_index("dp")
    r = lax.axis_index("rep")
    other = 1 - r
    mate = (d, other)
    partner = [(d + (1 - 2 * bit_of(d, bit)) * (1 << bit), r) for bit in range(bits)]
    sources = (early, late)
    outs = (early_out, late_out)
    barrier = pltpu.get_barrier_semaphore()
    for device in [mate] + partner:
        pl.semaphore_signal(barrier, inc=1, device_id=device, device_id_type=pl.DeviceIdType.MESH)
    pl.semaphore_wait(barrier, bits + 1)

    def remote(source, target, send, recv, device):
        copy = pltpu.make_async_remote_copy(
            src_ref=source, dst_ref=target, send_sem=send, recv_sem=recv,
            device_id=device, device_id_type=pl.DeviceIdType.MESH,
        )
        copy.start()
        return copy

    def rows_at(source, core, begin, rows):
        return pl.ds(pl.multiple_of(core * halves[source] + begin, 16), rows)

    wide = vector.shape[1]
    vector_out[:, :wide] = vector[...]
    vector_out[:, wide:] = entry_vector[...]
    mate_copies = []
    loads = []
    for k, (_, source, begin, rows, order) in enumerate(pieces):
        mate_copies.append(
            remote(
                sources[source].at[:, rows_at(source, other, begin, rows), :], mates[k],
                mate_send.at[k], mate_recv.at[k], mate,
            )
        )
        load = pltpu.make_async_copy(
            sources[source].at[:, rows_at(source, r, begin, rows), :], mine_in[k], load_sem.at[k]
        )
        load.start()
        loads.append(load)

    hops = {}
    ends = []

    def base_at(order, stage):
        base = 0
        for place in range(stage):
            base = base + bit_of(d, order[place]) * (1 << (bits - 1 - place))
        return base

    def send(k, stage):
        _, source, begin, rows, order = pieces[k]
        if stage == bits:
            result = kept[k].at[base_at(order, bits)]
            where = rows_at(source, r, begin, rows)
            ends.append(remote(result, outs[source].at[where, :], end_send.at[k], end_recv.at[k], mate))
            own = pltpu.make_async_copy(result, outs[source].at[where, :], end_load.at[k])
            own.start()
            ends.append(own)
            return
        size = 1 << (bits - 1 - stage)
        first = base_at(order, stage) + (1 - bit_of(d, order[stage])) * size
        hops[k, stage] = remote(
            kept[k].at[pl.ds(first, size)], landed[k][stage], hop_send.at[k, stage], hop_recv.at[k, stage],
            partner[order[stage]],
        )

    def join(k):
        order = pieces[k][4]
        loads[k].wait()
        mate_copies[k].wait_recv()

        def add(chunk, carry):
            place = 0
            for step in range(bits):
                place = place + bit_of(chunk, order[step]) * (1 << (bits - 1 - step))
            kept[k][place] = mine_in[k][chunk] + mates[k][chunk]
            return carry

        lax.fori_loop(0, peers, add, 0)

    def gather(k, stage):
        order = pieces[k][4]
        hops[k, stage].wait_recv()
        base = base_at(order, stage + 1)

        def add(chunk, carry):
            kept[k][base + chunk] = kept[k][base + chunk] + landed[k][stage][chunk]
            return carry

        lax.fori_loop(0, 1 << (bits - 1 - stage), add, 0)

    events = sorted(
        (stage + pieces[k][0], -stage, k) for k in range(amount) for stage in range(bits + 1)
    )
    vector_copies = []

    def vector_step(stage):
        if stage > 0:
            vector_copies[-1].wait()
            vector_out[...] = vector_out[...] + vector_land[stage - 1]
        if stage <= bits:
            device = mate if stage == 0 else partner[stage - 1]
            vector_copies.append(
                remote(vector_out, vector_land.at[stage], vector_send.at[stage], vector_recv.at[stage], device)
            )

    seen = -1
    for time, negative, k in events:
        if time != seen:
            if time <= bits + 1:
                vector_step(time)
            seen = time
        stage = -negative
        if stage == 0:
            join(k)
        else:
            gather(k, stage - 1)
        send(k, stage)
    for copy in mate_copies + list(hops.values()):
        copy.wait_send()
    for copy in ends:
        copy.wait()


def reduce_all(early, late, vector, entry_vector):
    joined = (vector.shape[0], vector.shape[1] + entry_vector.shape[1])
    peers, early_rows, width = early.shape
    late_rows = late.shape[1]
    bits = peers.bit_length() - 1
    pieces = reduce_plan(peers, early_rows, late_rows)
    amount = len(pieces)
    scratch = [pltpu.VMEM((peers, rows, width), BF) for _, _, _, rows, _ in pieces] * 3
    for _, _, _, rows, _ in pieces:
        for stage in range(bits):
            scratch.append(pltpu.VMEM((1 << (bits - 1 - stage), rows, width), BF))
    scratch.append(pltpu.VMEM((bits + 1,) + joined, F32))
    one = pltpu.SemaphoreType.DMA((amount,))
    many = pltpu.SemaphoreType.DMA((amount, bits))
    few = pltpu.SemaphoreType.DMA((bits + 1,))
    scratch += [one, one, one, many, many, one, one, one, few, few]
    anywhere = pl.BlockSpec(memory_space=pl.ANY)
    near = pl.BlockSpec(memory_space=pltpu.VMEM)
    return pl.pallas_call(
        partial(reduce_kernel, peers, (early_rows // 2, late_rows // 2), pieces),
        in_specs=[anywhere, anywhere, near, near],
        out_specs=[anywhere, anywhere, near],
        out_shape=[
            jax.ShapeDtypeStruct((early_rows, width), BF),
            jax.ShapeDtypeStruct((late_rows, width), BF),
            jax.ShapeDtypeStruct(joined, F32),
        ],
        scratch_shapes=scratch,
        compiler_params=pltpu.CompilerParams(
            vmem_limit_bytes=VMEM_LIMIT, collective_id=0, has_side_effects=True
        ),
        name="reduce",
    )(early, late, vector, entry_vector)


def unpack(early, late, unit_rows, kept, teach, pieces):
    width = early.shape[1]
    deep = pieces * unit_rows

    def beside(held, first, count):
        return jnp.concatenate(
            [held[first + k * unit_rows : first + (k + 1) * unit_rows] for k in range(count)], axis=1
        )

    extra = teach - width
    third = unit_rows * extra // width
    begin = 2 * deep + 2 * unit_rows
    tail = early[begin : begin + third]
    tail = jnp.concatenate([tail[:, k * extra : (k + 1) * extra] for k in range(width // extra)], axis=0)
    return {
        "down_weight": early[:deep],
        "up_weight": beside(early, deep, pieces),
        "out_weight": early[2 * deep : 2 * deep + unit_rows],
        "align_weight": jnp.concatenate([early[2 * deep + unit_rows : begin], tail], axis=1),
        "position": late[:kept],
        "heads_weight": beside(late, late.shape[0] - 3 * unit_rows, 3),
    }


def shards(
    long_clips,
    short_clips,
    long_index,
    short_index,
    long_length,
    short_length,
    destination,
    long_target,
    short_target,
    position,
    mixer_gain,
    mixer_shift,
    heads_weight,
    query_bias,
    value_bias,
    out_weight,
    out_bias,
    dense_gain,
    dense_shift,
    up_weight,
    up_bias,
    down_weight,
    down_bias,
    align_weight,
    align_bias,
):
    peers = lax.axis_size("dp")
    copies = lax.axis_size("rep")
    micros, _, long_rows, width = long_clips.shape
    home_slots, tile = short_clips.shape[1:3]
    bal_slots = home_slots // 2
    slots = micros * home_slots
    wide = up_weight.shape[1]
    teach = long_target.shape[-1]
    patches = position.shape[0]
    weights = dict(
        zip(
            WEIGHT_NAMES,
            (
                position, mixer_gain, mixer_shift, heads_weight, query_bias, value_bias, out_weight, out_bias,
                dense_gain, dense_shift, up_weight, up_bias, down_weight, down_bias, align_weight, align_bias,
            ),
        )
    )
    scalars = pl.BlockSpec(memory_space=pltpu.SMEM)
    anywhere = pl.BlockSpec(memory_space=pl.ANY)
    tile_total = micros * long_rows // tile + slots
    near = pl.BlockSpec(memory_space=pltpu.VMEM)
    tile_len, source, count, vectors, up_b, align_b = pl.pallas_call(
        partial(plan_kernel, tile, long_rows, home_slots, copies),
        in_specs=[scalars, scalars] + [near] * len(SMALL_NAMES),
        out_specs=[scalars] * 3 + [near] * 3,
        out_shape=[
            jax.ShapeDtypeStruct((tile_total,), jnp.int32),
            jax.ShapeDtypeStruct((tile_total,), jnp.int32),
            jax.ShapeDtypeStruct((2 * micros + 3,), jnp.int32),
            jax.ShapeDtypeStruct((len(SMALL_NAMES) - 2, width), F32),
            jax.ShapeDtypeStruct((1, wide), F32),
            jax.ShapeDtypeStruct((1, teach), F32),
        ],
        name="plan",
    )(long_length, short_length, *[weights[name] for name in SMALL_NAMES])
    index = jnp.concatenate([long_index.reshape(-1), short_index.reshape(-1)])
    groups = peers if copies == 2 and width % (16 * peers) == 0 else 1
    long_out, short_out, long_grad, short_grad, early, late, vector, entry_vector = run_block(
        long_clips.reshape(-1, width), short_clips.reshape(-1, width), index,
        long_target.reshape(-1, teach), short_target.reshape(-1, teach),
        tile_len, source, count, long_length.reshape(-1), tile, long_rows, micros, weights, groups,
        vectors, up_b, align_b,
    )
    send = pl.pallas_call(
        partial(send_kernel, home_slots, copies),
        in_specs=[scalars, scalars, whole((slots, tile, width))],
        out_specs=pl.BlockSpec(memory_space=pltpu.VMEM) if groups == peers else scalars,
        out_shape=jax.ShapeDtypeStruct((peers, micros, tile, width), BF),
        compiler_params=params(),
        name="send",
    )(short_length, destination, short_out.reshape(slots, tile, width)) if groups == peers else send_all(
        short_length, destination, short_out.reshape(slots, tile, width), peers, copies, home_slots
    )
    got = lax.all_to_all(send, "dp", split_axis=0, concat_axis=0, tiled=True)
    unit_rows = width // peers
    if groups == peers:
        early, late, vector = reduce_all(early, late, vector, entry_vector)
    else:
        matrices = unpack(early[0], late[0], width, patches, teach, wide // width)
        early, late = share_out(matrices, peers, copies, unit_rows, wide // width)
        vector = lax.psum(jnp.concatenate([vector, entry_vector], axis=1), ("dp", "rep"))
    near = pl.BlockSpec(memory_space=pltpu.VMEM)
    outs = pl.pallas_call(
        partial(finish_kernel, home_slots, copies),
        in_specs=[scalars, scalars, anywhere, near, near, near],
        out_specs=[near] * 17,
        out_shape=[
            jax.ShapeDtypeStruct((micros, bal_slots, tile, width), BF),
            jax.ShapeDtypeStruct((patches // peers, width), F32),
            jax.ShapeDtypeStruct((unit_rows, 3 * width), F32),
            jax.ShapeDtypeStruct((unit_rows, width), F32),
            jax.ShapeDtypeStruct((unit_rows, wide), F32),
            jax.ShapeDtypeStruct((wide // peers, width), F32),
            jax.ShapeDtypeStruct((unit_rows, teach), F32),
        ]
        + [jax.ShapeDtypeStruct((1, unit_rows), F32)] * 8
        + [jax.ShapeDtypeStruct((1, wide // peers), F32), jax.ShapeDtypeStruct((1, teach // peers), F32)],
        scratch_shapes=[pltpu.SemaphoreType.DMA((micros * bal_slots,))],
        compiler_params=params(),
        name="finish",
    )(short_length, destination, got, early, late, vector)
    short_bal, position_g, heads_g, out_g, up_g, down_g, align_g = outs[:7]
    shared = {
        "position": position_g, "heads_weight": heads_g, "out_weight": out_g, "up_weight": up_g,
        "down_weight": down_g, "align_weight": align_g,
    }
    order = (
        "out_bias", "dense_gain", "dense_shift", "down_bias", "query_bias", "mixer_gain", "value_bias",
        "mixer_shift", "up_bias", "align_bias",
    )
    for name, value in zip(order, outs[7:]):
        shared[name] = value.reshape(-1)
    return (
        long_out.reshape(micros, 1, long_rows, width),
        short_bal,
        long_grad.reshape(micros, 1, long_rows, width),
        short_grad.reshape(micros, home_slots, tile, width),
    ) + tuple(shared[name] for name in WEIGHT_NAMES)


def send_all(short_length, destination, shown, peers, copies, home):
    micros = short_length.shape[0]
    mine = lax.axis_index("dp") * copies + lax.axis_index("rep")

    def own(table):
        table = table.reshape(micros, peers * copies, home)
        return lax.dynamic_index_in_dim(table, mine, 1, keepdims=False)

    wanted = (own(destination)[None] == jnp.arange(peers)[:, None, None]) & (own(short_length)[None] > 0)
    shown = shown.reshape((micros, home) + shown.shape[1:])
    return jnp.einsum("pmj,mjtd->pmtd", wanted.astype(BF), shown)


def share_out(matrices, peers, copies, unit_rows, pieces):
    shared = {}
    for name, piece in matrices.items():
        rows = piece.shape[0] // peers
        padded = -(-rows // (8 * copies)) * 8 * copies
        if padded != rows:
            piece = piece.reshape(peers, rows, -1)
            piece = jnp.pad(piece, ((0, 0), (0, padded - rows), (0, 0)))
            piece = piece.reshape(peers * padded, -1)
        piece = lax.psum_scatter(piece, ("dp", "rep"), scatter_dimension=0, tiled=True)
        shared[name] = lax.all_gather(piece, "rep", axis=0, tiled=True)[:rows]
    width = shared["out_weight"].shape[1]
    up = shared["up_weight"].reshape(unit_rows, pieces, width).transpose(1, 0, 2).reshape(-1, width)
    heads = shared["heads_weight"].reshape(unit_rows, 3, width).transpose(1, 0, 2).reshape(-1, width)
    align = shared["align_weight"]
    extra = align.shape[1] - width
    parts = width // extra
    tail = align[:, width:].reshape(parts, unit_rows // parts, extra).transpose(1, 0, 2).reshape(-1, width)
    early = jnp.concatenate([shared["down_weight"], up, shared["out_weight"], align[:, :width], tail], axis=0)
    return early, jnp.concatenate([shared["position"], heads], axis=0)


def solution(mesh):
    placed = (
        P(None, ("dp", "rep"), None, None),
        P(None, ("dp", "rep"), None, None),
        P(None, ("dp", "rep"), None),
        P(None, ("dp", "rep"), None),
        P(None, ("dp", "rep")),
        P(),
        P(),
        P(None, ("dp", "rep"), None, None),
        P(None, ("dp", "rep"), None, None),
        P(),
        P(),
        P(),
        P(),
        P(),
        P(),
        P(),
        P(),
        P(),
        P(),
        P(),
        P(),
        P(),
        P(),
        P(),
        P(),
    )
    return jax.shard_map(
        shards,
        mesh=mesh,
        in_specs=placed,
        out_specs=(
            P(None, ("dp", "rep"), None, None),
            P(None, ("dp", "rep"), None, None),
            P(None, ("dp", "rep"), None, None),
            P(None, ("dp", "rep"), None, None),
            P("dp", None),
            P("dp"),
            P("dp"),
            P("dp", None),
            P("dp"),
            P("dp"),
            P("dp", None),
            P("dp"),
            P("dp"),
            P("dp"),
            P("dp", None),
            P("dp"),
            P("dp", None),
            P("dp"),
            P("dp", None),
            P("dp"),
        ),
        check_vma=False,
    )
```

```python
from functools import partial

import jax
import jax.numpy as jnp
from jax import lax
from jax.experimental import pallas as pl
from jax.experimental.pallas import tpu as pltpu
from jax.sharding import PartitionSpec as P

HEADS = 12
EPS = 1e-06
MASKED = -1000000000.0
WEIGHT_NAMES = (
    "position",
    "mixer_gain",
    "mixer_shift",
    "heads_weight",
    "query_bias",
    "value_bias",
    "out_weight",
    "out_bias",
    "dense_gain",
    "dense_shift",
    "up_weight",
    "up_bias",
    "down_weight",
    "down_bias",
    "align_weight",
    "align_bias",
)


BLOCK = 256
BF = jnp.bfloat16
F32 = jnp.float32
VMEM_LIMIT = 66_000_000


def dot(left, right, dims):
    return lax.dot_general(left, right, ((dims[:1], dims[1:]), ((), ())), preferred_element_type=F32)


def centre(values):
    mean = jnp.mean(values, axis=-1, keepdims=True)
    centered = values - mean
    spread = jnp.mean(centered * centered, axis=-1, keepdims=True)
    inverse = lax.rsqrt(spread + EPS)
    return centered * inverse, inverse


def centre_back(grad, unit, inverse):
    first = jnp.mean(grad, axis=-1, keepdims=True)
    second = jnp.mean(grad * unit, axis=-1, keepdims=True)
    return inverse * (grad - first - unit * second)


def valid_rows(tile_len, block, tile):
    row = lax.broadcasted_iota(jnp.int32, (BLOCK, 1), 0)
    parts = BLOCK // tile
    limit = tile_len[block * parts]
    for part in range(1, parts):
        limit = jnp.where(row >= part * tile, tile_len[block * parts + part], limit)
    return lax.rem(row, tile) < limit


def clip_cost(length):
    blocks = lax.div(length + BLOCK - 1, BLOCK)
    return 2 * lax.div(length + 127, 128) + blocks * blocks


def plan_kernel(tile, long_rows, home, copies, lengths, guest, short_len, *refs):
    amount = len(refs) - 7
    small, (tile_len, source, count, work, vectors, up_out, align_out) = refs[:amount], refs[amount:]
    for number, value in enumerate(small[:-2]):
        vectors[number : number + 1, :] = value[...].reshape(1, -1)
    up_out[...] = small[-2][...].reshape(1, -1)
    align_out[...] = small[-1][...].reshape(1, -1)
    micros = lengths.shape[0]
    slots = micros * home
    per = long_rows // tile
    step = 128 // tile
    d, r = lax.axis_index("dp"), lax.axis_index("rep")
    base = (d * copies + r) * home
    other = (d * copies + lax.rem(r + 1, copies)) * home

    def put(place, origin, size):
        source[place] = origin
        tile_len[place] = size

    mine, theirs = jnp.int32(0), jnp.int32(0)
    for slot in range(slots):
        mine = mine + jnp.where(short_len[slot // home, base + slot % home] > 0, 1, 0)
        theirs = theirs + jnp.where(short_len[slot // home, other + slot % home] > 0, 1, 0)
    for micro in range(micros - 1):
        mine = mine + clip_cost(lengths[micro, 0])
        theirs = theirs + clip_cost(guest[micro])
    held, offered = clip_cost(lengths[micros - 1, 0]), clip_cost(guest[micros - 1])
    apart = jnp.maximum(mine + held, theirs + offered)
    traded = jnp.maximum(mine + offered, theirs + held)
    swap = traded + 1 < apart
    count[2 * micros + 3] = swap.astype(jnp.int32)
    place = jnp.int32(0)
    taken = []
    origins = []
    for micro in range(micros):
        length = lengths[micro, 0]
        origin = jnp.int32(micro * per)
        if micro == micros - 1:
            length = jnp.where(swap, guest[micro], length)
            origin = jnp.where(swap, micros * per + slots, origin)
        origins.append(origin)
        work[micro] = length
        some = lax.div(length + 127, 128) * step
        count[micro] = lax.div(length + BLOCK - 1, BLOCK)
        count[micros + 1 + micro] = place

        def add(number, carry, origin=origin, length=length, place=place):
            put(place + number, origin + number, jnp.clip(length - number * tile, 0, tile))
            return carry

        lax.fori_loop(0, some, add, 0)
        taken.append(some)
        place = place + some
    first = place
    sizes = [short_len[slot // home, base + slot % home] for slot in range(slots)]
    for wanted in (True, False):
        for slot, size in enumerate(sizes):
            fits = (size > 0) if wanted else (size <= 0)

            @pl.when(fits)
            def _():
                put(place, micros * per + slot, size)

            place = place + jnp.where(fits, 1, 0)
        if wanted:
            parts = BLOCK // tile
            count[micros] = lax.div(place - first + parts - 1, parts)
            count[2 * micros + 1] = first
            count[2 * micros + 2] = lax.div(place + parts - 1, parts)
    for micro in range(micros):
        def fill(number, carry, micro=micro, place=place - taken[micro]):
            put(place + number, origins[micro] + number, 0)
            return carry

        lax.fori_loop(taken[micro], per, fill, 0)
        place = place + per - taken[micro]


def pieced(step, source, parts, border, refs):
    low, high = border
    chosen = []
    for part in range(parts):
        origin = source[step * parts + part]
        far = jnp.where(origin < high, refs[parts + part][...], refs[2 * parts + part][...])
        chosen.append(jnp.where(origin < low, refs[part][...], far))
    return jnp.concatenate(chosen, axis=0).astype(F32)


def put_tiles(step, value, source, border, tile, stage, sem, near, far, guest):
    low, high = border
    parts = BLOCK // tile
    slot = lax.rem(step, 2)

    def settle(which):
        for part in range(parts):
            pltpu.make_async_copy(
                stage.at[which, pl.ds(part * tile, tile), :], near.at[pl.ds(0, tile), :], sem.at[which, part]
            ).wait()

    @pl.when(step >= 2)
    def _():
        settle(slot)

    stage[slot] = value
    for part in range(parts):
        origin = source[step * parts + part]
        view = stage.at[slot, pl.ds(part * tile, tile), :]

        def push(target, first, view=view, part=part, origin=origin):
            where = pl.ds(pl.multiple_of((origin - first) * tile, tile), tile)
            pltpu.make_async_copy(view, target.at[where, :], sem.at[slot, part]).start()

        @pl.when(origin < low)
        def _():
            push(near, 0)

        @pl.when((origin >= low) & (origin < high))
        def _():
            push(far, low)

        @pl.when(origin >= high)
        def _():
            push(guest, high)

    @pl.when(step == pl.num_programs(0) - 1)
    def _():
        settle(1 - slot)
        settle(slot)


def project_kernel(tile, border, last, tile_len, source, count, index, *refs):
    parts = BLOCK // tile
    table_any, weight_any, vectors, out, start_out, table, stage, rows, weight, weight_sem, sem = refs[3 * parts :]
    step = pl.program_id(0)
    width = weight.shape[0]
    depth, chunk = stage.shape[:2]
    chunks = table.shape[0] // chunk

    def fetch(number):
        return pltpu.make_async_copy(
            table_any.at[pl.ds(pl.multiple_of(number * chunk, 16), chunk), :],
            stage.at[lax.rem(number, depth)],
            sem.at[lax.rem(number, depth)],
        )

    @pl.when(step == 0)
    def _():
        for number in range(depth):
            fetch(number).start()
        weight_load = pltpu.make_async_copy(weight_any, weight, weight_sem.at[0])
        weight_load.start()
        rows[...] = jnp.zeros_like(rows)

        def load(number, carry):
            fetch(number).wait()
            table[pl.ds(pl.multiple_of(number * chunk, 16), chunk), :] = stage[lax.rem(number, depth)].astype(F32)

            @pl.when(number + depth < chunks)
            def _():
                fetch(number + depth).start()

            return carry

        lax.fori_loop(0, chunks, load, 0)
        weight_load.wait()

    @pl.when(step == count[last])
    def _():
        out[...] = jnp.zeros_like(out)

    @pl.when(step < count[last])
    def _():
        def gather(part, carry):
            origin = source[step * parts + part] * tile
            first = part * tile

            def some(group, inner):
                base = pl.multiple_of(first + group * 8, 8)
                for row in range(8):
                    place = index[origin + group * 8 + row]
                    rows[pl.ds(base + row, 1), :] = table[pl.ds(place, 1), :]
                return inner

            lax.fori_loop(0, lax.div(tile_len[step * parts + part] + 7, 8), some, 0)
            return carry

        lax.fori_loop(0, parts, gather, 0)
        start = pieced(step, source, parts, border, refs) + rows[...]
        start_out[...] = start
        unit, _ = centre(start)
        normed = (unit * vectors[0:1, :width] + vectors[1:2, :width]).astype(BF)
        for part in range(3):
            cols = slice(part * width, (part + 1) * width)
            triple = dot(normed, weight[:, cols], (1, 0))
            if part == 0:
                triple = (triple + vectors[2:3, :width]).astype(BF) * BF(0.125)
            elif part == 1:
                triple = triple.astype(BF)
            else:
                triple = (triple + vectors[3:4, :width]).astype(BF)
            out[cols, :] = triple.T


def masked_tile(tile_scores, limit):
    key = lax.broadcasted_iota(jnp.int32, tile_scores.shape, 0)
    return jnp.where(key < limit, tile_scores, MASKED)


def block_mask(tile_len, first, tile):
    key = lax.broadcasted_iota(jnp.int32, (BLOCK, BLOCK), 0)
    asked = lax.broadcasted_iota(jnp.int32, (BLOCK, BLOCK), 1)
    limit = tile_len[first]
    for part in range(1, BLOCK // tile):
        limit = jnp.where(key >= part * tile, tile_len[first + part], limit)
    return (key // tile == asked // tile) & (lax.rem(key, tile) < limit)


def attend_kernel(tile, long_rows, clips, tile_len, length, count, query, keys, values, out, logsum, even, odd):
    head_dim = query.shape[0] // 2
    most = long_rows // BLOCK
    boards = (even, odd)

    def score(head, column, first, size, fix):
        lanes = slice(head * head_dim, (head + 1) * head_dim)
        asked = query[lanes, pl.ds(column, BLOCK)]
        for number in range(size):
            part = dot(keys[lanes, pl.ds(first + number * BLOCK, BLOCK)], asked, (0, 0))
            if number == size - 1:
                part = fix(part)
            boards[head][number * BLOCK : (number + 1) * BLOCK, :] = part

    def finish(head, column, first, size):
        lanes = slice(head * head_dim, (head + 1) * head_dim)
        board = boards[head]
        top = jnp.max(board[: size * BLOCK, :], axis=0, keepdims=True)
        total = None
        gathered = None
        for number in range(size):
            weight = jnp.exp(board[number * BLOCK : (number + 1) * BLOCK, :] - top)
            part = jnp.sum(weight, axis=0, keepdims=True)
            held = values[lanes, pl.ds(first + number * BLOCK, BLOCK)]
            term = dot(held, weight.astype(BF), (1, 0))
            total = part if total is None else total + part
            gathered = term if gathered is None else gathered + term
        out[lanes, pl.ds(column, BLOCK)] = (gathered / total).astype(BF)
        logsum[0, pl.ds(head, 1), pl.ds(column, BLOCK)] = top + jnp.log(total)

    def rows(first, size, fix):
        def at(block):
            return pl.multiple_of(first + block * BLOCK, 128)

        score(0, at(0), first, size, fix)

        def ask(block, carry):
            score(1, at(block), first, size, fix)
            finish(0, at(block), first, size)
            score(0, at(jnp.minimum(block + 1, size - 1)), first, size, fix)
            finish(1, at(block), first, size)
            return carry

        lax.fori_loop(0, size, ask, 0)

    def clip(number, carry):
        first = pl.multiple_of(count[clips + 1 + number] * tile, 128)
        blocks = count[number]
        rest = length[number]
        for size in range(1, most + 1):
            @pl.when(blocks == size)
            def _():
                rows(first, size, lambda part: masked_tile(part, rest - (size - 1) * BLOCK))
        return carry

    out[...] = jnp.zeros_like(out)
    lax.fori_loop(0, clips, clip, 0)

    def short(number, carry):
        begin = count[2 * clips + 1] + number * (BLOCK // tile)
        column = pl.multiple_of(begin * tile, 128)
        allowed = block_mask(tile_len, begin, tile)
        rows(column, 1, lambda part: jnp.where(allowed, part, MASKED))
        return carry

    lax.fori_loop(0, count[clips], short, 0)


def attend_back_kernel(
    tile, long_rows, clips, tile_len, length, count, query, keys, values, grad, logsum,
    query_out, key_out, value_out, key_sum, value_sum, even, odd, even_back, odd_back,
):
    head_dim = query.shape[0] // 2
    most = long_rows // BLOCK
    boards = (even, odd)
    backs = (even_back, odd_back)

    def score(head, column, first, size, fix):
        lanes = slice(head * head_dim, (head + 1) * head_dim)
        asked = query[lanes, pl.ds(column, BLOCK)]
        pulled = grad[lanes, pl.ds(column, BLOCK)]
        for number in range(size):
            here = pl.ds(first + number * BLOCK, BLOCK)
            there = slice(number * BLOCK, (number + 1) * BLOCK)
            part = dot(keys[lanes, here], asked, (0, 0))
            if number == size - 1:
                part = fix(part)
            boards[head][there, :] = part
            backs[head][there, :] = dot(values[lanes, here], pulled, (0, 0))

    def finish(head, column, first, size, limit):
        lanes = slice(head * head_dim, (head + 1) * head_dim)
        asked = query[lanes, pl.ds(column, BLOCK)]
        pulled = grad[lanes, pl.ds(column, BLOCK)]
        own = lax.broadcasted_iota(jnp.int32, (1, BLOCK), 1) < limit
        base = jnp.where(own, logsum[0, pl.ds(head, 1), pl.ds(column, BLOCK)], -1e3 * MASKED)
        inner = None
        for number in range(size):
            there = slice(number * BLOCK, (number + 1) * BLOCK)
            prob = jnp.exp(boards[head][there, :] - base)
            boards[head][there, :] = prob
            part = jnp.sum(prob * backs[head][there, :], axis=0, keepdims=True)
            inner = part if inner is None else inner + part
            value_sum[lanes, there] += dot(pulled, prob.astype(BF), (1, 1))
        query_sum = None
        for number in range(size):
            here = pl.ds(first + number * BLOCK, BLOCK)
            there = slice(number * BLOCK, (number + 1) * BLOCK)
            moved = (boards[head][there, :] * (backs[head][there, :] - inner)).astype(BF)
            key_sum[lanes, there] += dot(asked, moved, (1, 1))
            term = dot(keys[lanes, here], moved, (1, 0))
            query_sum = term if query_sum is None else query_sum + term
        query_out[lanes, pl.ds(column, BLOCK)] = (query_sum * 0.125).astype(BF)

    def rows(first, size, fix, rest):
        def at(block):
            return pl.multiple_of(first + block * BLOCK, 128)

        key_sum[:, : size * BLOCK] = jnp.zeros((2 * head_dim, size * BLOCK), F32)
        value_sum[:, : size * BLOCK] = jnp.zeros((2 * head_dim, size * BLOCK), F32)
        score(0, at(0), first, size, fix)

        def ask(block, carry):
            limit = rest - block * BLOCK
            after = jnp.minimum(block + 1, size - 1)
            score(1, at(block), first, size, fix)
            finish(0, at(block), first, size, limit)
            score(0, at(after), first, size, fix)
            finish(1, at(block), first, size, limit)
            return carry

        lax.fori_loop(0, size, ask, 0)
        key_out[:, pl.ds(first, size * BLOCK)] = key_sum[:, : size * BLOCK].astype(BF)
        value_out[:, pl.ds(first, size * BLOCK)] = value_sum[:, : size * BLOCK].astype(BF)

    def clip(number, carry):
        first = pl.multiple_of(count[clips + 1 + number] * tile, 128)
        blocks = count[number]
        rest = length[number]
        for size in range(1, most + 1):
            @pl.when(blocks == size)
            def _():
                rows(first, size, lambda part: masked_tile(part, rest - (size - 1) * BLOCK), rest)
        return carry

    for empty in (query_out, key_out, value_out):
        empty[...] = jnp.zeros_like(empty)
    lax.fori_loop(0, clips, clip, 0)

    def short(number, carry):
        begin = count[2 * clips + 1] + number * (BLOCK // tile)
        column = pl.multiple_of(begin * tile, 128)
        allowed = block_mask(tile_len, begin, tile)
        rows(column, 1, lambda part: jnp.where(allowed, part, MASKED), BLOCK)
        return carry

    lax.fori_loop(0, count[clips], short, 0)


def gelu_both(upper):
    spread = 0.5 * (1.0 + lax.erf(upper * 0.7071067811865476))
    bell = jnp.exp(-0.5 * upper * upper) * 0.3989422804014327
    return upper * spread, spread + upper * bell


def write_out(entries):
    waiting = {}
    counts = {}
    for source, stage, sem, target in entries:
        key = id(stage)
        slot = counts.get(key, 0) % stage.shape[0]
        counts[key] = counts.get(key, 0) + 1
        if (key, slot) in waiting:
            waiting[key, slot].wait()
        value = source()
        view = stage.at[slot, :, : value.shape[1], : value.shape[2]]
        stage[slot, :, : value.shape[1], : value.shape[2]] = value.astype(BF)
        copy = pltpu.make_async_copy(view, target, sem.at[slot])
        copy.start()
        waiting[key, slot] = copy
    for copy in waiting.values():
        copy.wait()


def middle_kernel(tile, border, last, tile_len, source, count, attended_t, start_in, *refs):
    parts = BLOCK // tile
    (
        out_any, up_any, down_any, align_any, vectors, up_b, align_b,
        long_out, short_out, guest_out, pull_out, grad_out, vector_out, sums_out,
        out_acc, up_acc, down_acc, align_acc, hidden, slope, stage, stage_down,
        out_w, up_w, down_w, align_w, weight_sem, down_sem, show, show_sem, sem,
    ) = refs[3 * parts :]
    step = pl.program_id(0)
    width = out_w.shape[0]
    wide = up_w.shape[1]
    teach = align_w.shape[1]
    pieces = wide // width
    live = step < count[last]
    loads = [
        pltpu.make_async_copy(source_ref, target, weight_sem.at[number])
        for number, (source_ref, target) in enumerate(
            ((out_any, out_w), (up_any, up_w), (down_any, down_w), (align_any, align_w))
        )
    ]

    @pl.when(step == 0)
    def _():
        for load in loads:
            load.start()
        for acc in (out_acc, up_acc, down_acc, align_acc):
            acc[...] = jnp.zeros_like(acc)
        vector_out[...] = jnp.zeros_like(vector_out)
        loads[0].wait()

    def put(value):
        put_tiles(step, value, source, border, tile, show, show_sem, long_out, short_out, guest_out)

    def add_vector(row, value):
        size = value.shape[1]
        vector_out[row : row + 1, :size] += value

    def over_rows(value):
        return jnp.sum(value, axis=0, keepdims=True)

    @pl.when(step == count[last])
    def _():
        pull_out[...] = jnp.zeros_like(pull_out)

    @pl.when(jnp.logical_not(live))
    def _():
        put(jnp.zeros((BLOCK, width), BF))

    @pl.when(live)
    def _():
        ok = valid_rows(tile_len, step, tile)
        across = attended_t[...]
        middle = start_in[...] + dot(across, out_w[...], (0, 0)) + vectors[4:5, :width]
        unit, inverse = centre(middle)
        dense = (unit * vectors[5:6, :width] + vectors[6:7, :width]).astype(BF)
        result = middle + vectors[7:8, :width]

        @pl.when(step == 0)
        def _():
            for load in loads[1:]:
                load.wait()

        for piece in range(pieces):
            cols = slice(piece * width, (piece + 1) * width)
            upper = dot(dense, up_w[:, cols], (1, 0)) + up_b[:, cols]
            bent, tilt = gelu_both(upper)
            low = bent.astype(BF)
            hidden[:, cols] = low
            slope[:, cols] = tilt
            result = result + dot(low, down_w[cols, :], (1, 0))
        shown = jnp.where(ok, result, 0.0).astype(BF)
        put(shown)
        projected = dot(shown, align_w[...], (1, 0)) + align_b[...]
        target = pieced(step, source, parts, border, refs)
        miss = jnp.where(ok, projected - target, 0.0).astype(BF)
        add_vector(5, over_rows(miss.astype(F32)))
        align_acc[...] += dot(shown, miss, (0, 0))
        pulled = dot(miss, align_w[...], (1, 1)).astype(BF)
        pulled_wide = pulled.astype(F32)
        add_vector(4, over_rows(pulled_wide))
        grad_dense = None
        for piece in range(pieces):
            cols = slice(piece * width, (piece + 1) * width)
            grad_upper = dot(pulled, down_w[cols, :], (1, 1)) * slope[:, cols]
            low = grad_upper.astype(BF)
            vector_out[0:1, cols] += over_rows(low.astype(F32))
            down_acc[piece] += dot(hidden[:, cols], pulled, (0, 0))
            up_acc[piece] += dot(dense, low, (0, 0))
            term = dot(low, up_w[:, cols], (1, 1))
            grad_dense = term if grad_dense is None else grad_dense + term
        add_vector(2, over_rows(grad_dense * unit))
        add_vector(3, over_rows(grad_dense))
        grad_middle = pulled_wide + centre_back(grad_dense * vectors[5:6, :width], unit, inverse)
        grad_out[...] = grad_middle
        branch = grad_middle.astype(BF)
        add_vector(1, over_rows(branch.astype(F32)))
        out_acc[...] += dot(across, branch, (1, 0))
        pull_out[...] = dot(out_w[...], branch, (1, 1)).astype(BF)

    @pl.when(step == pl.num_programs(0) - 1)
    def _():
        groups, unit_rows = stage.shape[1:3]
        deep = pieces * unit_rows
        some, tall = stage_down.shape[1:3]

        def grouped(value):
            return value.reshape(groups, unit_rows, value.shape[-1])

        entries = []
        for piece in range(pieces):
            if groups >= pieces:
                target = sums_out.at[pl.ds(piece * some, some), pl.ds(0, tall), :]
            else:
                target = sums_out.at[:, pl.ds(piece * tall, tall), :]
            entries.append(
                (lambda piece=piece: down_acc[piece].reshape(some, tall, width), stage_down, down_sem, target)
            )
            target = sums_out.at[:, pl.ds(deep + piece * unit_rows, unit_rows), :]
            entries.append((lambda piece=piece: grouped(up_acc[piece]), stage, sem, target))
        begin = 2 * deep
        entries.append((lambda: grouped(out_acc[...]), stage, sem, sums_out.at[:, pl.ds(begin, unit_rows), :]))
        begin += unit_rows
        entries.append(
            (lambda: grouped(align_acc[:, :width]), stage, sem, sums_out.at[:, pl.ds(begin, unit_rows), :])
        )
        begin += unit_rows
        extra = teach - width
        third = unit_rows * extra // width
        for part in range(width // extra):
            entries.append(
                (
                    lambda part=part: grouped(align_acc[:, width:])[:, part * third : (part + 1) * third],
                    stage,
                    sem,
                    sums_out.at[:, pl.ds(begin, third), pl.ds(part * extra, extra)],
                )
            )
        write_out(entries)


def entry_kernel(tile, border, last, tile_len, source, count, index, *refs):
    (
        query_t, key_t, value_t, start_in, grad_in, weight_any, vectors,
        long_out, short_out, guest_out, vector_out, sums_out,
        weight_acc, position_acc, moved, stage, stage_rows, weight, weight_sem, rows_sem, show, show_sem, sem,
    ) = refs
    step = pl.program_id(0)
    width = weight.shape[0]
    live = step < count[last]

    @pl.when(step == 0)
    def _():
        load = pltpu.make_async_copy(weight_any, weight, weight_sem.at[0])
        load.start()
        weight_acc[...] = jnp.zeros_like(weight_acc)
        vector_out[...] = jnp.zeros_like(vector_out)

        def clear(number, carry):
            position_acc[pl.ds(pl.multiple_of(number * 64, 64), 64), :] = jnp.zeros((64, width), F32)
            return carry

        lax.fori_loop(0, position_acc.shape[0] // 64, clear, 0)
        left = position_acc.shape[0] % 64
        if left:
            position_acc[position_acc.shape[0] - left :, :] = jnp.zeros((left, width), F32)
        load.wait()

    def put(value):
        put_tiles(step, value, source, border, tile, show, show_sem, long_out, short_out, guest_out)

    def over_rows(value):
        return jnp.sum(value, axis=0, keepdims=True)

    @pl.when(jnp.logical_not(live))
    def _():
        put(jnp.zeros((BLOCK, width), BF))

    @pl.when(live)
    def _():
        unit, inverse = centre(start_in[...])
        normed = (unit * vectors[0:1, :width] + vectors[1:2, :width]).astype(BF)
        grad_normed = None
        for part in range(3):
            cols = slice(part * width, (part + 1) * width)
            across = (query_t, key_t, value_t)[part][...]
            if part != 1:
                vector_out[part : part + 1, :] += over_rows(across.T.astype(F32))
            weight_acc[:, cols] += dot(normed, across, (0, 1))
            term = dot(across, weight[:, cols], (0, 1))
            grad_normed = term if grad_normed is None else grad_normed + term
        vector_out[1:2, :] += over_rows(grad_normed * unit)
        vector_out[3:4, :] += over_rows(grad_normed)
        grad_start = grad_in[...] + centre_back(grad_normed * vectors[0:1, :width], unit, inverse)
        put(grad_start.astype(BF))
        moved[...] = grad_start
        parts = BLOCK // tile

        def spread(number, carry):
            first = number * tile
            origin = source[step * parts + number] * tile

            def some(group, inner):
                base = pl.multiple_of(first + group * 8, 8)
                for row in range(8):
                    place = index[origin + group * 8 + row]
                    position_acc[pl.ds(place, 1), :] += moved[pl.ds(base + row, 1), :]
                return inner

            lax.fori_loop(0, lax.div(tile_len[step * parts + number] + 7, 8), some, 0)
            return carry

        lax.fori_loop(0, parts, spread, 0)

    @pl.when(step == pl.num_programs(0) - 1)
    def _():
        groups, unit_rows = stage.shape[1:3]
        depth, chunk = stage_rows.shape[:2]
        patches = position_acc.shape[0] - 8
        taken = patches // groups if groups > 1 else chunk
        begin = sums_out.shape[1] - 3 * unit_rows
        entries = []
        for part in range(3):
            cols = slice(part * width, (part + 1) * width)
            entries.append(
                (
                    lambda cols=cols: weight_acc[:, cols].reshape(groups, unit_rows, width),
                    stage,
                    sem,
                    sums_out.at[:, pl.ds(begin + part * unit_rows, unit_rows), :],
                )
            )
        write_out(entries)

        def copy(number):
            if groups > 1:
                target = sums_out.at[number, pl.ds(0, chunk), :]
            else:
                target = sums_out.at[0, pl.ds(pl.multiple_of(number * chunk, 16), chunk), :]
            slot = lax.rem(number, depth)
            return pltpu.make_async_copy(stage_rows.at[slot], target, rows_sem.at[slot])

        def drain(number, carry):
            @pl.when(number >= depth)
            def _():
                copy(number - depth).wait()

            stage_rows[lax.rem(number, depth)] = position_acc[
                pl.ds(pl.multiple_of(number * taken, 8), chunk), :
            ].astype(BF)
            copy(number).start()
            return carry

        chunks = patches // taken
        lax.fori_loop(0, chunks, drain, 0)
        for late in range(depth):
            copy(chunks - depth + late).wait()


def send_kernel(home, copies, short_len, destination, shown, out):
    base = (lax.axis_index("dp") * copies + lax.axis_index("rep")) * home
    out[...] = jnp.zeros_like(out)
    for slot in range(shown.shape[0]):
        micro, place = slot // home, base + slot % home

        @pl.when(short_len[micro, place] > 0)
        def _():
            out[destination[micro, place], micro] = shown[slot]


def finish_kernel(
    home, copies, flag, short_len, destination, count, got, early, late, vector, out_in, out_back, grad_in, grad_back,
    balanced, position_g, heads_g, out_g, up_g, down_g, align_g, *rest,
):
    *vector_outs, long_out, long_grad, carry, carry_sem, sem = rest
    tail = out_back.shape[0]
    swapped = count[flag] > 0
    backs = [
        pltpu.make_async_copy(ref, carry.at[number], carry_sem.at[number])
        for number, ref in enumerate((out_back, grad_back))
    ]
    homes = [
        pltpu.make_async_copy(
            carry.at[number], ref.at[pl.ds(ref.shape[0] - tail, tail), :], carry_sem.at[number]
        )
        for number, ref in enumerate((long_out, long_grad))
    ]

    @pl.when(swapped)
    def _():
        for copy in backs:
            copy.start()

    peers = got.shape[0]
    micros, bal = balanced.shape[:2]
    width = position_g.shape[1]
    unit_rows = out_g.shape[0]
    pieces = up_g.shape[1] // width
    d = lax.axis_index("dp")
    r = lax.axis_index("rep")
    number = 0
    found_all = []
    for micro in range(micros):
        for slot in range(bal):
            def look(peer, found):
                base = (peer * copies + r) * home
                for place in range(slot, home, bal):
                    fits = (short_len[micro, base + place] > 0) & (destination[micro, base + place] == d)
                    found = jnp.where(fits, peer, found)
                return found

            found = lax.fori_loop(0, peers, look, jnp.int32(-1))
            found_all.append(found)

            @pl.when(found >= 0)
            def _():
                pltpu.make_async_copy(
                    got.at[jnp.maximum(found, 0), micro], balanced.at[micro, slot], sem.at[number]
                ).start()

            @pl.when(found < 0)
            def _():
                balanced[micro, slot] = jnp.zeros(balanced.shape[2:], BF)

            number += 1
    position_g[...] = late[: position_g.shape[0], :].astype(F32)
    first = late.shape[0] - 3 * unit_rows
    for part in range(3):
        heads_g[:, part * width : (part + 1) * width] = late[
            first + part * unit_rows : first + (part + 1) * unit_rows, :
        ].astype(F32)
    deep = pieces * unit_rows
    down_g[...] = early[:deep, :].astype(F32)
    for part in range(pieces):
        up_g[:, part * width : (part + 1) * width] = early[
            deep + part * unit_rows : deep + (part + 1) * unit_rows, :
        ].astype(F32)
    out_g[...] = early[2 * deep : 2 * deep + unit_rows, :].astype(F32)
    align_g[:, :width] = early[2 * deep + unit_rows : 2 * deep + 2 * unit_rows, :].astype(F32)
    extra = align_g.shape[1] - width
    third = unit_rows * extra // width
    begin = 2 * deep + 2 * unit_rows
    for part in range(width // extra):
        align_g[part * third : (part + 1) * third, width:] = early[
            begin : begin + third, part * extra : (part + 1) * extra
        ].astype(F32)

    places = [(1, 0), (2, 0), (3, 0), (4, 0), (0, 1), (1, 1), (2, 1), (3, 1), (0, 0), (5, 0)]
    for target, (row, late_part) in zip(vector_outs, places):
        size = target.shape[1]
        first = d * size
        window = size if size % 128 == 0 else -(-size // 128) * 128 + 128
        begin = late_part * pieces * width
        origin = jnp.minimum(lax.div(first, 128) * 128, vector.shape[1] - begin - window)
        value = vector[:, pl.ds(pl.multiple_of(begin + origin, 128), window)]
        at = lax.broadcasted_iota(jnp.int32, (window, size), 0)
        want = lax.broadcasted_iota(jnp.int32, (window, size), 1) + (first - origin)
        chosen = jnp.where(at == want, 1.0, 0.0)
        picked = jnp.dot(value, chosen, preferred_element_type=F32, precision=lax.Precision.HIGHEST)
        target[...] = picked[row : row + 1]

    @pl.when(swapped)
    def _():
        for back, copy in zip(backs, homes):
            back.wait()
            copy.start()
        for copy in homes:
            copy.wait()

    for number, found in enumerate(found_all):
        @pl.when(found >= 0)
        def _():
            pltpu.make_async_copy(
                got.at[0, number // bal], balanced.at[number // bal, number % bal], sem.at[number]
            ).wait()


SMALL_NAMES = (
    "mixer_gain", "mixer_shift", "query_bias", "value_bias", "out_bias", "dense_gain", "dense_shift",
    "down_bias", "up_bias", "align_bias",
)


def whole(shape):
    return pl.BlockSpec(shape, lambda *_: (0,) * len(shape), pipeline_mode=pl.Buffered(1))


def params(**more):
    return pltpu.CompilerParams(vmem_limit_bytes=VMEM_LIMIT, **more)


def run_block(
    row_sources, index, target_sources, tile_len, source, count, lengths,
    tile, long_rows, micros, weights, groups, vectors, up_b, align_b,
):
    w = weights
    width = row_sources[0].shape[1]
    total = row_sources[0].shape[0] + row_sources[1].shape[0]
    wide = w["up_weight"].shape[1]
    teach = target_sources[0].shape[1]
    patches = w["position"].shape[0]
    blocks = total // BLOCK
    parts = BLOCK // tile
    border = (micros * long_rows // tile, total // tile)
    last = 2 * micros + 2
    pairs = HEADS // 2
    pair = width // pairs
    unit_rows = width // groups
    pieces = wide // width
    early_rows = (2 * pieces + 2) * unit_rows + unit_rows * (teach - width) // width
    early_rows = -(-early_rows // 512) * 512
    chunk = -(-(patches // groups) // 16) * 16 if groups > 1 else patches // 14
    late_rows = (chunk if groups > 1 else patches) + 3 * unit_rows
    def kept(i, count):
        return jnp.minimum(i, count[last] - 1)

    def tiles(sources):
        specs = []
        for first, held in zip((0,) + border, sources):
            most = held.shape[0] // tile - 1
            for part in range(parts):
                specs.append(
                    pl.BlockSpec(
                        (tile, held.shape[1]),
                        lambda i, tl, src, cnt, *_, part=part, first=first, most=most: (
                            jnp.clip(src[kept(i, cnt) * parts + part] - first, 0, most),
                            0,
                        ),
                    )
                )
        return specs, [held for held in sources for _ in range(parts)]

    row_specs, row_args = tiles(row_sources)
    target_specs, target_args = tiles(target_sources)

    by_block = lambda last_dim: pl.BlockSpec((BLOCK, last_dim), lambda i, tl, src, cnt, *_: (kept(i, cnt), 0))
    by_column = lambda first: pl.BlockSpec((first, BLOCK), lambda i, tl, src, cnt, *_: (0, kept(i, cnt)))
    guarded = lambda first: pl.BlockSpec(
        (first, BLOCK), lambda i, tl, src, cnt, *_: (0, jnp.minimum(i, cnt[last]))
    )
    anywhere = pl.BlockSpec(memory_space=pl.ANY)
    show = [
        pltpu.VMEM((2, BLOCK, width), BF),
        pltpu.SemaphoreType.DMA((2, parts)),
        pltpu.SemaphoreType.DMA((2,)),
    ]
    shown_shapes = [jax.ShapeDtypeStruct(held.shape, BF) for held in row_sources]

    triple_t, start = pl.pallas_call(
        partial(project_kernel, tile, border, last),
        grid_spec=pltpu.PrefetchScalarGridSpec(
            num_scalar_prefetch=4,
            grid=(blocks,),
            in_specs=row_specs + [anywhere, anywhere, whole(vectors.shape)],
            out_specs=[guarded(3 * width), by_block(width)],
            scratch_shapes=[
                pltpu.VMEM((patches, width), F32),
                pltpu.VMEM((4, patches // 14, width), BF),
                pltpu.VMEM((BLOCK, width), F32),
                pltpu.VMEM((width, 3 * width), BF),
                pltpu.SemaphoreType.DMA((1,)),
                pltpu.SemaphoreType.DMA((4,)),
            ],
        ),
        out_shape=[
            jax.ShapeDtypeStruct((3 * width, total), BF),
            jax.ShapeDtypeStruct((total, width), F32),
        ],
        compiler_params=params(),
        name="project",
    )(
        tile_len, source, count, index, *row_args,
        w["position"], w["heads_weight"], vectors,
    )

    def heads_spec(offset):
        return pl.BlockSpec((pair, total), lambda i, *_: (i + offset * pairs, 0))

    board = pltpu.VMEM((long_rows, BLOCK), F32)
    sums_spec = pl.BlockSpec((1, 2, total), lambda i, *_: (i, 0, 0))
    attended_t, sums = pl.pallas_call(
        partial(attend_kernel, tile, long_rows, micros),
        grid_spec=pltpu.PrefetchScalarGridSpec(
            num_scalar_prefetch=3,
            grid=(pairs,),
            in_specs=[heads_spec(0), heads_spec(1), heads_spec(2)],
            out_specs=[heads_spec(0), sums_spec],
            scratch_shapes=[board] * 2,
        ),
        out_shape=[
            jax.ShapeDtypeStruct((width, total), BF),
            jax.ShapeDtypeStruct((pairs, 2, total), F32),
        ],
        compiler_params=params(),
        name="attend",
    )(tile_len, lengths, count, triple_t, triple_t, triple_t)

    some = max(groups // pieces, 1)
    long_out, short_out, guest_out, pulled_t, grad_middle, vector, early = pl.pallas_call(
        partial(middle_kernel, tile, border, last),
        grid_spec=pltpu.PrefetchScalarGridSpec(
            num_scalar_prefetch=3,
            grid=(blocks,),
            in_specs=[by_column(width), by_block(width)]
            + target_specs
            + [
                anywhere, anywhere, anywhere, anywhere,
                whole(vectors.shape), whole(up_b.shape), whole(align_b.shape),
            ],
            out_specs=[
                anywhere, anywhere, anywhere, guarded(width), by_block(width), whole((8, wide)), anywhere,
            ],
            scratch_shapes=[
                pltpu.VMEM((width, width), F32),
                pltpu.VMEM((pieces, width, width), F32),
                pltpu.VMEM((pieces, width, width), F32),
                pltpu.VMEM((width, teach), F32),
                pltpu.VMEM((BLOCK, wide), BF),
                pltpu.VMEM((BLOCK, wide), F32),
                pltpu.VMEM((2, groups, unit_rows, width), BF),
                pltpu.VMEM((2, some, width // some, width), BF),
                pltpu.VMEM((width, width), BF),
                pltpu.VMEM((width, wide), BF),
                pltpu.VMEM((wide, width), BF),
                pltpu.VMEM((width, teach), BF),
                pltpu.SemaphoreType.DMA((4,)),
                pltpu.SemaphoreType.DMA((2,)),
            ]
            + show,
        ),
        out_shape=shown_shapes
        + [
            jax.ShapeDtypeStruct((width, total), BF),
            jax.ShapeDtypeStruct((total, width), F32),
            jax.ShapeDtypeStruct((8, wide), F32),
            jax.ShapeDtypeStruct((groups, early_rows, width), BF),
        ],
        compiler_params=params(),
        name="middle",
    )(
        tile_len, source, count, attended_t, start, *target_args,
        w["out_weight"], w["up_weight"], w["down_weight"], w["align_weight"], vectors, up_b, align_b,
    )

    grads = pl.pallas_call(
        partial(attend_back_kernel, tile, long_rows, micros),
        grid_spec=pltpu.PrefetchScalarGridSpec(
            num_scalar_prefetch=3,
            grid=(pairs,),
            in_specs=[heads_spec(0), heads_spec(1), heads_spec(2), heads_spec(0), sums_spec],
            out_specs=[heads_spec(0)] * 3,
            scratch_shapes=[pltpu.VMEM((pair, long_rows), F32)] * 2 + [board] * 4,
        ),
        out_shape=[jax.ShapeDtypeStruct((width, total), BF)] * 3,
        compiler_params=params(),
        name="attend_back",
    )(tile_len, lengths, count, triple_t, triple_t, triple_t, pulled_t, sums)

    long_grad, short_grad, guest_grad, entry_vector, late = pl.pallas_call(
        partial(entry_kernel, tile, border, last),
        grid_spec=pltpu.PrefetchScalarGridSpec(
            num_scalar_prefetch=4,
            grid=(blocks,),
            in_specs=[by_column(width)] * 3
            + [by_block(width), by_block(width), anywhere, whole(vectors.shape)],
            out_specs=[anywhere, anywhere, anywhere, whole((8, width)), anywhere],
            scratch_shapes=[
                pltpu.VMEM((width, 3 * width), F32),
                pltpu.VMEM((patches + 8, width), F32),
                pltpu.VMEM((BLOCK, width), F32),
                pltpu.VMEM((2, groups, unit_rows, width), BF),
                pltpu.VMEM((4, chunk, width), BF),
                pltpu.VMEM((width, 3 * width), BF),
                pltpu.SemaphoreType.DMA((1,)),
                pltpu.SemaphoreType.DMA((4,)),
            ]
            + show,
        ),
        out_shape=shown_shapes
        + [
            jax.ShapeDtypeStruct((8, width), F32),
            jax.ShapeDtypeStruct((groups, late_rows, width), BF),
        ],
        compiler_params=params(),
        name="entry",
    )(tile_len, source, count, index, *grads, start, grad_middle, w["heads_weight"], vectors)
    outs = (long_out, short_out, long_grad, short_grad)
    return outs, (guest_out, guest_grad), early, late, vector, entry_vector


def bit_of(number, bit):
    return lax.rem(number // (1 << bit), 2)


def reduce_plan(peers, early_rows, late_rows):
    bits = peers.bit_length() - 1
    forward = list(range(bits))
    swapped = forward[1::-1] + forward[2:]
    last = forward[2:] + forward[:2]
    pieces = []
    for source, rows in ((0, early_rows), (1, late_rows)):
        unit = 16
        units = rows // 2 // unit
        begin = 0
        for sub in range(2):
            here = units // 2 + (1 if sub < units % 2 else 0)
            first = int(here * 0.4 + 0.5)
            for order, parts in zip((forward, swapped, last), (first, first, here - 2 * first)):
                if parts > 0:
                    pieces.append((source * 2 + sub, source, begin, parts * unit, tuple(order)))
                    begin += parts * unit
    return pieces


def reduce_kernel(
    peers, halves, pieces, early, late, vector, entry_vector, early_out, late_out, vector_out, *scratch
):
    bits = peers.bit_length() - 1
    amount = len(pieces)
    kept = scratch[:amount]
    mates = scratch[amount : 2 * amount]
    mine_in = scratch[2 * amount : 3 * amount]
    landed = [scratch[3 * amount + k * bits : 3 * amount + (k + 1) * bits] for k in range(amount)]
    (
        vector_land, mate_send, mate_recv, load_sem, hop_send, hop_recv, end_send, end_recv, end_load,
        vector_send, vector_recv,
    ) = scratch[3 * amount + amount * bits :]
    d = lax.axis_index("dp")
    r = lax.axis_index("rep")
    other = 1 - r
    mate = (d, other)
    partner = [(d + (1 - 2 * bit_of(d, bit)) * (1 << bit), r) for bit in range(bits)]
    sources = (early, late)
    outs = (early_out, late_out)
    barrier = pltpu.get_barrier_semaphore()
    for device in [mate] + partner:
        pl.semaphore_signal(barrier, inc=1, device_id=device, device_id_type=pl.DeviceIdType.MESH)
    pl.semaphore_wait(barrier, bits + 1)

    def remote(source, target, send, recv, device):
        copy = pltpu.make_async_remote_copy(
            src_ref=source, dst_ref=target, send_sem=send, recv_sem=recv,
            device_id=device, device_id_type=pl.DeviceIdType.MESH,
        )
        copy.start()
        return copy

    def rows_at(source, core, begin, rows):
        return pl.ds(pl.multiple_of(core * halves[source] + begin, 16), rows)

    wide = vector.shape[1]
    vector_out[:, :wide] = vector[...]
    vector_out[:, wide:] = entry_vector[...]
    mate_copies = []
    loads = []
    for k, (_, source, begin, rows, order) in enumerate(pieces):
        mate_copies.append(
            remote(
                sources[source].at[:, rows_at(source, other, begin, rows), :], mates[k],
                mate_send.at[k], mate_recv.at[k], mate,
            )
        )
        load = pltpu.make_async_copy(
            sources[source].at[:, rows_at(source, r, begin, rows), :], mine_in[k], load_sem.at[k]
        )
        load.start()
        loads.append(load)

    hops = {}
    ends = []

    def base_at(order, stage):
        base = 0
        for place in range(stage):
            base = base + bit_of(d, order[place]) * (1 << (bits - 1 - place))
        return base

    def send(k, stage):
        _, source, begin, rows, order = pieces[k]
        if stage == bits:
            result = kept[k].at[base_at(order, bits)]
            where = rows_at(source, r, begin, rows)
            ends.append(remote(result, outs[source].at[where, :], end_send.at[k], end_recv.at[k], mate))
            own = pltpu.make_async_copy(result, outs[source].at[where, :], end_load.at[k])
            own.start()
            ends.append(own)
            return
        size = 1 << (bits - 1 - stage)
        first = base_at(order, stage) + (1 - bit_of(d, order[stage])) * size
        hops[k, stage] = remote(
            kept[k].at[pl.ds(first, size)], landed[k][stage], hop_send.at[k, stage], hop_recv.at[k, stage],
            partner[order[stage]],
        )

    def join(k):
        order = pieces[k][4]
        loads[k].wait()
        mate_copies[k].wait_recv()

        def add(chunk, carry):
            place = 0
            for step in range(bits):
                place = place + bit_of(chunk, order[step]) * (1 << (bits - 1 - step))
            kept[k][place] = mine_in[k][chunk] + mates[k][chunk]
            return carry

        lax.fori_loop(0, peers, add, 0)

    def gather(k, stage):
        order = pieces[k][4]
        hops[k, stage].wait_recv()
        base = base_at(order, stage + 1)

        def add(chunk, carry):
            kept[k][base + chunk] = kept[k][base + chunk] + landed[k][stage][chunk]
            return carry

        lax.fori_loop(0, 1 << (bits - 1 - stage), add, 0)

    events = sorted(
        (stage + pieces[k][0], -stage, k) for k in range(amount) for stage in range(bits + 1)
    )
    vector_copies = []

    def vector_step(stage):
        if stage > 0:
            vector_copies[-1].wait()
            vector_out[...] = vector_out[...] + vector_land[stage - 1]
        if stage <= bits:
            device = mate if stage == 0 else partner[stage - 1]
            vector_copies.append(
                remote(vector_out, vector_land.at[stage], vector_send.at[stage], vector_recv.at[stage], device)
            )

    seen = -1
    for time, negative, k in events:
        if time != seen:
            if time <= bits + 1:
                vector_step(time)
            seen = time
        stage = -negative
        if stage == 0:
            join(k)
        else:
            gather(k, stage - 1)
        send(k, stage)
    for copy in mate_copies + list(hops.values()):
        copy.wait_send()
    for copy in ends:
        copy.wait()


def reduce_all(early, late, vector, entry_vector):
    joined = (vector.shape[0], vector.shape[1] + entry_vector.shape[1])
    peers, early_rows, width = early.shape
    late_rows = late.shape[1]
    bits = peers.bit_length() - 1
    pieces = reduce_plan(peers, early_rows, late_rows)
    amount = len(pieces)
    scratch = [pltpu.VMEM((peers, rows, width), BF) for _, _, _, rows, _ in pieces] * 3
    for _, _, _, rows, _ in pieces:
        for stage in range(bits):
            scratch.append(pltpu.VMEM((1 << (bits - 1 - stage), rows, width), BF))
    scratch.append(pltpu.VMEM((bits + 1,) + joined, F32))
    one = pltpu.SemaphoreType.DMA((amount,))
    many = pltpu.SemaphoreType.DMA((amount, bits))
    few = pltpu.SemaphoreType.DMA((bits + 1,))
    scratch += [one, one, one, many, many, one, one, one, few, few]
    anywhere = pl.BlockSpec(memory_space=pl.ANY)
    near = pl.BlockSpec(memory_space=pltpu.VMEM)
    return pl.pallas_call(
        partial(reduce_kernel, peers, (early_rows // 2, late_rows // 2), pieces),
        in_specs=[anywhere, anywhere, near, near],
        out_specs=[anywhere, anywhere, near],
        out_shape=[
            jax.ShapeDtypeStruct((early_rows, width), BF),
            jax.ShapeDtypeStruct((late_rows, width), BF),
            jax.ShapeDtypeStruct(joined, F32),
        ],
        scratch_shapes=scratch,
        compiler_params=pltpu.CompilerParams(
            vmem_limit_bytes=VMEM_LIMIT, collective_id=0, has_side_effects=True
        ),
        name="reduce",
    )(early, late, vector, entry_vector)


def unpack(early, late, unit_rows, kept, teach, pieces):
    width = early.shape[1]
    deep = pieces * unit_rows

    def beside(held, first, count):
        return jnp.concatenate(
            [held[first + k * unit_rows : first + (k + 1) * unit_rows] for k in range(count)], axis=1
        )

    extra = teach - width
    third = unit_rows * extra // width
    begin = 2 * deep + 2 * unit_rows
    tail = early[begin : begin + third]
    tail = jnp.concatenate([tail[:, k * extra : (k + 1) * extra] for k in range(width // extra)], axis=0)
    return {
        "down_weight": early[:deep],
        "up_weight": beside(early, deep, pieces),
        "out_weight": early[2 * deep : 2 * deep + unit_rows],
        "align_weight": jnp.concatenate([early[2 * deep + unit_rows : begin], tail], axis=1),
        "position": late[:kept],
        "heads_weight": beside(late, late.shape[0] - 3 * unit_rows, 3),
    }


def shards(
    long_clips,
    short_clips,
    long_index,
    short_index,
    long_length,
    short_length,
    destination,
    long_target,
    short_target,
    position,
    mixer_gain,
    mixer_shift,
    heads_weight,
    query_bias,
    value_bias,
    out_weight,
    out_bias,
    dense_gain,
    dense_shift,
    up_weight,
    up_bias,
    down_weight,
    down_bias,
    align_weight,
    align_bias,
):
    peers = lax.axis_size("dp")
    copies = lax.axis_size("rep")
    micros, _, long_rows, width = long_clips.shape
    home_slots, tile = short_clips.shape[1:3]
    bal_slots = home_slots // 2
    slots = micros * home_slots
    wide = up_weight.shape[1]
    teach = long_target.shape[-1]
    patches = position.shape[0]
    weights = dict(
        zip(
            WEIGHT_NAMES,
            (
                position, mixer_gain, mixer_shift, heads_weight, query_bias, value_bias, out_weight, out_bias,
                dense_gain, dense_shift, up_weight, up_bias, down_weight, down_bias, align_weight, align_bias,
            ),
        )
    )
    scalars = pl.BlockSpec(memory_space=pltpu.SMEM)
    anywhere = pl.BlockSpec(memory_space=pl.ANY)
    tile_total = micros * long_rows // tile + slots
    near = pl.BlockSpec(memory_space=pltpu.VMEM)
    pairs = [(core, (core + 1) % copies) for core in range(copies)]

    def trade(value):
        return lax.ppermute(value, "rep", pairs)

    lengths = long_length.reshape(-1)
    facts = trade(jnp.concatenate([long_index[-1].reshape(-1), lengths]))
    guest_rows = trade(long_clips[-1, 0])
    guest_target = trade(long_target[-1, 0])
    tile_len, source, count, work, vectors, up_b, align_b = pl.pallas_call(
        partial(plan_kernel, tile, long_rows, home_slots, copies),
        in_specs=[scalars] * 3 + [near] * len(SMALL_NAMES),
        out_specs=[scalars] * 4 + [near] * 3,
        out_shape=[
            jax.ShapeDtypeStruct((tile_total,), jnp.int32),
            jax.ShapeDtypeStruct((tile_total,), jnp.int32),
            jax.ShapeDtypeStruct((2 * micros + 4,), jnp.int32),
            jax.ShapeDtypeStruct((micros,), jnp.int32),
            jax.ShapeDtypeStruct((len(SMALL_NAMES) - 2, width), F32),
            jax.ShapeDtypeStruct((1, wide), F32),
            jax.ShapeDtypeStruct((1, teach), F32),
        ],
        name="plan",
    )(long_length, facts[long_rows:], short_length, *[weights[name] for name in SMALL_NAMES])
    index = jnp.concatenate([long_index.reshape(-1), short_index.reshape(-1), facts[:long_rows]])
    groups = peers if copies == 2 and width % (16 * peers) == 0 else 1
    outs, guests, early, late, vector, entry_vector = run_block(
        (long_clips.reshape(-1, width), short_clips.reshape(-1, width), guest_rows), index,
        (long_target.reshape(-1, teach), short_target.reshape(-1, teach), guest_target),
        tile_len, source, count, work, tile, long_rows, micros, weights, groups, vectors, up_b, align_b,
    )
    long_out, short_out, long_grad, short_grad = outs
    out_back, grad_back = [trade(value) for value in guests]
    send = pl.pallas_call(
        partial(send_kernel, home_slots, copies),
        in_specs=[scalars, scalars, whole((slots, tile, width))],
        out_specs=pl.BlockSpec(memory_space=pltpu.VMEM) if groups == peers else scalars,
        out_shape=jax.ShapeDtypeStruct((peers, micros, tile, width), BF),
        compiler_params=params(),
        name="send",
    )(short_length, destination, short_out.reshape(slots, tile, width)) if groups == peers else send_all(
        short_length, destination, short_out.reshape(slots, tile, width), peers, copies, home_slots
    )
    got = lax.all_to_all(send, "dp", split_axis=0, concat_axis=0, tiled=True)
    unit_rows = width // peers
    if groups == peers:
        early, late, vector = reduce_all(early, late, vector, entry_vector)
    else:
        matrices = unpack(early[0], late[0], width, patches, teach, wide // width)
        early, late = share_out(matrices, peers, copies, unit_rows, wide // width)
        vector = lax.psum(jnp.concatenate([vector, entry_vector], axis=1), ("dp", "rep"))
    near = pl.BlockSpec(memory_space=pltpu.VMEM)
    outs = pl.pallas_call(
        partial(finish_kernel, home_slots, copies, 2 * micros + 3),
        in_specs=[scalars, scalars, scalars, anywhere, near, near, near] + [anywhere] * 4,
        out_specs=[near] * 17 + [anywhere] * 2,
        input_output_aliases={7: 17, 9: 18},
        out_shape=[
            jax.ShapeDtypeStruct((micros, bal_slots, tile, width), BF),
            jax.ShapeDtypeStruct((patches // peers, width), F32),
            jax.ShapeDtypeStruct((unit_rows, 3 * width), F32),
            jax.ShapeDtypeStruct((unit_rows, width), F32),
            jax.ShapeDtypeStruct((unit_rows, wide), F32),
            jax.ShapeDtypeStruct((wide // peers, width), F32),
            jax.ShapeDtypeStruct((unit_rows, teach), F32),
        ]
        + [jax.ShapeDtypeStruct((1, unit_rows), F32)] * 8
        + [jax.ShapeDtypeStruct((1, wide // peers), F32), jax.ShapeDtypeStruct((1, teach // peers), F32)]
        + [jax.ShapeDtypeStruct(long_out.shape, BF)] * 2,
        scratch_shapes=[
            pltpu.VMEM((2, long_rows, width), BF),
            pltpu.SemaphoreType.DMA((2,)),
            pltpu.SemaphoreType.DMA((micros * bal_slots,)),
        ],
        compiler_params=params(),
        name="finish",
    )(short_length, destination, count, got, early, late, vector, long_out, out_back, long_grad, grad_back)
    short_bal, position_g, heads_g, out_g, up_g, down_g, align_g = outs[:7]
    shared = {
        "position": position_g, "heads_weight": heads_g, "out_weight": out_g, "up_weight": up_g,
        "down_weight": down_g, "align_weight": align_g,
    }
    long_out, long_grad = outs[17:]
    order = (
        "out_bias", "dense_gain", "dense_shift", "down_bias", "query_bias", "mixer_gain", "value_bias",
        "mixer_shift", "up_bias", "align_bias",
    )
    for name, value in zip(order, outs[7:17]):
        shared[name] = value.reshape(-1)
    return (
        long_out.reshape(micros, 1, long_rows, width),
        short_bal,
        long_grad.reshape(micros, 1, long_rows, width),
        short_grad.reshape(micros, home_slots, tile, width),
    ) + tuple(shared[name] for name in WEIGHT_NAMES)


def send_all(short_length, destination, shown, peers, copies, home):
    micros = short_length.shape[0]
    mine = lax.axis_index("dp") * copies + lax.axis_index("rep")

    def own(table):
        table = table.reshape(micros, peers * copies, home)
        return lax.dynamic_index_in_dim(table, mine, 1, keepdims=False)

    wanted = (own(destination)[None] == jnp.arange(peers)[:, None, None]) & (own(short_length)[None] > 0)
    shown = shown.reshape((micros, home) + shown.shape[1:])
    return jnp.einsum("pmj,mjtd->pmtd", wanted.astype(BF), shown)


def share_out(matrices, peers, copies, unit_rows, pieces):
    shared = {}
    for name, piece in matrices.items():
        rows = piece.shape[0] // peers
        padded = -(-rows // (8 * copies)) * 8 * copies
        if padded != rows:
            piece = piece.reshape(peers, rows, -1)
            piece = jnp.pad(piece, ((0, 0), (0, padded - rows), (0, 0)))
            piece = piece.reshape(peers * padded, -1)
        piece = lax.psum_scatter(piece, ("dp", "rep"), scatter_dimension=0, tiled=True)
        shared[name] = lax.all_gather(piece, "rep", axis=0, tiled=True)[:rows]
    width = shared["out_weight"].shape[1]
    up = shared["up_weight"].reshape(unit_rows, pieces, width).transpose(1, 0, 2).reshape(-1, width)
    heads = shared["heads_weight"].reshape(unit_rows, 3, width).transpose(1, 0, 2).reshape(-1, width)
    align = shared["align_weight"]
    extra = align.shape[1] - width
    parts = width // extra
    tail = align[:, width:].reshape(parts, unit_rows // parts, extra).transpose(1, 0, 2).reshape(-1, width)
    early = jnp.concatenate([shared["down_weight"], up, shared["out_weight"], align[:, :width], tail], axis=0)
    return early, jnp.concatenate([shared["position"], heads], axis=0)


def solution(mesh):
    placed = (
        P(None, ("dp", "rep"), None, None),
        P(None, ("dp", "rep"), None, None),
        P(None, ("dp", "rep"), None),
        P(None, ("dp", "rep"), None),
        P(None, ("dp", "rep")),
        P(),
        P(),
        P(None, ("dp", "rep"), None, None),
        P(None, ("dp", "rep"), None, None),
        P(),
        P(),
        P(),
        P(),
        P(),
        P(),
        P(),
        P(),
        P(),
        P(),
        P(),
        P(),
        P(),
        P(),
        P(),
        P(),
    )
    return jax.shard_map(
        shards,
        mesh=mesh,
        in_specs=placed,
        out_specs=(
            P(None, ("dp", "rep"), None, None),
            P(None, ("dp", "rep"), None, None),
            P(None, ("dp", "rep"), None, None),
            P(None, ("dp", "rep"), None, None),
            P("dp", None),
            P("dp"),
            P("dp"),
            P("dp", None),
            P("dp"),
            P("dp"),
            P("dp", None),
            P("dp"),
            P("dp"),
            P("dp"),
            P("dp", None),
            P("dp"),
            P("dp", None),
            P("dp"),
            P("dp", None),
            P("dp"),
        ),
        check_vma=False,
    )
```

```python
from functools import partial

import jax
import jax.numpy as jnp
from jax import lax
from jax.experimental import pallas as pl
from jax.experimental.pallas import tpu as pltpu
from jax.sharding import PartitionSpec as P

HEADS = 12
EPS = 1e-06
MASKED = -1000000000.0
WEIGHT_NAMES = (
    "position",
    "mixer_gain",
    "mixer_shift",
    "heads_weight",
    "query_bias",
    "value_bias",
    "out_weight",
    "out_bias",
    "dense_gain",
    "dense_shift",
    "up_weight",
    "up_bias",
    "down_weight",
    "down_bias",
    "align_weight",
    "align_bias",
)


BLOCK = 256
BF = jnp.bfloat16
F32 = jnp.float32
VMEM_LIMIT = 66_000_000


def dot(left, right, dims):
    return lax.dot_general(left, right, ((dims[:1], dims[1:]), ((), ())), preferred_element_type=F32)


def centre(values):
    mean = jnp.mean(values, axis=-1, keepdims=True)
    centered = values - mean
    spread = jnp.mean(centered * centered, axis=-1, keepdims=True)
    inverse = lax.rsqrt(spread + EPS)
    return centered * inverse, inverse


def centre_back(grad, unit, inverse):
    first = jnp.mean(grad, axis=-1, keepdims=True)
    second = jnp.mean(grad * unit, axis=-1, keepdims=True)
    return inverse * (grad - first - unit * second)


def valid_rows(tile_len, block, tile):
    row = lax.broadcasted_iota(jnp.int32, (BLOCK, 1), 0)
    parts = BLOCK // tile
    limit = tile_len[block * parts]
    for part in range(1, parts):
        limit = jnp.where(row >= part * tile, tile_len[block * parts + part], limit)
    return lax.rem(row, tile) < limit


def clip_cost(length):
    blocks = lax.div(length + BLOCK - 1, BLOCK)
    return 2 * lax.div(length + 127, 128) + blocks * blocks


def plan_kernel(tile, long_rows, home, copies, lengths, guest, short_len, *refs):
    amount = len(refs) - 7
    small, (tile_len, source, count, work, vectors, up_out, align_out) = refs[:amount], refs[amount:]
    for number, value in enumerate(small[:-2]):
        vectors[number : number + 1, :] = value[...].reshape(1, -1)
    up_out[...] = small[-2][...].reshape(1, -1)
    align_out[...] = small[-1][...].reshape(1, -1)
    micros = lengths.shape[0]
    slots = micros * home
    per = long_rows // tile
    step = 128 // tile
    d, r = lax.axis_index("dp"), lax.axis_index("rep")
    base = (d * copies + r) * home
    other = (d * copies + lax.rem(r + 1, copies)) * home

    def put(place, origin, size):
        source[place] = origin
        tile_len[place] = size

    mine, theirs = jnp.int32(0), jnp.int32(0)
    for slot in range(slots):
        mine = mine + jnp.where(short_len[slot // home, base + slot % home] > 0, 1, 0)
        theirs = theirs + jnp.where(short_len[slot // home, other + slot % home] > 0, 1, 0)
    for micro in range(micros - 1):
        mine = mine + clip_cost(lengths[micro, 0])
        theirs = theirs + clip_cost(guest[micro])
    held, offered = clip_cost(lengths[micros - 1, 0]), clip_cost(guest[micros - 1])
    base0, base1 = jnp.where(r == 0, mine, theirs), jnp.where(r == 0, theirs, mine)
    last0, last1 = jnp.where(r == 0, held, offered), jnp.where(r == 0, offered, held)
    best = jnp.maximum(base0 + last0, base1 + last1)
    choice = jnp.int32(0)
    plans = (
        jnp.maximum(base0 + last1, base1 + last0),
        jnp.maximum(base0, base1 + last0 + last1),
        jnp.maximum(base0 + last0 + last1, base1),
    )
    for number, cost in enumerate(plans):
        better = cost + 1 < best
        choice = jnp.where(better, number + 1, choice)
        best = jnp.where(better, cost, best)
    gives = choice == jnp.where(r == 0, 2, 3)
    takes = choice == jnp.where(r == 0, 3, 2)
    swaps = choice == 1
    clips = micros + 1
    count[2 * clips + 3] = (gives | swaps).astype(jnp.int32)
    place = jnp.int32(0)
    taken = []
    origins = []
    for number in range(clips):
        if number < micros - 1:
            length, origin = lengths[number, 0], number * per
        elif number == micros - 1:
            length, origin = jnp.where(gives | swaps, 0, lengths[number, 0]), number * per
        else:
            length, origin = jnp.where(takes | swaps, guest[micros - 1], 0), micros * per + slots
        origins.append(origin)
        work[number] = length
        some = lax.div(length + 127, 128) * step
        count[number] = lax.div(length + BLOCK - 1, BLOCK)
        count[clips + 1 + number] = place

        def add(index, carry, origin=origin, length=length, place=place):
            put(place + index, origin + index, jnp.clip(length - index * tile, 0, tile))
            return carry

        lax.fori_loop(0, some, add, 0)
        taken.append(some)
        place = place + some
    first = place
    sizes = [short_len[slot // home, base + slot % home] for slot in range(slots)]
    for wanted in (True, False):
        for slot, size in enumerate(sizes):
            fits = (size > 0) if wanted else (size <= 0)

            @pl.when(fits)
            def _():
                put(place, micros * per + slot, size)

            place = place + jnp.where(fits, 1, 0)
        if wanted:
            parts = BLOCK // tile
            count[clips] = lax.div(place - first + parts - 1, parts)
            count[2 * clips + 1] = first
            count[2 * clips + 2] = lax.div(place + parts - 1, parts)
    for number in range(clips):
        def fill(index, carry, origin=origins[number], place=place - taken[number]):
            put(place + index, origin + index, 0)
            return carry

        lax.fori_loop(taken[number], per, fill, 0)
        place = place + per - taken[number]


def pieced(step, source, parts, border, refs):
    low, high = border
    chosen = []
    for part in range(parts):
        origin = source[step * parts + part]
        far = jnp.where(origin < high, refs[parts + part][...], refs[2 * parts + part][...])
        chosen.append(jnp.where(origin < low, refs[part][...], far))
    return jnp.concatenate(chosen, axis=0).astype(F32)


def put_tiles(step, value, source, border, tile, stage, sem, near, far, guest):
    low, high = border
    parts = BLOCK // tile
    slot = lax.rem(step, 2)

    def settle(which):
        for part in range(parts):
            pltpu.make_async_copy(
                stage.at[which, pl.ds(part * tile, tile), :], near.at[pl.ds(0, tile), :], sem.at[which, part]
            ).wait()

    @pl.when(step >= 2)
    def _():
        settle(slot)

    stage[slot] = value
    for part in range(parts):
        origin = source[step * parts + part]
        view = stage.at[slot, pl.ds(part * tile, tile), :]

        def push(target, first, view=view, part=part, origin=origin):
            where = pl.ds(pl.multiple_of((origin - first) * tile, tile), tile)
            pltpu.make_async_copy(view, target.at[where, :], sem.at[slot, part]).start()

        @pl.when(origin < low)
        def _():
            push(near, 0)

        @pl.when((origin >= low) & (origin < high))
        def _():
            push(far, low)

        @pl.when(origin >= high)
        def _():
            push(guest, high)

    @pl.when(step == pl.num_programs(0) - 1)
    def _():
        settle(1 - slot)
        settle(slot)


def project_kernel(tile, border, last, tile_len, source, count, index, *refs):
    parts = BLOCK // tile
    table_any, weight_any, vectors, out, start_out, table, stage, rows, weight, weight_sem, sem = refs[3 * parts :]
    step = pl.program_id(0)
    width = weight.shape[0]
    depth, chunk = stage.shape[:2]
    chunks = table.shape[0] // chunk

    def fetch(number):
        return pltpu.make_async_copy(
            table_any.at[pl.ds(pl.multiple_of(number * chunk, 16), chunk), :],
            stage.at[lax.rem(number, depth)],
            sem.at[lax.rem(number, depth)],
        )

    @pl.when(step == 0)
    def _():
        for number in range(depth):
            fetch(number).start()
        weight_load = pltpu.make_async_copy(weight_any, weight, weight_sem.at[0])
        weight_load.start()
        rows[...] = jnp.zeros_like(rows)

        def load(number, carry):
            fetch(number).wait()
            table[pl.ds(pl.multiple_of(number * chunk, 16), chunk), :] = stage[lax.rem(number, depth)].astype(F32)

            @pl.when(number + depth < chunks)
            def _():
                fetch(number + depth).start()

            return carry

        lax.fori_loop(0, chunks, load, 0)
        weight_load.wait()

    @pl.when(step == count[last])
    def _():
        out[...] = jnp.zeros_like(out)

    @pl.when(step < count[last])
    def _():
        def gather(part, carry):
            origin = source[step * parts + part] * tile
            first = part * tile

            def some(group, inner):
                base = pl.multiple_of(first + group * 8, 8)
                for row in range(8):
                    place = index[origin + group * 8 + row]
                    rows[pl.ds(base + row, 1), :] = table[pl.ds(place, 1), :]
                return inner

            lax.fori_loop(0, lax.div(tile_len[step * parts + part] + 7, 8), some, 0)
            return carry

        lax.fori_loop(0, parts, gather, 0)
        start = pieced(step, source, parts, border, refs) + rows[...]
        start_out[...] = start
        unit, _ = centre(start)
        normed = (unit * vectors[0:1, :width] + vectors[1:2, :width]).astype(BF)
        for part in range(3):
            cols = slice(part * width, (part + 1) * width)
            triple = dot(normed, weight[:, cols], (1, 0))
            if part == 0:
                triple = (triple + vectors[2:3, :width]).astype(BF) * BF(0.125)
            elif part == 1:
                triple = triple.astype(BF)
            else:
                triple = (triple + vectors[3:4, :width]).astype(BF)
            out[cols, :] = triple.T


def masked_tile(tile_scores, limit):
    key = lax.broadcasted_iota(jnp.int32, tile_scores.shape, 0)
    return jnp.where(key < limit, tile_scores, MASKED)


def block_mask(tile_len, first, tile):
    key = lax.broadcasted_iota(jnp.int32, (BLOCK, BLOCK), 0)
    asked = lax.broadcasted_iota(jnp.int32, (BLOCK, BLOCK), 1)
    limit = tile_len[first]
    for part in range(1, BLOCK // tile):
        limit = jnp.where(key >= part * tile, tile_len[first + part], limit)
    return (key // tile == asked // tile) & (lax.rem(key, tile) < limit)


def attend_kernel(tile, long_rows, clips, tile_len, length, count, query, keys, values, out, logsum, even, odd):
    head_dim = query.shape[0] // 2
    most = long_rows // BLOCK
    boards = (even, odd)

    def score(head, column, first, size, fix):
        lanes = slice(head * head_dim, (head + 1) * head_dim)
        asked = query[lanes, pl.ds(column, BLOCK)]
        for number in range(size):
            part = dot(keys[lanes, pl.ds(first + number * BLOCK, BLOCK)], asked, (0, 0))
            if number == size - 1:
                part = fix(part)
            boards[head][number * BLOCK : (number + 1) * BLOCK, :] = part

    def finish(head, column, first, size):
        lanes = slice(head * head_dim, (head + 1) * head_dim)
        board = boards[head]
        top = jnp.max(board[: size * BLOCK, :], axis=0, keepdims=True)
        total = None
        gathered = None
        for number in range(size):
            weight = jnp.exp(board[number * BLOCK : (number + 1) * BLOCK, :] - top)
            part = jnp.sum(weight, axis=0, keepdims=True)
            held = values[lanes, pl.ds(first + number * BLOCK, BLOCK)]
            term = dot(held, weight.astype(BF), (1, 0))
            total = part if total is None else total + part
            gathered = term if gathered is None else gathered + term
        out[lanes, pl.ds(column, BLOCK)] = (gathered / total).astype(BF)
        logsum[0, pl.ds(head, 1), pl.ds(column, BLOCK)] = top + jnp.log(total)

    def rows(first, size, fix):
        def at(block):
            return pl.multiple_of(first + block * BLOCK, 128)

        score(0, at(0), first, size, fix)

        def ask(block, carry):
            score(1, at(block), first, size, fix)
            finish(0, at(block), first, size)
            score(0, at(jnp.minimum(block + 1, size - 1)), first, size, fix)
            finish(1, at(block), first, size)
            return carry

        lax.fori_loop(0, size, ask, 0)

    def clip(number, carry):
        first = pl.multiple_of(count[clips + 1 + number] * tile, 128)
        blocks = count[number]
        rest = length[number]
        for size in range(1, most + 1):
            @pl.when(blocks == size)
            def _():
                rows(first, size, lambda part: masked_tile(part, rest - (size - 1) * BLOCK))
        return carry

    out[...] = jnp.zeros_like(out)
    lax.fori_loop(0, clips, clip, 0)

    def short(number, carry):
        begin = count[2 * clips + 1] + number * (BLOCK // tile)
        column = pl.multiple_of(begin * tile, 128)
        allowed = block_mask(tile_len, begin, tile)
        rows(column, 1, lambda part: jnp.where(allowed, part, MASKED))
        return carry

    lax.fori_loop(0, count[clips], short, 0)


def attend_back_kernel(
    tile, long_rows, clips, tile_len, length, count, query, keys, values, grad, logsum,
    query_out, key_out, value_out, key_sum, value_sum, even, odd, even_back, odd_back,
):
    head_dim = query.shape[0] // 2
    most = long_rows // BLOCK
    boards = (even, odd)
    backs = (even_back, odd_back)

    def score(head, column, first, size, fix):
        lanes = slice(head * head_dim, (head + 1) * head_dim)
        asked = query[lanes, pl.ds(column, BLOCK)]
        pulled = grad[lanes, pl.ds(column, BLOCK)]
        for number in range(size):
            here = pl.ds(first + number * BLOCK, BLOCK)
            there = slice(number * BLOCK, (number + 1) * BLOCK)
            part = dot(keys[lanes, here], asked, (0, 0))
            if number == size - 1:
                part = fix(part)
            boards[head][there, :] = part
            backs[head][there, :] = dot(values[lanes, here], pulled, (0, 0))

    def finish(head, column, first, size, limit):
        lanes = slice(head * head_dim, (head + 1) * head_dim)
        asked = query[lanes, pl.ds(column, BLOCK)]
        pulled = grad[lanes, pl.ds(column, BLOCK)]
        own = lax.broadcasted_iota(jnp.int32, (1, BLOCK), 1) < limit
        base = jnp.where(own, logsum[0, pl.ds(head, 1), pl.ds(column, BLOCK)], -1e3 * MASKED)
        inner = None
        for number in range(size):
            there = slice(number * BLOCK, (number + 1) * BLOCK)
            prob = jnp.exp(boards[head][there, :] - base)
            boards[head][there, :] = prob
            part = jnp.sum(prob * backs[head][there, :], axis=0, keepdims=True)
            inner = part if inner is None else inner + part
            value_sum[lanes, there] += dot(pulled, prob.astype(BF), (1, 1))
        query_sum = None
        for number in range(size):
            here = pl.ds(first + number * BLOCK, BLOCK)
            there = slice(number * BLOCK, (number + 1) * BLOCK)
            moved = (boards[head][there, :] * (backs[head][there, :] - inner)).astype(BF)
            key_sum[lanes, there] += dot(asked, moved, (1, 1))
            term = dot(keys[lanes, here], moved, (1, 0))
            query_sum = term if query_sum is None else query_sum + term
        query_out[lanes, pl.ds(column, BLOCK)] = (query_sum * 0.125).astype(BF)

    def rows(first, size, fix, rest):
        def at(block):
            return pl.multiple_of(first + block * BLOCK, 128)

        key_sum[:, : size * BLOCK] = jnp.zeros((2 * head_dim, size * BLOCK), F32)
        value_sum[:, : size * BLOCK] = jnp.zeros((2 * head_dim, size * BLOCK), F32)
        score(0, at(0), first, size, fix)

        def ask(block, carry):
            limit = rest - block * BLOCK
            after = jnp.minimum(block + 1, size - 1)
            score(1, at(block), first, size, fix)
            finish(0, at(block), first, size, limit)
            score(0, at(after), first, size, fix)
            finish(1, at(block), first, size, limit)
            return carry

        lax.fori_loop(0, size, ask, 0)
        key_out[:, pl.ds(first, size * BLOCK)] = key_sum[:, : size * BLOCK].astype(BF)
        value_out[:, pl.ds(first, size * BLOCK)] = value_sum[:, : size * BLOCK].astype(BF)

    def clip(number, carry):
        first = pl.multiple_of(count[clips + 1 + number] * tile, 128)
        blocks = count[number]
        rest = length[number]
        for size in range(1, most + 1):
            @pl.when(blocks == size)
            def _():
                rows(first, size, lambda part: masked_tile(part, rest - (size - 1) * BLOCK), rest)
        return carry

    for empty in (query_out, key_out, value_out):
        empty[...] = jnp.zeros_like(empty)
    lax.fori_loop(0, clips, clip, 0)

    def short(number, carry):
        begin = count[2 * clips + 1] + number * (BLOCK // tile)
        column = pl.multiple_of(begin * tile, 128)
        allowed = block_mask(tile_len, begin, tile)
        rows(column, 1, lambda part: jnp.where(allowed, part, MASKED), BLOCK)
        return carry

    lax.fori_loop(0, count[clips], short, 0)


def gelu_both(upper):
    spread = 0.5 * (1.0 + lax.erf(upper * 0.7071067811865476))
    bell = jnp.exp(-0.5 * upper * upper) * 0.3989422804014327
    return upper * spread, spread + upper * bell


def write_out(entries):
    waiting = {}
    counts = {}
    for source, stage, sem, target in entries:
        key = id(stage)
        slot = counts.get(key, 0) % stage.shape[0]
        counts[key] = counts.get(key, 0) + 1
        if (key, slot) in waiting:
            waiting[key, slot].wait()
        value = source()
        view = stage.at[slot, :, : value.shape[1], : value.shape[2]]
        stage[slot, :, : value.shape[1], : value.shape[2]] = value.astype(BF)
        copy = pltpu.make_async_copy(view, target, sem.at[slot])
        copy.start()
        waiting[key, slot] = copy
    for copy in waiting.values():
        copy.wait()


def middle_kernel(tile, border, last, tile_len, source, count, attended_t, start_in, *refs):
    parts = BLOCK // tile
    (
        out_any, up_any, down_any, align_any, vectors, up_b, align_b,
        long_out, short_out, guest_out, pull_out, grad_out, vector_out, sums_out,
        out_acc, up_acc, down_acc, align_acc, hidden, slope, stage, stage_down,
        out_w, up_w, down_w, align_w, weight_sem, down_sem, show, show_sem, sem,
    ) = refs[3 * parts :]
    step = pl.program_id(0)
    width = out_w.shape[0]
    wide = up_w.shape[1]
    teach = align_w.shape[1]
    pieces = wide // width
    live = step < count[last]
    loads = [
        pltpu.make_async_copy(source_ref, target, weight_sem.at[number])
        for number, (source_ref, target) in enumerate(
            ((out_any, out_w), (up_any, up_w), (down_any, down_w), (align_any, align_w))
        )
    ]

    @pl.when(step == 0)
    def _():
        for load in loads:
            load.start()
        for acc in (out_acc, up_acc, down_acc, align_acc):
            acc[...] = jnp.zeros_like(acc)
        vector_out[...] = jnp.zeros_like(vector_out)
        loads[0].wait()

    def put(value):
        put_tiles(step, value, source, border, tile, show, show_sem, long_out, short_out, guest_out)

    def add_vector(row, value):
        size = value.shape[1]
        vector_out[row : row + 1, :size] += value

    def over_rows(value):
        return jnp.sum(value, axis=0, keepdims=True)

    @pl.when(step == count[last])
    def _():
        pull_out[...] = jnp.zeros_like(pull_out)

    @pl.when(jnp.logical_not(live))
    def _():
        put(jnp.zeros((BLOCK, width), BF))

    @pl.when(live)
    def _():
        ok = valid_rows(tile_len, step, tile)
        across = attended_t[...]
        middle = start_in[...] + dot(across, out_w[...], (0, 0)) + vectors[4:5, :width]
        unit, inverse = centre(middle)
        dense = (unit * vectors[5:6, :width] + vectors[6:7, :width]).astype(BF)
        result = middle + vectors[7:8, :width]

        @pl.when(step == 0)
        def _():
            for load in loads[1:]:
                load.wait()

        for piece in range(pieces):
            cols = slice(piece * width, (piece + 1) * width)
            upper = dot(dense, up_w[:, cols], (1, 0)) + up_b[:, cols]
            bent, tilt = gelu_both(upper)
            low = bent.astype(BF)
            hidden[:, cols] = low
            slope[:, cols] = tilt
            result = result + dot(low, down_w[cols, :], (1, 0))
        shown = jnp.where(ok, result, 0.0).astype(BF)
        put(shown)
        projected = dot(shown, align_w[...], (1, 0)) + align_b[...]
        target = pieced(step, source, parts, border, refs)
        miss = jnp.where(ok, projected - target, 0.0).astype(BF)
        add_vector(5, over_rows(miss.astype(F32)))
        align_acc[...] += dot(shown, miss, (0, 0))
        pulled = dot(miss, align_w[...], (1, 1)).astype(BF)
        pulled_wide = pulled.astype(F32)
        add_vector(4, over_rows(pulled_wide))
        grad_dense = None
        for piece in range(pieces):
            cols = slice(piece * width, (piece + 1) * width)
            grad_upper = dot(pulled, down_w[cols, :], (1, 1)) * slope[:, cols]
            low = grad_upper.astype(BF)
            vector_out[0:1, cols] += over_rows(low.astype(F32))
            down_acc[piece] += dot(hidden[:, cols], pulled, (0, 0))
            up_acc[piece] += dot(dense, low, (0, 0))
            term = dot(low, up_w[:, cols], (1, 1))
            grad_dense = term if grad_dense is None else grad_dense + term
        add_vector(2, over_rows(grad_dense * unit))
        add_vector(3, over_rows(grad_dense))
        grad_middle = pulled_wide + centre_back(grad_dense * vectors[5:6, :width], unit, inverse)
        grad_out[...] = grad_middle
        branch = grad_middle.astype(BF)
        add_vector(1, over_rows(branch.astype(F32)))
        out_acc[...] += dot(across, branch, (1, 0))
        pull_out[...] = dot(out_w[...], branch, (1, 1)).astype(BF)

    @pl.when(step == pl.num_programs(0) - 1)
    def _():
        groups, unit_rows = stage.shape[1:3]
        deep = pieces * unit_rows
        some, tall = stage_down.shape[1:3]

        def grouped(value):
            return value.reshape(groups, unit_rows, value.shape[-1])

        entries = []
        for piece in range(pieces):
            if groups >= pieces:
                target = sums_out.at[pl.ds(piece * some, some), pl.ds(0, tall), :]
            else:
                target = sums_out.at[:, pl.ds(piece * tall, tall), :]
            entries.append(
                (lambda piece=piece: down_acc[piece].reshape(some, tall, width), stage_down, down_sem, target)
            )
            target = sums_out.at[:, pl.ds(deep + piece * unit_rows, unit_rows), :]
            entries.append((lambda piece=piece: grouped(up_acc[piece]), stage, sem, target))
        begin = 2 * deep
        entries.append((lambda: grouped(out_acc[...]), stage, sem, sums_out.at[:, pl.ds(begin, unit_rows), :]))
        begin += unit_rows
        entries.append(
            (lambda: grouped(align_acc[:, :width]), stage, sem, sums_out.at[:, pl.ds(begin, unit_rows), :])
        )
        begin += unit_rows
        extra = teach - width
        third = unit_rows * extra // width
        for part in range(width // extra):
            entries.append(
                (
                    lambda part=part: grouped(align_acc[:, width:])[:, part * third : (part + 1) * third],
                    stage,
                    sem,
                    sums_out.at[:, pl.ds(begin, third), pl.ds(part * extra, extra)],
                )
            )
        write_out(entries)


def entry_kernel(tile, border, last, tile_len, source, count, index, *refs):
    (
        query_t, key_t, value_t, start_in, grad_in, weight_any, vectors,
        long_out, short_out, guest_out, vector_out, sums_out,
        weight_acc, position_acc, moved, stage, stage_rows, weight, weight_sem, rows_sem, show, show_sem, sem,
    ) = refs
    step = pl.program_id(0)
    width = weight.shape[0]
    live = step < count[last]

    @pl.when(step == 0)
    def _():
        load = pltpu.make_async_copy(weight_any, weight, weight_sem.at[0])
        load.start()
        weight_acc[...] = jnp.zeros_like(weight_acc)
        vector_out[...] = jnp.zeros_like(vector_out)

        def clear(number, carry):
            position_acc[pl.ds(pl.multiple_of(number * 64, 64), 64), :] = jnp.zeros((64, width), F32)
            return carry

        lax.fori_loop(0, position_acc.shape[0] // 64, clear, 0)
        left = position_acc.shape[0] % 64
        if left:
            position_acc[position_acc.shape[0] - left :, :] = jnp.zeros((left, width), F32)
        load.wait()

    def put(value):
        put_tiles(step, value, source, border, tile, show, show_sem, long_out, short_out, guest_out)

    def over_rows(value):
        return jnp.sum(value, axis=0, keepdims=True)

    @pl.when(jnp.logical_not(live))
    def _():
        put(jnp.zeros((BLOCK, width), BF))

    @pl.when(live)
    def _():
        unit, inverse = centre(start_in[...])
        normed = (unit * vectors[0:1, :width] + vectors[1:2, :width]).astype(BF)
        grad_normed = None
        for part in range(3):
            cols = slice(part * width, (part + 1) * width)
            across = (query_t, key_t, value_t)[part][...]
            if part != 1:
                vector_out[part : part + 1, :] += over_rows(across.T.astype(F32))
            weight_acc[:, cols] += dot(normed, across, (0, 1))
            term = dot(across, weight[:, cols], (0, 1))
            grad_normed = term if grad_normed is None else grad_normed + term
        vector_out[1:2, :] += over_rows(grad_normed * unit)
        vector_out[3:4, :] += over_rows(grad_normed)
        grad_start = grad_in[...] + centre_back(grad_normed * vectors[0:1, :width], unit, inverse)
        put(grad_start.astype(BF))
        moved[...] = grad_start
        parts = BLOCK // tile

        def spread(number, carry):
            first = number * tile
            origin = source[step * parts + number] * tile

            def some(group, inner):
                base = pl.multiple_of(first + group * 8, 8)
                for row in range(8):
                    place = index[origin + group * 8 + row]
                    position_acc[pl.ds(place, 1), :] += moved[pl.ds(base + row, 1), :]
                return inner

            lax.fori_loop(0, lax.div(tile_len[step * parts + number] + 7, 8), some, 0)
            return carry

        lax.fori_loop(0, parts, spread, 0)

    @pl.when(step == pl.num_programs(0) - 1)
    def _():
        groups, unit_rows = stage.shape[1:3]
        depth, chunk = stage_rows.shape[:2]
        patches = position_acc.shape[0] - 8
        taken = patches // groups if groups > 1 else chunk
        begin = sums_out.shape[1] - 3 * unit_rows
        entries = []
        for part in range(3):
            cols = slice(part * width, (part + 1) * width)
            entries.append(
                (
                    lambda cols=cols: weight_acc[:, cols].reshape(groups, unit_rows, width),
                    stage,
                    sem,
                    sums_out.at[:, pl.ds(begin + part * unit_rows, unit_rows), :],
                )
            )
        write_out(entries)

        def copy(number):
            if groups > 1:
                target = sums_out.at[number, pl.ds(0, chunk), :]
            else:
                target = sums_out.at[0, pl.ds(pl.multiple_of(number * chunk, 16), chunk), :]
            slot = lax.rem(number, depth)
            return pltpu.make_async_copy(stage_rows.at[slot], target, rows_sem.at[slot])

        def drain(number, carry):
            @pl.when(number >= depth)
            def _():
                copy(number - depth).wait()

            stage_rows[lax.rem(number, depth)] = position_acc[
                pl.ds(pl.multiple_of(number * taken, 8), chunk), :
            ].astype(BF)
            copy(number).start()
            return carry

        chunks = patches // taken
        lax.fori_loop(0, chunks, drain, 0)
        for late in range(depth):
            copy(chunks - depth + late).wait()


def send_kernel(home, copies, short_len, destination, shown, out):
    base = (lax.axis_index("dp") * copies + lax.axis_index("rep")) * home
    out[...] = jnp.zeros_like(out)
    for slot in range(shown.shape[0]):
        micro, place = slot // home, base + slot % home

        @pl.when(short_len[micro, place] > 0)
        def _():
            out[destination[micro, place], micro] = shown[slot]


def finish_kernel(
    home, copies, flag, short_len, destination, count, got, early, late, vector, out_in, out_back, grad_in, grad_back,
    balanced, position_g, heads_g, out_g, up_g, down_g, align_g, *rest,
):
    *vector_outs, long_out, long_grad, carry, carry_sem, sem = rest
    tail = out_back.shape[0]
    swapped = count[flag] > 0
    backs = [
        pltpu.make_async_copy(ref, carry.at[number], carry_sem.at[number])
        for number, ref in enumerate((out_back, grad_back))
    ]
    homes = [
        pltpu.make_async_copy(
            carry.at[number], ref.at[pl.ds(ref.shape[0] - tail, tail), :], carry_sem.at[number]
        )
        for number, ref in enumerate((long_out, long_grad))
    ]

    @pl.when(swapped)
    def _():
        for copy in backs:
            copy.start()

    peers = got.shape[0]
    micros, bal = balanced.shape[:2]
    width = position_g.shape[1]
    unit_rows = out_g.shape[0]
    pieces = up_g.shape[1] // width
    d = lax.axis_index("dp")
    r = lax.axis_index("rep")
    number = 0
    found_all = []
    for micro in range(micros):
        for slot in range(bal):
            def look(peer, found):
                base = (peer * copies + r) * home
                for place in range(slot, home, bal):
                    fits = (short_len[micro, base + place] > 0) & (destination[micro, base + place] == d)
                    found = jnp.where(fits, peer, found)
                return found

            found = lax.fori_loop(0, peers, look, jnp.int32(-1))
            found_all.append(found)

            @pl.when(found >= 0)
            def _():
                pltpu.make_async_copy(
                    got.at[jnp.maximum(found, 0), micro], balanced.at[micro, slot], sem.at[number]
                ).start()

            @pl.when(found < 0)
            def _():
                balanced[micro, slot] = jnp.zeros(balanced.shape[2:], BF)

            number += 1
    position_g[...] = late[: position_g.shape[0], :].astype(F32)
    first = late.shape[0] - 3 * unit_rows
    for part in range(3):
        heads_g[:, part * width : (part + 1) * width] = late[
            first + part * unit_rows : first + (part + 1) * unit_rows, :
        ].astype(F32)
    deep = pieces * unit_rows
    down_g[...] = early[:deep, :].astype(F32)
    for part in range(pieces):
        up_g[:, part * width : (part + 1) * width] = early[
            deep + part * unit_rows : deep + (part + 1) * unit_rows, :
        ].astype(F32)
    out_g[...] = early[2 * deep : 2 * deep + unit_rows, :].astype(F32)
    align_g[:, :width] = early[2 * deep + unit_rows : 2 * deep + 2 * unit_rows, :].astype(F32)
    extra = align_g.shape[1] - width
    third = unit_rows * extra // width
    begin = 2 * deep + 2 * unit_rows
    for part in range(width // extra):
        align_g[part * third : (part + 1) * third, width:] = early[
            begin : begin + third, part * extra : (part + 1) * extra
        ].astype(F32)

    places = [(1, 0), (2, 0), (3, 0), (4, 0), (0, 1), (1, 1), (2, 1), (3, 1), (0, 0), (5, 0)]
    for target, (row, late_part) in zip(vector_outs, places):
        size = target.shape[1]
        first = d * size
        window = size if size % 128 == 0 else -(-size // 128) * 128 + 128
        begin = late_part * pieces * width
        origin = jnp.minimum(lax.div(first, 128) * 128, vector.shape[1] - begin - window)
        value = vector[:, pl.ds(pl.multiple_of(begin + origin, 128), window)]
        at = lax.broadcasted_iota(jnp.int32, (window, size), 0)
        want = lax.broadcasted_iota(jnp.int32, (window, size), 1) + (first - origin)
        chosen = jnp.where(at == want, 1.0, 0.0)
        picked = jnp.dot(value, chosen, preferred_element_type=F32, precision=lax.Precision.HIGHEST)
        target[...] = picked[row : row + 1]

    @pl.when(swapped)
    def _():
        for back, copy in zip(backs, homes):
            back.wait()
            copy.start()
        for copy in homes:
            copy.wait()

    for number, found in enumerate(found_all):
        @pl.when(found >= 0)
        def _():
            pltpu.make_async_copy(
                got.at[0, number // bal], balanced.at[number // bal, number % bal], sem.at[number]
            ).wait()


SMALL_NAMES = (
    "mixer_gain", "mixer_shift", "query_bias", "value_bias", "out_bias", "dense_gain", "dense_shift",
    "down_bias", "up_bias", "align_bias",
)


def whole(shape):
    return pl.BlockSpec(shape, lambda *_: (0,) * len(shape), pipeline_mode=pl.Buffered(1))


def params(**more):
    return pltpu.CompilerParams(vmem_limit_bytes=VMEM_LIMIT, **more)


def run_block(
    row_sources, index, target_sources, tile_len, source, count, lengths,
    tile, long_rows, micros, weights, groups, vectors, up_b, align_b,
):
    w = weights
    width = row_sources[0].shape[1]
    total = sum(held.shape[0] for held in row_sources)
    clips = micros + 1
    wide = w["up_weight"].shape[1]
    teach = target_sources[0].shape[1]
    patches = w["position"].shape[0]
    blocks = total // BLOCK
    parts = BLOCK // tile
    border = (micros * long_rows // tile, (total - long_rows) // tile)
    last = 2 * clips + 2
    pairs = HEADS // 2
    pair = width // pairs
    unit_rows = width // groups
    pieces = wide // width
    early_rows = (2 * pieces + 2) * unit_rows + unit_rows * (teach - width) // width
    early_rows = -(-early_rows // 512) * 512
    chunk = -(-(patches // groups) // 16) * 16 if groups > 1 else patches // 14
    late_rows = (chunk if groups > 1 else patches) + 3 * unit_rows
    def kept(i, count):
        return jnp.minimum(i, count[last] - 1)

    def tiles(sources):
        specs = []
        for first, held in zip((0,) + border, sources):
            most = held.shape[0] // tile - 1
            for part in range(parts):
                specs.append(
                    pl.BlockSpec(
                        (tile, held.shape[1]),
                        lambda i, tl, src, cnt, *_, part=part, first=first, most=most: (
                            jnp.clip(src[kept(i, cnt) * parts + part] - first, 0, most),
                            0,
                        ),
                    )
                )
        return specs, [held for held in sources for _ in range(parts)]

    row_specs, row_args = tiles(row_sources)
    target_specs, target_args = tiles(target_sources)

    by_block = lambda last_dim: pl.BlockSpec((BLOCK, last_dim), lambda i, tl, src, cnt, *_: (kept(i, cnt), 0))
    by_column = lambda first: pl.BlockSpec((first, BLOCK), lambda i, tl, src, cnt, *_: (0, kept(i, cnt)))
    guarded = lambda first: pl.BlockSpec(
        (first, BLOCK), lambda i, tl, src, cnt, *_: (0, jnp.minimum(i, cnt[last]))
    )
    anywhere = pl.BlockSpec(memory_space=pl.ANY)
    show = [
        pltpu.VMEM((2, BLOCK, width), BF),
        pltpu.SemaphoreType.DMA((2, parts)),
        pltpu.SemaphoreType.DMA((2,)),
    ]
    shown_shapes = [jax.ShapeDtypeStruct(held.shape, BF) for held in row_sources]

    triple_t, start = pl.pallas_call(
        partial(project_kernel, tile, border, last),
        grid_spec=pltpu.PrefetchScalarGridSpec(
            num_scalar_prefetch=4,
            grid=(blocks,),
            in_specs=row_specs + [anywhere, anywhere, whole(vectors.shape)],
            out_specs=[guarded(3 * width), by_block(width)],
            scratch_shapes=[
                pltpu.VMEM((patches, width), F32),
                pltpu.VMEM((4, patches // 14, width), BF),
                pltpu.VMEM((BLOCK, width), F32),
                pltpu.VMEM((width, 3 * width), BF),
                pltpu.SemaphoreType.DMA((1,)),
                pltpu.SemaphoreType.DMA((4,)),
            ],
        ),
        out_shape=[
            jax.ShapeDtypeStruct((3 * width, total), BF),
            jax.ShapeDtypeStruct((total, width), F32),
        ],
        compiler_params=params(),
        name="project",
    )(
        tile_len, source, count, index, *row_args,
        w["position"], w["heads_weight"], vectors,
    )

    def heads_spec(offset):
        return pl.BlockSpec((pair, total), lambda i, *_: (i + offset * pairs, 0))

    board = pltpu.VMEM((long_rows, BLOCK), F32)
    sums_spec = pl.BlockSpec((1, 2, total), lambda i, *_: (i, 0, 0))
    attended_t, sums = pl.pallas_call(
        partial(attend_kernel, tile, long_rows, clips),
        grid_spec=pltpu.PrefetchScalarGridSpec(
            num_scalar_prefetch=3,
            grid=(pairs,),
            in_specs=[heads_spec(0), heads_spec(1), heads_spec(2)],
            out_specs=[heads_spec(0), sums_spec],
            scratch_shapes=[board] * 2,
        ),
        out_shape=[
            jax.ShapeDtypeStruct((width, total), BF),
            jax.ShapeDtypeStruct((pairs, 2, total), F32),
        ],
        compiler_params=params(),
        name="attend",
    )(tile_len, lengths, count, triple_t, triple_t, triple_t)

    some = max(groups // pieces, 1)
    long_out, short_out, guest_out, pulled_t, grad_middle, vector, early = pl.pallas_call(
        partial(middle_kernel, tile, border, last),
        grid_spec=pltpu.PrefetchScalarGridSpec(
            num_scalar_prefetch=3,
            grid=(blocks,),
            in_specs=[by_column(width), by_block(width)]
            + target_specs
            + [
                anywhere, anywhere, anywhere, anywhere,
                whole(vectors.shape), whole(up_b.shape), whole(align_b.shape),
            ],
            out_specs=[
                anywhere, anywhere, anywhere, guarded(width), by_block(width), whole((8, wide)), anywhere,
            ],
            scratch_shapes=[
                pltpu.VMEM((width, width), F32),
                pltpu.VMEM((pieces, width, width), F32),
                pltpu.VMEM((pieces, width, width), F32),
                pltpu.VMEM((width, teach), F32),
                pltpu.VMEM((BLOCK, wide), BF),
                pltpu.VMEM((BLOCK, wide), F32),
                pltpu.VMEM((2, groups, unit_rows, width), BF),
                pltpu.VMEM((2, some, width // some, width), BF),
                pltpu.VMEM((width, width), BF),
                pltpu.VMEM((width, wide), BF),
                pltpu.VMEM((wide, width), BF),
                pltpu.VMEM((width, teach), BF),
                pltpu.SemaphoreType.DMA((4,)),
                pltpu.SemaphoreType.DMA((2,)),
            ]
            + show,
        ),
        out_shape=shown_shapes
        + [
            jax.ShapeDtypeStruct((width, total), BF),
            jax.ShapeDtypeStruct((total, width), F32),
            jax.ShapeDtypeStruct((8, wide), F32),
            jax.ShapeDtypeStruct((groups, early_rows, width), BF),
        ],
        compiler_params=params(),
        name="middle",
    )(
        tile_len, source, count, attended_t, start, *target_args,
        w["out_weight"], w["up_weight"], w["down_weight"], w["align_weight"], vectors, up_b, align_b,
    )

    grads = pl.pallas_call(
        partial(attend_back_kernel, tile, long_rows, clips),
        grid_spec=pltpu.PrefetchScalarGridSpec(
            num_scalar_prefetch=3,
            grid=(pairs,),
            in_specs=[heads_spec(0), heads_spec(1), heads_spec(2), heads_spec(0), sums_spec],
            out_specs=[heads_spec(0)] * 3,
            scratch_shapes=[pltpu.VMEM((pair, long_rows), F32)] * 2 + [board] * 4,
        ),
        out_shape=[jax.ShapeDtypeStruct((width, total), BF)] * 3,
        compiler_params=params(),
        name="attend_back",
    )(tile_len, lengths, count, triple_t, triple_t, triple_t, pulled_t, sums)

    long_grad, short_grad, guest_grad, entry_vector, late = pl.pallas_call(
        partial(entry_kernel, tile, border, last),
        grid_spec=pltpu.PrefetchScalarGridSpec(
            num_scalar_prefetch=4,
            grid=(blocks,),
            in_specs=[by_column(width)] * 3
            + [by_block(width), by_block(width), anywhere, whole(vectors.shape)],
            out_specs=[anywhere, anywhere, anywhere, whole((8, width)), anywhere],
            scratch_shapes=[
                pltpu.VMEM((width, 3 * width), F32),
                pltpu.VMEM((patches + 8, width), F32),
                pltpu.VMEM((BLOCK, width), F32),
                pltpu.VMEM((2, groups, unit_rows, width), BF),
                pltpu.VMEM((4, chunk, width), BF),
                pltpu.VMEM((width, 3 * width), BF),
                pltpu.SemaphoreType.DMA((1,)),
                pltpu.SemaphoreType.DMA((4,)),
            ]
            + show,
        ),
        out_shape=shown_shapes
        + [
            jax.ShapeDtypeStruct((8, width), F32),
            jax.ShapeDtypeStruct((groups, late_rows, width), BF),
        ],
        compiler_params=params(),
        name="entry",
    )(tile_len, source, count, index, *grads, start, grad_middle, w["heads_weight"], vectors)
    outs = (long_out, short_out, long_grad, short_grad)
    return outs, (guest_out, guest_grad), early, late, vector, entry_vector


def bit_of(number, bit):
    return lax.rem(number // (1 << bit), 2)


def reduce_plan(peers, early_rows, late_rows):
    bits = peers.bit_length() - 1
    forward = list(range(bits))
    swapped = forward[1::-1] + forward[2:]
    last = forward[2:] + forward[:2]
    pieces = []
    for source, rows in ((0, early_rows), (1, late_rows)):
        unit = 16
        units = rows // 2 // unit
        begin = 0
        for sub in range(2):
            here = units // 2 + (1 if sub < units % 2 else 0)
            first = int(here * 0.4 + 0.5)
            for order, parts in zip((forward, swapped, last), (first, first, here - 2 * first)):
                if parts > 0:
                    pieces.append((source * 2 + sub, source, begin, parts * unit, tuple(order)))
                    begin += parts * unit
    return pieces


def reduce_kernel(
    peers, halves, pieces, early, late, vector, entry_vector, early_out, late_out, vector_out, *scratch
):
    bits = peers.bit_length() - 1
    amount = len(pieces)
    kept = scratch[:amount]
    mates = scratch[amount : 2 * amount]
    mine_in = scratch[2 * amount : 3 * amount]
    landed = [scratch[3 * amount + k * bits : 3 * amount + (k + 1) * bits] for k in range(amount)]
    (
        vector_land, mate_send, mate_recv, load_sem, hop_send, hop_recv, end_send, end_recv, end_load,
        vector_send, vector_recv,
    ) = scratch[3 * amount + amount * bits :]
    d = lax.axis_index("dp")
    r = lax.axis_index("rep")
    other = 1 - r
    mate = (d, other)
    partner = [(d + (1 - 2 * bit_of(d, bit)) * (1 << bit), r) for bit in range(bits)]
    sources = (early, late)
    outs = (early_out, late_out)
    barrier = pltpu.get_barrier_semaphore()
    for device in [mate] + partner:
        pl.semaphore_signal(barrier, inc=1, device_id=device, device_id_type=pl.DeviceIdType.MESH)
    pl.semaphore_wait(barrier, bits + 1)

    def remote(source, target, send, recv, device):
        copy = pltpu.make_async_remote_copy(
            src_ref=source, dst_ref=target, send_sem=send, recv_sem=recv,
            device_id=device, device_id_type=pl.DeviceIdType.MESH,
        )
        copy.start()
        return copy

    def rows_at(source, core, begin, rows):
        return pl.ds(pl.multiple_of(core * halves[source] + begin, 16), rows)

    wide = vector.shape[1]
    vector_out[:, :wide] = vector[...]
    vector_out[:, wide:] = entry_vector[...]
    mate_copies = []
    loads = []
    for k, (_, source, begin, rows, order) in enumerate(pieces):
        mate_copies.append(
            remote(
                sources[source].at[:, rows_at(source, other, begin, rows), :], mates[k],
                mate_send.at[k], mate_recv.at[k], mate,
            )
        )
        load = pltpu.make_async_copy(
            sources[source].at[:, rows_at(source, r, begin, rows), :], mine_in[k], load_sem.at[k]
        )
        load.start()
        loads.append(load)

    hops = {}
    ends = []

    def base_at(order, stage):
        base = 0
        for place in range(stage):
            base = base + bit_of(d, order[place]) * (1 << (bits - 1 - place))
        return base

    def send(k, stage):
        _, source, begin, rows, order = pieces[k]
        if stage == bits:
            result = kept[k].at[base_at(order, bits)]
            where = rows_at(source, r, begin, rows)
            ends.append(remote(result, outs[source].at[where, :], end_send.at[k], end_recv.at[k], mate))
            own = pltpu.make_async_copy(result, outs[source].at[where, :], end_load.at[k])
            own.start()
            ends.append(own)
            return
        size = 1 << (bits - 1 - stage)
        first = base_at(order, stage) + (1 - bit_of(d, order[stage])) * size
        hops[k, stage] = remote(
            kept[k].at[pl.ds(first, size)], landed[k][stage], hop_send.at[k, stage], hop_recv.at[k, stage],
            partner[order[stage]],
        )

    def join(k):
        order = pieces[k][4]
        loads[k].wait()
        mate_copies[k].wait_recv()

        def add(chunk, carry):
            place = 0
            for step in range(bits):
                place = place + bit_of(chunk, order[step]) * (1 << (bits - 1 - step))
            kept[k][place] = mine_in[k][chunk] + mates[k][chunk]
            return carry

        lax.fori_loop(0, peers, add, 0)

    def gather(k, stage):
        order = pieces[k][4]
        hops[k, stage].wait_recv()
        base = base_at(order, stage + 1)

        def add(chunk, carry):
            kept[k][base + chunk] = kept[k][base + chunk] + landed[k][stage][chunk]
            return carry

        lax.fori_loop(0, 1 << (bits - 1 - stage), add, 0)

    events = sorted(
        (stage + pieces[k][0], -stage, k) for k in range(amount) for stage in range(bits + 1)
    )
    vector_copies = []

    def vector_step(stage):
        if stage > 0:
            vector_copies[-1].wait()
            vector_out[...] = vector_out[...] + vector_land[stage - 1]
        if stage <= bits:
            device = mate if stage == 0 else partner[stage - 1]
            vector_copies.append(
                remote(vector_out, vector_land.at[stage], vector_send.at[stage], vector_recv.at[stage], device)
            )

    seen = -1
    for time, negative, k in events:
        if time != seen:
            if time <= bits + 1:
                vector_step(time)
            seen = time
        stage = -negative
        if stage == 0:
            join(k)
        else:
            gather(k, stage - 1)
        send(k, stage)
    for copy in mate_copies + list(hops.values()):
        copy.wait_send()
    for copy in ends:
        copy.wait()


def reduce_all(early, late, vector, entry_vector):
    joined = (vector.shape[0], vector.shape[1] + entry_vector.shape[1])
    peers, early_rows, width = early.shape
    late_rows = late.shape[1]
    bits = peers.bit_length() - 1
    pieces = reduce_plan(peers, early_rows, late_rows)
    amount = len(pieces)
    scratch = [pltpu.VMEM((peers, rows, width), BF) for _, _, _, rows, _ in pieces] * 3
    for _, _, _, rows, _ in pieces:
        for stage in range(bits):
            scratch.append(pltpu.VMEM((1 << (bits - 1 - stage), rows, width), BF))
    scratch.append(pltpu.VMEM((bits + 1,) + joined, F32))
    one = pltpu.SemaphoreType.DMA((amount,))
    many = pltpu.SemaphoreType.DMA((amount, bits))
    few = pltpu.SemaphoreType.DMA((bits + 1,))
    scratch += [one, one, one, many, many, one, one, one, few, few]
    anywhere = pl.BlockSpec(memory_space=pl.ANY)
    near = pl.BlockSpec(memory_space=pltpu.VMEM)
    return pl.pallas_call(
        partial(reduce_kernel, peers, (early_rows // 2, late_rows // 2), pieces),
        in_specs=[anywhere, anywhere, near, near],
        out_specs=[anywhere, anywhere, near],
        out_shape=[
            jax.ShapeDtypeStruct((early_rows, width), BF),
            jax.ShapeDtypeStruct((late_rows, width), BF),
            jax.ShapeDtypeStruct(joined, F32),
        ],
        scratch_shapes=scratch,
        compiler_params=pltpu.CompilerParams(
            vmem_limit_bytes=VMEM_LIMIT, collective_id=0, has_side_effects=True
        ),
        name="reduce",
    )(early, late, vector, entry_vector)


def unpack(early, late, unit_rows, kept, teach, pieces):
    width = early.shape[1]
    deep = pieces * unit_rows

    def beside(held, first, count):
        return jnp.concatenate(
            [held[first + k * unit_rows : first + (k + 1) * unit_rows] for k in range(count)], axis=1
        )

    extra = teach - width
    third = unit_rows * extra // width
    begin = 2 * deep + 2 * unit_rows
    tail = early[begin : begin + third]
    tail = jnp.concatenate([tail[:, k * extra : (k + 1) * extra] for k in range(width // extra)], axis=0)
    return {
        "down_weight": early[:deep],
        "up_weight": beside(early, deep, pieces),
        "out_weight": early[2 * deep : 2 * deep + unit_rows],
        "align_weight": jnp.concatenate([early[2 * deep + unit_rows : begin], tail], axis=1),
        "position": late[:kept],
        "heads_weight": beside(late, late.shape[0] - 3 * unit_rows, 3),
    }


def shards(
    long_clips,
    short_clips,
    long_index,
    short_index,
    long_length,
    short_length,
    destination,
    long_target,
    short_target,
    position,
    mixer_gain,
    mixer_shift,
    heads_weight,
    query_bias,
    value_bias,
    out_weight,
    out_bias,
    dense_gain,
    dense_shift,
    up_weight,
    up_bias,
    down_weight,
    down_bias,
    align_weight,
    align_bias,
):
    peers = lax.axis_size("dp")
    copies = lax.axis_size("rep")
    micros, _, long_rows, width = long_clips.shape
    home_slots, tile = short_clips.shape[1:3]
    bal_slots = home_slots // 2
    slots = micros * home_slots
    wide = up_weight.shape[1]
    teach = long_target.shape[-1]
    patches = position.shape[0]
    weights = dict(
        zip(
            WEIGHT_NAMES,
            (
                position, mixer_gain, mixer_shift, heads_weight, query_bias, value_bias, out_weight, out_bias,
                dense_gain, dense_shift, up_weight, up_bias, down_weight, down_bias, align_weight, align_bias,
            ),
        )
    )
    scalars = pl.BlockSpec(memory_space=pltpu.SMEM)
    anywhere = pl.BlockSpec(memory_space=pl.ANY)
    clips = micros + 1
    tile_total = clips * long_rows // tile + slots
    near = pl.BlockSpec(memory_space=pltpu.VMEM)
    pairs = [(core, (core + 1) % copies) for core in range(copies)]

    def trade(value):
        return lax.ppermute(value, "rep", pairs)

    lengths = long_length.reshape(-1)
    facts = trade(jnp.concatenate([long_index[-1].reshape(-1), lengths]))
    guest_rows = trade(long_clips[-1, 0])
    guest_target = trade(long_target[-1, 0])
    tile_len, source, count, work, vectors, up_b, align_b = pl.pallas_call(
        partial(plan_kernel, tile, long_rows, home_slots, copies),
        in_specs=[scalars] * 3 + [near] * len(SMALL_NAMES),
        out_specs=[scalars] * 4 + [near] * 3,
        out_shape=[
            jax.ShapeDtypeStruct((tile_total,), jnp.int32),
            jax.ShapeDtypeStruct((tile_total,), jnp.int32),
            jax.ShapeDtypeStruct((2 * clips + 4,), jnp.int32),
            jax.ShapeDtypeStruct((clips,), jnp.int32),
            jax.ShapeDtypeStruct((len(SMALL_NAMES) - 2, width), F32),
            jax.ShapeDtypeStruct((1, wide), F32),
            jax.ShapeDtypeStruct((1, teach), F32),
        ],
        name="plan",
    )(long_length, facts[long_rows:], short_length, *[weights[name] for name in SMALL_NAMES])
    index = jnp.concatenate([long_index.reshape(-1), short_index.reshape(-1), facts[:long_rows]])
    groups = peers if copies == 2 and width % (16 * peers) == 0 else 1
    outs, guests, early, late, vector, entry_vector = run_block(
        (long_clips.reshape(-1, width), short_clips.reshape(-1, width), guest_rows), index,
        (long_target.reshape(-1, teach), short_target.reshape(-1, teach), guest_target),
        tile_len, source, count, work, tile, long_rows, micros, weights, groups, vectors, up_b, align_b,
    )
    long_out, short_out, long_grad, short_grad = outs
    out_back, grad_back = [trade(value) for value in guests]
    send = pl.pallas_call(
        partial(send_kernel, home_slots, copies),
        in_specs=[scalars, scalars, whole((slots, tile, width))],
        out_specs=pl.BlockSpec(memory_space=pltpu.VMEM) if groups == peers else scalars,
        out_shape=jax.ShapeDtypeStruct((peers, micros, tile, width), BF),
        compiler_params=params(),
        name="send",
    )(short_length, destination, short_out.reshape(slots, tile, width)) if groups == peers else send_all(
        short_length, destination, short_out.reshape(slots, tile, width), peers, copies, home_slots
    )
    got = lax.all_to_all(send, "dp", split_axis=0, concat_axis=0, tiled=True)
    unit_rows = width // peers
    if groups == peers:
        early, late, vector = reduce_all(early, late, vector, entry_vector)
    else:
        matrices = unpack(early[0], late[0], width, patches, teach, wide // width)
        early, late = share_out(matrices, peers, copies, unit_rows, wide // width)
        vector = lax.psum(jnp.concatenate([vector, entry_vector], axis=1), ("dp", "rep"))
    near = pl.BlockSpec(memory_space=pltpu.VMEM)
    outs = pl.pallas_call(
        partial(finish_kernel, home_slots, copies, 2 * clips + 3),
        in_specs=[scalars, scalars, scalars, anywhere, near, near, near] + [anywhere] * 4,
        out_specs=[near] * 17 + [anywhere] * 2,
        input_output_aliases={7: 17, 9: 18},
        out_shape=[
            jax.ShapeDtypeStruct((micros, bal_slots, tile, width), BF),
            jax.ShapeDtypeStruct((patches // peers, width), F32),
            jax.ShapeDtypeStruct((unit_rows, 3 * width), F32),
            jax.ShapeDtypeStruct((unit_rows, width), F32),
            jax.ShapeDtypeStruct((unit_rows, wide), F32),
            jax.ShapeDtypeStruct((wide // peers, width), F32),
            jax.ShapeDtypeStruct((unit_rows, teach), F32),
        ]
        + [jax.ShapeDtypeStruct((1, unit_rows), F32)] * 8
        + [jax.ShapeDtypeStruct((1, wide // peers), F32), jax.ShapeDtypeStruct((1, teach // peers), F32)]
        + [jax.ShapeDtypeStruct(long_out.shape, BF)] * 2,
        scratch_shapes=[
            pltpu.VMEM((2, long_rows, width), BF),
            pltpu.SemaphoreType.DMA((2,)),
            pltpu.SemaphoreType.DMA((micros * bal_slots,)),
        ],
        compiler_params=params(),
        name="finish",
    )(short_length, destination, count, got, early, late, vector, long_out, out_back, long_grad, grad_back)
    short_bal, position_g, heads_g, out_g, up_g, down_g, align_g = outs[:7]
    shared = {
        "position": position_g, "heads_weight": heads_g, "out_weight": out_g, "up_weight": up_g,
        "down_weight": down_g, "align_weight": align_g,
    }
    long_out, long_grad = outs[17:]
    order = (
        "out_bias", "dense_gain", "dense_shift", "down_bias", "query_bias", "mixer_gain", "value_bias",
        "mixer_shift", "up_bias", "align_bias",
    )
    for name, value in zip(order, outs[7:17]):
        shared[name] = value.reshape(-1)
    return (
        long_out.reshape(micros, 1, long_rows, width),
        short_bal,
        long_grad.reshape(micros, 1, long_rows, width),
        short_grad.reshape(micros, home_slots, tile, width),
    ) + tuple(shared[name] for name in WEIGHT_NAMES)


def send_all(short_length, destination, shown, peers, copies, home):
    micros = short_length.shape[0]
    mine = lax.axis_index("dp") * copies + lax.axis_index("rep")

    def own(table):
        table = table.reshape(micros, peers * copies, home)
        return lax.dynamic_index_in_dim(table, mine, 1, keepdims=False)

    wanted = (own(destination)[None] == jnp.arange(peers)[:, None, None]) & (own(short_length)[None] > 0)
    shown = shown.reshape((micros, home) + shown.shape[1:])
    return jnp.einsum("pmj,mjtd->pmtd", wanted.astype(BF), shown)


def share_out(matrices, peers, copies, unit_rows, pieces):
    shared = {}
    for name, piece in matrices.items():
        rows = piece.shape[0] // peers
        padded = -(-rows // (8 * copies)) * 8 * copies
        if padded != rows:
            piece = piece.reshape(peers, rows, -1)
            piece = jnp.pad(piece, ((0, 0), (0, padded - rows), (0, 0)))
            piece = piece.reshape(peers * padded, -1)
        piece = lax.psum_scatter(piece, ("dp", "rep"), scatter_dimension=0, tiled=True)
        shared[name] = lax.all_gather(piece, "rep", axis=0, tiled=True)[:rows]
    width = shared["out_weight"].shape[1]
    up = shared["up_weight"].reshape(unit_rows, pieces, width).transpose(1, 0, 2).reshape(-1, width)
    heads = shared["heads_weight"].reshape(unit_rows, 3, width).transpose(1, 0, 2).reshape(-1, width)
    align = shared["align_weight"]
    extra = align.shape[1] - width
    parts = width // extra
    tail = align[:, width:].reshape(parts, unit_rows // parts, extra).transpose(1, 0, 2).reshape(-1, width)
    early = jnp.concatenate([shared["down_weight"], up, shared["out_weight"], align[:, :width], tail], axis=0)
    return early, jnp.concatenate([shared["position"], heads], axis=0)


def solution(mesh):
    placed = (
        P(None, ("dp", "rep"), None, None),
        P(None, ("dp", "rep"), None, None),
        P(None, ("dp", "rep"), None),
        P(None, ("dp", "rep"), None),
        P(None, ("dp", "rep")),
        P(),
        P(),
        P(None, ("dp", "rep"), None, None),
        P(None, ("dp", "rep"), None, None),
        P(),
        P(),
        P(),
        P(),
        P(),
        P(),
        P(),
        P(),
        P(),
        P(),
        P(),
        P(),
        P(),
        P(),
        P(),
        P(),
    )
    return jax.shard_map(
        shards,
        mesh=mesh,
        in_specs=placed,
        out_specs=(
            P(None, ("dp", "rep"), None, None),
            P(None, ("dp", "rep"), None, None),
            P(None, ("dp", "rep"), None, None),
            P(None, ("dp", "rep"), None, None),
            P("dp", None),
            P("dp"),
            P("dp"),
            P("dp", None),
            P("dp"),
            P("dp"),
            P("dp", None),
            P("dp"),
            P("dp"),
            P("dp"),
            P("dp", None),
            P("dp"),
            P("dp", None),
            P("dp"),
            P("dp", None),
            P("dp"),
        ),
        check_vma=False,
    )
```

```python
from functools import partial

import jax
import jax.numpy as jnp
from jax import lax
from jax.experimental import pallas as pl
from jax.experimental.pallas import tpu as pltpu
from jax.sharding import PartitionSpec as P

HEADS = 12
EPS = 1e-06
MASKED = -1000000000.0
WEIGHT_NAMES = (
    "position",
    "mixer_gain",
    "mixer_shift",
    "heads_weight",
    "query_bias",
    "value_bias",
    "out_weight",
    "out_bias",
    "dense_gain",
    "dense_shift",
    "up_weight",
    "up_bias",
    "down_weight",
    "down_bias",
    "align_weight",
    "align_bias",
)


BLOCK = 256
BF = jnp.bfloat16
F32 = jnp.float32
VMEM_LIMIT = 66_000_000


def dot(left, right, dims):
    return lax.dot_general(left, right, ((dims[:1], dims[1:]), ((), ())), preferred_element_type=F32)


def centre(values):
    mean = jnp.mean(values, axis=-1, keepdims=True)
    centered = values - mean
    spread = jnp.mean(centered * centered, axis=-1, keepdims=True)
    inverse = lax.rsqrt(spread + EPS)
    return centered * inverse, inverse


def centre_back(grad, unit, inverse):
    first = jnp.mean(grad, axis=-1, keepdims=True)
    second = jnp.mean(grad * unit, axis=-1, keepdims=True)
    return inverse * (grad - first - unit * second)


def valid_rows(tile_len, block, tile):
    row = lax.broadcasted_iota(jnp.int32, (BLOCK, 1), 0)
    parts = BLOCK // tile
    limit = tile_len[block * parts]
    for part in range(1, parts):
        limit = jnp.where(row >= part * tile, tile_len[block * parts + part], limit)
    return lax.rem(row, tile) < limit


def clip_cost(length):
    blocks = lax.div(length + BLOCK - 1, BLOCK)
    return 2 * lax.div(length + 127, 128) + blocks * blocks


def plan_kernel(tile, long_rows, home, copies, lengths, guest, short_len, *refs):
    amount = len(refs) - 7
    small, (tile_len, source, count, work, vectors, up_out, align_out) = refs[:amount], refs[amount:]
    for number, value in enumerate(small[:-2]):
        vectors[number : number + 1, :] = value[...].reshape(1, -1)
    up_out[...] = small[-2][...].reshape(1, -1)
    align_out[...] = small[-1][...].reshape(1, -1)
    micros = lengths.shape[0]
    slots = micros * home
    per = long_rows // tile
    step = 128 // tile
    d, r = lax.axis_index("dp"), lax.axis_index("rep")
    base = (d * copies + r) * home
    other = (d * copies + lax.rem(r + 1, copies)) * home

    def put(place, origin, size):
        source[place] = origin
        tile_len[place] = size

    mine, theirs = jnp.int32(0), jnp.int32(0)
    for slot in range(slots):
        mine = mine + jnp.where(short_len[slot // home, base + slot % home] > 0, 1, 0)
        theirs = theirs + jnp.where(short_len[slot // home, other + slot % home] > 0, 1, 0)
    for micro in range(micros - 1):
        mine = mine + clip_cost(lengths[micro, 0])
        theirs = theirs + clip_cost(guest[micro])
    held, offered = clip_cost(lengths[micros - 1, 0]), clip_cost(guest[micros - 1])
    base0, base1 = jnp.where(r == 0, mine, theirs), jnp.where(r == 0, theirs, mine)
    last0, last1 = jnp.where(r == 0, held, offered), jnp.where(r == 0, offered, held)
    best = jnp.maximum(base0 + last0, base1 + last1)
    choice = jnp.int32(0)
    plans = (
        jnp.maximum(base0 + last1, base1 + last0),
        jnp.maximum(base0, base1 + last0 + last1),
        jnp.maximum(base0 + last0 + last1, base1),
    )
    for number, cost in enumerate(plans):
        better = cost + 1 < best
        choice = jnp.where(better, number + 1, choice)
        best = jnp.where(better, cost, best)
    gives = choice == jnp.where(r == 0, 2, 3)
    takes = choice == jnp.where(r == 0, 3, 2)
    swaps = choice == 1
    clips = micros + 1
    count[2 * clips + 3] = (gives | swaps).astype(jnp.int32)
    place = jnp.int32(0)
    taken = []
    origins = []
    needed = [jnp.int32(per)] * (micros - 1) + [
        jnp.where(gives | swaps, 0, per), jnp.where(takes | swaps, per, 0)
    ]
    for number in range(clips):
        if number < micros - 1:
            length, origin = lengths[number, 0], number * per
        elif number == micros - 1:
            length, origin = jnp.where(gives | swaps, 0, lengths[number, 0]), number * per
        else:
            length, origin = jnp.where(takes | swaps, guest[micros - 1], 0), micros * per + slots
        origins.append(origin)
        work[number] = length
        some = lax.div(length + 127, 128) * step
        count[number] = lax.div(length + BLOCK - 1, BLOCK)
        count[clips + 1 + number] = place

        def add(index, carry, origin=origin, length=length, place=place):
            put(place + index, origin + index, jnp.clip(length - index * tile, 0, tile))
            return carry

        lax.fori_loop(0, some, add, 0)
        taken.append(some)
        place = place + some
    first = place
    sizes = [short_len[slot // home, base + slot % home] for slot in range(slots)]
    for wanted in (True, False):
        for slot, size in enumerate(sizes):
            fits = (size > 0) if wanted else (size <= 0)

            @pl.when(fits)
            def _():
                put(place, micros * per + slot, size)

            place = place + jnp.where(fits, 1, 0)
        if wanted:
            parts = BLOCK // tile
            count[clips] = lax.div(place - first + parts - 1, parts)
            count[2 * clips + 1] = first
            count[2 * clips + 2] = lax.div(place + parts - 1, parts)
    for number in range(clips):
        def fill(index, carry, origin=origins[number], place=place - taken[number]):
            put(place + index, origin + index, 0)
            return carry

        whole = needed[number]
        lax.fori_loop(taken[number], whole, fill, 0)
        place = place + whole - taken[number]
    parts = BLOCK // tile
    count[2 * clips + 4] = lax.div(place + parts - 1, parts)


def pieced(step, source, parts, border, refs):
    low, high = border
    chosen = []
    for part in range(parts):
        origin = source[step * parts + part]
        far = jnp.where(origin < high, refs[parts + part][...], refs[2 * parts + part][...])
        chosen.append(jnp.where(origin < low, refs[part][...], far))
    return jnp.concatenate(chosen, axis=0).astype(F32)


def put_tiles(step, until, value, source, border, tile, stage, sem, near, far, guest):
    low, high = border
    parts = BLOCK // tile
    slot = lax.rem(step, 2)

    def settle(which):
        for part in range(parts):
            pltpu.make_async_copy(
                stage.at[which, pl.ds(part * tile, tile), :], near.at[pl.ds(0, tile), :], sem.at[which, part]
            ).wait()

    @pl.when(step >= 2)
    def _():
        settle(slot)

    stage[slot] = value
    for part in range(parts):
        origin = source[step * parts + part]
        view = stage.at[slot, pl.ds(part * tile, tile), :]

        def push(target, first, view=view, part=part, origin=origin):
            where = pl.ds(pl.multiple_of((origin - first) * tile, tile), tile)
            pltpu.make_async_copy(view, target.at[where, :], sem.at[slot, part]).start()

        @pl.when(origin < low)
        def _():
            push(near, 0)

        @pl.when((origin >= low) & (origin < high))
        def _():
            push(far, low)

        @pl.when(origin >= high)
        def _():
            push(guest, high)

    @pl.when(step == until - 1)
    def _():
        settle(1 - slot)
        settle(slot)


def project_kernel(tile, border, last, tile_len, source, count, index, *refs):
    parts = BLOCK // tile
    table_any, weight_any, vectors, out, start_out, table, stage, rows, weight, weight_sem, sem = refs[3 * parts :]
    step = pl.program_id(0)
    width = weight.shape[0]
    depth, chunk = stage.shape[:2]
    chunks = table.shape[0] // chunk

    def fetch(number):
        return pltpu.make_async_copy(
            table_any.at[pl.ds(pl.multiple_of(number * chunk, 16), chunk), :],
            stage.at[lax.rem(number, depth)],
            sem.at[lax.rem(number, depth)],
        )

    @pl.when(step == 0)
    def _():
        for number in range(depth):
            fetch(number).start()
        weight_load = pltpu.make_async_copy(weight_any, weight, weight_sem.at[0])
        weight_load.start()
        rows[...] = jnp.zeros_like(rows)

        def load(number, carry):
            fetch(number).wait()
            table[pl.ds(pl.multiple_of(number * chunk, 16), chunk), :] = stage[lax.rem(number, depth)].astype(F32)

            @pl.when(number + depth < chunks)
            def _():
                fetch(number + depth).start()

            return carry

        lax.fori_loop(0, chunks, load, 0)
        weight_load.wait()

    @pl.when(step == count[last])
    def _():
        out[...] = jnp.zeros_like(out)

    @pl.when(step < count[last])
    def _():
        def gather(part, carry):
            origin = source[step * parts + part] * tile
            first = part * tile

            def some(group, inner):
                base = pl.multiple_of(first + group * 8, 8)
                for row in range(8):
                    place = index[origin + group * 8 + row]
                    rows[pl.ds(base + row, 1), :] = table[pl.ds(place, 1), :]
                return inner

            lax.fori_loop(0, lax.div(tile_len[step * parts + part] + 7, 8), some, 0)
            return carry

        lax.fori_loop(0, parts, gather, 0)
        start = pieced(step, source, parts, border, refs) + rows[...]
        start_out[...] = start
        unit, _ = centre(start)
        normed = (unit * vectors[0:1, :width] + vectors[1:2, :width]).astype(BF)
        for part in range(3):
            cols = slice(part * width, (part + 1) * width)
            triple = dot(normed, weight[:, cols], (1, 0))
            if part == 0:
                triple = (triple + vectors[2:3, :width]).astype(BF) * BF(0.125)
            elif part == 1:
                triple = triple.astype(BF)
            else:
                triple = (triple + vectors[3:4, :width]).astype(BF)
            out[cols, :] = triple.T


def masked_tile(tile_scores, limit):
    key = lax.broadcasted_iota(jnp.int32, tile_scores.shape, 0)
    return jnp.where(key < limit, tile_scores, MASKED)


def block_mask(tile_len, first, tile):
    key = lax.broadcasted_iota(jnp.int32, (BLOCK, BLOCK), 0)
    asked = lax.broadcasted_iota(jnp.int32, (BLOCK, BLOCK), 1)
    limit = tile_len[first]
    for part in range(1, BLOCK // tile):
        limit = jnp.where(key >= part * tile, tile_len[first + part], limit)
    return (key // tile == asked // tile) & (lax.rem(key, tile) < limit)


def attend_kernel(tile, long_rows, clips, tile_len, length, count, query, keys, values, out, logsum, even, odd):
    head_dim = query.shape[0] // 2
    most = long_rows // BLOCK
    boards = (even, odd)

    def score(head, column, first, size, fix):
        lanes = slice(head * head_dim, (head + 1) * head_dim)
        asked = query[lanes, pl.ds(column, BLOCK)]
        for number in range(size):
            part = dot(keys[lanes, pl.ds(first + number * BLOCK, BLOCK)], asked, (0, 0))
            if number == size - 1:
                part = fix(part)
            boards[head][number * BLOCK : (number + 1) * BLOCK, :] = part

    def finish(head, column, first, size):
        lanes = slice(head * head_dim, (head + 1) * head_dim)
        board = boards[head]
        top = jnp.max(board[: size * BLOCK, :], axis=0, keepdims=True)
        total = None
        gathered = None
        for number in range(size):
            weight = jnp.exp(board[number * BLOCK : (number + 1) * BLOCK, :] - top)
            part = jnp.sum(weight, axis=0, keepdims=True)
            held = values[lanes, pl.ds(first + number * BLOCK, BLOCK)]
            term = dot(held, weight.astype(BF), (1, 0))
            total = part if total is None else total + part
            gathered = term if gathered is None else gathered + term
        out[lanes, pl.ds(column, BLOCK)] = (gathered / total).astype(BF)
        logsum[0, pl.ds(head, 1), pl.ds(column, BLOCK)] = top + jnp.log(total)

    def rows(first, size, fix):
        def at(block):
            return pl.multiple_of(first + block * BLOCK, 128)

        score(0, at(0), first, size, fix)

        def ask(block, carry):
            score(1, at(block), first, size, fix)
            finish(0, at(block), first, size)
            score(0, at(jnp.minimum(block + 1, size - 1)), first, size, fix)
            finish(1, at(block), first, size)
            return carry

        lax.fori_loop(0, size, ask, 0)

    def clip(number, carry):
        first = pl.multiple_of(count[clips + 1 + number] * tile, 128)
        blocks = count[number]
        rest = length[number]
        for size in range(1, most + 1):
            @pl.when(blocks == size)
            def _():
                rows(first, size, lambda part: masked_tile(part, rest - (size - 1) * BLOCK))
        return carry

    out[...] = jnp.zeros_like(out)
    lax.fori_loop(0, clips, clip, 0)

    def short(number, carry):
        begin = count[2 * clips + 1] + number * (BLOCK // tile)
        column = pl.multiple_of(begin * tile, 128)
        allowed = block_mask(tile_len, begin, tile)
        rows(column, 1, lambda part: jnp.where(allowed, part, MASKED))
        return carry

    lax.fori_loop(0, count[clips], short, 0)


def attend_back_kernel(
    tile, long_rows, clips, tile_len, length, count, query, keys, values, grad, logsum,
    query_out, key_out, value_out, key_sum, value_sum, even, odd, even_back, odd_back,
):
    head_dim = query.shape[0] // 2
    most = long_rows // BLOCK
    boards = (even, odd)
    backs = (even_back, odd_back)

    def score(head, column, first, size, fix):
        lanes = slice(head * head_dim, (head + 1) * head_dim)
        asked = query[lanes, pl.ds(column, BLOCK)]
        pulled = grad[lanes, pl.ds(column, BLOCK)]
        for number in range(size):
            here = pl.ds(first + number * BLOCK, BLOCK)
            there = slice(number * BLOCK, (number + 1) * BLOCK)
            part = dot(keys[lanes, here], asked, (0, 0))
            if number == size - 1:
                part = fix(part)
            boards[head][there, :] = part
            backs[head][there, :] = dot(values[lanes, here], pulled, (0, 0))

    def finish(head, column, first, size, limit):
        lanes = slice(head * head_dim, (head + 1) * head_dim)
        asked = query[lanes, pl.ds(column, BLOCK)]
        pulled = grad[lanes, pl.ds(column, BLOCK)]
        own = lax.broadcasted_iota(jnp.int32, (1, BLOCK), 1) < limit
        base = jnp.where(own, logsum[0, pl.ds(head, 1), pl.ds(column, BLOCK)], -1e3 * MASKED)
        inner = None
        for number in range(size):
            there = slice(number * BLOCK, (number + 1) * BLOCK)
            prob = jnp.exp(boards[head][there, :] - base)
            boards[head][there, :] = prob
            part = jnp.sum(prob * backs[head][there, :], axis=0, keepdims=True)
            inner = part if inner is None else inner + part
            value_sum[lanes, there] += dot(pulled, prob.astype(BF), (1, 1))
        query_sum = None
        for number in range(size):
            here = pl.ds(first + number * BLOCK, BLOCK)
            there = slice(number * BLOCK, (number + 1) * BLOCK)
            moved = (boards[head][there, :] * (backs[head][there, :] - inner)).astype(BF)
            key_sum[lanes, there] += dot(asked, moved, (1, 1))
            term = dot(keys[lanes, here], moved, (1, 0))
            query_sum = term if query_sum is None else query_sum + term
        query_out[lanes, pl.ds(column, BLOCK)] = (query_sum * 0.125).astype(BF)

    def rows(first, size, fix, rest):
        def at(block):
            return pl.multiple_of(first + block * BLOCK, 128)

        key_sum[:, : size * BLOCK] = jnp.zeros((2 * head_dim, size * BLOCK), F32)
        value_sum[:, : size * BLOCK] = jnp.zeros((2 * head_dim, size * BLOCK), F32)
        score(0, at(0), first, size, fix)

        def ask(block, carry):
            limit = rest - block * BLOCK
            after = jnp.minimum(block + 1, size - 1)
            score(1, at(block), first, size, fix)
            finish(0, at(block), first, size, limit)
            score(0, at(after), first, size, fix)
            finish(1, at(block), first, size, limit)
            return carry

        lax.fori_loop(0, size, ask, 0)
        key_out[:, pl.ds(first, size * BLOCK)] = key_sum[:, : size * BLOCK].astype(BF)
        value_out[:, pl.ds(first, size * BLOCK)] = value_sum[:, : size * BLOCK].astype(BF)

    def clip(number, carry):
        first = pl.multiple_of(count[clips + 1 + number] * tile, 128)
        blocks = count[number]
        rest = length[number]
        for size in range(1, most + 1):
            @pl.when(blocks == size)
            def _():
                rows(first, size, lambda part: masked_tile(part, rest - (size - 1) * BLOCK), rest)
        return carry

    for empty in (query_out, key_out, value_out):
        empty[...] = jnp.zeros_like(empty)
    lax.fori_loop(0, clips, clip, 0)

    def short(number, carry):
        begin = count[2 * clips + 1] + number * (BLOCK // tile)
        column = pl.multiple_of(begin * tile, 128)
        allowed = block_mask(tile_len, begin, tile)
        rows(column, 1, lambda part: jnp.where(allowed, part, MASKED), BLOCK)
        return carry

    lax.fori_loop(0, count[clips], short, 0)


def gelu_both(upper):
    spread = 0.5 * (1.0 + lax.erf(upper * 0.7071067811865476))
    bell = jnp.exp(-0.5 * upper * upper) * 0.3989422804014327
    return upper * spread, spread + upper * bell


def write_out(entries):
    waiting = {}
    counts = {}
    for source, stage, sem, target in entries:
        key = id(stage)
        slot = counts.get(key, 0) % stage.shape[0]
        counts[key] = counts.get(key, 0) + 1
        if (key, slot) in waiting:
            waiting[key, slot].wait()
        value = source()
        view = stage.at[slot, :, : value.shape[1], : value.shape[2]]
        stage[slot, :, : value.shape[1], : value.shape[2]] = value.astype(BF)
        copy = pltpu.make_async_copy(view, target, sem.at[slot])
        copy.start()
        waiting[key, slot] = copy
    for copy in waiting.values():
        copy.wait()


def middle_kernel(tile, border, last, tile_len, source, count, attended_t, start_in, *refs):
    parts = BLOCK // tile
    (
        out_any, up_any, down_any, align_any, vectors, up_b, align_b,
        long_out, short_out, guest_out, pull_out, grad_out, vector_out, sums_out,
        out_acc, up_acc, down_acc, align_acc, hidden, slope, stage, stage_down,
        out_w, up_w, down_w, align_w, weight_sem, down_sem, show, show_sem, sem,
    ) = refs[3 * parts :]
    step = pl.program_id(0)
    width = out_w.shape[0]
    wide = up_w.shape[1]
    teach = align_w.shape[1]
    pieces = wide // width
    live = step < count[last]
    loads = [
        pltpu.make_async_copy(source_ref, target, weight_sem.at[number])
        for number, (source_ref, target) in enumerate(
            ((out_any, out_w), (up_any, up_w), (down_any, down_w), (align_any, align_w))
        )
    ]

    @pl.when(step == 0)
    def _():
        for load in loads:
            load.start()
        for acc in (out_acc, up_acc, down_acc, align_acc):
            acc[...] = jnp.zeros_like(acc)
        vector_out[...] = jnp.zeros_like(vector_out)
        loads[0].wait()

    def put(value):
        put_tiles(step, count[last + 2], value, source, border, tile, show, show_sem, long_out, short_out, guest_out)

    def add_vector(row, value):
        size = value.shape[1]
        vector_out[row : row + 1, :size] += value

    def over_rows(value):
        return jnp.sum(value, axis=0, keepdims=True)

    @pl.when(step == count[last])
    def _():
        pull_out[...] = jnp.zeros_like(pull_out)

    @pl.when(jnp.logical_not(live) & (step < count[last + 2]))
    def _():
        put(jnp.zeros((BLOCK, width), BF))

    @pl.when(live)
    def _():
        ok = valid_rows(tile_len, step, tile)
        across = attended_t[...]
        middle = start_in[...] + dot(across, out_w[...], (0, 0)) + vectors[4:5, :width]
        unit, inverse = centre(middle)
        dense = (unit * vectors[5:6, :width] + vectors[6:7, :width]).astype(BF)
        result = middle + vectors[7:8, :width]

        @pl.when(step == 0)
        def _():
            for load in loads[1:]:
                load.wait()

        for piece in range(pieces):
            cols = slice(piece * width, (piece + 1) * width)
            upper = dot(dense, up_w[:, cols], (1, 0)) + up_b[:, cols]
            bent, tilt = gelu_both(upper)
            low = bent.astype(BF)
            hidden[:, cols] = low
            slope[:, cols] = tilt
            result = result + dot(low, down_w[cols, :], (1, 0))
        shown = jnp.where(ok, result, 0.0).astype(BF)
        put(shown)
        projected = dot(shown, align_w[...], (1, 0)) + align_b[...]
        target = pieced(step, source, parts, border, refs)
        miss = jnp.where(ok, projected - target, 0.0).astype(BF)
        add_vector(5, over_rows(miss.astype(F32)))
        align_acc[...] += dot(shown, miss, (0, 0))
        pulled = dot(miss, align_w[...], (1, 1)).astype(BF)
        pulled_wide = pulled.astype(F32)
        add_vector(4, over_rows(pulled_wide))
        grad_dense = None
        for piece in range(pieces):
            cols = slice(piece * width, (piece + 1) * width)
            grad_upper = dot(pulled, down_w[cols, :], (1, 1)) * slope[:, cols]
            low = grad_upper.astype(BF)
            vector_out[0:1, cols] += over_rows(low.astype(F32))
            down_acc[piece] += dot(hidden[:, cols], pulled, (0, 0))
            up_acc[piece] += dot(dense, low, (0, 0))
            term = dot(low, up_w[:, cols], (1, 1))
            grad_dense = term if grad_dense is None else grad_dense + term
        add_vector(2, over_rows(grad_dense * unit))
        add_vector(3, over_rows(grad_dense))
        grad_middle = pulled_wide + centre_back(grad_dense * vectors[5:6, :width], unit, inverse)
        grad_out[...] = grad_middle
        branch = grad_middle.astype(BF)
        add_vector(1, over_rows(branch.astype(F32)))
        out_acc[...] += dot(across, branch, (1, 0))
        pull_out[...] = dot(out_w[...], branch, (1, 1)).astype(BF)

    @pl.when(step == pl.num_programs(0) - 1)
    def _():
        groups, unit_rows = stage.shape[1:3]
        deep = pieces * unit_rows
        some, tall = stage_down.shape[1:3]

        def grouped(value):
            return value.reshape(groups, unit_rows, value.shape[-1])

        entries = []
        for piece in range(pieces):
            if groups >= pieces:
                target = sums_out.at[pl.ds(piece * some, some), pl.ds(0, tall), :]
            else:
                target = sums_out.at[:, pl.ds(piece * tall, tall), :]
            entries.append(
                (lambda piece=piece: down_acc[piece].reshape(some, tall, width), stage_down, down_sem, target)
            )
            target = sums_out.at[:, pl.ds(deep + piece * unit_rows, unit_rows), :]
            entries.append((lambda piece=piece: grouped(up_acc[piece]), stage, sem, target))
        begin = 2 * deep
        entries.append((lambda: grouped(out_acc[...]), stage, sem, sums_out.at[:, pl.ds(begin, unit_rows), :]))
        begin += unit_rows
        entries.append(
            (lambda: grouped(align_acc[:, :width]), stage, sem, sums_out.at[:, pl.ds(begin, unit_rows), :])
        )
        begin += unit_rows
        extra = teach - width
        third = unit_rows * extra // width
        for part in range(width // extra):
            entries.append(
                (
                    lambda part=part: grouped(align_acc[:, width:])[:, part * third : (part + 1) * third],
                    stage,
                    sem,
                    sums_out.at[:, pl.ds(begin, third), pl.ds(part * extra, extra)],
                )
            )
        write_out(entries)


def entry_kernel(tile, border, last, tile_len, source, count, index, *refs):
    (
        query_t, key_t, value_t, start_in, grad_in, weight_any, vectors,
        long_out, short_out, guest_out, vector_out, sums_out,
        weight_acc, position_acc, moved, stage, stage_rows, weight, weight_sem, rows_sem, show, show_sem, sem,
    ) = refs
    step = pl.program_id(0)
    width = weight.shape[0]
    live = step < count[last]

    @pl.when(step == 0)
    def _():
        load = pltpu.make_async_copy(weight_any, weight, weight_sem.at[0])
        load.start()
        weight_acc[...] = jnp.zeros_like(weight_acc)
        vector_out[...] = jnp.zeros_like(vector_out)

        def clear(number, carry):
            position_acc[pl.ds(pl.multiple_of(number * 64, 64), 64), :] = jnp.zeros((64, width), F32)
            return carry

        lax.fori_loop(0, position_acc.shape[0] // 64, clear, 0)
        left = position_acc.shape[0] % 64
        if left:
            position_acc[position_acc.shape[0] - left :, :] = jnp.zeros((left, width), F32)
        load.wait()

    def put(value):
        put_tiles(step, count[last + 2], value, source, border, tile, show, show_sem, long_out, short_out, guest_out)

    def over_rows(value):
        return jnp.sum(value, axis=0, keepdims=True)

    @pl.when(jnp.logical_not(live) & (step < count[last + 2]))
    def _():
        put(jnp.zeros((BLOCK, width), BF))

    @pl.when(live)
    def _():
        unit, inverse = centre(start_in[...])
        normed = (unit * vectors[0:1, :width] + vectors[1:2, :width]).astype(BF)
        grad_normed = None
        for part in range(3):
            cols = slice(part * width, (part + 1) * width)
            across = (query_t, key_t, value_t)[part][...]
            if part != 1:
                vector_out[part : part + 1, :] += over_rows(across.T.astype(F32))
            weight_acc[:, cols] += dot(normed, across, (0, 1))
            term = dot(across, weight[:, cols], (0, 1))
            grad_normed = term if grad_normed is None else grad_normed + term
        vector_out[1:2, :] += over_rows(grad_normed * unit)
        vector_out[3:4, :] += over_rows(grad_normed)
        grad_start = grad_in[...] + centre_back(grad_normed * vectors[0:1, :width], unit, inverse)
        put(grad_start.astype(BF))
        moved[...] = grad_start
        parts = BLOCK // tile

        def spread(number, carry):
            first = number * tile
            origin = source[step * parts + number] * tile

            def some(group, inner):
                base = pl.multiple_of(first + group * 8, 8)
                for row in range(8):
                    place = index[origin + group * 8 + row]
                    position_acc[pl.ds(place, 1), :] += moved[pl.ds(base + row, 1), :]
                return inner

            lax.fori_loop(0, lax.div(tile_len[step * parts + number] + 7, 8), some, 0)
            return carry

        lax.fori_loop(0, parts, spread, 0)

    @pl.when(step == pl.num_programs(0) - 1)
    def _():
        groups, unit_rows = stage.shape[1:3]
        depth, chunk = stage_rows.shape[:2]
        patches = position_acc.shape[0] - 8
        taken = patches // groups if groups > 1 else chunk
        begin = sums_out.shape[1] - 3 * unit_rows
        entries = []
        for part in range(3):
            cols = slice(part * width, (part + 1) * width)
            entries.append(
                (
                    lambda cols=cols: weight_acc[:, cols].reshape(groups, unit_rows, width),
                    stage,
                    sem,
                    sums_out.at[:, pl.ds(begin + part * unit_rows, unit_rows), :],
                )
            )
        write_out(entries)

        def copy(number):
            if groups > 1:
                target = sums_out.at[number, pl.ds(0, chunk), :]
            else:
                target = sums_out.at[0, pl.ds(pl.multiple_of(number * chunk, 16), chunk), :]
            slot = lax.rem(number, depth)
            return pltpu.make_async_copy(stage_rows.at[slot], target, rows_sem.at[slot])

        def drain(number, carry):
            @pl.when(number >= depth)
            def _():
                copy(number - depth).wait()

            stage_rows[lax.rem(number, depth)] = position_acc[
                pl.ds(pl.multiple_of(number * taken, 8), chunk), :
            ].astype(BF)
            copy(number).start()
            return carry

        chunks = patches // taken
        lax.fori_loop(0, chunks, drain, 0)
        for late in range(depth):
            copy(chunks - depth + late).wait()


def send_kernel(home, copies, short_len, destination, shown, out):
    base = (lax.axis_index("dp") * copies + lax.axis_index("rep")) * home
    out[...] = jnp.zeros_like(out)
    for slot in range(shown.shape[0]):
        micro, place = slot // home, base + slot % home

        @pl.when(short_len[micro, place] > 0)
        def _():
            out[destination[micro, place], micro] = shown[slot]


def finish_kernel(
    home, copies, flag, short_len, destination, count, got, early, late, vector, out_in, out_back, grad_in, grad_back,
    balanced, position_g, heads_g, out_g, up_g, down_g, align_g, *rest,
):
    *vector_outs, long_out, long_grad, carry, carry_sem, sem = rest
    tail = out_back.shape[0]
    swapped = count[flag] > 0
    backs = [
        pltpu.make_async_copy(ref, carry.at[number], carry_sem.at[number])
        for number, ref in enumerate((out_back, grad_back))
    ]
    homes = [
        pltpu.make_async_copy(
            carry.at[number], ref.at[pl.ds(ref.shape[0] - tail, tail), :], carry_sem.at[number]
        )
        for number, ref in enumerate((long_out, long_grad))
    ]

    @pl.when(swapped)
    def _():
        for copy in backs:
            copy.start()

    peers = got.shape[0]
    micros, bal = balanced.shape[:2]
    width = position_g.shape[1]
    unit_rows = out_g.shape[0]
    pieces = up_g.shape[1] // width
    d = lax.axis_index("dp")
    r = lax.axis_index("rep")
    number = 0
    found_all = []
    for micro in range(micros):
        for slot in range(bal):
            def look(peer, found):
                base = (peer * copies + r) * home
                for place in range(slot, home, bal):
                    fits = (short_len[micro, base + place] > 0) & (destination[micro, base + place] == d)
                    found = jnp.where(fits, peer, found)
                return found

            found = lax.fori_loop(0, peers, look, jnp.int32(-1))
            found_all.append(found)

            @pl.when(found >= 0)
            def _():
                pltpu.make_async_copy(
                    got.at[jnp.maximum(found, 0), micro], balanced.at[micro, slot], sem.at[number]
                ).start()

            @pl.when(found < 0)
            def _():
                balanced[micro, slot] = jnp.zeros(balanced.shape[2:], BF)

            number += 1
    position_g[...] = late[: position_g.shape[0], :].astype(F32)
    first = late.shape[0] - 3 * unit_rows
    for part in range(3):
        heads_g[:, part * width : (part + 1) * width] = late[
            first + part * unit_rows : first + (part + 1) * unit_rows, :
        ].astype(F32)
    deep = pieces * unit_rows
    down_g[...] = early[:deep, :].astype(F32)
    for part in range(pieces):
        up_g[:, part * width : (part + 1) * width] = early[
            deep + part * unit_rows : deep + (part + 1) * unit_rows, :
        ].astype(F32)
    out_g[...] = early[2 * deep : 2 * deep + unit_rows, :].astype(F32)
    align_g[:, :width] = early[2 * deep + unit_rows : 2 * deep + 2 * unit_rows, :].astype(F32)
    extra = align_g.shape[1] - width
    third = unit_rows * extra // width
    begin = 2 * deep + 2 * unit_rows
    for part in range(width // extra):
        align_g[part * third : (part + 1) * third, width:] = early[
            begin : begin + third, part * extra : (part + 1) * extra
        ].astype(F32)

    places = [(1, 0), (2, 0), (3, 0), (4, 0), (0, 1), (1, 1), (2, 1), (3, 1), (0, 0), (5, 0)]
    for target, (row, late_part) in zip(vector_outs, places):
        size = target.shape[1]
        first = d * size
        window = size if size % 128 == 0 else -(-size // 128) * 128 + 128
        begin = late_part * pieces * width
        origin = jnp.minimum(lax.div(first, 128) * 128, vector.shape[1] - begin - window)
        value = vector[:, pl.ds(pl.multiple_of(begin + origin, 128), window)]
        at = lax.broadcasted_iota(jnp.int32, (window, size), 0)
        want = lax.broadcasted_iota(jnp.int32, (window, size), 1) + (first - origin)
        chosen = jnp.where(at == want, 1.0, 0.0)
        picked = jnp.dot(value, chosen, preferred_element_type=F32, precision=lax.Precision.HIGHEST)
        target[...] = picked[row : row + 1]

    @pl.when(swapped)
    def _():
        for back, copy in zip(backs, homes):
            back.wait()
            copy.start()
        for copy in homes:
            copy.wait()

    for number, found in enumerate(found_all):
        @pl.when(found >= 0)
        def _():
            pltpu.make_async_copy(
                got.at[0, number // bal], balanced.at[number // bal, number % bal], sem.at[number]
            ).wait()


SMALL_NAMES = (
    "mixer_gain", "mixer_shift", "query_bias", "value_bias", "out_bias", "dense_gain", "dense_shift",
    "down_bias", "up_bias", "align_bias",
)


def whole(shape):
    return pl.BlockSpec(shape, lambda *_: (0,) * len(shape), pipeline_mode=pl.Buffered(1))


def params(**more):
    return pltpu.CompilerParams(vmem_limit_bytes=VMEM_LIMIT, **more)


def run_block(
    row_sources, index, target_sources, tile_len, source, count, lengths,
    tile, long_rows, micros, weights, groups, vectors, up_b, align_b,
):
    w = weights
    width = row_sources[0].shape[1]
    total = sum(held.shape[0] for held in row_sources)
    clips = micros + 1
    wide = w["up_weight"].shape[1]
    teach = target_sources[0].shape[1]
    patches = w["position"].shape[0]
    blocks = total // BLOCK
    parts = BLOCK // tile
    border = (micros * long_rows // tile, (total - long_rows) // tile)
    last = 2 * clips + 2
    pairs = HEADS // 2
    pair = width // pairs
    unit_rows = width // groups
    pieces = wide // width
    early_rows = (2 * pieces + 2) * unit_rows + unit_rows * (teach - width) // width
    early_rows = -(-early_rows // 512) * 512
    chunk = -(-(patches // groups) // 16) * 16 if groups > 1 else patches // 14
    late_rows = (chunk if groups > 1 else patches) + 3 * unit_rows
    def kept(i, count):
        return jnp.minimum(i, count[last] - 1)

    def tiles(sources):
        specs = []
        for first, held in zip((0,) + border, sources):
            most = held.shape[0] // tile - 1
            for part in range(parts):
                specs.append(
                    pl.BlockSpec(
                        (tile, held.shape[1]),
                        lambda i, tl, src, cnt, *_, part=part, first=first, most=most: (
                            jnp.clip(src[kept(i, cnt) * parts + part] - first, 0, most),
                            0,
                        ),
                    )
                )
        return specs, [held for held in sources for _ in range(parts)]

    row_specs, row_args = tiles(row_sources)
    target_specs, target_args = tiles(target_sources)

    by_block = lambda last_dim: pl.BlockSpec((BLOCK, last_dim), lambda i, tl, src, cnt, *_: (kept(i, cnt), 0))
    by_column = lambda first: pl.BlockSpec((first, BLOCK), lambda i, tl, src, cnt, *_: (0, kept(i, cnt)))
    guarded = lambda first: pl.BlockSpec(
        (first, BLOCK), lambda i, tl, src, cnt, *_: (0, jnp.minimum(i, cnt[last]))
    )
    anywhere = pl.BlockSpec(memory_space=pl.ANY)
    show = [
        pltpu.VMEM((2, BLOCK, width), BF),
        pltpu.SemaphoreType.DMA((2, parts)),
        pltpu.SemaphoreType.DMA((2,)),
    ]
    shown_shapes = [jax.ShapeDtypeStruct(held.shape, BF) for held in row_sources]

    triple_t, start = pl.pallas_call(
        partial(project_kernel, tile, border, last),
        grid_spec=pltpu.PrefetchScalarGridSpec(
            num_scalar_prefetch=4,
            grid=(blocks,),
            in_specs=row_specs + [anywhere, anywhere, whole(vectors.shape)],
            out_specs=[guarded(3 * width), by_block(width)],
            scratch_shapes=[
                pltpu.VMEM((patches, width), F32),
                pltpu.VMEM((4, patches // 14, width), BF),
                pltpu.VMEM((BLOCK, width), F32),
                pltpu.VMEM((width, 3 * width), BF),
                pltpu.SemaphoreType.DMA((1,)),
                pltpu.SemaphoreType.DMA((4,)),
            ],
        ),
        out_shape=[
            jax.ShapeDtypeStruct((3 * width, total), BF),
            jax.ShapeDtypeStruct((total, width), F32),
        ],
        compiler_params=params(),
        name="project",
    )(
        tile_len, source, count, index, *row_args,
        w["position"], w["heads_weight"], vectors,
    )

    def heads_spec(offset):
        return pl.BlockSpec((pair, total), lambda i, *_: (i + offset * pairs, 0))

    board = pltpu.VMEM((long_rows, BLOCK), F32)
    sums_spec = pl.BlockSpec((1, 2, total), lambda i, *_: (i, 0, 0))
    attended_t, sums = pl.pallas_call(
        partial(attend_kernel, tile, long_rows, clips),
        grid_spec=pltpu.PrefetchScalarGridSpec(
            num_scalar_prefetch=3,
            grid=(pairs,),
            in_specs=[heads_spec(0), heads_spec(1), heads_spec(2)],
            out_specs=[heads_spec(0), sums_spec],
            scratch_shapes=[board] * 2,
        ),
        out_shape=[
            jax.ShapeDtypeStruct((width, total), BF),
            jax.ShapeDtypeStruct((pairs, 2, total), F32),
        ],
        compiler_params=params(),
        name="attend",
    )(tile_len, lengths, count, triple_t, triple_t, triple_t)

    some = max(groups // pieces, 1)
    long_out, short_out, guest_out, pulled_t, grad_middle, vector, early = pl.pallas_call(
        partial(middle_kernel, tile, border, last),
        grid_spec=pltpu.PrefetchScalarGridSpec(
            num_scalar_prefetch=3,
            grid=(blocks,),
            in_specs=[by_column(width), by_block(width)]
            + target_specs
            + [
                anywhere, anywhere, anywhere, anywhere,
                whole(vectors.shape), whole(up_b.shape), whole(align_b.shape),
            ],
            out_specs=[
                anywhere, anywhere, anywhere, guarded(width), by_block(width), whole((8, wide)), anywhere,
            ],
            scratch_shapes=[
                pltpu.VMEM((width, width), F32),
                pltpu.VMEM((pieces, width, width), F32),
                pltpu.VMEM((pieces, width, width), F32),
                pltpu.VMEM((width, teach), F32),
                pltpu.VMEM((BLOCK, wide), BF),
                pltpu.VMEM((BLOCK, wide), F32),
                pltpu.VMEM((2, groups, unit_rows, width), BF),
                pltpu.VMEM((2, some, width // some, width), BF),
                pltpu.VMEM((width, width), BF),
                pltpu.VMEM((width, wide), BF),
                pltpu.VMEM((wide, width), BF),
                pltpu.VMEM((width, teach), BF),
                pltpu.SemaphoreType.DMA((4,)),
                pltpu.SemaphoreType.DMA((2,)),
            ]
            + show,
        ),
        out_shape=shown_shapes
        + [
            jax.ShapeDtypeStruct((width, total), BF),
            jax.ShapeDtypeStruct((total, width), F32),
            jax.ShapeDtypeStruct((8, wide), F32),
            jax.ShapeDtypeStruct((groups, early_rows, width), BF),
        ],
        compiler_params=params(),
        name="middle",
    )(
        tile_len, source, count, attended_t, start, *target_args,
        w["out_weight"], w["up_weight"], w["down_weight"], w["align_weight"], vectors, up_b, align_b,
    )

    grads = pl.pallas_call(
        partial(attend_back_kernel, tile, long_rows, clips),
        grid_spec=pltpu.PrefetchScalarGridSpec(
            num_scalar_prefetch=3,
            grid=(pairs,),
            in_specs=[heads_spec(0), heads_spec(1), heads_spec(2), heads_spec(0), sums_spec],
            out_specs=[heads_spec(0)] * 3,
            scratch_shapes=[pltpu.VMEM((pair, long_rows), F32)] * 2 + [board] * 4,
        ),
        out_shape=[jax.ShapeDtypeStruct((width, total), BF)] * 3,
        compiler_params=params(),
        name="attend_back",
    )(tile_len, lengths, count, triple_t, triple_t, triple_t, pulled_t, sums)

    long_grad, short_grad, guest_grad, entry_vector, late = pl.pallas_call(
        partial(entry_kernel, tile, border, last),
        grid_spec=pltpu.PrefetchScalarGridSpec(
            num_scalar_prefetch=4,
            grid=(blocks,),
            in_specs=[by_column(width)] * 3
            + [by_block(width), by_block(width), anywhere, whole(vectors.shape)],
            out_specs=[anywhere, anywhere, anywhere, whole((8, width)), anywhere],
            scratch_shapes=[
                pltpu.VMEM((width, 3 * width), F32),
                pltpu.VMEM((patches + 8, width), F32),
                pltpu.VMEM((BLOCK, width), F32),
                pltpu.VMEM((2, groups, unit_rows, width), BF),
                pltpu.VMEM((4, chunk, width), BF),
                pltpu.VMEM((width, 3 * width), BF),
                pltpu.SemaphoreType.DMA((1,)),
                pltpu.SemaphoreType.DMA((4,)),
            ]
            + show,
        ),
        out_shape=shown_shapes
        + [
            jax.ShapeDtypeStruct((8, width), F32),
            jax.ShapeDtypeStruct((groups, late_rows, width), BF),
        ],
        compiler_params=params(),
        name="entry",
    )(tile_len, source, count, index, *grads, start, grad_middle, w["heads_weight"], vectors)
    outs = (long_out, short_out, long_grad, short_grad)
    return outs, (guest_out, guest_grad), early, late, vector, entry_vector


def bit_of(number, bit):
    return lax.rem(number // (1 << bit), 2)


def reduce_plan(peers, early_rows, late_rows):
    bits = peers.bit_length() - 1
    forward = list(range(bits))
    swapped = forward[1::-1] + forward[2:]
    last = forward[2:] + forward[:2]
    pieces = []
    for source, rows in ((0, early_rows), (1, late_rows)):
        unit = 16
        units = rows // 2 // unit
        begin = 0
        for sub in range(2):
            here = units // 2 + (1 if sub < units % 2 else 0)
            first = int(here * 0.4 + 0.5)
            for order, parts in zip((forward, swapped, last), (first, first, here - 2 * first)):
                if parts > 0:
                    pieces.append((source * 2 + sub, source, begin, parts * unit, tuple(order)))
                    begin += parts * unit
    return pieces


def reduce_kernel(
    peers, halves, pieces, early, late, vector, entry_vector, early_out, late_out, vector_out, *scratch
):
    bits = peers.bit_length() - 1
    amount = len(pieces)
    kept = scratch[:amount]
    mates = scratch[amount : 2 * amount]
    mine_in = scratch[2 * amount : 3 * amount]
    landed = [scratch[3 * amount + k * bits : 3 * amount + (k + 1) * bits] for k in range(amount)]
    (
        vector_land, mate_send, mate_recv, load_sem, hop_send, hop_recv, end_send, end_recv, end_load,
        vector_send, vector_recv,
    ) = scratch[3 * amount + amount * bits :]
    d = lax.axis_index("dp")
    r = lax.axis_index("rep")
    other = 1 - r
    mate = (d, other)
    partner = [(d + (1 - 2 * bit_of(d, bit)) * (1 << bit), r) for bit in range(bits)]
    sources = (early, late)
    outs = (early_out, late_out)
    barrier = pltpu.get_barrier_semaphore()
    for device in [mate] + partner:
        pl.semaphore_signal(barrier, inc=1, device_id=device, device_id_type=pl.DeviceIdType.MESH)
    pl.semaphore_wait(barrier, bits + 1)

    def remote(source, target, send, recv, device):
        copy = pltpu.make_async_remote_copy(
            src_ref=source, dst_ref=target, send_sem=send, recv_sem=recv,
            device_id=device, device_id_type=pl.DeviceIdType.MESH,
        )
        copy.start()
        return copy

    def rows_at(source, core, begin, rows):
        return pl.ds(pl.multiple_of(core * halves[source] + begin, 16), rows)

    wide = vector.shape[1]
    vector_out[:, :wide] = vector[...]
    vector_out[:, wide:] = entry_vector[...]
    mate_copies = []
    loads = []
    for k, (_, source, begin, rows, order) in enumerate(pieces):
        mate_copies.append(
            remote(
                sources[source].at[:, rows_at(source, other, begin, rows), :], mates[k],
                mate_send.at[k], mate_recv.at[k], mate,
            )
        )
        load = pltpu.make_async_copy(
            sources[source].at[:, rows_at(source, r, begin, rows), :], mine_in[k], load_sem.at[k]
        )
        load.start()
        loads.append(load)

    hops = {}
    ends = []

    def base_at(order, stage):
        base = 0
        for place in range(stage):
            base = base + bit_of(d, order[place]) * (1 << (bits - 1 - place))
        return base

    def send(k, stage):
        _, source, begin, rows, order = pieces[k]
        if stage == bits:
            result = kept[k].at[base_at(order, bits)]
            where = rows_at(source, r, begin, rows)
            ends.append(remote(result, outs[source].at[where, :], end_send.at[k], end_recv.at[k], mate))
            own = pltpu.make_async_copy(result, outs[source].at[where, :], end_load.at[k])
            own.start()
            ends.append(own)
            return
        size = 1 << (bits - 1 - stage)
        first = base_at(order, stage) + (1 - bit_of(d, order[stage])) * size
        hops[k, stage] = remote(
            kept[k].at[pl.ds(first, size)], landed[k][stage], hop_send.at[k, stage], hop_recv.at[k, stage],
            partner[order[stage]],
        )

    def join(k):
        order = pieces[k][4]
        loads[k].wait()
        mate_copies[k].wait_recv()

        def add(chunk, carry):
            place = 0
            for step in range(bits):
                place = place + bit_of(chunk, order[step]) * (1 << (bits - 1 - step))
            kept[k][place] = mine_in[k][chunk] + mates[k][chunk]
            return carry

        lax.fori_loop(0, peers, add, 0)

    def gather(k, stage):
        order = pieces[k][4]
        hops[k, stage].wait_recv()
        base = base_at(order, stage + 1)

        def add(chunk, carry):
            kept[k][base + chunk] = kept[k][base + chunk] + landed[k][stage][chunk]
            return carry

        lax.fori_loop(0, 1 << (bits - 1 - stage), add, 0)

    events = sorted(
        (stage + pieces[k][0], -stage, k) for k in range(amount) for stage in range(bits + 1)
    )
    vector_copies = []

    def vector_step(stage):
        if stage > 0:
            vector_copies[-1].wait()
            vector_out[...] = vector_out[...] + vector_land[stage - 1]
        if stage <= bits:
            device = mate if stage == 0 else partner[stage - 1]
            vector_copies.append(
                remote(vector_out, vector_land.at[stage], vector_send.at[stage], vector_recv.at[stage], device)
            )

    seen = -1
    for time, negative, k in events:
        if time != seen:
            if time <= bits + 1:
                vector_step(time)
            seen = time
        stage = -negative
        if stage == 0:
            join(k)
        else:
            gather(k, stage - 1)
        send(k, stage)
    for copy in mate_copies + list(hops.values()):
        copy.wait_send()
    for copy in ends:
        copy.wait()


def reduce_all(early, late, vector, entry_vector):
    joined = (vector.shape[0], vector.shape[1] + entry_vector.shape[1])
    peers, early_rows, width = early.shape
    late_rows = late.shape[1]
    bits = peers.bit_length() - 1
    pieces = reduce_plan(peers, early_rows, late_rows)
    amount = len(pieces)
    scratch = [pltpu.VMEM((peers, rows, width), BF) for _, _, _, rows, _ in pieces] * 3
    for _, _, _, rows, _ in pieces:
        for stage in range(bits):
            scratch.append(pltpu.VMEM((1 << (bits - 1 - stage), rows, width), BF))
    scratch.append(pltpu.VMEM((bits + 1,) + joined, F32))
    one = pltpu.SemaphoreType.DMA((amount,))
    many = pltpu.SemaphoreType.DMA((amount, bits))
    few = pltpu.SemaphoreType.DMA((bits + 1,))
    scratch += [one, one, one, many, many, one, one, one, few, few]
    anywhere = pl.BlockSpec(memory_space=pl.ANY)
    near = pl.BlockSpec(memory_space=pltpu.VMEM)
    return pl.pallas_call(
        partial(reduce_kernel, peers, (early_rows // 2, late_rows // 2), pieces),
        in_specs=[anywhere, anywhere, near, near],
        out_specs=[anywhere, anywhere, near],
        out_shape=[
            jax.ShapeDtypeStruct((early_rows, width), BF),
            jax.ShapeDtypeStruct((late_rows, width), BF),
            jax.ShapeDtypeStruct(joined, F32),
        ],
        scratch_shapes=scratch,
        compiler_params=pltpu.CompilerParams(
            vmem_limit_bytes=VMEM_LIMIT, collective_id=0, has_side_effects=True
        ),
        name="reduce",
    )(early, late, vector, entry_vector)


def unpack(early, late, unit_rows, kept, teach, pieces):
    width = early.shape[1]
    deep = pieces * unit_rows

    def beside(held, first, count):
        return jnp.concatenate(
            [held[first + k * unit_rows : first + (k + 1) * unit_rows] for k in range(count)], axis=1
        )

    extra = teach - width
    third = unit_rows * extra // width
    begin = 2 * deep + 2 * unit_rows
    tail = early[begin : begin + third]
    tail = jnp.concatenate([tail[:, k * extra : (k + 1) * extra] for k in range(width // extra)], axis=0)
    return {
        "down_weight": early[:deep],
        "up_weight": beside(early, deep, pieces),
        "out_weight": early[2 * deep : 2 * deep + unit_rows],
        "align_weight": jnp.concatenate([early[2 * deep + unit_rows : begin], tail], axis=1),
        "position": late[:kept],
        "heads_weight": beside(late, late.shape[0] - 3 * unit_rows, 3),
    }


def shards(
    long_clips,
    short_clips,
    long_index,
    short_index,
    long_length,
    short_length,
    destination,
    long_target,
    short_target,
    position,
    mixer_gain,
    mixer_shift,
    heads_weight,
    query_bias,
    value_bias,
    out_weight,
    out_bias,
    dense_gain,
    dense_shift,
    up_weight,
    up_bias,
    down_weight,
    down_bias,
    align_weight,
    align_bias,
):
    peers = lax.axis_size("dp")
    copies = lax.axis_size("rep")
    micros, _, long_rows, width = long_clips.shape
    home_slots, tile = short_clips.shape[1:3]
    bal_slots = home_slots // 2
    slots = micros * home_slots
    wide = up_weight.shape[1]
    teach = long_target.shape[-1]
    patches = position.shape[0]
    weights = dict(
        zip(
            WEIGHT_NAMES,
            (
                position, mixer_gain, mixer_shift, heads_weight, query_bias, value_bias, out_weight, out_bias,
                dense_gain, dense_shift, up_weight, up_bias, down_weight, down_bias, align_weight, align_bias,
            ),
        )
    )
    scalars = pl.BlockSpec(memory_space=pltpu.SMEM)
    anywhere = pl.BlockSpec(memory_space=pl.ANY)
    clips = micros + 1
    tile_total = clips * long_rows // tile + slots
    near = pl.BlockSpec(memory_space=pltpu.VMEM)
    pairs = [(core, (core + 1) % copies) for core in range(copies)]

    def trade(value):
        return lax.ppermute(value, "rep", pairs)

    lengths = long_length.reshape(-1)
    facts = trade(jnp.concatenate([long_index[-1].reshape(-1), lengths]))
    guest_rows = trade(long_clips[-1, 0])
    guest_target = trade(long_target[-1, 0])
    tile_len, source, count, work, vectors, up_b, align_b = pl.pallas_call(
        partial(plan_kernel, tile, long_rows, home_slots, copies),
        in_specs=[scalars] * 3 + [near] * len(SMALL_NAMES),
        out_specs=[scalars] * 4 + [near] * 3,
        out_shape=[
            jax.ShapeDtypeStruct((tile_total,), jnp.int32),
            jax.ShapeDtypeStruct((tile_total,), jnp.int32),
            jax.ShapeDtypeStruct((2 * clips + 5,), jnp.int32),
            jax.ShapeDtypeStruct((clips,), jnp.int32),
            jax.ShapeDtypeStruct((len(SMALL_NAMES) - 2, width), F32),
            jax.ShapeDtypeStruct((1, wide), F32),
            jax.ShapeDtypeStruct((1, teach), F32),
        ],
        name="plan",
    )(long_length, facts[long_rows:], short_length, *[weights[name] for name in SMALL_NAMES])
    index = jnp.concatenate([long_index.reshape(-1), short_index.reshape(-1), facts[:long_rows]])
    groups = peers if copies == 2 and width % (16 * peers) == 0 else 1
    outs, guests, early, late, vector, entry_vector = run_block(
        (long_clips.reshape(-1, width), short_clips.reshape(-1, width), guest_rows), index,
        (long_target.reshape(-1, teach), short_target.reshape(-1, teach), guest_target),
        tile_len, source, count, work, tile, long_rows, micros, weights, groups, vectors, up_b, align_b,
    )
    long_out, short_out, long_grad, short_grad = outs
    out_back, grad_back = [trade(value) for value in guests]
    send = pl.pallas_call(
        partial(send_kernel, home_slots, copies),
        in_specs=[scalars, scalars, whole((slots, tile, width))],
        out_specs=pl.BlockSpec(memory_space=pltpu.VMEM) if groups == peers else scalars,
        out_shape=jax.ShapeDtypeStruct((peers, micros, tile, width), BF),
        compiler_params=params(),
        name="send",
    )(short_length, destination, short_out.reshape(slots, tile, width)) if groups == peers else send_all(
        short_length, destination, short_out.reshape(slots, tile, width), peers, copies, home_slots
    )
    got = lax.all_to_all(send, "dp", split_axis=0, concat_axis=0, tiled=True)
    unit_rows = width // peers
    if groups == peers:
        early, late, vector = reduce_all(early, late, vector, entry_vector)
    else:
        matrices = unpack(early[0], late[0], width, patches, teach, wide // width)
        early, late = share_out(matrices, peers, copies, unit_rows, wide // width)
        vector = lax.psum(jnp.concatenate([vector, entry_vector], axis=1), ("dp", "rep"))
    near = pl.BlockSpec(memory_space=pltpu.VMEM)
    outs = pl.pallas_call(
        partial(finish_kernel, home_slots, copies, 2 * clips + 3),
        in_specs=[scalars, scalars, scalars, anywhere, near, near, near] + [anywhere] * 4,
        out_specs=[near] * 17 + [anywhere] * 2,
        input_output_aliases={7: 17, 9: 18},
        out_shape=[
            jax.ShapeDtypeStruct((micros, bal_slots, tile, width), BF),
            jax.ShapeDtypeStruct((patches // peers, width), F32),
            jax.ShapeDtypeStruct((unit_rows, 3 * width), F32),
            jax.ShapeDtypeStruct((unit_rows, width), F32),
            jax.ShapeDtypeStruct((unit_rows, wide), F32),
            jax.ShapeDtypeStruct((wide // peers, width), F32),
            jax.ShapeDtypeStruct((unit_rows, teach), F32),
        ]
        + [jax.ShapeDtypeStruct((1, unit_rows), F32)] * 8
        + [jax.ShapeDtypeStruct((1, wide // peers), F32), jax.ShapeDtypeStruct((1, teach // peers), F32)]
        + [jax.ShapeDtypeStruct(long_out.shape, BF)] * 2,
        scratch_shapes=[
            pltpu.VMEM((2, long_rows, width), BF),
            pltpu.SemaphoreType.DMA((2,)),
            pltpu.SemaphoreType.DMA((micros * bal_slots,)),
        ],
        compiler_params=params(),
        name="finish",
    )(short_length, destination, count, got, early, late, vector, long_out, out_back, long_grad, grad_back)
    short_bal, position_g, heads_g, out_g, up_g, down_g, align_g = outs[:7]
    shared = {
        "position": position_g, "heads_weight": heads_g, "out_weight": out_g, "up_weight": up_g,
        "down_weight": down_g, "align_weight": align_g,
    }
    long_out, long_grad = outs[17:]
    order = (
        "out_bias", "dense_gain", "dense_shift", "down_bias", "query_bias", "mixer_gain", "value_bias",
        "mixer_shift", "up_bias", "align_bias",
    )
    for name, value in zip(order, outs[7:17]):
        shared[name] = value.reshape(-1)
    return (
        long_out.reshape(micros, 1, long_rows, width),
        short_bal,
        long_grad.reshape(micros, 1, long_rows, width),
        short_grad.reshape(micros, home_slots, tile, width),
    ) + tuple(shared[name] for name in WEIGHT_NAMES)


def send_all(short_length, destination, shown, peers, copies, home):
    micros = short_length.shape[0]
    mine = lax.axis_index("dp") * copies + lax.axis_index("rep")

    def own(table):
        table = table.reshape(micros, peers * copies, home)
        return lax.dynamic_index_in_dim(table, mine, 1, keepdims=False)

    wanted = (own(destination)[None] == jnp.arange(peers)[:, None, None]) & (own(short_length)[None] > 0)
    shown = shown.reshape((micros, home) + shown.shape[1:])
    return jnp.einsum("pmj,mjtd->pmtd", wanted.astype(BF), shown)


def share_out(matrices, peers, copies, unit_rows, pieces):
    shared = {}
    for name, piece in matrices.items():
        rows = piece.shape[0] // peers
        padded = -(-rows // (8 * copies)) * 8 * copies
        if padded != rows:
            piece = piece.reshape(peers, rows, -1)
            piece = jnp.pad(piece, ((0, 0), (0, padded - rows), (0, 0)))
            piece = piece.reshape(peers * padded, -1)
        piece = lax.psum_scatter(piece, ("dp", "rep"), scatter_dimension=0, tiled=True)
        shared[name] = lax.all_gather(piece, "rep", axis=0, tiled=True)[:rows]
    width = shared["out_weight"].shape[1]
    up = shared["up_weight"].reshape(unit_rows, pieces, width).transpose(1, 0, 2).reshape(-1, width)
    heads = shared["heads_weight"].reshape(unit_rows, 3, width).transpose(1, 0, 2).reshape(-1, width)
    align = shared["align_weight"]
    extra = align.shape[1] - width
    parts = width // extra
    tail = align[:, width:].reshape(parts, unit_rows // parts, extra).transpose(1, 0, 2).reshape(-1, width)
    early = jnp.concatenate([shared["down_weight"], up, shared["out_weight"], align[:, :width], tail], axis=0)
    return early, jnp.concatenate([shared["position"], heads], axis=0)


def solution(mesh):
    placed = (
        P(None, ("dp", "rep"), None, None),
        P(None, ("dp", "rep"), None, None),
        P(None, ("dp", "rep"), None),
        P(None, ("dp", "rep"), None),
        P(None, ("dp", "rep")),
        P(),
        P(),
        P(None, ("dp", "rep"), None, None),
        P(None, ("dp", "rep"), None, None),
        P(),
        P(),
        P(),
        P(),
        P(),
        P(),
        P(),
        P(),
        P(),
        P(),
        P(),
        P(),
        P(),
        P(),
        P(),
        P(),
    )
    return jax.shard_map(
        shards,
        mesh=mesh,
        in_specs=placed,
        out_specs=(
            P(None, ("dp", "rep"), None, None),
            P(None, ("dp", "rep"), None, None),
            P(None, ("dp", "rep"), None, None),
            P(None, ("dp", "rep"), None, None),
            P("dp", None),
            P("dp"),
            P("dp"),
            P("dp", None),
            P("dp"),
            P("dp"),
            P("dp", None),
            P("dp"),
            P("dp"),
            P("dp"),
            P("dp", None),
            P("dp"),
            P("dp", None),
            P("dp"),
            P("dp", None),
            P("dp"),
        ),
        check_vma=False,
    )
```

```python
from functools import partial

import jax
import jax.numpy as jnp
from jax import lax
from jax.experimental import pallas as pl
from jax.experimental.pallas import tpu as pltpu
from jax.sharding import PartitionSpec as P

HEADS = 12
EPS = 1e-06
MASKED = -1000000000.0
WEIGHT_NAMES = (
    "position",
    "mixer_gain",
    "mixer_shift",
    "heads_weight",
    "query_bias",
    "value_bias",
    "out_weight",
    "out_bias",
    "dense_gain",
    "dense_shift",
    "up_weight",
    "up_bias",
    "down_weight",
    "down_bias",
    "align_weight",
    "align_bias",
)


BLOCK = 256
BF = jnp.bfloat16
F32 = jnp.float32
VMEM_LIMIT = 66_000_000


def dot(left, right, dims):
    return lax.dot_general(left, right, ((dims[:1], dims[1:]), ((), ())), preferred_element_type=F32)


def centre(values):
    mean = jnp.mean(values, axis=-1, keepdims=True)
    centered = values - mean
    spread = jnp.mean(centered * centered, axis=-1, keepdims=True)
    inverse = lax.rsqrt(spread + EPS)
    return centered * inverse, inverse


def centre_back(grad, unit, inverse):
    first = jnp.mean(grad, axis=-1, keepdims=True)
    second = jnp.mean(grad * unit, axis=-1, keepdims=True)
    return inverse * (grad - first - unit * second)


def valid_rows(tile_len, block, tile):
    row = lax.broadcasted_iota(jnp.int32, (BLOCK, 1), 0)
    parts = BLOCK // tile
    limit = tile_len[block * parts]
    for part in range(1, parts):
        limit = jnp.where(row >= part * tile, tile_len[block * parts + part], limit)
    return lax.rem(row, tile) < limit


def clip_cost(length):
    blocks = lax.div(length + BLOCK - 1, BLOCK)
    return 2 * lax.div(length + 127, 128) + blocks * blocks


def plan_kernel(tile, long_rows, home, copies, lengths, guest, short_len, *refs):
    amount = len(refs) - 7
    small, (tile_len, source, count, work, vectors, up_out, align_out) = refs[:amount], refs[amount:]
    for number, value in enumerate(small[:-2]):
        vectors[number : number + 1, :] = value[...].reshape(1, -1)
    up_out[...] = small[-2][...].reshape(1, -1)
    align_out[...] = small[-1][...].reshape(1, -1)
    micros = lengths.shape[0]
    slots = micros * home
    per = long_rows // tile
    step = 128 // tile
    d, r = lax.axis_index("dp"), lax.axis_index("rep")
    base = (d * copies + r) * home
    other = (d * copies + lax.rem(r + 1, copies)) * home

    def put(place, origin, size):
        source[place] = origin
        tile_len[place] = size

    mine, theirs = jnp.int32(0), jnp.int32(0)
    for slot in range(slots):
        mine = mine + jnp.where(short_len[slot // home, base + slot % home] > 0, 1, 0)
        theirs = theirs + jnp.where(short_len[slot // home, other + slot % home] > 0, 1, 0)
    for micro in range(micros - 1):
        mine = mine + clip_cost(lengths[micro, 0])
        theirs = theirs + clip_cost(guest[micro])
    held, offered = clip_cost(lengths[micros - 1, 0]), clip_cost(guest[micros - 1])
    base0, base1 = jnp.where(r == 0, mine, theirs), jnp.where(r == 0, theirs, mine)
    last0, last1 = jnp.where(r == 0, held, offered), jnp.where(r == 0, offered, held)
    best = jnp.maximum(base0 + last0, base1 + last1)
    choice = jnp.int32(0)
    plans = (
        jnp.maximum(base0 + last1, base1 + last0),
        jnp.maximum(base0, base1 + last0 + last1),
        jnp.maximum(base0 + last0 + last1, base1),
    )
    for number, cost in enumerate(plans):
        better = cost + 1 < best
        choice = jnp.where(better, number + 1, choice)
        best = jnp.where(better, cost, best)
    gives = choice == jnp.where(r == 0, 2, 3)
    takes = choice == jnp.where(r == 0, 3, 2)
    swaps = choice == 1
    clips = micros + 1
    count[2 * clips + 3] = (gives | swaps).astype(jnp.int32)
    place = jnp.int32(0)
    taken = []
    origins = []
    needed = [jnp.int32(per)] * (micros - 1) + [
        jnp.where(gives | swaps, 0, per), jnp.where(takes | swaps, per, 0)
    ]
    for number in range(clips):
        if number < micros - 1:
            length, origin = lengths[number, 0], number * per
        elif number == micros - 1:
            length, origin = jnp.where(gives | swaps, 0, lengths[number, 0]), number * per
        else:
            length, origin = jnp.where(takes | swaps, guest[micros - 1], 0), micros * per + slots
        origins.append(origin)
        work[number] = length
        some = lax.div(length + 127, 128) * step
        count[number] = lax.div(length + BLOCK - 1, BLOCK)
        count[clips + 1 + number] = place

        def add(index, carry, origin=origin, length=length, place=place):
            put(place + index, origin + index, jnp.clip(length - index * tile, 0, tile))
            return carry

        lax.fori_loop(0, some, add, 0)
        taken.append(some)
        place = place + some
    first = place
    sizes = [short_len[slot // home, base + slot % home] for slot in range(slots)]
    for wanted in (True, False):
        for slot, size in enumerate(sizes):
            fits = (size > 0) if wanted else (size <= 0)

            @pl.when(fits)
            def _():
                put(place, micros * per + slot, size)

            place = place + jnp.where(fits, 1, 0)
        if wanted:
            parts = BLOCK // tile
            count[clips] = lax.div(place - first + parts - 1, parts)
            count[2 * clips + 1] = first
            count[2 * clips + 2] = lax.div(place + parts - 1, parts)
    for number in range(clips):
        def fill(index, carry, origin=origins[number], place=place - taken[number]):
            put(place + index, origin + index, 0)
            return carry

        whole = needed[number]
        lax.fori_loop(taken[number], whole, fill, 0)
        place = place + whole - taken[number]
    parts = BLOCK // tile
    count[2 * clips + 4] = lax.div(place + parts - 1, parts)


def pieced(step, source, parts, border, refs):
    low, high = border
    chosen = []
    for part in range(parts):
        origin = source[step * parts + part]
        far = jnp.where(origin < high, refs[parts + part][...], refs[2 * parts + part][...])
        chosen.append(jnp.where(origin < low, refs[part][...], far))
    return jnp.concatenate(chosen, axis=0).astype(F32)


def put_tiles(step, until, value, source, border, tile, stage, sem, near, far, guest):
    low, high = border
    parts = BLOCK // tile
    slot = lax.rem(step, 2)

    def settle(which):
        for part in range(parts):
            pltpu.make_async_copy(
                stage.at[which, pl.ds(part * tile, tile), :], near.at[pl.ds(0, tile), :], sem.at[which, part]
            ).wait()

    @pl.when(step >= 2)
    def _():
        settle(slot)

    stage[slot] = value
    for part in range(parts):
        origin = source[step * parts + part]
        view = stage.at[slot, pl.ds(part * tile, tile), :]

        def push(target, first, view=view, part=part, origin=origin):
            where = pl.ds(pl.multiple_of((origin - first) * tile, tile), tile)
            pltpu.make_async_copy(view, target.at[where, :], sem.at[slot, part]).start()

        @pl.when(origin < low)
        def _():
            push(near, 0)

        @pl.when((origin >= low) & (origin < high))
        def _():
            push(far, low)

        @pl.when(origin >= high)
        def _():
            push(guest, high)

    @pl.when(step == until - 1)
    def _():
        settle(1 - slot)
        settle(slot)


def project_kernel(tile, border, last, tile_len, source, count, index, *refs):
    parts = BLOCK // tile
    table_any, weight_any, vectors, out, start_out, table, stage, rows, weight, weight_sem, sem = refs[3 * parts :]
    step = pl.program_id(0)
    width = weight.shape[0]
    depth, chunk = stage.shape[:2]
    chunks = table.shape[0] // chunk

    def fetch(number):
        return pltpu.make_async_copy(
            table_any.at[pl.ds(pl.multiple_of(number * chunk, 16), chunk), :],
            stage.at[lax.rem(number, depth)],
            sem.at[lax.rem(number, depth)],
        )

    @pl.when(step == 0)
    def _():
        for number in range(depth):
            fetch(number).start()
        weight_load = pltpu.make_async_copy(weight_any, weight, weight_sem.at[0])
        weight_load.start()
        rows[...] = jnp.zeros_like(rows)

        def load(number, carry):
            fetch(number).wait()
            table[pl.ds(pl.multiple_of(number * chunk, 16), chunk), :] = stage[lax.rem(number, depth)].astype(F32)

            @pl.when(number + depth < chunks)
            def _():
                fetch(number + depth).start()

            return carry

        lax.fori_loop(0, chunks, load, 0)
        weight_load.wait()

    @pl.when(step == count[last])
    def _():
        out[...] = jnp.zeros_like(out)

    @pl.when(step < count[last])
    def _():
        def gather(part, carry):
            origin = source[step * parts + part] * tile
            first = part * tile

            def some(group, inner):
                base = pl.multiple_of(first + group * 8, 8)
                for row in range(8):
                    place = index[origin + group * 8 + row]
                    rows[pl.ds(base + row, 1), :] = table[pl.ds(place, 1), :]
                return inner

            lax.fori_loop(0, lax.div(tile_len[step * parts + part] + 7, 8), some, 0)
            return carry

        lax.fori_loop(0, parts, gather, 0)
        start = pieced(step, source, parts, border, refs) + rows[...]
        start_out[...] = start
        unit, _ = centre(start)
        normed = (unit * vectors[0:1, :width] + vectors[1:2, :width]).astype(BF)
        for part in range(3):
            cols = slice(part * width, (part + 1) * width)
            triple = dot(normed, weight[:, cols], (1, 0))
            if part == 0:
                triple = (triple + vectors[2:3, :width]).astype(BF) * BF(0.125)
            elif part == 1:
                triple = triple.astype(BF)
            else:
                triple = (triple + vectors[3:4, :width]).astype(BF)
            out[cols, :] = triple.T


def masked_tile(tile_scores, limit):
    key = lax.broadcasted_iota(jnp.int32, tile_scores.shape, 0)
    return jnp.where(key < limit, tile_scores, MASKED)


def block_mask(tile_len, first, tile):
    key = lax.broadcasted_iota(jnp.int32, (BLOCK, BLOCK), 0)
    asked = lax.broadcasted_iota(jnp.int32, (BLOCK, BLOCK), 1)
    limit = tile_len[first]
    for part in range(1, BLOCK // tile):
        limit = jnp.where(key >= part * tile, tile_len[first + part], limit)
    return (key // tile == asked // tile) & (lax.rem(key, tile) < limit)


def attend_kernel(tile, long_rows, clips, tile_len, length, count, query, keys, values, out, logsum, even, odd):
    head_dim = query.shape[0] // 2
    most = long_rows // BLOCK
    boards = (even, odd)

    def score(head, column, first, size, fix):
        lanes = slice(head * head_dim, (head + 1) * head_dim)
        asked = query[lanes, pl.ds(column, BLOCK)]
        for number in range(size):
            part = dot(keys[lanes, pl.ds(first + number * BLOCK, BLOCK)], asked, (0, 0))
            if number == size - 1:
                part = fix(part)
            boards[head][number * BLOCK : (number + 1) * BLOCK, :] = part

    def finish(head, column, first, size):
        lanes = slice(head * head_dim, (head + 1) * head_dim)
        board = boards[head]
        top = jnp.max(board[: size * BLOCK, :], axis=0, keepdims=True)
        total = None
        gathered = None
        for number in range(size):
            weight = jnp.exp(board[number * BLOCK : (number + 1) * BLOCK, :] - top)
            part = jnp.sum(weight, axis=0, keepdims=True)
            held = values[lanes, pl.ds(first + number * BLOCK, BLOCK)]
            term = dot(held, weight.astype(BF), (1, 0))
            total = part if total is None else total + part
            gathered = term if gathered is None else gathered + term
        out[lanes, pl.ds(column, BLOCK)] = (gathered / total).astype(BF)
        logsum[0, pl.ds(head, 1), pl.ds(column, BLOCK)] = top + jnp.log(total)

    def rows(first, size, fix):
        def at(block):
            return pl.multiple_of(first + block * BLOCK, 128)

        score(0, at(0), first, size, fix)

        def ask(block, carry):
            score(1, at(block), first, size, fix)
            finish(0, at(block), first, size)
            score(0, at(jnp.minimum(block + 1, size - 1)), first, size, fix)
            finish(1, at(block), first, size)
            return carry

        lax.fori_loop(0, size, ask, 0)

    def clip(number, carry):
        first = pl.multiple_of(count[clips + 1 + number] * tile, 128)
        blocks = count[number]
        rest = length[number]
        for size in range(1, most + 1):
            @pl.when(blocks == size)
            def _():
                rows(first, size, lambda part: masked_tile(part, rest - (size - 1) * BLOCK))
        return carry

    out[...] = jnp.zeros_like(out)
    lax.fori_loop(0, clips, clip, 0)

    def short(number, carry):
        begin = count[2 * clips + 1] + number * (BLOCK // tile)
        column = pl.multiple_of(begin * tile, 128)
        allowed = block_mask(tile_len, begin, tile)
        rows(column, 1, lambda part: jnp.where(allowed, part, MASKED))
        return carry

    lax.fori_loop(0, count[clips], short, 0)


def attend_back_kernel(
    tile, long_rows, clips, tile_len, length, count, query, keys, values, grad, logsum,
    query_out, key_out, value_out, key_sum, value_sum, even, odd, even_back, odd_back,
):
    head_dim = query.shape[0] // 2
    most = long_rows // BLOCK
    boards = (even, odd)
    backs = (even_back, odd_back)

    def score(head, column, first, size, fix):
        lanes = slice(head * head_dim, (head + 1) * head_dim)
        asked = query[lanes, pl.ds(column, BLOCK)]
        pulled = grad[lanes, pl.ds(column, BLOCK)]
        for number in range(size):
            here = pl.ds(first + number * BLOCK, BLOCK)
            there = slice(number * BLOCK, (number + 1) * BLOCK)
            part = dot(keys[lanes, here], asked, (0, 0))
            if number == size - 1:
                part = fix(part)
            boards[head][there, :] = part
            backs[head][there, :] = dot(values[lanes, here], pulled, (0, 0))

    def finish(head, column, first, size, limit):
        lanes = slice(head * head_dim, (head + 1) * head_dim)
        asked = query[lanes, pl.ds(column, BLOCK)]
        pulled = grad[lanes, pl.ds(column, BLOCK)]
        own = lax.broadcasted_iota(jnp.int32, (1, BLOCK), 1) < limit
        base = jnp.where(own, logsum[0, pl.ds(head, 1), pl.ds(column, BLOCK)], -1e3 * MASKED)
        inner = None
        for number in range(size):
            there = slice(number * BLOCK, (number + 1) * BLOCK)
            prob = jnp.exp(boards[head][there, :] - base)
            boards[head][there, :] = prob
            part = jnp.sum(prob * backs[head][there, :], axis=0, keepdims=True)
            inner = part if inner is None else inner + part
            value_sum[lanes, there] += dot(pulled, prob.astype(BF), (1, 1))
        query_sum = None
        for number in range(size):
            here = pl.ds(first + number * BLOCK, BLOCK)
            there = slice(number * BLOCK, (number + 1) * BLOCK)
            moved = (boards[head][there, :] * (backs[head][there, :] - inner)).astype(BF)
            key_sum[lanes, there] += dot(asked, moved, (1, 1))
            term = dot(keys[lanes, here], moved, (1, 0))
            query_sum = term if query_sum is None else query_sum + term
        query_out[lanes, pl.ds(column, BLOCK)] = (query_sum * 0.125).astype(BF)

    def rows(first, size, fix, rest):
        def at(block):
            return pl.multiple_of(first + block * BLOCK, 128)

        key_sum[:, : size * BLOCK] = jnp.zeros((2 * head_dim, size * BLOCK), F32)
        value_sum[:, : size * BLOCK] = jnp.zeros((2 * head_dim, size * BLOCK), F32)
        score(0, at(0), first, size, fix)

        def ask(block, carry):
            limit = rest - block * BLOCK
            after = jnp.minimum(block + 1, size - 1)
            score(1, at(block), first, size, fix)
            finish(0, at(block), first, size, limit)
            score(0, at(after), first, size, fix)
            finish(1, at(block), first, size, limit)
            return carry

        lax.fori_loop(0, size, ask, 0)
        key_out[:, pl.ds(first, size * BLOCK)] = key_sum[:, : size * BLOCK].astype(BF)
        value_out[:, pl.ds(first, size * BLOCK)] = value_sum[:, : size * BLOCK].astype(BF)

    def clip(number, carry):
        first = pl.multiple_of(count[clips + 1 + number] * tile, 128)
        blocks = count[number]
        rest = length[number]
        for size in range(1, most + 1):
            @pl.when(blocks == size)
            def _():
                rows(first, size, lambda part: masked_tile(part, rest - (size - 1) * BLOCK), rest)
        return carry

    for empty in (query_out, key_out, value_out):
        empty[...] = jnp.zeros_like(empty)
    lax.fori_loop(0, clips, clip, 0)

    def short(number, carry):
        begin = count[2 * clips + 1] + number * (BLOCK // tile)
        column = pl.multiple_of(begin * tile, 128)
        allowed = block_mask(tile_len, begin, tile)
        rows(column, 1, lambda part: jnp.where(allowed, part, MASKED), BLOCK)
        return carry

    lax.fori_loop(0, count[clips], short, 0)


def gelu_both(upper):
    spread = 0.5 * (1.0 + lax.erf(upper * 0.7071067811865476))
    bell = jnp.exp(-0.5 * upper * upper) * 0.3989422804014327
    return upper * spread, spread + upper * bell


def write_out(entries):
    waiting = {}
    counts = {}
    for source, stage, sem, target in entries:
        key = id(stage)
        slot = counts.get(key, 0) % stage.shape[0]
        counts[key] = counts.get(key, 0) + 1
        if (key, slot) in waiting:
            waiting[key, slot].wait()
        value = source()
        view = stage.at[slot, :, : value.shape[1], : value.shape[2]]
        stage[slot, :, : value.shape[1], : value.shape[2]] = value.astype(BF)
        copy = pltpu.make_async_copy(view, target, sem.at[slot])
        copy.start()
        waiting[key, slot] = copy
    for copy in waiting.values():
        copy.wait()


def middle_kernel(tile, border, last, tile_len, source, count, attended_t, start_in, *refs):
    parts = BLOCK // tile
    (
        out_any, up_any, down_any, align_any, vectors, up_b, align_b,
        long_out, short_out, guest_out, pull_out, grad_out, vector_out, sums_out,
        out_acc, up_acc, down_acc, align_acc, hidden, slope, stage, stage_down,
        out_w, up_w, down_w, align_w, weight_sem, down_sem, show, show_sem, sem,
    ) = refs[3 * parts :]
    step = pl.program_id(0)
    width = out_w.shape[0]
    wide = up_w.shape[1]
    teach = align_w.shape[1]
    pieces = wide // width
    live = step < count[last]
    loads = [
        pltpu.make_async_copy(source_ref, target, weight_sem.at[number])
        for number, (source_ref, target) in enumerate(
            ((out_any, out_w), (up_any, up_w), (down_any, down_w), (align_any, align_w))
        )
    ]

    @pl.when(step == 0)
    def _():
        for load in loads:
            load.start()
        for acc in (out_acc, up_acc, down_acc, align_acc):
            acc[...] = jnp.zeros_like(acc)
        vector_out[...] = jnp.zeros_like(vector_out)
        loads[0].wait()

    def put(value):
        put_tiles(step, count[last + 2], value, source, border, tile, show, show_sem, long_out, short_out, guest_out)

    def add_vector(row, value):
        size = value.shape[1]
        vector_out[row : row + 1, :size] += value

    def over_rows(value):
        return jnp.sum(value, axis=0, keepdims=True)

    @pl.when(step == count[last])
    def _():
        pull_out[...] = jnp.zeros_like(pull_out)

    @pl.when(jnp.logical_not(live) & (step < count[last + 2]))
    def _():
        put(jnp.zeros((BLOCK, width), BF))

    @pl.when(live)
    def _():
        ok = valid_rows(tile_len, step, tile)
        across = attended_t[...]
        middle = start_in[...] + dot(across, out_w[...], (0, 0)) + vectors[4:5, :width]
        unit, inverse = centre(middle)
        dense = (unit * vectors[5:6, :width] + vectors[6:7, :width]).astype(BF)
        result = middle + vectors[7:8, :width]

        @pl.when(step == 0)
        def _():
            for load in loads[1:]:
                load.wait()

        for piece in range(pieces):
            cols = slice(piece * width, (piece + 1) * width)
            upper = dot(dense, up_w[:, cols], (1, 0)) + up_b[:, cols]
            bent, tilt = gelu_both(upper)
            low = bent.astype(BF)
            hidden[:, cols] = low
            slope[:, cols] = tilt
            result = result + dot(low, down_w[cols, :], (1, 0))
        shown = jnp.where(ok, result, 0.0).astype(BF)
        put(shown)
        projected = dot(shown, align_w[...], (1, 0)) + align_b[...]
        target = pieced(step, source, parts, border, refs)
        miss = jnp.where(ok, projected - target, 0.0).astype(BF)
        add_vector(5, over_rows(miss.astype(F32)))
        align_acc[...] += dot(shown, miss, (0, 0))
        pulled = dot(miss, align_w[...], (1, 1)).astype(BF)
        pulled_wide = pulled.astype(F32)
        add_vector(4, over_rows(pulled_wide))
        grad_dense = None
        for piece in range(pieces):
            cols = slice(piece * width, (piece + 1) * width)
            grad_upper = dot(pulled, down_w[cols, :], (1, 1)) * slope[:, cols]
            low = grad_upper.astype(BF)
            vector_out[0:1, cols] += over_rows(low.astype(F32))
            down_acc[piece] += dot(hidden[:, cols], pulled, (0, 0))
            up_acc[piece] += dot(dense, low, (0, 0))
            term = dot(low, up_w[:, cols], (1, 1))
            grad_dense = term if grad_dense is None else grad_dense + term
        add_vector(2, over_rows(grad_dense * unit))
        add_vector(3, over_rows(grad_dense))
        grad_middle = pulled_wide + centre_back(grad_dense * vectors[5:6, :width], unit, inverse)
        grad_out[...] = grad_middle
        branch = grad_middle.astype(BF)
        add_vector(1, over_rows(branch.astype(F32)))
        out_acc[...] += dot(across, branch, (1, 0))
        pull_out[...] = dot(out_w[...], branch, (1, 1)).astype(BF)

    @pl.when(step == pl.num_programs(0) - 1)
    def _():
        groups, unit_rows = stage.shape[1:3]
        deep = pieces * unit_rows
        some, tall = stage_down.shape[1:3]

        def grouped(value):
            return value.reshape(groups, unit_rows, value.shape[-1])

        entries = []
        for piece in range(pieces):
            if groups >= pieces:
                target = sums_out.at[pl.ds(piece * some, some), pl.ds(0, tall), :]
            else:
                target = sums_out.at[:, pl.ds(piece * tall, tall), :]
            entries.append(
                (lambda piece=piece: down_acc[piece].reshape(some, tall, width), stage_down, down_sem, target)
            )
            target = sums_out.at[:, pl.ds(deep + piece * unit_rows, unit_rows), :]
            entries.append((lambda piece=piece: grouped(up_acc[piece]), stage, sem, target))
        begin = 2 * deep
        entries.append((lambda: grouped(out_acc[...]), stage, sem, sums_out.at[:, pl.ds(begin, unit_rows), :]))
        begin += unit_rows
        entries.append(
            (lambda: grouped(align_acc[:, :width]), stage, sem, sums_out.at[:, pl.ds(begin, unit_rows), :])
        )
        begin += unit_rows
        extra = teach - width
        third = unit_rows * extra // width
        for part in range(width // extra):
            entries.append(
                (
                    lambda part=part: grouped(align_acc[:, width:])[:, part * third : (part + 1) * third],
                    stage,
                    sem,
                    sums_out.at[:, pl.ds(begin, third), pl.ds(part * extra, extra)],
                )
            )
        write_out(entries)


def entry_kernel(tile, border, last, tile_len, source, count, index, *refs):
    (
        query_t, key_t, value_t, start_in, grad_in, weight_any, vectors,
        long_out, short_out, guest_out, vector_out, sums_out,
        weight_acc, position_acc, moved, stage, stage_rows, weight, weight_sem, rows_sem, show, show_sem, sem,
    ) = refs
    step = pl.program_id(0)
    width = weight.shape[0]
    live = step < count[last]

    @pl.when(step == 0)
    def _():
        load = pltpu.make_async_copy(weight_any, weight, weight_sem.at[0])
        load.start()
        weight_acc[...] = jnp.zeros_like(weight_acc)
        vector_out[...] = jnp.zeros_like(vector_out)

        def clear(number, carry):
            position_acc[pl.ds(pl.multiple_of(number * 64, 64), 64), :] = jnp.zeros((64, width), F32)
            return carry

        lax.fori_loop(0, position_acc.shape[0] // 64, clear, 0)
        left = position_acc.shape[0] % 64
        if left:
            position_acc[position_acc.shape[0] - left :, :] = jnp.zeros((left, width), F32)
        load.wait()

    def put(value):
        put_tiles(step, count[last + 2], value, source, border, tile, show, show_sem, long_out, short_out, guest_out)

    def over_rows(value):
        return jnp.sum(value, axis=0, keepdims=True)

    @pl.when(jnp.logical_not(live) & (step < count[last + 2]))
    def _():
        put(jnp.zeros((BLOCK, width), BF))

    @pl.when(live)
    def _():
        unit, inverse = centre(start_in[...])
        normed = (unit * vectors[0:1, :width] + vectors[1:2, :width]).astype(BF)
        grad_normed = None
        for part in range(3):
            cols = slice(part * width, (part + 1) * width)
            across = (query_t, key_t, value_t)[part][...]
            if part != 1:
                vector_out[part : part + 1, :] += over_rows(across.T.astype(F32))
            weight_acc[:, cols] += dot(normed, across, (0, 1))
            term = dot(across, weight[:, cols], (0, 1))
            grad_normed = term if grad_normed is None else grad_normed + term
        vector_out[1:2, :] += over_rows(grad_normed * unit)
        vector_out[3:4, :] += over_rows(grad_normed)
        grad_start = grad_in[...] + centre_back(grad_normed * vectors[0:1, :width], unit, inverse)
        put(grad_start.astype(BF))
        moved[...] = grad_start
        parts = BLOCK // tile

        def spread(number, carry):
            first = number * tile
            origin = source[step * parts + number] * tile

            def some(group, inner):
                base = pl.multiple_of(first + group * 8, 8)
                for row in range(8):
                    place = index[origin + group * 8 + row]
                    position_acc[pl.ds(place, 1), :] += moved[pl.ds(base + row, 1), :]
                return inner

            lax.fori_loop(0, lax.div(tile_len[step * parts + number] + 7, 8), some, 0)
            return carry

        lax.fori_loop(0, parts, spread, 0)

    @pl.when(step == pl.num_programs(0) - 1)
    def _():
        groups, unit_rows = stage.shape[1:3]
        depth, chunk = stage_rows.shape[:2]
        patches = position_acc.shape[0] - 8
        taken = patches // groups if groups > 1 else chunk
        begin = sums_out.shape[1] - 3 * unit_rows
        entries = []
        for part in range(3):
            cols = slice(part * width, (part + 1) * width)
            entries.append(
                (
                    lambda cols=cols: weight_acc[:, cols].reshape(groups, unit_rows, width),
                    stage,
                    sem,
                    sums_out.at[:, pl.ds(begin + part * unit_rows, unit_rows), :],
                )
            )
        write_out(entries)

        def copy(number):
            if groups > 1:
                target = sums_out.at[number, pl.ds(0, chunk), :]
            else:
                target = sums_out.at[0, pl.ds(pl.multiple_of(number * chunk, 16), chunk), :]
            slot = lax.rem(number, depth)
            return pltpu.make_async_copy(stage_rows.at[slot], target, rows_sem.at[slot])

        def drain(number, carry):
            @pl.when(number >= depth)
            def _():
                copy(number - depth).wait()

            stage_rows[lax.rem(number, depth)] = position_acc[
                pl.ds(pl.multiple_of(number * taken, 8), chunk), :
            ].astype(BF)
            copy(number).start()
            return carry

        chunks = patches // taken
        lax.fori_loop(0, chunks, drain, 0)
        for late in range(depth):
            copy(chunks - depth + late).wait()


def send_kernel(home, copies, short_len, destination, shown, out):
    base = (lax.axis_index("dp") * copies + lax.axis_index("rep")) * home
    out[...] = jnp.zeros_like(out)
    for slot in range(shown.shape[0]):
        micro, place = slot // home, base + slot % home

        @pl.when(short_len[micro, place] > 0)
        def _():
            out[destination[micro, place], micro] = shown[slot]


def finish_kernel(
    home, copies, flag, short_len, destination, count, got, early, late, vector, out_in, out_back, grad_in, grad_back,
    balanced, position_g, heads_g, out_g, up_g, down_g, align_g, *rest,
):
    *vector_outs, long_out, long_grad, carry, carry_sem, sem = rest
    tail = out_back.shape[0]
    swapped = count[flag] > 0
    backs = [
        pltpu.make_async_copy(ref, carry.at[number], carry_sem.at[number])
        for number, ref in enumerate((out_back, grad_back))
    ]
    homes = [
        pltpu.make_async_copy(
            carry.at[number], ref.at[pl.ds(ref.shape[0] - tail, tail), :], carry_sem.at[number]
        )
        for number, ref in enumerate((long_out, long_grad))
    ]

    @pl.when(swapped)
    def _():
        for copy in backs:
            copy.start()

    peers = got.shape[0]
    micros, bal = balanced.shape[:2]
    width = position_g.shape[1]
    unit_rows = out_g.shape[0]
    pieces = up_g.shape[1] // width
    d = lax.axis_index("dp")
    r = lax.axis_index("rep")
    number = 0
    found_all = []
    for micro in range(micros):
        for slot in range(bal):
            def look(peer, found):
                base = (peer * copies + r) * home
                for place in range(slot, home, bal):
                    fits = (short_len[micro, base + place] > 0) & (destination[micro, base + place] == d)
                    found = jnp.where(fits, peer, found)
                return found

            found = lax.fori_loop(0, peers, look, jnp.int32(-1))
            found_all.append(found)

            @pl.when(found >= 0)
            def _():
                pltpu.make_async_copy(
                    got.at[jnp.maximum(found, 0), micro], balanced.at[micro, slot], sem.at[number]
                ).start()

            @pl.when(found < 0)
            def _():
                balanced[micro, slot] = jnp.zeros(balanced.shape[2:], BF)

            number += 1
    position_g[...] = late[: position_g.shape[0], :].astype(F32)
    first = late.shape[0] - 3 * unit_rows
    for part in range(3):
        heads_g[:, part * width : (part + 1) * width] = late[
            first + part * unit_rows : first + (part + 1) * unit_rows, :
        ].astype(F32)
    deep = pieces * unit_rows
    down_g[...] = early[:deep, :].astype(F32)
    for part in range(pieces):
        up_g[:, part * width : (part + 1) * width] = early[
            deep + part * unit_rows : deep + (part + 1) * unit_rows, :
        ].astype(F32)
    out_g[...] = early[2 * deep : 2 * deep + unit_rows, :].astype(F32)
    align_g[:, :width] = early[2 * deep + unit_rows : 2 * deep + 2 * unit_rows, :].astype(F32)
    extra = align_g.shape[1] - width
    third = unit_rows * extra // width
    begin = 2 * deep + 2 * unit_rows
    for part in range(width // extra):
        align_g[part * third : (part + 1) * third, width:] = early[
            begin : begin + third, part * extra : (part + 1) * extra
        ].astype(F32)

    places = [(1, 0), (2, 0), (3, 0), (4, 0), (0, 1), (1, 1), (2, 1), (3, 1), (0, 0), (5, 0)]
    for target, (row, late_part) in zip(vector_outs, places):
        size = target.shape[1]
        first = d * size
        window = size if size % 128 == 0 else -(-size // 128) * 128 + 128
        begin = late_part * pieces * width
        origin = jnp.minimum(lax.div(first, 128) * 128, vector.shape[1] - begin - window)
        value = vector[:, pl.ds(pl.multiple_of(begin + origin, 128), window)]
        at = lax.broadcasted_iota(jnp.int32, (window, size), 0)
        want = lax.broadcasted_iota(jnp.int32, (window, size), 1) + (first - origin)
        chosen = jnp.where(at == want, 1.0, 0.0)
        picked = jnp.dot(value, chosen, preferred_element_type=F32, precision=lax.Precision.HIGHEST)
        target[...] = picked[row : row + 1]

    @pl.when(swapped)
    def _():
        for back, copy in zip(backs, homes):
            back.wait()
            copy.start()
        for copy in homes:
            copy.wait()

    for number, found in enumerate(found_all):
        @pl.when(found >= 0)
        def _():
            pltpu.make_async_copy(
                got.at[0, number // bal], balanced.at[number // bal, number % bal], sem.at[number]
            ).wait()


SMALL_NAMES = (
    "mixer_gain", "mixer_shift", "query_bias", "value_bias", "out_bias", "dense_gain", "dense_shift",
    "down_bias", "up_bias", "align_bias",
)


def whole(shape):
    return pl.BlockSpec(shape, lambda *_: (0,) * len(shape), pipeline_mode=pl.Buffered(1))


def params(**more):
    return pltpu.CompilerParams(vmem_limit_bytes=VMEM_LIMIT, **more)


def run_block(
    row_sources, index, target_sources, tile_len, source, count, lengths,
    tile, long_rows, micros, weights, groups, vectors, up_b, align_b,
):
    w = weights
    width = row_sources[0].shape[1]
    total = sum(held.shape[0] for held in row_sources)
    clips = micros + 1
    wide = w["up_weight"].shape[1]
    teach = target_sources[0].shape[1]
    patches = w["position"].shape[0]
    blocks = total // BLOCK
    parts = BLOCK // tile
    border = (micros * long_rows // tile, (total - long_rows) // tile)
    last = 2 * clips + 2
    pairs = HEADS // 2
    pair = width // pairs
    unit_rows = width // groups
    pieces = wide // width
    early_rows = (2 * pieces + 2) * unit_rows + unit_rows * (teach - width) // width
    early_rows = -(-early_rows // 512) * 512
    chunk = -(-(patches // groups) // 16) * 16 if groups > 1 else patches // 14
    late_rows = (chunk if groups > 1 else patches) + 3 * unit_rows
    def kept(i, count):
        return jnp.minimum(i, count[last] - 1)

    def tiles(sources):
        specs = []
        for first, held in zip((0,) + border, sources):
            most = held.shape[0] // tile - 1
            for part in range(parts):
                specs.append(
                    pl.BlockSpec(
                        (tile, held.shape[1]),
                        lambda i, tl, src, cnt, *_, part=part, first=first, most=most: (
                            jnp.clip(src[kept(i, cnt) * parts + part] - first, 0, most),
                            0,
                        ),
                    )
                )
        return specs, [held for held in sources for _ in range(parts)]

    row_specs, row_args = tiles(row_sources)
    target_specs, target_args = tiles(target_sources)

    by_block = lambda last_dim: pl.BlockSpec((BLOCK, last_dim), lambda i, tl, src, cnt, *_: (kept(i, cnt), 0))
    by_column = lambda first: pl.BlockSpec((first, BLOCK), lambda i, tl, src, cnt, *_: (0, kept(i, cnt)))
    guarded = lambda first: pl.BlockSpec(
        (first, BLOCK), lambda i, tl, src, cnt, *_: (0, jnp.minimum(i, cnt[last]))
    )
    anywhere = pl.BlockSpec(memory_space=pl.ANY)
    show = [
        pltpu.VMEM((2, BLOCK, width), BF),
        pltpu.SemaphoreType.DMA((2, parts)),
        pltpu.SemaphoreType.DMA((3,)),
    ]
    shown_shapes = [jax.ShapeDtypeStruct(held.shape, BF) for held in row_sources]

    triple_t, start = pl.pallas_call(
        partial(project_kernel, tile, border, last),
        grid_spec=pltpu.PrefetchScalarGridSpec(
            num_scalar_prefetch=4,
            grid=(blocks,),
            in_specs=row_specs + [anywhere, anywhere, whole(vectors.shape)],
            out_specs=[guarded(3 * width), by_block(width)],
            scratch_shapes=[
                pltpu.VMEM((patches, width), F32),
                pltpu.VMEM((4, patches // 14, width), BF),
                pltpu.VMEM((BLOCK, width), F32),
                pltpu.VMEM((width, 3 * width), BF),
                pltpu.SemaphoreType.DMA((1,)),
                pltpu.SemaphoreType.DMA((4,)),
            ],
        ),
        out_shape=[
            jax.ShapeDtypeStruct((3 * width, total), BF),
            jax.ShapeDtypeStruct((total, width), F32),
        ],
        compiler_params=params(),
        name="project",
    )(
        tile_len, source, count, index, *row_args,
        w["position"], w["heads_weight"], vectors,
    )

    def heads_spec(offset):
        return pl.BlockSpec((pair, total), lambda i, *_: (i + offset * pairs, 0))

    board = pltpu.VMEM((long_rows, BLOCK), F32)
    sums_spec = pl.BlockSpec((1, 2, total), lambda i, *_: (i, 0, 0))
    attended_t, sums = pl.pallas_call(
        partial(attend_kernel, tile, long_rows, clips),
        grid_spec=pltpu.PrefetchScalarGridSpec(
            num_scalar_prefetch=3,
            grid=(pairs,),
            in_specs=[heads_spec(0), heads_spec(1), heads_spec(2)],
            out_specs=[heads_spec(0), sums_spec],
            scratch_shapes=[board] * 2,
        ),
        out_shape=[
            jax.ShapeDtypeStruct((width, total), BF),
            jax.ShapeDtypeStruct((pairs, 2, total), F32),
        ],
        compiler_params=params(),
        name="attend",
    )(tile_len, lengths, count, triple_t, triple_t, triple_t)

    some = max(groups // pieces, 1)
    long_out, short_out, guest_out, pulled_t, grad_middle, vector, early = pl.pallas_call(
        partial(middle_kernel, tile, border, last),
        grid_spec=pltpu.PrefetchScalarGridSpec(
            num_scalar_prefetch=3,
            grid=(blocks,),
            in_specs=[by_column(width), by_block(width)]
            + target_specs
            + [
                anywhere, anywhere, anywhere, anywhere,
                whole(vectors.shape), whole(up_b.shape), whole(align_b.shape),
            ],
            out_specs=[
                anywhere, anywhere, anywhere, guarded(width), by_block(width), whole((8, wide)), anywhere,
            ],
            scratch_shapes=[
                pltpu.VMEM((width, width), F32),
                pltpu.VMEM((pieces, width, width), F32),
                pltpu.VMEM((pieces, width, width), F32),
                pltpu.VMEM((width, teach), F32),
                pltpu.VMEM((BLOCK, wide), BF),
                pltpu.VMEM((BLOCK, wide), F32),
                pltpu.VMEM((3, groups, unit_rows, width), BF),
                pltpu.VMEM((2, some, width // some, width), BF),
                pltpu.VMEM((width, width), BF),
                pltpu.VMEM((width, wide), BF),
                pltpu.VMEM((wide, width), BF),
                pltpu.VMEM((width, teach), BF),
                pltpu.SemaphoreType.DMA((4,)),
                pltpu.SemaphoreType.DMA((2,)),
            ]
            + show,
        ),
        out_shape=shown_shapes
        + [
            jax.ShapeDtypeStruct((width, total), BF),
            jax.ShapeDtypeStruct((total, width), F32),
            jax.ShapeDtypeStruct((8, wide), F32),
            jax.ShapeDtypeStruct((groups, early_rows, width), BF),
        ],
        compiler_params=params(),
        name="middle",
    )(
        tile_len, source, count, attended_t, start, *target_args,
        w["out_weight"], w["up_weight"], w["down_weight"], w["align_weight"], vectors, up_b, align_b,
    )

    grads = pl.pallas_call(
        partial(attend_back_kernel, tile, long_rows, clips),
        grid_spec=pltpu.PrefetchScalarGridSpec(
            num_scalar_prefetch=3,
            grid=(pairs,),
            in_specs=[heads_spec(0), heads_spec(1), heads_spec(2), heads_spec(0), sums_spec],
            out_specs=[heads_spec(0)] * 3,
            scratch_shapes=[pltpu.VMEM((pair, long_rows), F32)] * 2 + [board] * 4,
        ),
        out_shape=[jax.ShapeDtypeStruct((width, total), BF)] * 3,
        compiler_params=params(),
        name="attend_back",
    )(tile_len, lengths, count, triple_t, triple_t, triple_t, pulled_t, sums)

    long_grad, short_grad, guest_grad, entry_vector, late = pl.pallas_call(
        partial(entry_kernel, tile, border, last),
        grid_spec=pltpu.PrefetchScalarGridSpec(
            num_scalar_prefetch=4,
            grid=(blocks,),
            in_specs=[by_column(width)] * 3
            + [by_block(width), by_block(width), anywhere, whole(vectors.shape)],
            out_specs=[anywhere, anywhere, anywhere, whole((8, width)), anywhere],
            scratch_shapes=[
                pltpu.VMEM((width, 3 * width), F32),
                pltpu.VMEM((patches + 8, width), F32),
                pltpu.VMEM((BLOCK, width), F32),
                pltpu.VMEM((3, groups, unit_rows, width), BF),
                pltpu.VMEM((4, chunk, width), BF),
                pltpu.VMEM((width, 3 * width), BF),
                pltpu.SemaphoreType.DMA((1,)),
                pltpu.SemaphoreType.DMA((4,)),
            ]
            + show,
        ),
        out_shape=shown_shapes
        + [
            jax.ShapeDtypeStruct((8, width), F32),
            jax.ShapeDtypeStruct((groups, late_rows, width), BF),
        ],
        compiler_params=params(),
        name="entry",
    )(tile_len, source, count, index, *grads, start, grad_middle, w["heads_weight"], vectors)
    outs = (long_out, short_out, long_grad, short_grad)
    return outs, (guest_out, guest_grad), early, late, vector, entry_vector


def bit_of(number, bit):
    return lax.rem(number // (1 << bit), 2)


def reduce_plan(peers, early_rows, late_rows):
    bits = peers.bit_length() - 1
    forward = list(range(bits))
    swapped = forward[1::-1] + forward[2:]
    last = forward[2:] + forward[:2]
    pieces = []
    for source, rows in ((0, early_rows), (1, late_rows)):
        unit = 16
        units = rows // 2 // unit
        begin = 0
        for sub in range(2):
            here = units // 2 + (1 if sub < units % 2 else 0)
            first = int(here * 0.4 + 0.5)
            for order, parts in zip((forward, swapped, last), (first, first, here - 2 * first)):
                if parts > 0:
                    pieces.append((source * 2 + sub, source, begin, parts * unit, tuple(order)))
                    begin += parts * unit
    return pieces


def reduce_kernel(
    peers, halves, pieces, early, late, vector, entry_vector, early_out, late_out, vector_out, *scratch
):
    bits = peers.bit_length() - 1
    amount = len(pieces)
    kept = scratch[:amount]
    mates = scratch[amount : 2 * amount]
    mine_in = scratch[2 * amount : 3 * amount]
    landed = [scratch[3 * amount + k * bits : 3 * amount + (k + 1) * bits] for k in range(amount)]
    (
        vector_land, mate_send, mate_recv, load_sem, hop_send, hop_recv, end_send, end_recv, end_load,
        vector_send, vector_recv,
    ) = scratch[3 * amount + amount * bits :]
    d = lax.axis_index("dp")
    r = lax.axis_index("rep")
    other = 1 - r
    mate = (d, other)
    partner = [(d + (1 - 2 * bit_of(d, bit)) * (1 << bit), r) for bit in range(bits)]
    sources = (early, late)
    outs = (early_out, late_out)
    barrier = pltpu.get_barrier_semaphore()
    for device in [mate] + partner:
        pl.semaphore_signal(barrier, inc=1, device_id=device, device_id_type=pl.DeviceIdType.MESH)
    pl.semaphore_wait(barrier, bits + 1)

    def remote(source, target, send, recv, device):
        copy = pltpu.make_async_remote_copy(
            src_ref=source, dst_ref=target, send_sem=send, recv_sem=recv,
            device_id=device, device_id_type=pl.DeviceIdType.MESH,
        )
        copy.start()
        return copy

    def rows_at(source, core, begin, rows):
        return pl.ds(pl.multiple_of(core * halves[source] + begin, 16), rows)

    wide = vector.shape[1]
    vector_out[:, :wide] = vector[...]
    vector_out[:, wide:] = entry_vector[...]
    mate_copies = []
    loads = []
    for k, (_, source, begin, rows, order) in enumerate(pieces):
        mate_copies.append(
            remote(
                sources[source].at[:, rows_at(source, other, begin, rows), :], mates[k],
                mate_send.at[k], mate_recv.at[k], mate,
            )
        )
        load = pltpu.make_async_copy(
            sources[source].at[:, rows_at(source, r, begin, rows), :], mine_in[k], load_sem.at[k]
        )
        load.start()
        loads.append(load)

    hops = {}
    ends = []

    def base_at(order, stage):
        base = 0
        for place in range(stage):
            base = base + bit_of(d, order[place]) * (1 << (bits - 1 - place))
        return base

    def send(k, stage):
        _, source, begin, rows, order = pieces[k]
        if stage == bits:
            result = kept[k].at[base_at(order, bits)]
            where = rows_at(source, r, begin, rows)
            ends.append(remote(result, outs[source].at[where, :], end_send.at[k], end_recv.at[k], mate))
            own = pltpu.make_async_copy(result, outs[source].at[where, :], end_load.at[k])
            own.start()
            ends.append(own)
            return
        size = 1 << (bits - 1 - stage)
        first = base_at(order, stage) + (1 - bit_of(d, order[stage])) * size
        hops[k, stage] = remote(
            kept[k].at[pl.ds(first, size)], landed[k][stage], hop_send.at[k, stage], hop_recv.at[k, stage],
            partner[order[stage]],
        )

    def join(k):
        order = pieces[k][4]
        loads[k].wait()
        mate_copies[k].wait_recv()

        def add(chunk, carry):
            place = 0
            for step in range(bits):
                place = place + bit_of(chunk, order[step]) * (1 << (bits - 1 - step))
            kept[k][place] = mine_in[k][chunk] + mates[k][chunk]
            return carry

        lax.fori_loop(0, peers, add, 0)

    def gather(k, stage):
        order = pieces[k][4]
        hops[k, stage].wait_recv()
        base = base_at(order, stage + 1)

        def add(chunk, carry):
            kept[k][base + chunk] = kept[k][base + chunk] + landed[k][stage][chunk]
            return carry

        lax.fori_loop(0, 1 << (bits - 1 - stage), add, 0)

    events = sorted(
        (stage + pieces[k][0], -stage, k) for k in range(amount) for stage in range(bits + 1)
    )
    vector_copies = []

    def vector_step(stage):
        if stage > 0:
            vector_copies[-1].wait()
            vector_out[...] = vector_out[...] + vector_land[stage - 1]
        if stage <= bits:
            device = mate if stage == 0 else partner[stage - 1]
            vector_copies.append(
                remote(vector_out, vector_land.at[stage], vector_send.at[stage], vector_recv.at[stage], device)
            )

    seen = -1
    for time, negative, k in events:
        if time != seen:
            if time <= bits + 1:
                vector_step(time)
            seen = time
        stage = -negative
        if stage == 0:
            join(k)
        else:
            gather(k, stage - 1)
        send(k, stage)
    for copy in mate_copies + list(hops.values()):
        copy.wait_send()
    for copy in ends:
        copy.wait()


def reduce_all(early, late, vector, entry_vector):
    joined = (vector.shape[0], vector.shape[1] + entry_vector.shape[1])
    peers, early_rows, width = early.shape
    late_rows = late.shape[1]
    bits = peers.bit_length() - 1
    pieces = reduce_plan(peers, early_rows, late_rows)
    amount = len(pieces)
    scratch = [pltpu.VMEM((peers, rows, width), BF) for _, _, _, rows, _ in pieces] * 3
    for _, _, _, rows, _ in pieces:
        for stage in range(bits):
            scratch.append(pltpu.VMEM((1 << (bits - 1 - stage), rows, width), BF))
    scratch.append(pltpu.VMEM((bits + 1,) + joined, F32))
    one = pltpu.SemaphoreType.DMA((amount,))
    many = pltpu.SemaphoreType.DMA((amount, bits))
    few = pltpu.SemaphoreType.DMA((bits + 1,))
    scratch += [one, one, one, many, many, one, one, one, few, few]
    anywhere = pl.BlockSpec(memory_space=pl.ANY)
    near = pl.BlockSpec(memory_space=pltpu.VMEM)
    return pl.pallas_call(
        partial(reduce_kernel, peers, (early_rows // 2, late_rows // 2), pieces),
        in_specs=[anywhere, anywhere, near, near],
        out_specs=[anywhere, anywhere, near],
        out_shape=[
            jax.ShapeDtypeStruct((early_rows, width), BF),
            jax.ShapeDtypeStruct((late_rows, width), BF),
            jax.ShapeDtypeStruct(joined, F32),
        ],
        scratch_shapes=scratch,
        compiler_params=pltpu.CompilerParams(
            vmem_limit_bytes=VMEM_LIMIT, collective_id=0, has_side_effects=True
        ),
        name="reduce",
    )(early, late, vector, entry_vector)


def unpack(early, late, unit_rows, kept, teach, pieces):
    width = early.shape[1]
    deep = pieces * unit_rows

    def beside(held, first, count):
        return jnp.concatenate(
            [held[first + k * unit_rows : first + (k + 1) * unit_rows] for k in range(count)], axis=1
        )

    extra = teach - width
    third = unit_rows * extra // width
    begin = 2 * deep + 2 * unit_rows
    tail = early[begin : begin + third]
    tail = jnp.concatenate([tail[:, k * extra : (k + 1) * extra] for k in range(width // extra)], axis=0)
    return {
        "down_weight": early[:deep],
        "up_weight": beside(early, deep, pieces),
        "out_weight": early[2 * deep : 2 * deep + unit_rows],
        "align_weight": jnp.concatenate([early[2 * deep + unit_rows : begin], tail], axis=1),
        "position": late[:kept],
        "heads_weight": beside(late, late.shape[0] - 3 * unit_rows, 3),
    }


def shards(
    long_clips,
    short_clips,
    long_index,
    short_index,
    long_length,
    short_length,
    destination,
    long_target,
    short_target,
    position,
    mixer_gain,
    mixer_shift,
    heads_weight,
    query_bias,
    value_bias,
    out_weight,
    out_bias,
    dense_gain,
    dense_shift,
    up_weight,
    up_bias,
    down_weight,
    down_bias,
    align_weight,
    align_bias,
):
    peers = lax.axis_size("dp")
    copies = lax.axis_size("rep")
    micros, _, long_rows, width = long_clips.shape
    home_slots, tile = short_clips.shape[1:3]
    bal_slots = home_slots // 2
    slots = micros * home_slots
    wide = up_weight.shape[1]
    teach = long_target.shape[-1]
    patches = position.shape[0]
    weights = dict(
        zip(
            WEIGHT_NAMES,
            (
                position, mixer_gain, mixer_shift, heads_weight, query_bias, value_bias, out_weight, out_bias,
                dense_gain, dense_shift, up_weight, up_bias, down_weight, down_bias, align_weight, align_bias,
            ),
        )
    )
    scalars = pl.BlockSpec(memory_space=pltpu.SMEM)
    anywhere = pl.BlockSpec(memory_space=pl.ANY)
    clips = micros + 1
    tile_total = clips * long_rows // tile + slots
    near = pl.BlockSpec(memory_space=pltpu.VMEM)
    pairs = [(core, (core + 1) % copies) for core in range(copies)]

    def trade(value):
        return lax.ppermute(value, "rep", pairs)

    lengths = long_length.reshape(-1)
    facts = trade(jnp.concatenate([long_index[-1].reshape(-1), lengths]))
    guest_rows = trade(long_clips[-1, 0])
    guest_target = trade(long_target[-1, 0])
    tile_len, source, count, work, vectors, up_b, align_b = pl.pallas_call(
        partial(plan_kernel, tile, long_rows, home_slots, copies),
        in_specs=[scalars] * 3 + [near] * len(SMALL_NAMES),
        out_specs=[scalars] * 4 + [near] * 3,
        out_shape=[
            jax.ShapeDtypeStruct((tile_total,), jnp.int32),
            jax.ShapeDtypeStruct((tile_total,), jnp.int32),
            jax.ShapeDtypeStruct((2 * clips + 5,), jnp.int32),
            jax.ShapeDtypeStruct((clips,), jnp.int32),
            jax.ShapeDtypeStruct((len(SMALL_NAMES) - 2, width), F32),
            jax.ShapeDtypeStruct((1, wide), F32),
            jax.ShapeDtypeStruct((1, teach), F32),
        ],
        name="plan",
    )(long_length, facts[long_rows:], short_length, *[weights[name] for name in SMALL_NAMES])
    index = jnp.concatenate([long_index.reshape(-1), short_index.reshape(-1), facts[:long_rows]])
    groups = peers if copies == 2 and width % (16 * peers) == 0 else 1
    outs, guests, early, late, vector, entry_vector = run_block(
        (long_clips.reshape(-1, width), short_clips.reshape(-1, width), guest_rows), index,
        (long_target.reshape(-1, teach), short_target.reshape(-1, teach), guest_target),
        tile_len, source, count, work, tile, long_rows, micros, weights, groups, vectors, up_b, align_b,
    )
    long_out, short_out, long_grad, short_grad = outs
    out_back, grad_back = [trade(value) for value in guests]
    send = pl.pallas_call(
        partial(send_kernel, home_slots, copies),
        in_specs=[scalars, scalars, whole((slots, tile, width))],
        out_specs=pl.BlockSpec(memory_space=pltpu.VMEM) if groups == peers else scalars,
        out_shape=jax.ShapeDtypeStruct((peers, micros, tile, width), BF),
        compiler_params=params(),
        name="send",
    )(short_length, destination, short_out.reshape(slots, tile, width)) if groups == peers else send_all(
        short_length, destination, short_out.reshape(slots, tile, width), peers, copies, home_slots
    )
    got = lax.all_to_all(send, "dp", split_axis=0, concat_axis=0, tiled=True)
    unit_rows = width // peers
    if groups == peers:
        early, late, vector = reduce_all(early, late, vector, entry_vector)
    else:
        matrices = unpack(early[0], late[0], width, patches, teach, wide // width)
        early, late = share_out(matrices, peers, copies, unit_rows, wide // width)
        vector = lax.psum(jnp.concatenate([vector, entry_vector], axis=1), ("dp", "rep"))
    near = pl.BlockSpec(memory_space=pltpu.VMEM)
    outs = pl.pallas_call(
        partial(finish_kernel, home_slots, copies, 2 * clips + 3),
        in_specs=[scalars, scalars, scalars, anywhere, near, near, near] + [anywhere] * 4,
        out_specs=[near] * 17 + [anywhere] * 2,
        input_output_aliases={7: 17, 9: 18},
        out_shape=[
            jax.ShapeDtypeStruct((micros, bal_slots, tile, width), BF),
            jax.ShapeDtypeStruct((patches // peers, width), F32),
            jax.ShapeDtypeStruct((unit_rows, 3 * width), F32),
            jax.ShapeDtypeStruct((unit_rows, width), F32),
            jax.ShapeDtypeStruct((unit_rows, wide), F32),
            jax.ShapeDtypeStruct((wide // peers, width), F32),
            jax.ShapeDtypeStruct((unit_rows, teach), F32),
        ]
        + [jax.ShapeDtypeStruct((1, unit_rows), F32)] * 8
        + [jax.ShapeDtypeStruct((1, wide // peers), F32), jax.ShapeDtypeStruct((1, teach // peers), F32)]
        + [jax.ShapeDtypeStruct(long_out.shape, BF)] * 2,
        scratch_shapes=[
            pltpu.VMEM((2, long_rows, width), BF),
            pltpu.SemaphoreType.DMA((2,)),
            pltpu.SemaphoreType.DMA((micros * bal_slots,)),
        ],
        compiler_params=params(),
        name="finish",
    )(short_length, destination, count, got, early, late, vector, long_out, out_back, long_grad, grad_back)
    short_bal, position_g, heads_g, out_g, up_g, down_g, align_g = outs[:7]
    shared = {
        "position": position_g, "heads_weight": heads_g, "out_weight": out_g, "up_weight": up_g,
        "down_weight": down_g, "align_weight": align_g,
    }
    long_out, long_grad = outs[17:]
    order = (
        "out_bias", "dense_gain", "dense_shift", "down_bias", "query_bias", "mixer_gain", "value_bias",
        "mixer_shift", "up_bias", "align_bias",
    )
    for name, value in zip(order, outs[7:17]):
        shared[name] = value.reshape(-1)
    return (
        long_out.reshape(micros, 1, long_rows, width),
        short_bal,
        long_grad.reshape(micros, 1, long_rows, width),
        short_grad.reshape(micros, home_slots, tile, width),
    ) + tuple(shared[name] for name in WEIGHT_NAMES)


def send_all(short_length, destination, shown, peers, copies, home):
    micros = short_length.shape[0]
    mine = lax.axis_index("dp") * copies + lax.axis_index("rep")

    def own(table):
        table = table.reshape(micros, peers * copies, home)
        return lax.dynamic_index_in_dim(table, mine, 1, keepdims=False)

    wanted = (own(destination)[None] == jnp.arange(peers)[:, None, None]) & (own(short_length)[None] > 0)
    shown = shown.reshape((micros, home) + shown.shape[1:])
    return jnp.einsum("pmj,mjtd->pmtd", wanted.astype(BF), shown)


def share_out(matrices, peers, copies, unit_rows, pieces):
    shared = {}
    for name, piece in matrices.items():
        rows = piece.shape[0] // peers
        padded = -(-rows // (8 * copies)) * 8 * copies
        if padded != rows:
            piece = piece.reshape(peers, rows, -1)
            piece = jnp.pad(piece, ((0, 0), (0, padded - rows), (0, 0)))
            piece = piece.reshape(peers * padded, -1)
        piece = lax.psum_scatter(piece, ("dp", "rep"), scatter_dimension=0, tiled=True)
        shared[name] = lax.all_gather(piece, "rep", axis=0, tiled=True)[:rows]
    width = shared["out_weight"].shape[1]
    up = shared["up_weight"].reshape(unit_rows, pieces, width).transpose(1, 0, 2).reshape(-1, width)
    heads = shared["heads_weight"].reshape(unit_rows, 3, width).transpose(1, 0, 2).reshape(-1, width)
    align = shared["align_weight"]
    extra = align.shape[1] - width
    parts = width // extra
    tail = align[:, width:].reshape(parts, unit_rows // parts, extra).transpose(1, 0, 2).reshape(-1, width)
    early = jnp.concatenate([shared["down_weight"], up, shared["out_weight"], align[:, :width], tail], axis=0)
    return early, jnp.concatenate([shared["position"], heads], axis=0)


def solution(mesh):
    placed = (
        P(None, ("dp", "rep"), None, None),
        P(None, ("dp", "rep"), None, None),
        P(None, ("dp", "rep"), None),
        P(None, ("dp", "rep"), None),
        P(None, ("dp", "rep")),
        P(),
        P(),
        P(None, ("dp", "rep"), None, None),
        P(None, ("dp", "rep"), None, None),
        P(),
        P(),
        P(),
        P(),
        P(),
        P(),
        P(),
        P(),
        P(),
        P(),
        P(),
        P(),
        P(),
        P(),
        P(),
        P(),
    )
    return jax.shard_map(
        shards,
        mesh=mesh,
        in_specs=placed,
        out_specs=(
            P(None, ("dp", "rep"), None, None),
            P(None, ("dp", "rep"), None, None),
            P(None, ("dp", "rep"), None, None),
            P(None, ("dp", "rep"), None, None),
            P("dp", None),
            P("dp"),
            P("dp"),
            P("dp", None),
            P("dp"),
            P("dp"),
            P("dp", None),
            P("dp"),
            P("dp"),
            P("dp"),
            P("dp", None),
            P("dp"),
            P("dp", None),
            P("dp"),
            P("dp", None),
            P("dp"),
        ),
        check_vma=False,
    )
```
